32 devices in a mesh: fsdp: 8 (over z, y), seq: 4 (over x, core).
Axes of the slice: x: 2, y: 2, z: 4, core: 2. Of those that a mesh axis runs over, the one named last changes fastest.
Arguments:
- tokens: bfloat16 [2, 8, 1024, 1024], P(None, 'fsdp', 'seq'), may hold values from -6 to 6
- doc_lengths: int32 [2, 8, 16], P(None, 'fsdp'), may hold values from 1 to 256, 1024 in all within a row
- cotangent: bfloat16 [2, 8, 1024, 1024], P(None, 'fsdp', 'seq'), may hold values from -6 to 6
- query_weight: bfloat16 [2, 1024, 1024], P(None, ('fsdp', 'seq')), may hold values from -0.1875 to 0.1875
- key_weight: bfloat16 [2, 1024, 1024], P(None, ('fsdp', 'seq')), may hold values from -0.1875 to 0.1875
- value_weight: bfloat16 [2, 1024, 1024], P(None, ('fsdp', 'seq')), may hold values from -0.1875 to 0.1875
- mix_weight: bfloat16 [2, 1024, 1024], P(None, ('fsdp', 'seq')), may hold values from -0.75 to 0.75
- query_bias: bfloat16 [2, 1024], P(None, ('fsdp', 'seq')), may hold values from -3 to 3
- value_bias: bfloat16 [2, 1024], P(None, ('fsdp', 'seq')), may hold values from -1.1953125 to 1.1953125
- mix_bias: bfloat16 [2, 1024], P(None, ('fsdp', 'seq')), may hold values from -1.796875 to 1.796875
- first_gain: bfloat16 [2, 1024], P(None, ('fsdp', 'seq')), may hold values from 0.5 to 1.5
- first_shift: bfloat16 [2, 1024], P(None, ('fsdp', 'seq')), may hold values from -1.796875 to 1.796875
- inner_weight: bfloat16 [2, 1024, 4096], P(None, ('fsdp', 'seq')), may hold values from -0.1875 to 0.1875
- inner_bias: bfloat16 [2, 4096], P(None, ('fsdp', 'seq')), may hold values from -1.796875 to 1.796875
- outer_weight: bfloat16 [2, 4096, 1024], P(None, ('fsdp', 'seq')), may hold values from -0.125 to 0.125
- outer_bias: bfloat16 [2, 1024], P(None, ('fsdp', 'seq')), may hold values from -1.796875 to 1.796875
- second_gain: bfloat16 [2, 1024], P(None, ('fsdp', 'seq')), may hold values from 0.5 to 1.5
- second_shift: bfloat16 [2, 1024], P(None, ('fsdp', 'seq')), may hold values from -1.796875 to 1.796875
Outputs:
- activations: float32 [2, 8, 1024, 1024], P(None, 'fsdp', 'seq')
- token_grad: float32 [2, 8, 1024, 1024], P(None, 'fsdp', 'seq')
- weight_query: float32 [2, 1024, 1024], P(None, ('fsdp', 'seq'))
- weight_key: float32 [2, 1024, 1024], P(None, ('fsdp', 'seq'))
- weight_value: float32 [2, 1024, 1024], P(None, ('fsdp', 'seq'))
- weight_mix: float32 [2, 1024, 1024], P(None, ('fsdp', 'seq'))
- bias_query: float32 [2, 1024], P(None, ('fsdp', 'seq'))
- bias_value: float32 [2, 1024], P(None, ('fsdp', 'seq'))
- bias_mix: float32 [2, 1024], P(None, ('fsdp', 'seq'))
- gain_first: float32 [2, 1024], P(None, ('fsdp', 'seq'))
- shift_first: float32 [2, 1024], P(None, ('fsdp', 'seq'))
- weight_inner: float32 [2, 1024, 4096], P(None, ('fsdp', 'seq'))
- bias_inner: float32 [2, 4096], P(None, ('fsdp', 'seq'))
- weight_outer: float32 [2, 4096, 1024], P(None, ('fsdp', 'seq'))
- bias_outer: float32 [2, 1024], P(None, ('fsdp', 'seq'))
- gain_second: float32 [2, 1024], P(None, ('fsdp', 'seq'))
- shift_second: float32 [2, 1024], P(None, ('fsdp', 'seq'))
The draws below stay inside these ranges and needn't reach their ends.
Inputs may be any that keep to these rules, and one draw needn't show every extreme that they name: `doc_lengths`: in each packed row the first 15 entries are the documents in order and the last is padding at the row's end; the entries sum to 1024 and the largest is 256.
All inputs are finite; a program needn't handle non-finite values.
Results may differ from the reference program's by a relative error of at most 0.024.
Values may be sent and summed in bfloat16 or wider, within the bound.
No kernel may reach another device: no remote copies, remote signals or barrier semaphores. Data moves between devices by JAX's collectives and lax.ppermute only.
A program may use at most 384 MiB of HBM per device.

```python
import math
import jax
import jax.numpy as jnp
import numpy as np
from jax import lax

D = 1024
HEADS = 16
HEAD_DIM = 64
FF = 4096
LAYERS = 2
MICRO = 2
SEQ_LEN = 1024
NDOC = 16
MOST_DOC = 256
ROWS = 8


def with_spikes(result, stream_key, source, target, shards_of, factor):
    owner, partner = [(jnp.arange(result.shape[dim]) // (result.shape[dim] // shards_of)).reshape([-1 if axis == dim else 1 for axis in range(result.ndim)]) for dim in (source, target)]
    chosen = jax.random.permutation(stream_key, shards_of)[partner]
    strong = (owner == chosen) | (owner == (partner + shards_of // 2) % shards_of)
    return jnp.where(strong, factor * result, result)


def shard_levels(stream_key, dims, cuts, least, top_value):
    def one(position, shards_of):
        heights = jax.random.uniform(jax.random.fold_in(jax.random.fold_in(stream_key, 6), position), (shards_of,), jnp.float32, least / len(cuts), top_value / len(cuts))
        return jnp.repeat(jnp.exp(heights), dims[position] // shards_of).reshape((-1,) + (1,) * (len(dims) - position - 1))

    factor_of = one(*cuts[0])
    for cut in cuts[1:]:
        factor_of = factor_of * one(*cut)
    return factor_of


def profile(number_of, total, reach, lean):
    portions = [(1 << 20) // math.isqrt(standing ** lean) + 1 for standing in range(2, number_of + 1)]
    surplus, given = total - reach - (number_of - 1), [1] * (number_of - 1)
    while surplus > 0:
        free = [i for i in range(number_of - 1) if given[i] < reach]
        pool, left = sum([portions[i] for i in free]), surplus
        for i in free:
            extra = min(reach - given[i], max(1, left * portions[i] // pool), surplus)
            given[i] = given[i] + extra
            surplus = surplus - extra
    return np.array([reach] + given)


def ragged(rng, amount, total, limit, lean):
    if amount == 2:
        one = jax.random.randint(rng, (), max(1, total - limit), min(limit, total - 1) + 1)
        return jnp.stack([one, total - one])
    tallies = jnp.asarray(profile(amount, total, limit, lean), jnp.int32)
    twos = (amount - 1) // 2
    donor, receiver = tallies[1:1 + 2 * twos:2], tallies[2:2 + 2 * twos:2]
    room = jnp.minimum(donor - 1, limit - receiver)
    shifted = jax.random.randint(jax.random.fold_in(rng, 1), (twos,), 0, 1 << 20) % (room + 1)
    tallies = tallies.at[1:1 + 2 * twos:2].set(donor - shifted).at[2:2 + 2 * twos:2].set(receiver + shifted)
    return tallies[jax.random.permutation(jax.random.fold_in(rng, 2), amount)]


def noise(key, extent, width, reach, split=(), held_as=jnp.bfloat16):
    result = jax.random.normal(key, extent, jnp.float32) * width
    if len(split) > 0:
        result = shard_levels(key, extent, split, -0.22, 0.18) * result
    return jnp.clip(result, min=-reach, max=reach).astype(held_as)


def gaussian_with(key, shape, scale, bound, split, heavy, kind=jnp.bfloat16):
    result = scale * jax.random.normal(key, shape, jnp.float32)
    if split:
        result = result * shard_levels(key, shape, split, -0.22, 0.18)
    return jnp.clip(with_spikes(result, jax.random.fold_in(key, 3), *heavy), -bound, bound).astype(kind)


def setup_inputs(seed: int = 0) -> dict:
    arg_keys = jax.random.split(jax.random.key(seed), 19)
    tokens = gaussian_with(arg_keys[0], (MICRO, ROWS, SEQ_LEN, D), 1.0, 6.0, ((1, 8), (2, 4)), (1, 3, 8, 2.0))
    doc_lengths = jax.vmap(lambda own: ragged(own, NDOC, SEQ_LEN, MOST_DOC, 2))(jax.random.split(arg_keys[1], MICRO * ROWS)).reshape((MICRO, ROWS, NDOC)).astype(jnp.int32)
    cotangent = noise(arg_keys[2], (MICRO, ROWS, SEQ_LEN, D), 1.0, 6.0, ((1, 8), (2, 4)))
    query_weight = noise(arg_keys[3], (LAYERS, D, D), D ** -0.5, 0.1875, ((1, 32),))
    key_weight = noise(arg_keys[4], (LAYERS, D, D), D ** -0.5, 0.1875, ((1, 32),))
    value_weight = noise(arg_keys[5], (LAYERS, D, D), D ** -0.5, 0.1875, ((1, 32),))
    mix_weight = noise(arg_keys[6], (LAYERS, D, D), (D // 16) ** -0.5, 0.75, ((1, 32),))
    query_bias = noise(arg_keys[7], (LAYERS, D), 0.5, 3.0, ((1, 32),))
    value_bias = noise(arg_keys[8], (LAYERS, D), 0.2, 1.1953125, ((1, 32),))
    mix_bias = noise(arg_keys[9], (LAYERS, D), 0.3, 1.796875, ((1, 32),))
    first_gain = jnp.clip(1.0 + 0.1 * jax.random.normal(arg_keys[10], (LAYERS, D), jnp.float32), 0.5, 1.5).astype(jnp.bfloat16)
    first_shift = noise(arg_keys[11], (LAYERS, D), 0.3, 1.796875, ((1, 32),))
    inner_weight = noise(arg_keys[12], (LAYERS, D, FF), D ** -0.5, 0.1875, ((1, 32),))
    inner_bias = noise(arg_keys[13], (LAYERS, FF), 0.3, 1.796875, ((1, 32),))
    outer_weight = noise(arg_keys[14], (LAYERS, FF, D), (FF // 2) ** -0.5, 0.125, ((1, 32),))
    outer_bias = noise(arg_keys[15], (LAYERS, D), 0.3, 1.796875, ((1, 32),))
    second_gain = jnp.clip(1.0 + 0.1 * jax.random.normal(arg_keys[16], (LAYERS, D), jnp.float32), 0.5, 1.5).astype(jnp.bfloat16)
    second_shift = noise(arg_keys[17], (LAYERS, D), 0.3, 1.796875, ((1, 32),))
    return {"tokens": tokens, "doc_lengths": doc_lengths, "cotangent": cotangent, "query_weight": query_weight, "key_weight": key_weight, "value_weight": value_weight, "mix_weight": mix_weight, "query_bias": query_bias, "value_bias": value_bias, "mix_bias": mix_bias, "first_gain": first_gain, "first_shift": first_shift, "inner_weight": inner_weight, "inner_bias": inner_bias, "outer_weight": outer_weight, "outer_bias": outer_bias, "second_gain": second_gain, "second_shift": second_shift}


@jax.custom_vjp
def low(v):
    return lax.optimization_barrier(v.astype(jnp.bfloat16)).astype(jnp.float32)

@jax.custom_vjp
def low_back(v):
    return v

def low_keep(v):
    return (low(v), None)

def low_pass(kept, grad):
    return (grad,)

def back_keep(v):
    return (v, None)

def back_low(kept, grad):
    return (low(grad),)
low.defvjp(low_keep, low_pass)
low_back.defvjp(back_keep, back_low)
epsilon = 1e-05
highest = lax.Precision.HIGHEST

def product(left, right):
    return jnp.dot(left, right, precision=highest)

def layer_norm(total, gain, shift):
    center = lax.optimization_barrier(jnp.mean(total, axis=-1, keepdims=True))
    centered = total - center
    spread = lax.optimization_barrier(jnp.mean(centered * centered, axis=-1, keepdims=True))
    return centered * lax.rsqrt(spread + epsilon) * gain + shift

def segments_of(lengths):
    bounds = jnp.cumsum(lengths, axis=-1).astype(jnp.int32)
    places = jnp.arange(SEQ_LEN, dtype=jnp.int32)
    return lax.optimization_barrier(jnp.sum((places[:, None] >= bounds[None, :]).astype(jnp.int32), axis=1))

def allowed_of(segment):
    places = jnp.arange(SEQ_LEN, dtype=jnp.int32)
    same = (segment[:, None] == segment[None, :]) & (segment[None, :] != NDOC - 1)
    return same | (places[:, None] == places[None, :])

@jax.checkpoint
def attend(queries, key_rows, values, allowed):
    query_heads = queries.reshape(SEQ_LEN, HEADS, HEAD_DIM)
    key_heads = key_rows.reshape(SEQ_LEN, HEADS, HEAD_DIM)
    value_heads = values.reshape(SEQ_LEN, HEADS, HEAD_DIM)
    scores = jnp.einsum('qhd,khd->hqk', query_heads, key_heads, precision=highest) * HEAD_DIM ** (-0.5)
    scores = low_back(scores)
    scores = jnp.where(allowed[None], scores, -1e+30)
    top_score = lax.optimization_barrier(jnp.max(scores, axis=-1, keepdims=True))
    raised = jnp.exp(scores - top_score)
    shares = raised / lax.optimization_barrier(jnp.sum(raised, axis=-1, keepdims=True))
    mixed = jnp.einsum('hqk,khd->qhd', low(shares), value_heads, precision=highest)
    return mixed.reshape(SEQ_LEN, D)

def layer(stream, layer_params, allowed):
    query_weight, key_weight, value_weight, mix_weight, query_bias, value_bias, mix_bias, first_gain, first_shift, inner_weight, inner_bias, outer_weight, outer_bias, second_gain, second_shift = layer_params
    stream_low = low(stream)
    queries = low_back(low(product(stream_low, query_weight) + query_bias))
    key_rows = low_back(low(product(stream_low, key_weight)))
    values = low_back(low(product(stream_low, value_weight) + value_bias))
    mixed = low_back(low(attend(queries, key_rows, values, allowed)))
    branch = low_back(product(mixed, mix_weight) + mix_bias)
    first = layer_norm(stream + branch, first_gain, first_shift)
    inner = low_back(product(low(first), inner_weight) + inner_bias)
    active = low(jax.nn.gelu(inner, approximate=False))
    second = low_back(product(active, outer_weight) + outer_bias)
    return layer_norm(first + second, second_gain, second_shift)

def reference(tokens, doc_lengths, cotangent, query_weight, key_weight, value_weight, mix_weight, query_bias, value_bias, mix_bias, first_gain, first_shift, inner_weight, inner_bias, outer_weight, outer_bias, second_gain, second_shift):
    params = tuple((tensor.astype(jnp.float32) for tensor in (query_weight, key_weight, value_weight, mix_weight, query_bias, value_bias, mix_bias, first_gain, first_shift, inner_weight, inner_bias, outer_weight, outer_bias, second_gain, second_shift)))
    stream_rows = tokens.reshape(-1, SEQ_LEN, D).astype(jnp.float32)
    upstream_rows = cotangent.reshape(-1, SEQ_LEN, D).astype(jnp.float32)
    length_rows = doc_lengths.reshape(-1, NDOC)

    def one_row(totals, item):
        stream, upstream, lengths = item
        allowed = allowed_of(segments_of(lengths))

        def forward(start, weights):
            current = start
            for layer_index in range(LAYERS):
                current = layer(current, tuple((tensor[layer_index] for tensor in weights)), allowed)
            return current
        outputs, pullback = jax.vjp(forward, stream, params)
        stream_grad, param_grads = pullback(upstream)
        return (jax.tree.map(jnp.add, totals, param_grads), (outputs, stream_grad))
    zeros = jax.tree.map(jnp.zeros_like, params)
    totals, (outputs, stream_grads) = lax.scan(one_row, zeros, (stream_rows, upstream_rows, length_rows))
    activations = outputs.reshape(tokens.shape)
    token_grad = stream_grads.reshape(tokens.shape)
    return (activations, token_grad, totals[0], totals[1], totals[2], totals[3], totals[4], totals[5], totals[6], totals[7], totals[8], totals[9], totals[10], totals[11], totals[12], totals[13], totals[14])
```

```python
import math

import jax
import jax.numpy as jnp
from jax import lax
from jax.experimental import pallas as pl
from jax.experimental.pallas import tpu as pltpu
from jax.sharding import PartitionSpec as P

D = 1024
FF = 4096
HEAD_DIM = 64
HEADS = D // HEAD_DIM
SEQ_LEN = 1024
NDOC = 16
epsilon = 1e-05
AXES = ("fsdp", "seq")
f32 = jnp.float32
bf16 = jnp.bfloat16


def dot(left, right):
    return jnp.dot(left, right, preferred_element_type=f32)


def contract_rows(left, right):
    return lax.dot_general(left, right, (((0,), (0,)), ((), ())), preferred_element_type=f32)


def contract_cols(left, right):
    return lax.dot_general(left, right, (((1,), (1,)), ((), ())), preferred_element_type=f32)


def tie(value, *others):
    return lax.optimization_barrier((value, others))[0]


def pairs(move):
    out = []
    for i in range(32):
        z, y, x, c = i // 8, i // 4 % 2, i // 2 % 2, i % 2
        z, y, x, c = move(z, y, x, c)
        out.append((i, z * 8 + y * 4 + x * 2 + c))
    return out


TO_CORE = pairs(lambda z, y, x, c: (z, y, x, 1 - c))
TO_X = pairs(lambda z, y, x, c: (z, y, 1 - x, c))
TO_Y = pairs(lambda z, y, x, c: (z, 1 - y, x, c))
TO_Z = [pairs(lambda z, y, x, c, k=k: ((z + k) % 4, y, x, c)) for k in range(4)]


def send(value, to):
    return lax.ppermute(value, AXES, to)


def coordinates():
    fsdp, seq = lax.axis_index("fsdp"), lax.axis_index("seq")
    return jnp.stack([fsdp // 2, fsdp % 2, seq // 2, seq % 2]).astype(jnp.int32)


def place(coords, pieces, shapes, moves):
    count = len(moves(0, 0, 0, 0, None, None))

    total = len(pieces)

    def kernel(coords_ref, *refs):
        sources, targets = refs[:total], refs[total : total + len(shapes)]
        buffers, in_sems, out_sems = refs[total + len(shapes) : -2], refs[-2], refs[-1]
        loads = [
            pltpu.make_async_copy(source, buffer, in_sems.at[n])
            for n, (source, buffer) in enumerate(zip(sources, buffers))
        ]
        for load in loads:
            load.start()
        todo = moves(coords_ref[0], coords_ref[1], coords_ref[2], coords_ref[3], buffers, targets)
        stores = [
            (n, pltpu.make_async_copy(view, target, out_sems.at[k]))
            for k, (n, view, target) in enumerate(todo)
        ]
        for piece, load in enumerate(loads):
            load.wait()
            for n, store in stores:
                if n == piece:
                    store.start()
        for _, store in stores:
            store.wait()

    size = sum(math.prod(shape) for shape in shapes) * 4
    return pl.pallas_call(
        kernel,
        in_specs=[pl.BlockSpec(memory_space=pltpu.SMEM)]
        + [pl.BlockSpec(memory_space=pl.ANY)] * len(pieces),
        out_specs=[pl.BlockSpec(memory_space=pl.ANY)] * len(shapes),
        out_shape=[jax.ShapeDtypeStruct(shape, bf16) for shape in shapes],
        scratch_shapes=[pltpu.VMEM(p.shape, bf16) for p in pieces]
        + [pltpu.SemaphoreType.DMA((total,)), pltpu.SemaphoreType.DMA((count,))],
        compiler_params=pltpu.CompilerParams(vmem_limit_bytes=40 << 20),
        cost_estimate=pl.CostEstimate(flops=0, bytes_accessed=size, transcendentals=0),
    )(coords, *pieces)


class Gather:
    def __init__(self, coords):
        self.coords = coords
        self.last_z = ()
        self.last_xy = ()

    def __call__(self, pack, split, shapes, routed):
        rows, width = pack.shape
        if self.last_z:
            pack = tie(pack, *self.last_z)
        from_z = [pack] + [send(pack, TO_Z[4 - k]) for k in (1, 2, 3)]
        self.last_z = from_z[1:]
        sizes = (split, rows - split)

        def by_z(z, y, x, c, src, dst):
            return [
                (k, src and src[k].at[lo : lo + n], dst and dst[r].at[(z + k) % 4])
                for k in range(4)
                for r, (lo, n) in enumerate(zip((0, split), sizes))
            ]

        first, second = place(self.coords, from_z, [(4, n, width) for n in sizes], by_z)
        if self.last_xy:
            first, second = tie((first, second), *self.last_xy)
        first_y, second_x = send(first, TO_Y), send(second, TO_X)

        def by_two(z, y, x, c, src, dst):
            return [
                (0, src and src[0], dst and dst[0].at[:, y]),
                (1, src and src[1], dst and dst[0].at[:, 1 - y]),
                (2, src and src[2], dst and dst[1].at[:, x]),
                (3, src and src[3], dst and dst[1].at[:, 1 - x]),
            ]

        first, second = place(
            self.coords,
            [first, first_y, second, second_x],
            [(4, 2, n, width) for n in sizes],
            by_two,
        )
        first_x, second_y = send(first, TO_X), send(second, TO_Y)
        self.last_xy = (first_x, second_y)
        first_c, second_c = send(first, TO_CORE), send(second, TO_CORE)
        first_xc, second_yc = send(first_x, TO_CORE), send(second_y, TO_CORE)

        def by_block(z, y, x, c, src, dst):
            out = []
            for n, (x2, c2) in enumerate(((x, c), (1 - x, c), (x, 1 - c), (1 - x, 1 - c))):
                for lo, hi, target, column in routed[0]:
                    for z2 in range(4):
                        out.append(
                            (
                                n,
                                src and src[n].at[z2, :, lo:hi],
                                dst
                                and dst[target].at[
                                    z2, :, x2, c2, :, column * width : (column + 1) * width
                                ],
                            )
                        )
            for n, (y2, c2) in enumerate(((y, c), (1 - y, c), (y, 1 - c), (1 - y, 1 - c))):
                for lo, hi, target, column in routed[1]:
                    for z2 in range(4):
                        out.append(
                            (
                                4 + n,
                                src and src[4 + n].at[z2, :, lo:hi],
                                dst
                                and dst[target].at[
                                    z2, y2, :, c2, :, column * width : (column + 1) * width
                                ],
                            )
                        )
            return out

        return place(
            self.coords,
            [first, first_x, first_c, first_xc, second, second_y, second_c, second_yc],
            [(4, 2, 2, 2) + shape for shape in shapes],
            by_block,
        )


def pick(value, index, axis):
    return lax.dynamic_index_in_dim(value, index, axis, keepdims=False)


def summed_shards(coords, grads, x_first):
    z, y, x, c = coords[0], coords[1], coords[2], coords[3]
    blocks = [g.reshape(16, 2, g.shape[0] // 32, g.shape[1]) for g in grads]

    def joined(index):
        return jnp.concatenate([pick(b, index, 1) for b in blocks], axis=1)

    other = send(joined(1 - c).astype(bf16), TO_CORE)
    own = joined(c)
    rows, width = own.shape[1:]
    own = own.reshape(4, 2, 2, rows, width)
    other = other.reshape(4, 2, 2, rows, width)
    axis, index, to = (2, x, TO_X) if x_first else (1, y, TO_Y)

    def total(where):
        return pick(own, where, axis).astype(f32) + pick(other, where, axis).astype(f32)

    own, other = total(index), send(total(1 - index).astype(bf16), to)
    index, to = (y, TO_Y) if x_first else (x, TO_X)

    def total_two(where):
        return pick(own, where, 1).astype(f32) + pick(other, where, 1).astype(f32)

    other2 = send(total_two(1 - index).astype(bf16), to)
    quarter = total_two(index) + other2.astype(f32)
    result = pick(quarter, z, 0)
    for k in (1, 2, 3):
        result = result + send(pick(quarter, (z + k) % 4, 0).astype(bf16), TO_Z[k]).astype(f32)
    parts, start = [], 0
    for g in grads:
        size = g.shape[0] // 32
        parts.append(result[start : start + size])
        start += size
    return parts


def norm_forward(total):
    center = jnp.mean(total, axis=-1, keepdims=True)
    centered = total - center
    spread = jnp.mean(centered * centered, axis=-1, keepdims=True)
    scale = lax.rsqrt(spread + epsilon)
    return centered * scale, scale


def norm_backward(total, gain, upstream):
    unit, scale = norm_forward(total)
    lifted = upstream * gain
    grad = scale * (
        lifted
        - jnp.mean(lifted, axis=-1, keepdims=True)
        - unit * jnp.mean(lifted * unit, axis=-1, keepdims=True)
    )
    return grad, jnp.sum(upstream * unit, axis=0), jnp.sum(upstream, axis=0)


def column_sum(values):
    return jnp.sum(values.astype(f32), axis=0)


def heads_of(rows):
    return rows.reshape(rows.shape[0], HEADS, HEAD_DIM)


def masked_scores(queries, keys, allowed):
    scores = jnp.einsum("qhd,khd->hqk", queries, keys, preferred_element_type=f32)
    return jnp.where(allowed[None], scores * HEAD_DIM ** (-0.5), -1e30)


def attend_forward(queries, keys, values, allowed):
    scores = masked_scores(heads_of(queries), heads_of(keys), allowed)
    top_score = jnp.max(scores, axis=2, keepdims=True)
    raised = jnp.exp(scores - top_score)
    totals = jnp.sum(raised, axis=2, keepdims=True)
    shares = (raised / totals).astype(bf16)
    mixed = jnp.einsum("hqk,khd->qhd", shares, heads_of(values), preferred_element_type=f32)
    return mixed.astype(bf16).reshape(queries.shape), top_score + jnp.log(totals)


def attend_backward(queries, keys, values, allowed, log_total, grads):
    queries, keys, values, grads = map(heads_of, (queries, keys, values, grads))
    scale = HEAD_DIM ** (-0.5)
    shares = jnp.exp(masked_scores(queries, keys, allowed) - log_total)
    share_grads = jnp.einsum("qhd,khd->hqk", grads, values, preferred_element_type=f32)
    inner_sums = jnp.sum(shares * share_grads, axis=2, keepdims=True)
    score_grads = (shares * (share_grads - inner_sums)).astype(bf16)
    query_grad = jnp.einsum("hqk,khd->qhd", score_grads, keys, preferred_element_type=f32) * scale
    key_grad = jnp.einsum("hqk,qhd->khd", score_grads, queries, preferred_element_type=f32) * scale
    value_grad = jnp.einsum(
        "hqk,qhd->khd", shares.astype(bf16), grads, preferred_element_type=f32
    )
    flat = lambda a: a.reshape(a.shape[0], D)
    return flat(query_grad).astype(bf16), flat(key_grad), flat(value_grad)


def make_body(fsdp_size, seq_size):
    half = seq_size // 2
    staged = (fsdp_size, seq_size) == (8, 4)
    device_count = fsdp_size * seq_size
    across = [(i, (i + half) % seq_size) for i in range(seq_size)]
    groups = [[m * half + j for j in range(half)] for m in range(2)]
    length = SEQ_LEN // seq_size

    def gather_siblings(rows):
        if staged:
            return jnp.stack([rows, send(rows, TO_CORE)])
        return lax.all_gather(rows, "seq", axis_index_groups=groups)

    def scatter_siblings(own_order):
        if staged:
            return own_order[0] + send(own_order[1].astype(bf16), TO_CORE).astype(f32)
        return lax.psum_scatter(own_order, "seq", axis_index_groups=groups)

    def body(tokens, doc_lengths, cotangent, *shards):
        (
            query_weight,
            key_weight,
            value_weight,
            mix_weight,
            query_bias,
            value_bias,
            mix_bias,
            first_gain,
            first_shift,
            inner_weight,
            inner_bias,
            outer_weight,
            outer_bias,
            second_gain,
            second_shift,
        ) = shards
        layer_count = query_weight.shape[0]
        seq = lax.axis_index("seq")
        row = seq // half
        coords = coordinates()
        rows_held = D // device_count
        inner_held = FF // device_count

        def vector_rows(small, wide):
            return jnp.concatenate(
                [jnp.concatenate([v[layer] for v in small]) for layer in range(layer_count)]
                + [wide.reshape(-1)]
            )

        small_vectors = (
            query_bias,
            value_bias,
            mix_bias,
            first_gain,
            first_shift,
            outer_bias,
            second_gain,
            second_shift,
        )
        vector_count = len(small_vectors) * layer_count
        mine = vector_rows(small_vectors, inner_bias)
        held = mine.shape[0]
        if staged:
            padded = jnp.pad(mine, (0, 1024 - held)).reshape(8, 128)
            parts = jnp.stack([padded] + [send(padded, TO_Z[4 - k]) for k in (1, 2, 3)])
            z, y, x, c = coords[0], coords[1], coords[2], coords[3]
            parts = jnp.roll(parts, z, axis=0)

            def both(own, other, place_of, axis):
                return jnp.where(
                    place_of == 0,
                    jnp.stack([own, other], axis),
                    jnp.stack([other, own], axis),
                )

            parts = both(parts, send(parts, TO_Y), y, 1)
            parts = both(parts, send(parts, TO_X), x, 2)
            parts = both(parts, send(parts, TO_CORE), c, 3)
            every = parts.reshape(device_count, 1024)[:, :held]
        else:
            every = lax.all_gather(mine, AXES)
        every = every.astype(f32)
        small_held = vector_count * rows_held
        small_all = (
            every[:, :small_held]
            .reshape(device_count, vector_count, rows_held)
            .transpose(1, 0, 2)
            .reshape(layer_count, len(small_vectors), D)
        )
        wide_all = (
            every[:, small_held:]
            .reshape(device_count, layer_count, inner_held)
            .transpose(1, 0, 2)
            .reshape(layer_count, FF)
        )

        gather = Gather(coords)

        def attention_weights(layer):
            parts = [w[layer] for w in (query_weight, key_weight, value_weight, mix_weight)]
            if not staged:
                return [lax.all_gather(p, AXES, axis=0, tiled=True) for p in parts]
            r = rows_held
            got = gather(
                jnp.concatenate(parts),
                2 * r,
                [(r, D)] * 4,
                (((0, r, 0, 0), (r, 2 * r, 1, 0)), ((0, r, 2, 0), (r, 2 * r, 3, 0))),
            )
            return [g.reshape(D, D) for g in got]

        def forward_weights(layer):
            inner, outer = inner_weight[layer], outer_weight[layer]
            if not staged:
                return [lax.all_gather(p, AXES, axis=0, tiled=True) for p in (inner, outer)]
            r = rows_held
            blocks = FF // D
            got = gather(
                jnp.concatenate([inner[:, D * n : D * (n + 1)] for n in range(blocks)] + [outer]),
                blocks * r,
                [(r, FF), (inner_held, D)],
                (
                    tuple((r * n, r * (n + 1), 0, n) for n in range(blocks)),
                    ((0, inner_held, 1, 0),),
                ),
            )
            return [got[0].reshape(D, FF), got[1].reshape(FF, D)]

        def own_row(both_rows):
            kept = pick(both_rows, row, 0)
            return jnp.concatenate(
                [kept, lax.ppermute(pick(both_rows, 1 - row, 0), "seq", across)]
            )

        def both_rows(values):
            kept = values[:length]
            other = lax.ppermute(values[length:].astype(bf16), "seq", across).astype(f32)
            return jnp.where(row == 0, jnp.stack([kept, other]), jnp.stack([other, kept]))

        stream_start = own_row(tokens.reshape(2, length, D))
        upstream_start = own_row(cotangent.reshape(2, length, D))

        lengths = pick(doc_lengths.reshape(2, NDOC), row, 0)
        bounds = jnp.cumsum(lengths)
        within = lax.iota(jnp.int32, length)

        def positions(s):
            return jnp.concatenate([s * length + within, (s + half) % seq_size * length + within])

        def segments(places):
            return jnp.sum((places[:, None] >= bounds[None, :]).astype(jnp.int32), axis=1)

        query_places = positions(seq)
        if staged:
            key_places = jnp.concatenate([positions(seq), positions(seq ^ 1)])
        else:
            key_places = jnp.concatenate([positions(row * half + j) for j in range(half)])
        query_segment, key_segment = segments(query_places), segments(key_places)
        allowed = (
            (query_segment[:, None] == key_segment[None, :]) & (key_segment[None, :] != NDOC - 1)
        ) | (query_places[:, None] == key_places[None, :])

        stream = stream_start.astype(f32)
        saved = []
        for layer in range(layer_count):
            q_bias, v_bias, m_bias, gain1, shift1, o_bias, gain2, shift2 = [
                small_all[layer, n] for n in range(len(small_vectors))
            ]
            w_query, w_key, w_value, w_mix = attention_weights(layer)
            w_inner, w_outer = forward_weights(layer)
            stream_low = stream.astype(bf16)
            queries = (dot(stream_low, w_query) + q_bias).astype(bf16)
            key_rows = dot(stream_low, w_key).astype(bf16)
            values = (dot(stream_low, w_value) + v_bias).astype(bf16)
            all_keys = gather_siblings(key_rows).reshape(SEQ_LEN, D)
            all_values = gather_siblings(values).reshape(SEQ_LEN, D)
            mixed, log_total = attend_forward(queries, all_keys, all_values, allowed)
            first_sum = stream + (dot(mixed, w_mix) + m_bias)
            first = norm_forward(first_sum)[0] * gain1 + shift1
            first_low = first.astype(bf16)
            inner = dot(first_low, w_inner) + wide_all[layer]
            below = 0.5 * (1.0 + lax.erf(inner * (0.5**0.5)))
            active = (inner * below).astype(bf16)
            slope = (below + inner * jnp.exp(-0.5 * inner * inner) * (2 * math.pi) ** -0.5).astype(
                bf16
            )
            second_sum = first + (dot(active, w_outer) + o_bias)
            stream = norm_forward(second_sum)[0] * gain2 + shift2
            saved.append(
                (
                    (w_query, w_key, w_value, w_mix, w_inner, w_outer, gain1, gain2),
                    (stream_low, queries, all_keys, all_values, log_total, mixed),
                    (first_sum, first_low, slope, active, second_sum),
                )
            )
        activations = both_rows(stream)

        upstream = upstream_start.astype(f32)
        small_grads = [None] * layer_count
        wide_grads = [None] * layer_count
        results = [None] * layer_count

        def reduced(grads, x_first):
            if staged:
                return summed_shards(coords, [g.astype(bf16) for g in grads], x_first)
            return [lax.psum_scatter(g, AXES, scatter_dimension=0, tiled=True) for g in grads]

        for layer in reversed(range(layer_count)):
            (w_query, w_key, w_value, w_mix, w_inner, w_outer, gain1, gain2), kept, rest = saved[layer]
            stream_low, queries, all_keys, all_values, log_total, mixed = kept
            first_sum, first_low, slope, active, second_sum = rest
            second_grad, gain2_grad, shift2_grad = norm_backward(second_sum, gain2, upstream)
            second_low = second_grad.astype(bf16)
            (outer_grad,) = reduced([contract_rows(active, second_low)], False)
            inner_low = (contract_cols(second_low, w_outer) * slope).astype(bf16)
            (inner_grad,) = reduced([contract_rows(first_low, inner_low)], True)
            first_grad = second_grad + contract_cols(inner_low, w_inner)
            first_sum_grad, gain1_grad, shift1_grad = norm_backward(first_sum, gain1, first_grad)
            branch_low = first_sum_grad.astype(bf16)
            mix_terms = contract_rows(mixed, branch_low)
            mixed_grad = contract_cols(branch_low, w_mix).astype(bf16)
            query_low, key_terms, value_terms = attend_backward(
                queries, all_keys, all_values, allowed, log_total, mixed_grad
            )
            n = 2 * length
            key_low = scatter_siblings(key_terms.reshape(half, n, D)).astype(bf16)
            value_low = scatter_siblings(value_terms.reshape(half, n, D)).astype(bf16)
            value_grad, mix_grad = reduced([contract_rows(stream_low, value_low), mix_terms], False)
            query_grad, key_grad = reduced(
                [contract_rows(stream_low, query_low), contract_rows(stream_low, key_low)], True
            )
            upstream = (
                first_sum_grad
                + contract_cols(query_low, w_query)
                + contract_cols(key_low, w_key)
                + contract_cols(value_low, w_value)
            )
            small_grads[layer] = jnp.stack(
                [
                    column_sum(query_low),
                    column_sum(value_low),
                    column_sum(branch_low),
                    gain1_grad,
                    shift1_grad,
                    column_sum(second_low),
                    gain2_grad,
                    shift2_grad,
                ]
            )
            wide_grads[layer] = column_sum(inner_low)
            results[layer] = (query_grad, key_grad, value_grad, mix_grad, inner_grad, outer_grad)
        token_grad = both_rows(upstream)

        small_terms = (
            jnp.stack(small_grads)
            .reshape(vector_count, device_count, rows_held)
            .transpose(1, 0, 2)
            .reshape(device_count, small_held)
        )
        wide_terms = (
            jnp.stack(wide_grads)
            .reshape(layer_count, device_count, inner_held)
            .transpose(1, 0, 2)
            .reshape(device_count, layer_count * inner_held)
        )
        terms = jnp.concatenate([small_terms, wide_terms], axis=1)
        if staged:
            terms = jnp.pad(terms, ((0, 0), (0, 1024 - held))).reshape(device_count * 8, 128)
            (own_terms,) = summed_shards(coords, [terms], True)
            own_terms = own_terms.reshape(-1)[:held]
        else:
            own_terms = lax.psum_scatter(terms, AXES, scatter_dimension=0, tiled=False)
        small_own = own_terms[:small_held].reshape(layer_count, len(small_vectors), rows_held)
        wide_own = own_terms[small_held:].reshape(layer_count, inner_held)
        query_g, key_g, value_g, mix_g, inner_g, outer_g = [
            jnp.stack([results[layer][n] for layer in range(layer_count)]) for n in range(6)
        ]
        return (
            activations.reshape(tokens.shape),
            token_grad.reshape(tokens.shape),
            query_g,
            key_g,
            value_g,
            mix_g,
            small_own[:, 0],
            small_own[:, 1],
            small_own[:, 2],
            small_own[:, 3],
            small_own[:, 4],
            inner_g,
            wide_own,
            outer_g,
            small_own[:, 5],
            small_own[:, 6],
            small_own[:, 7],
        )

    return body


def solution(mesh):
    tokens = P(None, "fsdp", "seq", None)
    matrix, vector = P(None, AXES, None), P(None, AXES)
    in_specs = (tokens, P(None, "fsdp", None), tokens) + (matrix,) * 4 + (vector,) * 5
    in_specs += (matrix, vector, matrix, vector, vector, vector)
    out_specs = (tokens, tokens) + (matrix,) * 4 + (vector,) * 5
    out_specs += (matrix, vector, matrix, vector, vector, vector)
    body = make_body(mesh.shape["fsdp"], mesh.shape["seq"])
    return jax.shard_map(body, mesh=mesh, in_specs=in_specs, out_specs=out_specs, check_vma=False)
```

```python
import math

import jax
import jax.numpy as jnp
from jax import lax
from jax.experimental import pallas as pl
from jax.experimental.pallas import tpu as pltpu
from jax.sharding import PartitionSpec as P

D = 1024
FF = 4096
HEAD_DIM = 64
HEADS = D // HEAD_DIM
SEQ_LEN = 1024
NDOC = 16
epsilon = 1e-05
AXES = ("fsdp", "seq")
f32 = jnp.float32
bf16 = jnp.bfloat16


def dot(left, right):
    return jnp.dot(left, right, preferred_element_type=f32)


def contract_rows(left, right):
    return lax.dot_general(left, right, (((0,), (0,)), ((), ())), preferred_element_type=f32)


def contract_cols(left, right):
    return lax.dot_general(left, right, (((1,), (1,)), ((), ())), preferred_element_type=f32)


def tie(value, *others):
    return lax.optimization_barrier((value, others))[0]


def pairs(move):
    out = []
    for i in range(32):
        z, y, x, c = i // 8, i // 4 % 2, i // 2 % 2, i % 2
        z, y, x, c = move(z, y, x, c)
        out.append((i, z * 8 + y * 4 + x * 2 + c))
    return out


TO_CORE = pairs(lambda z, y, x, c: (z, y, x, 1 - c))
TO_X = pairs(lambda z, y, x, c: (z, y, 1 - x, c))
TO_Y = pairs(lambda z, y, x, c: (z, 1 - y, x, c))
TO_FAR = pairs(lambda z, y, x, c: (z, y if c == 0 else 1 - y, 1 - x if c == 0 else x, c))
TO_NEAR = pairs(lambda z, y, x, c: (z, 1 - y if c == 0 else y, x if c == 0 else 1 - x, c))
TO_Z = [pairs(lambda z, y, x, c, k=k: ((z + k) % 4, y, x, c)) for k in range(4)]


def send(value, to):
    return lax.ppermute(value, AXES, to)


def coordinates():
    fsdp, seq = lax.axis_index("fsdp"), lax.axis_index("seq")
    return jnp.stack([fsdp // 2, fsdp % 2, seq // 2, seq % 2]).astype(jnp.int32)


def place(coords, pieces, shapes, moves):
    count = len(moves(0, 0, 0, 0, None, None))

    total = len(pieces)

    def kernel(coords_ref, *refs):
        sources, targets = refs[:total], refs[total : total + len(shapes)]
        buffers, in_sems, out_sems = refs[total + len(shapes) : -2], refs[-2], refs[-1]
        loads = [
            pltpu.make_async_copy(source, buffer, in_sems.at[n])
            for n, (source, buffer) in enumerate(zip(sources, buffers))
        ]
        for load in loads:
            load.start()
        todo = moves(coords_ref[0], coords_ref[1], coords_ref[2], coords_ref[3], buffers, targets)
        stores = [
            (n, pltpu.make_async_copy(view, target, out_sems.at[k]))
            for k, (n, view, target) in enumerate(todo)
        ]
        for piece, load in enumerate(loads):
            load.wait()
            for n, store in stores:
                if n == piece:
                    store.start()
        for _, store in stores:
            store.wait()

    size = sum(math.prod(shape) for shape in shapes) * 4
    return pl.pallas_call(
        kernel,
        in_specs=[pl.BlockSpec(memory_space=pltpu.SMEM)]
        + [pl.BlockSpec(memory_space=pl.ANY)] * len(pieces),
        out_specs=[pl.BlockSpec(memory_space=pl.ANY)] * len(shapes),
        out_shape=[jax.ShapeDtypeStruct(shape, bf16) for shape in shapes],
        scratch_shapes=[pltpu.VMEM(p.shape, bf16) for p in pieces]
        + [pltpu.SemaphoreType.DMA((total,)), pltpu.SemaphoreType.DMA((count,))],
        compiler_params=pltpu.CompilerParams(vmem_limit_bytes=40 << 20),
        cost_estimate=pl.CostEstimate(flops=0, bytes_accessed=size, transcendentals=0),
    )(coords, *pieces)


def pick(value, index, axis):
    return lax.dynamic_index_in_dim(value, index, axis, keepdims=False)


def by_place(own, other, at, axis):
    return jnp.where(at == 0, jnp.stack([own, other], axis), jnp.stack([other, own], axis))


def phase(values, *units):
    values, flights = lax.optimization_barrier((values, [u.flight for u in units]))
    nexts = [u.local(flight) for u, flight in zip(units, flights)]
    values, sends = lax.optimization_barrier((values, [[v for v, _ in n] for n in nexts]))
    for unit, arrays, targets in zip(units, sends, nexts):
        unit.flight = [send(array, to) for array, (_, to) in zip(arrays, targets)]
    return values


class GatherUnit:
    def __init__(self, coords, pack, shapes, parts):
        self.coords, self.pack, self.shapes, self.parts = coords, pack, shapes, parts
        self.flight, self.step = [], 0

    def local(self, got):
        rows, width = self.pack.shape
        self.step += 1
        if self.step == 1:
            return [(self.pack, TO_Z[4 - k]) for k in (1, 2, 3)]
        if self.step == 2:
            self.kept = jnp.concatenate([self.pack] + got).reshape(4, rows, width)
            return [(self.kept, TO_NEAR)]
        if self.step == 3:
            self.kept = jnp.stack([self.kept, got[0]])
            return [(self.kept, TO_FAR), (self.kept, TO_CORE)]
        self.kept = [self.kept, got[0], got[1]]
        return [(got[0], TO_CORE)]

    def result(self):
        width = self.pack.shape[1]

        def by_block(z, y, x, c, src, dst):
            out = []
            for n in range(4):
                core = c if n < 2 else 1 - c
                for near in range(2):
                    far = n % 2
                    y2 = y ^ jnp.where(core == 0, near, far)
                    x2 = x ^ jnp.where(core == 0, far, near)
                    for k in range(4):
                        for lo, hi, target, column in self.parts:
                            view = None
                            if dst:
                                spans = (slice(0, hi - lo), slice(column * width, (column + 1) * width))
                                view = dst[target].at[((z + k) % 4, y2, x2, core) + spans]
                            out.append((n, src and src[n].at[near, k, lo:hi], view))
            return out

        return place(
            self.coords, self.kept + self.flight, [(4, 2, 2, 2) + shape for shape in self.shapes], by_block
        )


class SumUnit:
    def __init__(self, parts):
        self.parts = parts
        self.flight, self.step = [], 0

    def local(self, got):
        self.step += 1
        if self.step == 1:
            leaving, self.kept = self.parts
            return [(leaving, TO_FAR)]
        if self.step == 2:
            half = self.kept.shape[0] // 2
            add = lambda a, b: (a.astype(f32) + b.astype(f32)).astype(bf16)
            leaving = add(self.kept[:half], got[0][:half])
            self.kept = add(self.kept[half:], got[0][half:])
            return [(leaving, TO_NEAR)]
        if self.step == 3:
            kept, rows = self.kept, self.kept.shape[0] // 4
            cut = lambda array, k: array[k * rows : (k + 1) * rows].astype(f32)
            add = lambda k: cut(kept, k) + cut(got[0], k)
            self.kept = add(3)
            return [(add(k - 1).astype(bf16), TO_Z[k]) for k in (1, 2, 3)]
        self.kept = self.kept + (got[0].astype(f32) + got[1].astype(f32) + got[2].astype(f32))
        return []


def block_order(coords):
    z, y, x, c = coords[0], coords[1], coords[2], coords[3]
    order = []
    for core in (c, 1 - c):
        for far in (1, 0):
            for near in (1, 0):
                for k in (1, 2, 3, 0):
                    y2 = y ^ jnp.where(core == 0, near, far)
                    x2 = x ^ jnp.where(core == 0, far, near)
                    order.append((z + k) % 4 * 8 + y2 * 4 + x2 * 2 + core)
    return jnp.stack(order).astype(jnp.int32)


def order_matrices(order):
    block = D // 32
    wanted = (order[:, None] * block + lax.iota(jnp.int32, block)[None, :]).reshape(2, 1, D // 2)
    rows = lax.broadcasted_iota(jnp.int32, (2, D, D // 2), 1)
    chosen = (rows == wanted).astype(bf16)
    return chosen[0], chosen[1]


def selected(matrices, rows):
    return [
        lax.dot_general(m, rows, (((0,), (1,)), ((), ())), preferred_element_type=f32).astype(bf16)
        for m in matrices
    ]


def weight_terms(*pairs_of):
    rows, tokens = pairs_of[0][0][0].shape
    tile = (1 << 19) // rows
    counts = [pair[1][0].shape[1] // tile for pair in pairs_of]
    starts = [sum(counts[:n]) for n in range(len(counts))]
    columns, half = sum(counts) * tile, rows // 2

    def kernel(*refs):
        leaving, kept = refs[-2:]
        j = pl.program_id(0)
        for n, (start, count) in enumerate(zip(starts, counts)):

            @pl.when((j >= start) & (j < start + count))
            def _(a1=refs[4 * n], a2=refs[4 * n + 1], b1=refs[4 * n + 2], b2=refs[4 * n + 3]):
                total = jnp.dot(a1[...], b1[...], preferred_element_type=f32)
                total = total + jnp.dot(a2[...], b2[...], preferred_element_type=f32)
                leaving[...] = total[:half].astype(bf16)
                kept[...] = total[half:].astype(bf16)

    in_specs, args = [], []
    for (left, right), start, count in zip(pairs_of, starts, counts):
        whole = pl.BlockSpec((rows, tokens), lambda j: (0, 0))
        cut = pl.BlockSpec((tokens, tile), lambda j, s=start, n=count: (0, jnp.clip(j - s, 0, n - 1)))
        in_specs += [whole, whole, cut, cut]
        args += [*left, *right]
    out = jax.ShapeDtypeStruct((half, columns), bf16)
    return pl.pallas_call(
        kernel,
        grid=(columns // tile,),
        in_specs=in_specs,
        out_specs=[pl.BlockSpec((half, tile), lambda j: (0, j))] * 2,
        out_shape=[out, out],
        compiler_params=pltpu.CompilerParams(vmem_limit_bytes=48 << 20),
        cost_estimate=pl.CostEstimate(
            flops=4 * rows * tokens * columns,
            bytes_accessed=4 * rows * tokens + 4 * tokens * columns + 2 * rows * columns,
            transcendentals=0,
        ),
    )(*args)


def wide_terms_of(order, left, right):
    tokens, width = left[0].shape
    block = width // 32

    def kernel(order_ref, a1, a2, b1, b2, leaving, kept):
        rows_dot = lambda a, b: lax.dot_general(
            a[...], b[...], (((0,), (0,)), ((), ())), preferred_element_type=f32
        )
        total = (rows_dot(a1, b1) + rows_dot(a2, b2)).astype(bf16)

        @pl.when(pl.program_id(0) < 8)
        def _():
            leaving[...] = total

        @pl.when(pl.program_id(0) >= 8)
        def _():
            kept[...] = total

    columns = right[0].shape[1]
    cut = pl.BlockSpec((tokens, block), lambda j, order: (0, order[j]))
    whole = pl.BlockSpec((tokens, columns), lambda j, order: (0, 0))
    out = jax.ShapeDtypeStruct((width // 4, columns), bf16)
    return pl.pallas_call(
        kernel,
        grid_spec=pltpu.PrefetchScalarGridSpec(
            num_scalar_prefetch=1,
            grid=(16,),
            in_specs=[cut, cut, whole, whole],
            out_specs=[
                pl.BlockSpec((block, columns), lambda j, order: (jnp.minimum(j, 7), 0)),
                pl.BlockSpec((block, columns), lambda j, order: (jnp.maximum(j - 8, 0), 0)),
            ],
        ),
        out_shape=[out, out],
        compiler_params=pltpu.CompilerParams(vmem_limit_bytes=48 << 20),
        cost_estimate=pl.CostEstimate(
            flops=2 * tokens * width * columns, bytes_accessed=3 * tokens * width, transcendentals=0
        ),
    )(order, *left, *right)


BLOCK = 256
WINDOW = 3 * BLOCK
PAIR = 2 * HEAD_DIM


def window_start(s, slot):
    block = s ^ (2 * slot)
    return jnp.clip(block - 1, 0, 1) * BLOCK


def nt_dot(left, right):
    return lax.dot_general(left, right, (((1,), (1,)), ((), ())), preferred_element_type=f32)


def only_head(value, head, axis):
    lane = lax.broadcasted_iota(jnp.int32, value.shape, axis)
    return jnp.where((lane < HEAD_DIM) if head == 0 else (lane >= HEAD_DIM), value, jnp.zeros_like(value))


def in_order(s, mine, other, scratch):
    for n, ref in ((0, mine), (1, other)):
        for slot in range(2):
            scratch[pl.ds((s ^ (n + 2 * slot)) * BLOCK, BLOCK), :] = ref[slot * BLOCK : (slot + 1) * BLOCK, :]


def attend_forward_kernel(
    s_ref, q_ref, km_ref, ko_ref, vm_ref, vo_ref, bias_ref, mixed_ref, total_ref, keys, values
):
    s = s_ref[0]
    in_order(s, km_ref, ko_ref, keys)
    in_order(s, vm_ref, vo_ref, values)
    for slot in range(2):
        start = pl.multiple_of(window_start(s, slot), BLOCK)
        k = keys[pl.ds(start, WINDOW), :]
        v_t = values[pl.ds(start, WINDOW), :].T
        q = q_ref[slot * BLOCK : (slot + 1) * BLOCK, :] * jnp.asarray(HEAD_DIM**-0.5, bf16)
        bias = bias_ref[slot]
        halves = []
        for head in range(2):
            scores = nt_dot(k, only_head(q, head, 1)) + bias
            top = jnp.max(scores, axis=0, keepdims=True)
            raised = jnp.exp(scores - top)
            total = jnp.sum(raised, axis=0, keepdims=True)
            mixed = jnp.dot(
                v_t[head * HEAD_DIM : (head + 1) * HEAD_DIM],
                raised.astype(bf16),
                preferred_element_type=f32,
            )
            halves.append(mixed / total)
            total_ref[0, head : head + 1, slot * BLOCK : (slot + 1) * BLOCK] = top + jnp.log(total)
        mixed_ref[slot * BLOCK : (slot + 1) * BLOCK, :] = jnp.concatenate(halves, axis=0).T.astype(bf16)


def attend_backward_kernel(
    s_ref, q_ref, km_ref, ko_ref, vm_ref, vo_ref, bias_ref, mixed_ref, total_ref, grad_ref,
    dq_ref, mine_ref, sent_ref, keys, values, key_sum, value_sum,
):
    s = s_ref[0]
    in_order(s, km_ref, ko_ref, keys)
    in_order(s, vm_ref, vo_ref, values)
    key_sum[...] = jnp.zeros_like(key_sum)
    value_sum[...] = jnp.zeros_like(value_sum)
    for slot in range(2):
        rows = slice(slot * BLOCK, (slot + 1) * BLOCK)
        start = pl.multiple_of(window_start(s, slot), BLOCK)
        window = pl.ds(start, WINDOW)
        k, v = keys[window, :], values[window, :]
        k_t = k.T
        q = q_ref[rows, :] * jnp.asarray(HEAD_DIM**-0.5, bf16)
        g = grad_ref[rows, :]
        bias = bias_ref[slot]
        along = (g.astype(f32) * mixed_ref[rows, :].astype(f32)).T
        shares_low, grads_low, queries, grads, query_grads = [], [], [], [], []
        for head in range(2):
            span = slice(head * HEAD_DIM, (head + 1) * HEAD_DIM)
            queries.append(only_head(q, head, 1))
            grads.append(only_head(g, head, 1))
            scores = nt_dot(k, queries[head]) + bias
            shares = jnp.exp(scores - total_ref[0, head : head + 1, rows])
            inner = jnp.sum(along[span], axis=0, keepdims=True)
            score_grads = (shares * (nt_dot(v, grads[head]) - inner)).astype(bf16)
            shares_low.append(shares.astype(bf16))
            grads_low.append(score_grads)
            query_grads.append(jnp.dot(k_t[span], score_grads, preferred_element_type=f32))
        dq_ref[rows, :] = (jnp.concatenate(query_grads, axis=0).T * HEAD_DIM**-0.5).astype(bf16)
        key_sum[window, :] += jnp.dot(
            jnp.concatenate(grads_low, axis=1), jnp.concatenate(queries, axis=0), preferred_element_type=f32
        )
        value_sum[window, :] += jnp.dot(
            jnp.concatenate(shares_low, axis=1), jnp.concatenate(grads, axis=0), preferred_element_type=f32
        )
    for slot in range(2):
        rows = slice(slot * BLOCK, (slot + 1) * BLOCK)
        mine, other = pl.ds((s ^ (2 * slot)) * BLOCK, BLOCK), pl.ds((s ^ (1 + 2 * slot)) * BLOCK, BLOCK)
        mine_ref[0, rows, :] = key_sum[mine, :]
        mine_ref[1, rows, :] = value_sum[mine, :]
        sent_ref[0, rows, :] = key_sum[other, :].astype(bf16)
        sent_ref[1, rows, :] = value_sum[other, :].astype(bf16)


def call_attention(kernel, s, own, other, bias, kept, outs, scratch):
    pairs_count = D // PAIR
    third = lambda n: pl.BlockSpec((2 * BLOCK, PAIR), lambda h: (0, h + n * pairs_count))
    cut = third(0)
    double = pl.BlockSpec((2, 2 * BLOCK, PAIR), lambda h: (0, 0, h))
    per_pair = pl.BlockSpec((1, 2, 2 * BLOCK), lambda h: (h, 0, 0))
    whole = pl.BlockSpec(bias.shape, lambda h: (0, 0, 0))
    in_specs = [pl.BlockSpec(memory_space=pltpu.SMEM), third(0), third(1), third(1), third(2), third(2), whole]
    args = [s, own, own, other, own, other, bias]
    if kept:
        in_specs += [cut, per_pair, cut]
        args += kept
    shapes, specs = [], []
    for kind, spec in outs:
        shapes.append(
            {
                0: jax.ShapeDtypeStruct((2 * BLOCK, D), kind),
                1: jax.ShapeDtypeStruct((pairs_count, 2, 2 * BLOCK), kind),
                2: jax.ShapeDtypeStruct((2, 2 * BLOCK, D), kind),
            }[spec]
        )
        specs.append((cut, per_pair, double)[spec])
    flops = 2 * (5 if kept else 2) * HEADS * 2 * BLOCK * WINDOW * HEAD_DIM
    return pl.pallas_call(
        kernel,
        grid=(pairs_count,),
        in_specs=in_specs,
        out_specs=specs,
        out_shape=shapes,
        scratch_shapes=scratch,
        compiler_params=pltpu.CompilerParams(vmem_limit_bytes=48 << 20),
        cost_estimate=pl.CostEstimate(
            flops=flops * 8, bytes_accessed=16 << 20, transcendentals=HEADS * 2 * BLOCK * WINDOW
        ),
    )(*args)


def attend_forward_blocks(s, own, other, bias):
    scratch = [pltpu.VMEM((SEQ_LEN, PAIR), bf16)] * 2
    return call_attention(attend_forward_kernel, s, own, other, bias, (), ((bf16, 0), (f32, 1)), scratch)


def attend_backward_blocks(s, own, other, bias, mixed, totals, grads):
    scratch = [pltpu.VMEM((SEQ_LEN, PAIR), bf16)] * 2 + [pltpu.VMEM((SEQ_LEN, PAIR), f32)] * 2
    outs = ((bf16, 0), (f32, 2), (bf16, 2))
    kept = (mixed, totals, grads)
    return call_attention(attend_backward_kernel, s, own, other, bias, kept, outs, scratch)


def window_bias(s, ids):
    out = []
    for slot in range(2):
        keys = lax.dynamic_slice_in_dim(ids, window_start(s, slot), WINDOW)
        queries = lax.dynamic_slice_in_dim(ids, (s ^ (2 * slot)) * BLOCK, BLOCK)
        out.append(jnp.where(keys[:, None] == queries[None, :], 0.0, -1e30))
    return jnp.stack(out).astype(f32)


def norm_forward(total):
    center = jnp.mean(total, axis=-1, keepdims=True)
    centered = total - center
    spread = jnp.mean(centered * centered, axis=-1, keepdims=True)
    scale = lax.rsqrt(spread + epsilon)
    return centered * scale, scale


def norm_backward(total, gain, upstream):
    unit, scale = norm_forward(total)
    lifted = upstream * gain
    grad = scale * (
        lifted
        - jnp.mean(lifted, axis=-1, keepdims=True)
        - unit * jnp.mean(lifted * unit, axis=-1, keepdims=True)
    )
    return grad, jnp.sum(upstream * unit, axis=0), jnp.sum(upstream, axis=0)


def column_sum(values):
    return jnp.sum(values.astype(f32), axis=0)


def heads_of(rows):
    return rows.reshape(rows.shape[0], HEADS, HEAD_DIM)


def masked_scores(queries, keys, allowed):
    scores = jnp.einsum("qhd,khd->hqk", queries, keys, preferred_element_type=f32)
    return jnp.where(allowed[None], scores * HEAD_DIM ** (-0.5), -1e30)


def attend_forward(queries, keys, values, allowed):
    scores = masked_scores(heads_of(queries), heads_of(keys), allowed)
    top_score = jnp.max(scores, axis=2, keepdims=True)
    raised = jnp.exp(scores - top_score)
    totals = jnp.sum(raised, axis=2, keepdims=True)
    shares = (raised / totals).astype(bf16)
    mixed = jnp.einsum("hqk,khd->qhd", shares, heads_of(values), preferred_element_type=f32)
    return mixed.astype(bf16).reshape(queries.shape), top_score + jnp.log(totals)


def attend_backward(queries, keys, values, allowed, log_total, grads):
    queries, keys, values, grads = map(heads_of, (queries, keys, values, grads))
    scale = HEAD_DIM ** (-0.5)
    shares = jnp.exp(masked_scores(queries, keys, allowed) - log_total)
    share_grads = jnp.einsum("qhd,khd->hqk", grads, values, preferred_element_type=f32)
    inner_sums = jnp.sum(shares * share_grads, axis=2, keepdims=True)
    score_grads = (shares * (share_grads - inner_sums)).astype(bf16)
    query_grad = jnp.einsum("hqk,khd->qhd", score_grads, keys, preferred_element_type=f32) * scale
    key_grad = jnp.einsum("hqk,qhd->khd", score_grads, queries, preferred_element_type=f32) * scale
    value_grad = jnp.einsum(
        "hqk,qhd->khd", shares.astype(bf16), grads, preferred_element_type=f32
    )
    flat = lambda a: a.reshape(a.shape[0], D)
    return flat(query_grad).astype(bf16), flat(key_grad), flat(value_grad)


SMALL = 8


def staged_body(tokens, doc_lengths, cotangent, *shards):
    (
        query_weight,
        key_weight,
        value_weight,
        mix_weight,
        query_bias,
        value_bias,
        mix_bias,
        first_gain,
        first_shift,
        inner_weight,
        inner_bias,
        outer_weight,
        outer_bias,
        second_gain,
        second_shift,
    ) = shards
    layer_count = query_weight.shape[0]
    devices = 32
    length = SEQ_LEN // 4
    rows_held, inner_held = D // devices, FF // devices
    seq = lax.axis_index("seq")
    row = seq // 2
    coords = coordinates()
    z, y, x, c = coords[0], coords[1], coords[2], coords[3]
    place_of = seq.reshape(1).astype(jnp.int32)

    def split_rows(both):
        both = both.reshape(2, length, D)
        return pick(both, row, 0), pick(both, 1 - row, 0)

    token_kept, token_left = split_rows(tokens)
    upstream_kept, upstream_left = split_rows(cotangent)
    token_got = send(token_left, TO_X)

    def unit_a(layer):
        r = rows_held
        parts = [w[layer] for w in (query_weight, key_weight, value_weight, mix_weight)]
        outs = (((0, 0), (0, 1), (0, 2), (1, 0)))
        return GatherUnit(
            coords,
            jnp.concatenate(parts),
            [(r, 3 * D), (r, D)],
            [(r * n, r * (n + 1), target, column) for n, (target, column) in enumerate(outs)],
        )

    def unit_i(layer):
        r, inner = rows_held, inner_weight[layer]
        return GatherUnit(
            coords,
            jnp.concatenate([inner[:, D * n : D * (n + 1)] for n in range(4)]),
            [(r, FF)],
            [(r * n, r * (n + 1), 0, n) for n in range(4)],
        )

    def unit_o(layer):
        return GatherUnit(coords, outer_weight[layer], [(inner_held, D)], [(0, inner_held, 0, 0)])

    units = [[make(layer) for make in (unit_a, unit_i, unit_o)] for layer in range(layer_count)]

    small_vectors = (
        query_bias,
        value_bias,
        mix_bias,
        first_gain,
        first_shift,
        outer_bias,
        second_gain,
        second_shift,
    )
    vector_count = SMALL * layer_count
    small_held = vector_count * rows_held
    mine = jnp.concatenate(
        [jnp.concatenate([v[layer] for v in small_vectors]) for layer in range(layer_count)]
        + [inner_bias.reshape(-1)]
    )
    held = mine.shape[0]
    padded = jnp.pad(mine, (0, 1024 - held)).reshape(8, 128)

    tok = phase(token_got, units[0][0])
    every = jnp.stack([padded] + [send(padded, TO_Z[4 - k]) for k in (1, 2, 3)])
    every = jnp.roll(every, z, axis=0)
    tok = phase(tok, units[0][0])
    tok, every = phase((tok, every), units[0][1])
    every = by_place(every, send(every, TO_Y), y, 1)
    tok, every = phase((tok, every), units[0][0])
    every = by_place(every, send(every, TO_X), x, 2)
    every = by_place(every, send(every, TO_CORE), c, 3)

    lengths = pick(doc_lengths.reshape(2, NDOC), row, 0)
    places = lax.iota(jnp.int32, SEQ_LEN)
    segment = jnp.sum((places[:, None] >= jnp.cumsum(lengths)[None, :]).astype(jnp.int32), axis=1)
    bias = window_bias(seq, jnp.where(segment == NDOC - 1, NDOC + places, segment))
    order = block_order(coords)
    matrices = order_matrices(order)

    every = every.reshape(devices, 1024)[:, :held].astype(f32)
    small_all = (
        every[:, :small_held]
        .reshape(devices, vector_count, rows_held)
        .transpose(1, 0, 2)
        .reshape(layer_count, SMALL, D)
    )
    wide_all = (
        every[:, small_held:]
        .reshape(devices, layer_count, inner_held)
        .transpose(1, 0, 2)
        .reshape(layer_count, FF)
    )
    tok, bias, matrices, small_all, wide_all = phase((tok, bias, matrices, small_all, wide_all), units[0][1])
    tok = phase(tok, units[0][2])
    tok = phase(tok, units[0][0])

    stream = jnp.concatenate([token_kept, tok]).astype(f32)
    saved = []
    for layer in range(layer_count):
        a_unit, i_unit, o_unit = units[layer]
        later = units[layer + 1] if layer + 1 < layer_count else None
        q_bias, v_bias, m_bias, gain1, shift1, o_bias, gain2, shift2 = [small_all[layer, n] for n in range(SMALL)]
        w_three, w_mix = a_unit.result()
        w_three, w_mix = w_three.reshape(D, 3 * D), w_mix.reshape(D, D)
        stream_low = stream.astype(bf16)
        three = (dot(stream_low, w_three) + jnp.concatenate([q_bias, jnp.zeros_like(q_bias), v_bias])).astype(bf16)
        three_got = send(three, TO_CORE)
        stream, stream_low, three = phase((stream, stream_low, three), i_unit)
        if later:
            stream_low = phase(stream_low, later[0])
        left_stream = selected(matrices, stream_low)
        left_stream, three, three_got = phase((left_stream, three, three_got), o_unit)
        left_stream = (left_stream[0], send(left_stream[1], TO_CORE))
        mixed, totals = attend_forward_blocks(place_of, three, three_got, bias)
        mixed, totals = phase((mixed, totals), i_unit, o_unit)
        left_mix = selected(matrices, mixed)
        first_sum = stream + (dot(mixed, w_mix) + m_bias)
        first = norm_forward(first_sum)[0] * gain1 + shift1
        first_low = first.astype(bf16)
        left_first = selected(matrices, first_low)
        (w_inner,) = i_unit.result()
        w_inner = w_inner.reshape(D, FF)
        first, first_low, left_mix, left_first = lax.optimization_barrier(
            (first, first_low, left_mix, left_first)
        )
        left_mix, left_first = [(m, send(t, TO_CORE)) for m, t in (left_mix, left_first)]
        if later:
            first, first_low = phase((first, first_low), later[0])
            first, first_low = phase((first, first_low), later[1])
        else:
            (upstream_left,) = (tie(upstream_left, first_low),)
            upstream_got = send(upstream_left, TO_X)
        inner = dot(first_low, w_inner) + wide_all[layer]
        below = 0.5 * (1.0 + lax.erf(inner * (0.5**0.5)))
        active = (inner * below).astype(bf16)
        slope = (below + inner * jnp.exp(-0.5 * inner * inner) * (2 * math.pi) ** -0.5).astype(bf16)
        active, slope = phase((active, slope), o_unit)
        if later:
            active = phase(active, later[0])
        (w_outer,) = o_unit.result()
        w_outer = w_outer.reshape(FF, D)
        second_sum = first + (dot(active, w_outer) + o_bias)
        left_active = (active, send(active, TO_CORE))
        stream = norm_forward(second_sum)[0] * gain2 + shift2
        if later:
            stream = phase(stream, later[1])
            stream = phase(stream, later[2])
            stream = phase(stream, later[0])
        saved.append(
            (
                (w_three, w_mix, w_inner, w_outer, gain1, gain2),
                (three, three_got, totals, mixed),
                (first_sum, slope, second_sum),
                (left_stream, left_mix, left_first, left_active),
            )
        )

    def both_rows(kept, got):
        got = got.astype(f32)
        return jnp.where(row == 0, jnp.stack([kept, got]), jnp.stack([got, kept])).reshape(tokens.shape)

    output = stream
    output_got = send(output[length:].astype(bf16), TO_X)

    upstream = jnp.concatenate([upstream_kept, upstream_got]).astype(f32)
    small_grads, wide_grads = [None] * layer_count, [None] * layer_count
    sums = [None] * layer_count
    before = None
    for layer in reversed(range(layer_count)):
        weights, kept, rest, lefts = saved[layer]
        w_three, w_mix, w_inner, w_outer, gain1, gain2 = weights
        three, three_got, totals, mixed = kept
        first_sum, slope, second_sum = rest
        left_stream, left_mix, left_first, left_active = lefts
        second_grad, gain2_grad, shift2_grad = norm_backward(second_sum, gain2, upstream)
        second_low = second_grad.astype(bf16)
        second_got = send(second_low, TO_CORE)
        inner_low = (contract_cols(second_low, w_outer) * slope).astype(bf16)
        inner_got = send(inner_low, TO_CORE)
        o_sum = SumUnit(wide_terms_of(order, left_active, (second_low, second_got)))
        second_grad, inner_low = phase((second_grad, inner_low), o_sum)
        if before:
            second_grad, inner_low = phase((second_grad, inner_low), before[0], before[2])
        first_grad = second_grad + contract_cols(inner_low, w_inner)
        first_sum_grad, gain1_grad, shift1_grad = norm_backward(first_sum, gain1, first_grad)
        branch_low = first_sum_grad.astype(bf16)
        branch_got = send(branch_low, TO_CORE)
        i_sum = SumUnit(weight_terms((left_first, (inner_low, inner_got))))
        first_sum_grad, branch_low = phase((first_sum_grad, branch_low), i_sum)
        mixed_grad = contract_cols(branch_low, w_mix).astype(bf16)
        if before:
            mixed_grad = phase(mixed_grad, before[1], before[0])
        else:
            mixed_grad, output_got = lax.optimization_barrier((mixed_grad, output_got))
        query_low, own_grads, sent_grads = attend_backward_blocks(
            place_of, three, three_got, bias, mixed, totals, mixed_grad
        )
        grads_back = send(sent_grads, TO_CORE)
        own_grads = phase(own_grads, o_sum)
        if before:
            own_grads = phase(own_grads, before[1])
        sums_low = (own_grads + grads_back.astype(f32)).astype(bf16)
        low = jnp.concatenate([query_low, sums_low[0], sums_low[1]], axis=1)
        low_got = send(low, TO_CORE)
        first_sum_grad, low = phase((first_sum_grad, low), i_sum)
        upstream = first_sum_grad + contract_cols(low, w_three)
        a_sum = SumUnit(weight_terms((left_stream, (low, low_got)), (left_mix, (branch_low, branch_got))))
        upstream = phase(upstream, a_sum)
        if before:
            upstream = phase(upstream, before[1])
        upstream = phase(upstream, o_sum)
        small_grads[layer] = jnp.stack(
            [
                column_sum(low[:, :D]),
                column_sum(low[:, 2 * D :]),
                column_sum(branch_low),
                gain1_grad,
                shift1_grad,
                column_sum(second_low),
                gain2_grad,
                shift2_grad,
            ]
        )
        wide_grads[layer] = column_sum(inner_low)
        before = sums[layer] = (i_sum, a_sum, o_sum)

    token_back = send(upstream[length:].astype(bf16), TO_X)
    small_terms = (
        jnp.stack(small_grads)
        .reshape(vector_count, devices, rows_held)
        .transpose(1, 0, 2)
        .reshape(devices, small_held)
    )
    wide_terms = (
        jnp.stack(wide_grads)
        .reshape(layer_count, devices, inner_held)
        .transpose(1, 0, 2)
        .reshape(devices, layer_count * inner_held)
    )
    terms = jnp.pad(jnp.concatenate([small_terms, wide_terms], axis=1), ((0, 0), (0, 1024 - held)))
    chosen = (order[:, None] == lax.iota(jnp.int32, devices)[None, :]).astype(f32)
    terms = jnp.dot(chosen, terms, precision=lax.Precision.HIGHEST).reshape(2, 128, 128)
    terms = (terms[0] + send(terms[1].astype(bf16), TO_CORE).astype(f32)).astype(bf16)
    small_sum = SumUnit((terms[:64], terms[64:]))

    i_sum, a_sum, o_sum = sums[0]
    phase((), small_sum)
    phase((), i_sum, o_sum)
    phase((), a_sum, small_sum)
    phase((), i_sum)
    phase((), a_sum, small_sum)
    phase((), a_sum, small_sum)
    own_terms = small_sum.kept.reshape(-1)[:held]
    small_own = own_terms[:small_held].reshape(layer_count, SMALL, rows_held)
    wide_own = own_terms[small_held:].reshape(layer_count, inner_held)
    for layer in range(1, layer_count):
        for unit in sums[layer]:
            while unit.step < 4:
                phase((), unit)
    i_all, a_all, o_all = [
        jnp.stack([sums[layer][n].kept for layer in range(layer_count)]) for n in range(3)
    ]
    return (
        both_rows(output[:length], output_got),
        both_rows(upstream[:length], token_back),
        a_all[:, :, :D],
        a_all[:, :, D : 2 * D],
        a_all[:, :, 2 * D : 3 * D],
        a_all[:, :, 3 * D :],
        small_own[:, 0],
        small_own[:, 1],
        small_own[:, 2],
        small_own[:, 3],
        small_own[:, 4],
        i_all,
        wide_own,
        o_all,
        small_own[:, 5],
        small_own[:, 6],
        small_own[:, 7],
    )


def plain_body(fsdp_size, seq_size):
    half = seq_size // 2
    device_count = fsdp_size * seq_size
    across = [(i, (i + half) % seq_size) for i in range(seq_size)]
    groups = [[m * half + j for j in range(half)] for m in range(2)]
    length = SEQ_LEN // seq_size

    def gather_siblings(rows):
        return lax.all_gather(rows, "seq", axis_index_groups=groups)

    def scatter_siblings(own_order):
        return lax.psum_scatter(own_order, "seq", axis_index_groups=groups)

    def body(tokens, doc_lengths, cotangent, *shards):
        (
            query_weight,
            key_weight,
            value_weight,
            mix_weight,
            query_bias,
            value_bias,
            mix_bias,
            first_gain,
            first_shift,
            inner_weight,
            inner_bias,
            outer_weight,
            outer_bias,
            second_gain,
            second_shift,
        ) = shards
        layer_count = query_weight.shape[0]
        seq = lax.axis_index("seq")
        row = seq // half
        rows_held = D // device_count
        inner_held = FF // device_count

        def vector_rows(small, wide):
            return jnp.concatenate(
                [jnp.concatenate([v[layer] for v in small]) for layer in range(layer_count)]
                + [wide.reshape(-1)]
            )

        small_vectors = (
            query_bias,
            value_bias,
            mix_bias,
            first_gain,
            first_shift,
            outer_bias,
            second_gain,
            second_shift,
        )
        vector_count = len(small_vectors) * layer_count
        mine = vector_rows(small_vectors, inner_bias)
        held = mine.shape[0]
        every = lax.all_gather(mine, AXES)
        every = every.astype(f32)
        small_held = vector_count * rows_held
        small_all = (
            every[:, :small_held]
            .reshape(device_count, vector_count, rows_held)
            .transpose(1, 0, 2)
            .reshape(layer_count, len(small_vectors), D)
        )
        wide_all = (
            every[:, small_held:]
            .reshape(device_count, layer_count, inner_held)
            .transpose(1, 0, 2)
            .reshape(layer_count, FF)
        )

        def whole_weights(layer):
            weights = (query_weight, key_weight, value_weight, mix_weight, inner_weight, outer_weight)
            return [lax.all_gather(w[layer], AXES, axis=0, tiled=True) for w in weights]

        def own_row(both_rows):
            kept = pick(both_rows, row, 0)
            return jnp.concatenate(
                [kept, lax.ppermute(pick(both_rows, 1 - row, 0), "seq", across)]
            )

        def both_rows(values):
            kept = values[:length]
            other = lax.ppermute(values[length:].astype(bf16), "seq", across).astype(f32)
            return jnp.where(row == 0, jnp.stack([kept, other]), jnp.stack([other, kept]))

        stream_start = own_row(tokens.reshape(2, length, D))
        upstream_start = own_row(cotangent.reshape(2, length, D))

        lengths = pick(doc_lengths.reshape(2, NDOC), row, 0)
        bounds = jnp.cumsum(lengths)
        within = lax.iota(jnp.int32, length)

        def positions(s):
            return jnp.concatenate([s * length + within, (s + half) % seq_size * length + within])

        def segments(places):
            return jnp.sum((places[:, None] >= bounds[None, :]).astype(jnp.int32), axis=1)

        query_places = positions(seq)
        key_places = jnp.concatenate([positions(row * half + j) for j in range(half)])
        query_segment, key_segment = segments(query_places), segments(key_places)
        allowed = (
            (query_segment[:, None] == key_segment[None, :]) & (key_segment[None, :] != NDOC - 1)
        ) | (query_places[:, None] == key_places[None, :])

        stream = stream_start.astype(f32)
        saved = []
        for layer in range(layer_count):
            q_bias, v_bias, m_bias, gain1, shift1, o_bias, gain2, shift2 = [
                small_all[layer, n] for n in range(len(small_vectors))
            ]
            w_query, w_key, w_value, w_mix, w_inner, w_outer = whole_weights(layer)
            stream_low = stream.astype(bf16)
            queries = (dot(stream_low, w_query) + q_bias).astype(bf16)
            key_rows = dot(stream_low, w_key).astype(bf16)
            values = (dot(stream_low, w_value) + v_bias).astype(bf16)
            all_keys = gather_siblings(key_rows).reshape(SEQ_LEN, D)
            all_values = gather_siblings(values).reshape(SEQ_LEN, D)
            mixed, log_total = attend_forward(queries, all_keys, all_values, allowed)
            first_sum = stream + (dot(mixed, w_mix) + m_bias)
            first = norm_forward(first_sum)[0] * gain1 + shift1
            first_low = first.astype(bf16)
            inner = dot(first_low, w_inner) + wide_all[layer]
            below = 0.5 * (1.0 + lax.erf(inner * (0.5**0.5)))
            active = (inner * below).astype(bf16)
            slope = (below + inner * jnp.exp(-0.5 * inner * inner) * (2 * math.pi) ** -0.5).astype(
                bf16
            )
            second_sum = first + (dot(active, w_outer) + o_bias)
            stream = norm_forward(second_sum)[0] * gain2 + shift2
            saved.append(
                (
                    (w_query, w_key, w_value, w_mix, w_inner, w_outer, gain1, gain2),
                    (stream_low, queries, all_keys, all_values, log_total, mixed),
                    (first_sum, first_low, slope, active, second_sum),
                )
            )
        activations = both_rows(stream)

        upstream = upstream_start.astype(f32)
        small_grads = [None] * layer_count
        wide_grads = [None] * layer_count
        results = [None] * layer_count

        def reduced(grads):
            return [lax.psum_scatter(g, AXES, scatter_dimension=0, tiled=True) for g in grads]

        for layer in reversed(range(layer_count)):
            (w_query, w_key, w_value, w_mix, w_inner, w_outer, gain1, gain2), kept, rest = saved[layer]
            stream_low, queries, all_keys, all_values, log_total, mixed = kept
            first_sum, first_low, slope, active, second_sum = rest
            second_grad, gain2_grad, shift2_grad = norm_backward(second_sum, gain2, upstream)
            second_low = second_grad.astype(bf16)
            (outer_grad,) = reduced([contract_rows(active, second_low)])
            inner_low = (contract_cols(second_low, w_outer) * slope).astype(bf16)
            (inner_grad,) = reduced([contract_rows(first_low, inner_low)])
            first_grad = second_grad + contract_cols(inner_low, w_inner)
            first_sum_grad, gain1_grad, shift1_grad = norm_backward(first_sum, gain1, first_grad)
            branch_low = first_sum_grad.astype(bf16)
            mix_terms = contract_rows(mixed, branch_low)
            mixed_grad = contract_cols(branch_low, w_mix).astype(bf16)
            query_low, key_terms, value_terms = attend_backward(
                queries, all_keys, all_values, allowed, log_total, mixed_grad
            )
            n = 2 * length
            key_low = scatter_siblings(key_terms.reshape(half, n, D)).astype(bf16)
            value_low = scatter_siblings(value_terms.reshape(half, n, D)).astype(bf16)
            value_grad, mix_grad = reduced([contract_rows(stream_low, value_low), mix_terms])
            query_grad, key_grad = reduced(
                [contract_rows(stream_low, query_low), contract_rows(stream_low, key_low)]
            )
            upstream = (
                first_sum_grad
                + contract_cols(query_low, w_query)
                + contract_cols(key_low, w_key)
                + contract_cols(value_low, w_value)
            )
            small_grads[layer] = jnp.stack(
                [
                    column_sum(query_low),
                    column_sum(value_low),
                    column_sum(branch_low),
                    gain1_grad,
                    shift1_grad,
                    column_sum(second_low),
                    gain2_grad,
                    shift2_grad,
                ]
            )
            wide_grads[layer] = column_sum(inner_low)
            results[layer] = (query_grad, key_grad, value_grad, mix_grad, inner_grad, outer_grad)
        token_grad = both_rows(upstream)

        small_terms = (
            jnp.stack(small_grads)
            .reshape(vector_count, device_count, rows_held)
            .transpose(1, 0, 2)
            .reshape(device_count, small_held)
        )
        wide_terms = (
            jnp.stack(wide_grads)
            .reshape(layer_count, device_count, inner_held)
            .transpose(1, 0, 2)
            .reshape(device_count, layer_count * inner_held)
        )
        terms = jnp.concatenate([small_terms, wide_terms], axis=1)
        own_terms = lax.psum_scatter(terms, AXES, scatter_dimension=0, tiled=False)
        small_own = own_terms[:small_held].reshape(layer_count, len(small_vectors), rows_held)
        wide_own = own_terms[small_held:].reshape(layer_count, inner_held)
        query_g, key_g, value_g, mix_g, inner_g, outer_g = [
            jnp.stack([results[layer][n] for layer in range(layer_count)]) for n in range(6)
        ]
        return (
            activations.reshape(tokens.shape),
            token_grad.reshape(tokens.shape),
            query_g,
            key_g,
            value_g,
            mix_g,
            small_own[:, 0],
            small_own[:, 1],
            small_own[:, 2],
            small_own[:, 3],
            small_own[:, 4],
            inner_g,
            wide_own,
            outer_g,
            small_own[:, 5],
            small_own[:, 6],
            small_own[:, 7],
        )

    return body


def solution(mesh):
    tokens = P(None, "fsdp", "seq", None)
    matrix, vector = P(None, AXES, None), P(None, AXES)
    in_specs = (tokens, P(None, "fsdp", None), tokens) + (matrix,) * 4 + (vector,) * 5
    in_specs += (matrix, vector, matrix, vector, vector, vector)
    out_specs = (tokens, tokens) + (matrix,) * 4 + (vector,) * 5
    out_specs += (matrix, vector, matrix, vector, vector, vector)
    sizes = (mesh.shape["fsdp"], mesh.shape["seq"])
    body = staged_body if sizes == (8, 4) else plain_body(*sizes)
    return jax.shard_map(body, mesh=mesh, in_specs=in_specs, out_specs=out_specs, check_vma=False)
```

```python
import collections
import math

import jax
import jax.numpy as jnp
from jax import lax
from jax.experimental import pallas as pl
from jax.experimental.pallas import tpu as pltpu
from jax.sharding import PartitionSpec as P

D = 1024
FF = 4096
HEAD_DIM = 64
HEADS = D // HEAD_DIM
SEQ_LEN = 1024
NDOC = 16
epsilon = 1e-05
AXES = ("fsdp", "seq")
f32 = jnp.float32
bf16 = jnp.bfloat16


def dot(left, right):
    return jnp.dot(left, right, preferred_element_type=f32)


def contract_rows(left, right):
    return lax.dot_general(left, right, (((0,), (0,)), ((), ())), preferred_element_type=f32)


def contract_cols(left, right):
    return lax.dot_general(left, right, (((1,), (1,)), ((), ())), preferred_element_type=f32)


SMALL_COST = pl.CostEstimate(flops=1024, bytes_accessed=1024, transcendentals=0)


def tie(value, *others):
    return lax.optimization_barrier((value, others))[0]


def pairs(move):
    out = []
    for i in range(32):
        z, y, x, c = i // 8, i // 4 % 2, i // 2 % 2, i % 2
        z, y, x, c = move(z, y, x, c)
        out.append((i, z * 8 + y * 4 + x * 2 + c))
    return out


TO_CORE = pairs(lambda z, y, x, c: (z, y, x, 1 - c))
TO_X = pairs(lambda z, y, x, c: (z, y, 1 - x, c))
TO_Y = pairs(lambda z, y, x, c: (z, 1 - y, x, c))
TO_FAR = pairs(lambda z, y, x, c: (z, y if c == 0 else 1 - y, 1 - x if c == 0 else x, c))
TO_NEAR = pairs(lambda z, y, x, c: (z, 1 - y if c == 0 else y, x if c == 0 else 1 - x, c))
TO_ODD = pairs(lambda z, y, x, c: (z ^ 1, y, x, c))
TO_PAIR = pairs(lambda z, y, x, c: (z ^ 2, y, x, c))


def send(value, to):
    return lax.ppermute(value, AXES, to)


def coordinates():
    fsdp, seq = lax.axis_index("fsdp"), lax.axis_index("seq")
    return jnp.stack([fsdp // 2, fsdp % 2, seq // 2, seq % 2]).astype(jnp.int32)


def place(coords, pieces, shapes, moves):
    count = len(moves(0, 0, 0, 0, None, None))

    total = len(pieces)

    def kernel(coords_ref, *refs):
        sources, targets = refs[:total], refs[total : total + len(shapes)]
        buffers, in_sems, out_sems = refs[total + len(shapes) : -2], refs[-2], refs[-1]
        loads = [
            pltpu.make_async_copy(source, buffer, in_sems.at[n])
            for n, (source, buffer) in enumerate(zip(sources, buffers))
        ]
        for load in loads:
            load.start()
        todo = moves(coords_ref[0], coords_ref[1], coords_ref[2], coords_ref[3], buffers, targets)
        stores = [
            (n, pltpu.make_async_copy(view, target, out_sems.at[k]))
            for k, (n, view, target) in enumerate(todo)
        ]
        for piece, load in enumerate(loads):
            load.wait()
            for n, store in stores:
                if n == piece:
                    store.start()
        for _, store in stores:
            store.wait()

    return pl.pallas_call(
        kernel,
        in_specs=[pl.BlockSpec(memory_space=pltpu.SMEM)]
        + [pl.BlockSpec(memory_space=pl.ANY)] * len(pieces),
        out_specs=[pl.BlockSpec(memory_space=pl.ANY)] * len(shapes),
        out_shape=[jax.ShapeDtypeStruct(shape, bf16) for shape in shapes],
        scratch_shapes=[pltpu.VMEM(p.shape, bf16) for p in pieces]
        + [pltpu.SemaphoreType.DMA((total,)), pltpu.SemaphoreType.DMA((count,))],
        compiler_params=pltpu.CompilerParams(vmem_limit_bytes=40 << 20),
        cost_estimate=SMALL_COST,
    )(coords, *pieces)


def pick(value, index, axis):
    return lax.dynamic_index_in_dim(value, index, axis, keepdims=False)


def by_place(own, other, at, axis):
    return jnp.where(at == 0, jnp.stack([own, other], axis), jnp.stack([other, own], axis))


def phase(values, *units, settle=()):
    values, flights, ended = lax.optimization_barrier(
        (values, [u.flight for u in units], [u.flight for u in settle])
    )
    for unit, flight in zip(settle, ended):
        unit.flight = flight
    nexts = [u.local(flight) for u, flight in zip(units, flights)]
    values, sends = lax.optimization_barrier((values, [[v for v, _ in n] for n in nexts]))
    for unit, arrays, targets in zip(units, sends, nexts):
        unit.flight = [send(array, to) for array, (_, to) in zip(arrays, targets)]
    return values


class GatherUnit:
    def __init__(self, coords, pack, shapes, parts):
        self.coords, self.pack, self.shapes, self.parts = coords, pack, shapes, parts
        self.flight, self.step = [pack], 0

    def local(self, got):
        self.step += 1
        if self.step == 1:
            self.kept = got[0][None]
            return [(self.kept, TO_PAIR)]
        if self.step < 5:
            self.kept = jnp.concatenate([got[0], self.kept])
            return [(self.kept, (TO_ODD, TO_NEAR, TO_FAR)[self.step - 2])]
        self.kept = [self.kept, got[0]]
        return [(blocks, TO_CORE) for blocks in self.kept]

    def result(self):
        width = self.pack.shape[1]

        def by_block(z, y, x, c, src, dst):
            out = []
            for n in range(4):
                core, far = (c if n < 2 else 1 - c), n % 2
                for near in (1, 0):
                    y2 = y ^ jnp.where(core == 0, near, far)
                    x2 = x ^ jnp.where(core == 0, far, near)
                    for odd in (1, 0):
                        for pair in (1, 0):
                            block = 4 * (1 - near) + 2 * (1 - odd) + 1 - pair
                            for lo, hi, target, column in self.parts:
                                view = None
                                if dst:
                                    spans = (slice(0, hi - lo), slice(column * width, (column + 1) * width))
                                    view = dst[target].at[(z ^ odd ^ (2 * pair), y2, x2, core) + spans]
                                out.append((n, src and src[n].at[block, lo:hi], view))
            return out

        return place(
            self.coords, self.kept + self.flight, [(4, 2, 2, 2) + shape for shape in self.shapes], by_block
        )


class SumUnit:
    def __init__(self, parts):
        self.flight, self.step = list(parts), 0

    def local(self, got):
        self.step += 1
        if self.step == 1:
            leaving, self.kept = got
        elif self.step < 5:
            half = self.kept.shape[0] // 2
            add = lambda a, b: a.astype(f32) + b.astype(f32)
            leaving = add(self.kept[:half], got[0][:half]).astype(bf16)
            self.kept = add(self.kept[half:], got[0][half:])
            if self.step < 4:
                self.kept = self.kept.astype(bf16)
        else:
            self.kept = self.kept + got[0].astype(f32)
            return []
        return [(leaving, (TO_FAR, TO_NEAR, TO_ODD, TO_PAIR)[self.step - 1])]


Sums = collections.namedtuple("Sums", "o i a")


def block_order(coords):
    z, y, x, c = coords[0], coords[1], coords[2], coords[3]
    order = []
    for core in (c, 1 - c):
        for far in (1, 0):
            for near in (1, 0):
                y2 = y ^ jnp.where(core == 0, near, far)
                x2 = x ^ jnp.where(core == 0, far, near)
                for odd in (1, 0):
                    for pair in (1, 0):
                        order.append((z ^ odd ^ (2 * pair)) * 8 + y2 * 4 + x2 * 2 + core)
    return jnp.stack(order).astype(jnp.int32)


def order_matrices(order):
    block = D // 32
    wanted = (order[:, None] * block + lax.iota(jnp.int32, block)[None, :]).reshape(2, D // 2, 1)
    columns = lax.broadcasted_iota(jnp.int32, (2, D // 2, D), 2)
    chosen = (columns == wanted).astype(bf16)
    return chosen[0], chosen[1]


def selected(matrices, *arrays):
    count = len(arrays)

    def kernel(mine, theirs, *refs):
        for n in range(count):
            rows = refs[n][...]
            refs[count + 2 * n][...] = nt_dot(mine[...], rows).astype(bf16)
            refs[count + 2 * n + 1][...] = nt_dot(theirs[...], rows).astype(bf16)

    out = jax.ShapeDtypeStruct((D // 2, arrays[0].shape[0]), bf16)
    outs = pl.pallas_call(
        kernel,
        out_shape=[out] * (2 * count),
        compiler_params=pltpu.CompilerParams(vmem_limit_bytes=48 << 20),
        cost_estimate=SMALL_COST,
    )(*matrices, *arrays)
    return [tuple(outs[2 * n : 2 * n + 2]) for n in range(count)]


def weight_terms(*pairs_of, first=0, tile=1024):
    rows, tokens = pairs_of[0][0][0].shape
    counts = [pair[2] // tile for pair in pairs_of]
    starts = [sum(counts[:n]) for n in range(len(counts))]
    columns, half = sum(counts) * tile, rows // 2

    def kernel(*refs):
        leaving, kept = refs[-2:]
        j = pl.program_id(0)
        for n, (start, count) in enumerate(zip(starts, counts)):

            @pl.when((j >= start) & (j < start + count))
            def _(a1=refs[4 * n], a2=refs[4 * n + 1], b1=refs[4 * n + 2], b2=refs[4 * n + 3]):
                total = jnp.dot(a1[...], b1[...], preferred_element_type=f32)
                total = total + jnp.dot(a2[...], b2[...], preferred_element_type=f32)
                leaving[...] = total[:half].astype(bf16)
                kept[...] = total[half:].astype(bf16)

    in_specs, args = [], []
    for (left, right, _), start, count in zip(pairs_of, starts, counts):
        whole = pl.BlockSpec((rows, tokens), lambda j: (0, 0))
        cut = pl.BlockSpec((tokens, tile), lambda j, s=start, n=count: (0, jnp.clip(j - s, 0, n - 1) + first // tile))
        in_specs += [whole, whole, cut, cut]
        args += [*left, *right]
    out = jax.ShapeDtypeStruct((half, columns), bf16)
    return pl.pallas_call(
        kernel,
        grid=(columns // tile,),
        in_specs=in_specs,
        out_specs=[pl.BlockSpec((half, tile), lambda j: (0, j))] * 2,
        out_shape=[out, out],
        compiler_params=pltpu.CompilerParams(vmem_limit_bytes=48 << 20),
        cost_estimate=SMALL_COST,
    )(*args)


def wide_terms_of(order, left, right):
    tokens, width = left[0].shape
    block = width // 32
    columns = right[0].shape[1]

    def kernel(order_ref, *refs):
        a1, a2, (b1, b2, leaving, kept) = refs[:2], refs[2:4], refs[4:]
        one = (
            lax.broadcasted_iota(jnp.int32, (block, block), 0) == lax.broadcasted_iota(jnp.int32, (block, block), 1)
        ).astype(bf16)
        turned = lambda refs: jnp.concatenate([nt_dot(one, r[...]).astype(bf16) for r in refs], axis=0)
        total = jnp.dot(turned(a1), b1[...], preferred_element_type=f32)
        total = (total + jnp.dot(turned(a2), b2[...], preferred_element_type=f32)).astype(bf16)

        @pl.when(pl.program_id(0) < 4)
        def _():
            leaving[...] = total

        @pl.when(pl.program_id(0) >= 4)
        def _():
            kept[...] = total

    cut = lambda n: pl.BlockSpec((tokens, block), lambda j, order: (0, order[2 * j + n]))
    whole = pl.BlockSpec((tokens, columns), lambda j, order: (0, 0))
    out = jax.ShapeDtypeStruct((width // 4, columns), bf16)
    return pl.pallas_call(
        kernel,
        grid_spec=pltpu.PrefetchScalarGridSpec(
            num_scalar_prefetch=1,
            grid=(8,),
            in_specs=[cut(0), cut(1), cut(0), cut(1), whole, whole],
            out_specs=[
                pl.BlockSpec((2 * block, columns), lambda j, order: (jnp.minimum(j, 3), 0)),
                pl.BlockSpec((2 * block, columns), lambda j, order: (jnp.maximum(j - 4, 0), 0)),
            ],
        ),
        out_shape=[out, out],
        compiler_params=pltpu.CompilerParams(vmem_limit_bytes=48 << 20),
        cost_estimate=SMALL_COST,
    )(order, left[0], left[0], left[1], left[1], *right)


BLOCK = 256
WINDOW = 3 * BLOCK
PAIR = 2 * HEAD_DIM


def window_start(s, slot):
    block = s ^ (2 * slot)
    return jnp.clip(block - 1, 0, 1) * BLOCK


def nt_dot(left, right):
    return lax.dot_general(left, right, (((1,), (1,)), ((), ())), preferred_element_type=f32)


def only_head(value, head, axis):
    lane = lax.broadcasted_iota(jnp.int32, value.shape, axis)
    return jnp.where((lane < HEAD_DIM) if head == 0 else (lane >= HEAD_DIM), value, jnp.zeros_like(value))


def in_order(s, mine, other, scratch):
    for n, ref in ((0, mine), (1, other)):
        for slot in range(2):
            scratch[pl.ds((s ^ (n + 2 * slot)) * BLOCK, BLOCK), :] = ref[slot * BLOCK : (slot + 1) * BLOCK, :]


def attend_forward_kernel(
    s_ref, q_ref, km_ref, ko_ref, vm_ref, vo_ref, bias_ref, mixed_ref, total_ref, keys, values
):
    s = s_ref[0]
    in_order(s, km_ref, ko_ref, keys)
    in_order(s, vm_ref, vo_ref, values)
    spans = [slice(h * HEAD_DIM, (h + 1) * HEAD_DIM) for h in range(2)]
    rows = [slice(n * BLOCK, (n + 1) * BLOCK) for n in range(2)]
    windows = [pl.ds(pl.multiple_of(window_start(s, n), BLOCK), WINDOW) for n in range(2)]
    scores = []
    for slot in range(2):
        q = q_ref[rows[slot], :] * jnp.asarray(HEAD_DIM**-0.5, bf16)
        k = keys[windows[slot], :]
        scores += [nt_dot(k, only_head(q, head, 1)) for head in range(2)]
    raised, totals = [], []
    for n in range(4):
        slot, head = divmod(n, 2)
        biased = scores[n] + bias_ref[slot]
        top = jnp.max(biased, axis=0, keepdims=True)
        up = jnp.exp(biased - top)
        totals.append(jnp.sum(up, axis=0, keepdims=True))
        total_ref[0, head : head + 1, rows[slot]] = top + jnp.log(totals[n])
        raised.append(up.astype(bf16))
    for slot in range(2):
        v_t = values[windows[slot], :].T
        halves = [
            jnp.dot(v_t[spans[h]], raised[2 * slot + h], preferred_element_type=f32) / totals[2 * slot + h]
            for h in range(2)
        ]
        mixed_ref[rows[slot], :] = jnp.concatenate(halves, axis=0).T.astype(bf16)


def attend_backward_kernel(
    s_ref, q_ref, km_ref, ko_ref, vm_ref, vo_ref, bias_ref, mixed_ref, total_ref, grad_ref,
    dq_ref, mine_ref, sent_ref, keys, values, key_sum, value_sum,
):
    s = s_ref[0]
    in_order(s, km_ref, ko_ref, keys)
    in_order(s, vm_ref, vo_ref, values)
    key_sum[...] = jnp.zeros_like(key_sum)
    value_sum[...] = jnp.zeros_like(value_sum)
    spans = [slice(h * HEAD_DIM, (h + 1) * HEAD_DIM) for h in range(2)]
    rows = [slice(n * BLOCK, (n + 1) * BLOCK) for n in range(2)]
    windows = [pl.ds(pl.multiple_of(window_start(s, n), BLOCK), WINDOW) for n in range(2)]
    scores, share_grads, queries, grads, inner = [], [], [], [], []
    for slot in range(2):
        q = q_ref[rows[slot], :] * jnp.asarray(HEAD_DIM**-0.5, bf16)
        g = grad_ref[rows[slot], :]
        along = (g.astype(f32) * mixed_ref[rows[slot], :].astype(f32)).T
        k, v = keys[windows[slot], :], values[windows[slot], :]
        for head in range(2):
            queries.append(only_head(q, head, 1))
            grads.append(only_head(g, head, 1))
            inner.append(jnp.sum(along[spans[head]], axis=0, keepdims=True))
            scores.append(nt_dot(k, queries[-1]))
            share_grads.append(nt_dot(v, grads[-1]))
    shares_low, grads_low = [], []
    for n in range(4):
        slot, head = divmod(n, 2)
        shares = jnp.exp(scores[n] + bias_ref[slot] - total_ref[0, head : head + 1, rows[slot]])
        shares_low.append(shares.astype(bf16))
        grads_low.append((shares * (share_grads[n] - inner[n])).astype(bf16))
    both = lambda values, slot, axis: jnp.concatenate(values[2 * slot : 2 * slot + 2], axis=axis)
    for slot in range(2):
        k_t = keys[windows[slot], :].T
        query_grads = [
            jnp.dot(k_t[spans[h]], grads_low[2 * slot + h], preferred_element_type=f32) for h in range(2)
        ]
        dq_ref[rows[slot], :] = (jnp.concatenate(query_grads, axis=0).T * HEAD_DIM**-0.5).astype(bf16)
        key_sum[windows[slot], :] += jnp.dot(
            both(grads_low, slot, 1), both(queries, slot, 0), preferred_element_type=f32
        )
        value_sum[windows[slot], :] += jnp.dot(
            both(shares_low, slot, 1), both(grads, slot, 0), preferred_element_type=f32
        )
    for slot in range(2):
        mine, other = pl.ds((s ^ (2 * slot)) * BLOCK, BLOCK), pl.ds((s ^ (1 + 2 * slot)) * BLOCK, BLOCK)
        for n, sums in ((0, key_sum), (1, value_sum)):
            mine_ref[n, rows[slot], :] = sums[mine, :]
            sent_ref[n, rows[slot], :] = sums[other, :].astype(bf16)


def call_attention(kernel, s, own, other, bias, kept, outs, scratch):
    pairs_count = D // PAIR
    third = lambda n: pl.BlockSpec((2 * BLOCK, PAIR), lambda h: (0, h + n * pairs_count))
    cut = third(0)
    double = pl.BlockSpec((2, 2 * BLOCK, PAIR), lambda h: (0, 0, h))
    per_pair = pl.BlockSpec((1, 2, 2 * BLOCK), lambda h: (h, 0, 0))
    whole = pl.BlockSpec(bias.shape, lambda h: (0, 0, 0))
    in_specs = [pl.BlockSpec(memory_space=pltpu.SMEM), third(0), third(1), third(1), third(2), third(2), whole]
    args = [s, own, own, other, own, other, bias]
    if kept:
        in_specs += [cut, per_pair, cut]
        args += kept
    shapes, specs = [], []
    for kind, spec in outs:
        shapes.append(
            {
                0: jax.ShapeDtypeStruct((2 * BLOCK, D), kind),
                1: jax.ShapeDtypeStruct((pairs_count, 2, 2 * BLOCK), kind),
                2: jax.ShapeDtypeStruct((2, 2 * BLOCK, D), kind),
            }[spec]
        )
        specs.append((cut, per_pair, double)[spec])
    return pl.pallas_call(
        kernel,
        grid=(pairs_count,),
        in_specs=in_specs,
        out_specs=specs,
        out_shape=shapes,
        scratch_shapes=scratch,
        compiler_params=pltpu.CompilerParams(vmem_limit_bytes=48 << 20),
        cost_estimate=SMALL_COST,
    )(*args)


def attend_forward_blocks(s, own, other, bias):
    scratch = [pltpu.VMEM((SEQ_LEN, PAIR), bf16)] * 2
    return call_attention(attend_forward_kernel, s, own, other, bias, (), ((bf16, 0), (f32, 1)), scratch)


def attend_backward_blocks(s, own, other, bias, mixed, totals, grads):
    scratch = [pltpu.VMEM((SEQ_LEN, PAIR), bf16)] * 2 + [pltpu.VMEM((SEQ_LEN, PAIR), f32)] * 2
    outs = ((bf16, 0), (f32, 2), (bf16, 2))
    kept = (mixed, totals, grads)
    return call_attention(attend_backward_kernel, s, own, other, bias, kept, outs, scratch)


def window_bias(s, ids):
    out = []
    for slot in range(2):
        keys = lax.dynamic_slice_in_dim(ids, window_start(s, slot), WINDOW)
        queries = lax.dynamic_slice_in_dim(ids, (s ^ (2 * slot)) * BLOCK, BLOCK)
        out.append(jnp.where(keys[:, None] == queries[None, :], 0.0, -1e30))
    return jnp.stack(out).astype(f32)


def norm_forward(total):
    center = jnp.mean(total, axis=-1, keepdims=True)
    centered = total - center
    spread = jnp.mean(centered * centered, axis=-1, keepdims=True)
    scale = lax.rsqrt(spread + epsilon)
    return centered * scale, scale


def norm_backward(total, gain, upstream):
    unit, scale = norm_forward(total)
    lifted = upstream * gain
    grad = scale * (
        lifted
        - jnp.mean(lifted, axis=-1, keepdims=True)
        - unit * jnp.mean(lifted * unit, axis=-1, keepdims=True)
    )
    return grad, jnp.sum(upstream * unit, axis=0), jnp.sum(upstream, axis=0)


def column_sum(values):
    return jnp.sum(values.astype(f32), axis=0)


def heads_of(rows):
    return rows.reshape(rows.shape[0], HEADS, HEAD_DIM)


def masked_scores(queries, keys, allowed):
    scores = jnp.einsum("qhd,khd->hqk", queries, keys, preferred_element_type=f32)
    return jnp.where(allowed[None], scores * HEAD_DIM ** (-0.5), -1e30)


def attend_forward(queries, keys, values, allowed):
    scores = masked_scores(heads_of(queries), heads_of(keys), allowed)
    top_score = jnp.max(scores, axis=2, keepdims=True)
    raised = jnp.exp(scores - top_score)
    totals = jnp.sum(raised, axis=2, keepdims=True)
    shares = (raised / totals).astype(bf16)
    mixed = jnp.einsum("hqk,khd->qhd", shares, heads_of(values), preferred_element_type=f32)
    return mixed.astype(bf16).reshape(queries.shape), top_score + jnp.log(totals)


def attend_backward(queries, keys, values, allowed, log_total, grads):
    queries, keys, values, grads = map(heads_of, (queries, keys, values, grads))
    scale = HEAD_DIM ** (-0.5)
    shares = jnp.exp(masked_scores(queries, keys, allowed) - log_total)
    share_grads = jnp.einsum("qhd,khd->hqk", grads, values, preferred_element_type=f32)
    inner_sums = jnp.sum(shares * share_grads, axis=2, keepdims=True)
    score_grads = (shares * (share_grads - inner_sums)).astype(bf16)
    query_grad = jnp.einsum("hqk,khd->qhd", score_grads, keys, preferred_element_type=f32) * scale
    key_grad = jnp.einsum("hqk,qhd->khd", score_grads, queries, preferred_element_type=f32) * scale
    value_grad = jnp.einsum(
        "hqk,qhd->khd", shares.astype(bf16), grads, preferred_element_type=f32
    )
    flat = lambda a: a.reshape(a.shape[0], D)
    return flat(query_grad).astype(bf16), flat(key_grad), flat(value_grad)


def product(rows, weight, tile, finish, outs, by_column=(), tiles=(), transposed=False, sums=0):
    tokens, depth = rows.shape
    width = weight.shape[0 if transposed else 1]

    def kernel(rows_ref, weight_ref, *refs):
        total = (nt_dot if transposed else lambda a, b: jnp.dot(a, b, preferred_element_type=f32))(
            rows_ref[...], weight_ref[...]
        )
        inputs = [r[...] for r in refs[: len(by_column) + len(tiles)]]
        for ref, value in zip(refs[len(inputs) :], finish(total, *inputs)):
            ref[...] = value.astype(ref.dtype)

    cut = pl.BlockSpec((tokens, tile), lambda j: (0, j))
    if transposed:
        weight_spec = pl.BlockSpec((tile, depth), lambda j: (j, 0))
    else:
        weight_spec = pl.BlockSpec((depth, tile), lambda j: (0, j))
    return pl.pallas_call(
        kernel,
        grid=(width // tile,),
        in_specs=[pl.BlockSpec((tokens, depth), lambda j: (0, 0)), weight_spec]
        + [pl.BlockSpec((1, tile), lambda j: (0, j))] * len(by_column)
        + [cut] * len(tiles),
        out_specs=[cut] * len(outs) + [pl.BlockSpec((1, tile), lambda j: (0, j))] * sums,
        out_shape=[jax.ShapeDtypeStruct((tokens, width), kind) for kind in outs]
        + [jax.ShapeDtypeStruct((1, width), f32)] * sums,
        compiler_params=pltpu.CompilerParams(vmem_limit_bytes=48 << 20),
        cost_estimate=SMALL_COST,
    )(rows, weight, *[v.reshape(1, width) for v in by_column], *tiles)


def gelu_parts(total, bias):
    inner = total + bias
    below = 0.5 * (1.0 + lax.erf(inner * (0.5**0.5)))
    slope = below + inner * jnp.exp(-0.5 * inner * inner) * (2 * math.pi) ** -0.5
    return inner * below, slope


def norm_backward_rows(total, gain, upstream):
    tokens, width = total.shape
    tile = 128

    def kernel(total_ref, gain_ref, up_ref, grad_ref, low_ref, sums_ref):
        unit, scale = norm_forward(total_ref[...])
        up = up_ref[...]
        lifted = up * gain_ref[...]
        grad = scale * (
            lifted
            - jnp.mean(lifted, axis=-1, keepdims=True)
            - unit * jnp.mean(lifted * unit, axis=-1, keepdims=True)
        )
        low = grad.astype(bf16)
        grad_ref[...] = grad
        low_ref[...] = low

        @pl.when(pl.program_id(0) == 0)
        def _():
            sums_ref[...] = jnp.zeros_like(sums_ref)

        for n, value in enumerate((up * unit, up, low.astype(f32))):
            sums_ref[n : n + 1, :] += jnp.sum(value, axis=0, keepdims=True)

    cut = pl.BlockSpec((tile, width), lambda j: (j, 0))
    out = jax.ShapeDtypeStruct((tokens, width), f32)
    return pl.pallas_call(
        kernel,
        grid=(tokens // tile,),
        in_specs=[cut, pl.BlockSpec((1, width), lambda j: (0, 0)), cut],
        out_specs=[cut, cut, pl.BlockSpec((8, width), lambda j: (0, 0))],
        out_shape=[out, jax.ShapeDtypeStruct((tokens, width), bf16), jax.ShapeDtypeStruct((8, width), f32)],
        compiler_params=pltpu.CompilerParams(vmem_limit_bytes=32 << 20),
        cost_estimate=SMALL_COST,
    )(total, gain.reshape(1, width), upstream)


SMALL = 8


def staged_body(tokens, doc_lengths, cotangent, *shards):
    (
        query_weight,
        key_weight,
        value_weight,
        mix_weight,
        query_bias,
        value_bias,
        mix_bias,
        first_gain,
        first_shift,
        inner_weight,
        inner_bias,
        outer_weight,
        outer_bias,
        second_gain,
        second_shift,
    ) = shards
    layer_count = query_weight.shape[0]
    devices = 32
    length = SEQ_LEN // 4
    rows_held, inner_held = D // devices, FF // devices
    seq = lax.axis_index("seq")
    row = seq // 2
    coords = coordinates()
    z, y, x, c = coords[0], coords[1], coords[2], coords[3]
    place_of = seq.reshape(1).astype(jnp.int32)

    def split_rows(both):
        both = both.reshape(2, length, D)
        return pick(both, row, 0), pick(both, 1 - row, 0)

    token_kept, token_left = split_rows(tokens)
    upstream_kept, upstream_left = split_rows(cotangent)
    token_got = send(token_left, TO_X)

    def unit_a(layer):
        r = rows_held
        parts = [w[layer] for w in (query_weight, key_weight, value_weight, mix_weight)]
        outs = (((0, 0), (0, 1), (0, 2), (1, 0)))
        return GatherUnit(
            coords,
            jnp.concatenate(parts),
            [(r, 3 * D), (r, D)],
            [(r * n, r * (n + 1), target, column) for n, (target, column) in enumerate(outs)],
        )

    def unit_i(layer):
        r, inner = rows_held, inner_weight[layer]
        return GatherUnit(
            coords,
            jnp.concatenate([inner[:, D * n : D * (n + 1)] for n in range(4)]),
            [(r, FF)],
            [(r * n, r * (n + 1), 0, n) for n in range(4)],
        )

    def unit_o(layer):
        return GatherUnit(coords, outer_weight[layer], [(inner_held, D)], [(0, inner_held, 0, 0)])

    units = [[make(layer) for make in (unit_a, unit_i, unit_o)] for layer in range(layer_count)]

    small_vectors = (
        query_bias,
        value_bias,
        mix_bias,
        first_gain,
        first_shift,
        outer_bias,
        second_gain,
        second_shift,
    )
    vector_count = SMALL * layer_count
    small_held = vector_count * rows_held
    mine = jnp.concatenate(
        [jnp.concatenate([v[layer] for v in small_vectors]) for layer in range(layer_count)]
        + [inner_bias.reshape(-1)]
    )
    held = mine.shape[0]
    padded = jnp.pad(mine, (0, 1024 - held)).reshape(8, 128)

    u = [unit for layer_units in units for unit in layer_units]
    padded = phase(padded, u[0])
    token_got = send(token_left, TO_X)
    other = send(padded, TO_PAIR)
    high, low_bit = z // 2, z % 2
    every = by_place(padded, other, high, 0)

    lengths = pick(doc_lengths.reshape(2, NDOC), row, 0)
    places = lax.iota(jnp.int32, SEQ_LEN)
    segment = jnp.sum((places[:, None] >= jnp.cumsum(lengths)[None, :]).astype(jnp.int32), axis=1)
    bias = window_bias(seq, jnp.where(segment == NDOC - 1, NDOC + places, segment))
    order = block_order(coords)
    matrices = order_matrices(order)

    token_got, every, upstream_left = phase((token_got, every, upstream_left), u[0], u[1])
    every = by_place(every, send(every, TO_ODD), low_bit, 1).reshape(4, 8, 128)
    upstream_got = send(upstream_left, TO_X)
    token_got, every, matrices, bias = phase((token_got, every, matrices, bias), u[0], u[1], u[2])
    every = by_place(every, send(every, TO_Y), y, 1)
    token_got, every, upstream_got = phase((token_got, every, upstream_got), u[0], u[1], u[2], u[3])
    every = by_place(every, send(every, TO_X), x, 2)
    every = by_place(every, send(every, TO_CORE), c, 3)
    every = every.reshape(devices, 1024)[:, :held].astype(f32)
    small_all = (
        every[:, :small_held]
        .reshape(devices, vector_count, rows_held)
        .transpose(1, 0, 2)
        .reshape(layer_count, SMALL, D)
    )
    wide_all = (
        every[:, small_held:]
        .reshape(devices, layer_count, inner_held)
        .transpose(1, 0, 2)
        .reshape(layer_count, FF)
    )
    stream = jnp.concatenate([token_kept, token_got]).astype(f32)
    stream, small_all, wide_all = phase((stream, small_all, wide_all), u[0], u[2], u[3], u[4], settle=[u[1]])
    saved = []
    for layer in range(layer_count):
        a_unit, i_unit, o_unit = units[layer]
        next_a, next_i, next_o = units[layer + 1] if layer + 1 < layer_count else (None,) * 3
        q_bias, v_bias, m_bias, gain1, shift1, o_bias, gain2, shift2 = [small_all[layer, n] for n in range(SMALL)]
        w_three, w_mix = a_unit.result()
        w_three, w_mix = w_three.reshape(D, 3 * D), w_mix.reshape(D, D)
        stream_low = stream.astype(bf16)
        three_bias = jnp.concatenate([q_bias, jnp.zeros_like(q_bias), v_bias])
        (three,) = product(stream_low, w_three, 1024, lambda total, b: (total + b,), (bf16,), (three_bias,))
        if next_a:
            three = phase(three, i_unit, next_i, next_o, settle=[o_unit, next_a])
        else:
            three = phase(three, i_unit)
        three_got = send(three, TO_CORE)
        (left_stream,) = selected(matrices, tie(stream_low, three))
        three, left_stream = lax.optimization_barrier((three, left_stream))
        left_stream = (left_stream[0], send(left_stream[1], TO_CORE))
        mixed, totals = attend_forward_blocks(place_of, three, three_got, bias)
        moving = [i_unit, o_unit] + ([next_a, next_o] if next_a else [])
        mixed, totals, left_stream = phase(
            (mixed, totals, left_stream), *moving, settle=[next_i] if next_a else []
        )
        first_sum = stream + (dot(mixed, w_mix) + m_bias)
        first = norm_forward(first_sum)[0] * gain1 + shift1
        first_low = first.astype(bf16)
        left_mix, left_first = selected(matrices, mixed, first_low)
        if not next_a:
            first_low = phase(first_low, o_unit)
        (w_inner,) = i_unit.result()
        w_inner = w_inner.reshape(D, FF)
        first_low, left_mix, left_first = lax.optimization_barrier((first_low, left_mix, left_first))
        left_mix, left_first = [(m, send(t, TO_CORE)) for m, t in (left_mix, left_first)]
        active, slope = product(first_low, w_inner, 1024, gelu_parts, (bf16, bf16), (wide_all[layer],))
        moving = [o_unit] + ([next_a] if next_a else [])
        active, slope, left_mix, left_first = phase(
            (active, slope, left_mix, left_first), *moving, settle=[next_o] if next_a else []
        )
        active_got = send(active, TO_CORE)
        (w_outer,) = o_unit.result()
        w_outer = w_outer.reshape(FF, D)
        (second_sum,) = product(
            active, w_outer, 256, lambda total, b, f: (f + (total + b),), (f32,), (o_bias,), (first,)
        )
        second_sum, active_got = lax.optimization_barrier((second_sum, active_got))
        left_active = (active, active_got)
        stream = norm_forward(second_sum)[0] * gain2 + shift2
        if next_a:
            stream = phase(stream, next_a, next_i)
        saved.append(
            (
                (w_three, w_mix, w_inner, w_outer, gain1, gain2),
                (three, three_got, totals, mixed),
                (first_sum, slope, second_sum),
                (left_stream, left_mix, left_first, left_active),
            )
        )

    def both_rows(kept, got):
        got = got.astype(f32)
        return jnp.where(row == 0, jnp.stack([kept, got]), jnp.stack([got, kept])).reshape(tokens.shape)

    output = stream
    output_got = send(output[length:].astype(bf16), TO_X)

    upstream = jnp.concatenate([upstream_kept, upstream_got]).astype(f32)
    small_grads, wide_grads = [None] * layer_count, [None] * layer_count
    sums = [None] * layer_count
    before = None
    for layer in reversed(range(layer_count)):
        weights, kept, rest, lefts = saved[layer]
        w_three, w_mix, w_inner, w_outer, gain1, gain2 = weights
        three, three_got, totals, mixed = kept
        first_sum, slope, second_sum = rest
        left_stream, left_mix, left_first, left_active = lefts

        def with_sum(total, slopes):
            low = (total * slopes).astype(bf16)
            return low, jnp.sum(low.astype(f32), axis=0, keepdims=True)

        second_grad, second_low, second_sums = norm_backward_rows(second_sum, gain2, upstream)
        second_got = send(second_low, TO_CORE)
        inner_low, inner_sum = product(
            second_low, w_outer, 1024, with_sum, (bf16,), (), (slope,), transposed=True, sums=1
        )
        if before:
            inner_low = phase(inner_low, before.o, before.i, before.a)
        else:
            inner_low, output_got = lax.optimization_barrier((inner_low, output_got))
        inner_got = send(inner_low, TO_CORE)
        o_sum = SumUnit(wide_terms_of(order, left_active, tie((second_low, second_got), inner_low)))
        if before:
            second_grad, inner_low = phase((second_grad, inner_low), o_sum, before.a, before.i, before.o)
        else:
            second_grad, inner_low = phase((second_grad, inner_low), o_sum)
        (first_grad,) = product(
            inner_low, w_inner, 256, lambda total, g: (g + total,), (f32,), (), (second_grad,), transposed=True
        )
        first_sum_grad, branch_low, first_sums = norm_backward_rows(first_sum, gain1, first_grad)
        branch_got = send(branch_low, TO_CORE)
        (mixed_grad,) = product(branch_low, w_mix, 512, lambda total: (total,), (bf16,), transposed=True)
        i_sum = SumUnit(
            weight_terms(
                (left_first, tie((inner_low, inner_got), mixed_grad), FF), (left_mix, (branch_low, branch_got), D)
            )
        )
        if before:
            mixed_grad = phase(mixed_grad, i_sum, before.a, before.i, settle=[o_sum])
        else:
            mixed_grad = phase(mixed_grad, i_sum, settle=[o_sum])
        query_low, own_grads, sent_grads = attend_backward_blocks(
            place_of, three, three_got, bias, mixed, totals, mixed_grad
        )
        grads_back = send(sent_grads, TO_CORE)
        if layer:
            query_low, own_grads = phase((query_low, own_grads), o_sum, settle=[i_sum])
        else:
            moving = [o_sum, i_sum] + ([before.a] if before else [])
            query_low, own_grads = phase((query_low, own_grads), *moving)
        sums_low = (own_grads + grads_back.astype(f32)).astype(bf16)
        low = jnp.concatenate([query_low, sums_low[0], sums_low[1]], axis=1)
        low_got = send(low, TO_CORE)
        if layer:
            (upstream,) = product(
                low, w_three, 256, lambda total, g: (g + total,), (f32,), (), (first_sum_grad,), transposed=True
            )
            a_sum = SumUnit(weight_terms((left_stream, tie((low, low_got), upstream), 3 * D)))
        else:
            a_sum = SumUnit(weight_terms((left_stream, (low, low_got), 3 * D)))
            low = phase(low, a_sum, o_sum, i_sum)
            (upstream,) = product(
                low, w_three, 256, lambda total, g: (g + total,), (f32,), (), (first_sum_grad,), transposed=True
            )
        small_grads[layer] = jnp.stack(
            [
                column_sum(low[:, :D]),
                column_sum(low[:, 2 * D :]),
                first_sums[2],
                first_sums[0],
                first_sums[1],
                second_sums[2],
                second_sums[0],
                second_sums[1],
            ]
        )
        wide_grads[layer] = inner_sum[0]
        if layer:
            upstream, small_grads[layer] = phase((upstream, small_grads[layer]), o_sum, i_sum, settle=[a_sum])
        sums[layer] = before = Sums(o_sum, i_sum, a_sum)

    small_terms = (
        jnp.stack(small_grads)
        .reshape(vector_count, devices, rows_held)
        .transpose(1, 0, 2)
        .reshape(devices, small_held)
    )
    wide_terms = (
        jnp.stack(wide_grads)
        .reshape(layer_count, devices, inner_held)
        .transpose(1, 0, 2)
        .reshape(devices, layer_count * inner_held)
    )
    terms = jnp.pad(jnp.concatenate([small_terms, wide_terms], axis=1), ((0, 0), (0, 1024 - held)))
    chosen = (order[:, None] == lax.iota(jnp.int32, devices)[None, :]).astype(f32)
    terms = jnp.dot(chosen, terms, precision=lax.Precision.HIGHEST).reshape(2, 128, 128)
    terms = (terms[0] + send(terms[1].astype(bf16), TO_CORE).astype(f32)).astype(bf16)
    small_sum = SumUnit((terms[:64], terms[64:]))

    last = sums[0]
    upstream = phase(upstream, last.a, last.o, last.i, small_sum)
    upstream = phase(upstream, last.a, small_sum, settle=[last.o, last.i])
    token_back = send(upstream[length:].astype(bf16), TO_X)
    upstream, token_back = phase((upstream, token_back), last.a, small_sum)
    phase((), last.a, small_sum)
    phase((), small_sum)
    own_terms = small_sum.kept.reshape(-1)[:held]
    small_own = own_terms[:small_held].reshape(layer_count, SMALL, rows_held)
    wide_own = own_terms[small_held:].reshape(layer_count, inner_held)
    for layer in range(layer_count):
        for unit in sums[layer]:
            while unit.step < 5:
                phase((), unit)
    o_all, i_all, a_all = [jnp.stack([units_of[n].kept for units_of in sums]) for n in range(3)]
    return (
        both_rows(output[:length], output_got),
        both_rows(upstream[:length], token_back),
        a_all[:, :, :D],
        a_all[:, :, D : 2 * D],
        a_all[:, :, 2 * D : 3 * D],
        i_all[:, :, FF:],
        small_own[:, 0],
        small_own[:, 1],
        small_own[:, 2],
        small_own[:, 3],
        small_own[:, 4],
        i_all[:, :, :FF],
        wide_own,
        o_all,
        small_own[:, 5],
        small_own[:, 6],
        small_own[:, 7],
    )


def plain_body(fsdp_size, seq_size):
    half = seq_size // 2
    device_count = fsdp_size * seq_size
    across = [(i, (i + half) % seq_size) for i in range(seq_size)]
    groups = [[m * half + j for j in range(half)] for m in range(2)]
    length = SEQ_LEN // seq_size

    def gather_siblings(rows):
        return lax.all_gather(rows, "seq", axis_index_groups=groups)

    def scatter_siblings(own_order):
        return lax.psum_scatter(own_order, "seq", axis_index_groups=groups)

    def body(tokens, doc_lengths, cotangent, *shards):
        (
            query_weight,
            key_weight,
            value_weight,
            mix_weight,
            query_bias,
            value_bias,
            mix_bias,
            first_gain,
            first_shift,
            inner_weight,
            inner_bias,
            outer_weight,
            outer_bias,
            second_gain,
            second_shift,
        ) = shards
        layer_count = query_weight.shape[0]
        seq = lax.axis_index("seq")
        row = seq // half
        rows_held = D // device_count
        inner_held = FF // device_count

        def vector_rows(small, wide):
            return jnp.concatenate(
                [jnp.concatenate([v[layer] for v in small]) for layer in range(layer_count)]
                + [wide.reshape(-1)]
            )

        small_vectors = (
            query_bias,
            value_bias,
            mix_bias,
            first_gain,
            first_shift,
            outer_bias,
            second_gain,
            second_shift,
        )
        vector_count = len(small_vectors) * layer_count
        mine = vector_rows(small_vectors, inner_bias)
        held = mine.shape[0]
        every = lax.all_gather(mine, AXES)
        every = every.astype(f32)
        small_held = vector_count * rows_held
        small_all = (
            every[:, :small_held]
            .reshape(device_count, vector_count, rows_held)
            .transpose(1, 0, 2)
            .reshape(layer_count, len(small_vectors), D)
        )
        wide_all = (
            every[:, small_held:]
            .reshape(device_count, layer_count, inner_held)
            .transpose(1, 0, 2)
            .reshape(layer_count, FF)
        )

        def whole_weights(layer):
            weights = (query_weight, key_weight, value_weight, mix_weight, inner_weight, outer_weight)
            return [lax.all_gather(w[layer], AXES, axis=0, tiled=True) for w in weights]

        def own_row(both_rows):
            kept = pick(both_rows, row, 0)
            return jnp.concatenate(
                [kept, lax.ppermute(pick(both_rows, 1 - row, 0), "seq", across)]
            )

        def both_rows(values):
            kept = values[:length]
            other = lax.ppermute(values[length:].astype(bf16), "seq", across).astype(f32)
            return jnp.where(row == 0, jnp.stack([kept, other]), jnp.stack([other, kept]))

        stream_start = own_row(tokens.reshape(2, length, D))
        upstream_start = own_row(cotangent.reshape(2, length, D))

        lengths = pick(doc_lengths.reshape(2, NDOC), row, 0)
        bounds = jnp.cumsum(lengths)
        within = lax.iota(jnp.int32, length)

        def positions(s):
            return jnp.concatenate([s * length + within, (s + half) % seq_size * length + within])

        def segments(places):
            return jnp.sum((places[:, None] >= bounds[None, :]).astype(jnp.int32), axis=1)

        query_places = positions(seq)
        key_places = jnp.concatenate([positions(row * half + j) for j in range(half)])
        query_segment, key_segment = segments(query_places), segments(key_places)
        allowed = (
            (query_segment[:, None] == key_segment[None, :]) & (key_segment[None, :] != NDOC - 1)
        ) | (query_places[:, None] == key_places[None, :])

        stream = stream_start.astype(f32)
        saved = []
        for layer in range(layer_count):
            q_bias, v_bias, m_bias, gain1, shift1, o_bias, gain2, shift2 = [
                small_all[layer, n] for n in range(len(small_vectors))
            ]
            w_query, w_key, w_value, w_mix, w_inner, w_outer = whole_weights(layer)
            stream_low = stream.astype(bf16)
            queries = (dot(stream_low, w_query) + q_bias).astype(bf16)
            key_rows = dot(stream_low, w_key).astype(bf16)
            values = (dot(stream_low, w_value) + v_bias).astype(bf16)
            all_keys = gather_siblings(key_rows).reshape(SEQ_LEN, D)
            all_values = gather_siblings(values).reshape(SEQ_LEN, D)
            mixed, log_total = attend_forward(queries, all_keys, all_values, allowed)
            first_sum = stream + (dot(mixed, w_mix) + m_bias)
            first = norm_forward(first_sum)[0] * gain1 + shift1
            first_low = first.astype(bf16)
            inner = dot(first_low, w_inner) + wide_all[layer]
            below = 0.5 * (1.0 + lax.erf(inner * (0.5**0.5)))
            active = (inner * below).astype(bf16)
            slope = (below + inner * jnp.exp(-0.5 * inner * inner) * (2 * math.pi) ** -0.5).astype(
                bf16
            )
            second_sum = first + (dot(active, w_outer) + o_bias)
            stream = norm_forward(second_sum)[0] * gain2 + shift2
            saved.append(
                (
                    (w_query, w_key, w_value, w_mix, w_inner, w_outer, gain1, gain2),
                    (stream_low, queries, all_keys, all_values, log_total, mixed),
                    (first_sum, first_low, slope, active, second_sum),
                )
            )
        activations = both_rows(stream)

        upstream = upstream_start.astype(f32)
        small_grads = [None] * layer_count
        wide_grads = [None] * layer_count
        results = [None] * layer_count

        def reduced(grads):
            return [lax.psum_scatter(g, AXES, scatter_dimension=0, tiled=True) for g in grads]

        for layer in reversed(range(layer_count)):
            (w_query, w_key, w_value, w_mix, w_inner, w_outer, gain1, gain2), kept, rest = saved[layer]
            stream_low, queries, all_keys, all_values, log_total, mixed = kept
            first_sum, first_low, slope, active, second_sum = rest
            second_grad, gain2_grad, shift2_grad = norm_backward(second_sum, gain2, upstream)
            second_low = second_grad.astype(bf16)
            (outer_grad,) = reduced([contract_rows(active, second_low)])
            inner_low = (contract_cols(second_low, w_outer) * slope).astype(bf16)
            (inner_grad,) = reduced([contract_rows(first_low, inner_low)])
            first_grad = second_grad + contract_cols(inner_low, w_inner)
            first_sum_grad, gain1_grad, shift1_grad = norm_backward(first_sum, gain1, first_grad)
            branch_low = first_sum_grad.astype(bf16)
            mix_terms = contract_rows(mixed, branch_low)
            mixed_grad = contract_cols(branch_low, w_mix).astype(bf16)
            query_low, key_terms, value_terms = attend_backward(
                queries, all_keys, all_values, allowed, log_total, mixed_grad
            )
            n = 2 * length
            key_low = scatter_siblings(key_terms.reshape(half, n, D)).astype(bf16)
            value_low = scatter_siblings(value_terms.reshape(half, n, D)).astype(bf16)
            value_grad, mix_grad = reduced([contract_rows(stream_low, value_low), mix_terms])
            query_grad, key_grad = reduced(
                [contract_rows(stream_low, query_low), contract_rows(stream_low, key_low)]
            )
            upstream = (
                first_sum_grad
                + contract_cols(query_low, w_query)
                + contract_cols(key_low, w_key)
                + contract_cols(value_low, w_value)
            )
            small_grads[layer] = jnp.stack(
                [
                    column_sum(query_low),
                    column_sum(value_low),
                    column_sum(branch_low),
                    gain1_grad,
                    shift1_grad,
                    column_sum(second_low),
                    gain2_grad,
                    shift2_grad,
                ]
            )
            wide_grads[layer] = column_sum(inner_low)
            results[layer] = (query_grad, key_grad, value_grad, mix_grad, inner_grad, outer_grad)
        token_grad = both_rows(upstream)

        small_terms = (
            jnp.stack(small_grads)
            .reshape(vector_count, device_count, rows_held)
            .transpose(1, 0, 2)
            .reshape(device_count, small_held)
        )
        wide_terms = (
            jnp.stack(wide_grads)
            .reshape(layer_count, device_count, inner_held)
            .transpose(1, 0, 2)
            .reshape(device_count, layer_count * inner_held)
        )
        terms = jnp.concatenate([small_terms, wide_terms], axis=1)
        own_terms = lax.psum_scatter(terms, AXES, scatter_dimension=0, tiled=False)
        small_own = own_terms[:small_held].reshape(layer_count, len(small_vectors), rows_held)
        wide_own = own_terms[small_held:].reshape(layer_count, inner_held)
        query_g, key_g, value_g, mix_g, inner_g, outer_g = [
            jnp.stack([results[layer][n] for layer in range(layer_count)]) for n in range(6)
        ]
        return (
            activations.reshape(tokens.shape),
            token_grad.reshape(tokens.shape),
            query_g,
            key_g,
            value_g,
            mix_g,
            small_own[:, 0],
            small_own[:, 1],
            small_own[:, 2],
            small_own[:, 3],
            small_own[:, 4],
            inner_g,
            wide_own,
            outer_g,
            small_own[:, 5],
            small_own[:, 6],
            small_own[:, 7],
        )

    return body


def solution(mesh):
    tokens = P(None, "fsdp", "seq", None)
    matrix, vector = P(None, AXES, None), P(None, AXES)
    in_specs = (tokens, P(None, "fsdp", None), tokens) + (matrix,) * 4 + (vector,) * 5
    in_specs += (matrix, vector, matrix, vector, vector, vector)
    out_specs = (tokens, tokens) + (matrix,) * 4 + (vector,) * 5
    out_specs += (matrix, vector, matrix, vector, vector, vector)
    sizes = (mesh.shape["fsdp"], mesh.shape["seq"])
    body = staged_body if sizes == (8, 4) else plain_body(*sizes)
    return jax.shard_map(body, mesh=mesh, in_specs=in_specs, out_specs=out_specs, check_vma=False)
```

```python
import collections
import math

import jax
import jax.numpy as jnp
from jax import lax
from jax.experimental import pallas as pl
from jax.experimental.pallas import tpu as pltpu
from jax.sharding import PartitionSpec as P

D = 1024
FF = 4096
HEAD_DIM = 64
HEADS = D // HEAD_DIM
SEQ_LEN = 1024
NDOC = 16
epsilon = 1e-05
AXES = ("fsdp", "seq")
f32 = jnp.float32
bf16 = jnp.bfloat16


def dot(left, right):
    return jnp.dot(left, right, preferred_element_type=f32)


def contract_rows(left, right):
    return lax.dot_general(left, right, (((0,), (0,)), ((), ())), preferred_element_type=f32)


def contract_cols(left, right):
    return lax.dot_general(left, right, (((1,), (1,)), ((), ())), preferred_element_type=f32)


SMALL_COST = pl.CostEstimate(flops=1024, bytes_accessed=1024, transcendentals=0)


def tie(value, *others):
    return lax.optimization_barrier((value, others))[0]


def pairs(move):
    out = []
    for i in range(32):
        z, y, x, c = i // 8, i // 4 % 2, i // 2 % 2, i % 2
        z, y, x, c = move(z, y, x, c)
        out.append((i, z * 8 + y * 4 + x * 2 + c))
    return out


TO_CORE = pairs(lambda z, y, x, c: (z, y, x, 1 - c))
TO_X = pairs(lambda z, y, x, c: (z, y, 1 - x, c))
TO_Y = pairs(lambda z, y, x, c: (z, 1 - y, x, c))
TO_FAR = pairs(lambda z, y, x, c: (z, y if c == 0 else 1 - y, 1 - x if c == 0 else x, c))
TO_NEAR = pairs(lambda z, y, x, c: (z, 1 - y if c == 0 else y, x if c == 0 else 1 - x, c))
TO_ODD = pairs(lambda z, y, x, c: (z ^ 1, y, x, c))
TO_PAIR = pairs(lambda z, y, x, c: (z ^ 2, y, x, c))
TO_BOTH = pairs(lambda z, y, x, c: (z ^ 3, y, x, c))
TO_Z = [pairs(lambda z, y, x, c, k=k: ((z + k) % 4, y, x, c)) for k in range(4)]


def send(value, to):
    return lax.ppermute(value, AXES, to)


def coordinates():
    fsdp, seq = lax.axis_index("fsdp"), lax.axis_index("seq")
    return jnp.stack([fsdp // 2, fsdp % 2, seq // 2, seq % 2]).astype(jnp.int32)


def place(coords, pieces, shapes, moves):
    count = len(moves(0, 0, 0, 0, None, None))

    total = len(pieces)

    def kernel(coords_ref, *refs):
        sources, targets = refs[:total], refs[total : total + len(shapes)]
        buffers, in_sems, out_sems = refs[total + len(shapes) : -2], refs[-2], refs[-1]
        loads = [
            pltpu.make_async_copy(source, buffer, in_sems.at[n])
            for n, (source, buffer) in enumerate(zip(sources, buffers))
        ]
        for load in loads:
            load.start()
        todo = moves(coords_ref[0], coords_ref[1], coords_ref[2], coords_ref[3], buffers, targets)
        stores = [
            (n, pltpu.make_async_copy(view, target, out_sems.at[k]))
            for k, (n, view, target) in enumerate(todo)
        ]
        for piece, load in enumerate(loads):
            load.wait()
            for n, store in stores:
                if n == piece:
                    store.start()
        for _, store in stores:
            store.wait()

    return pl.pallas_call(
        kernel,
        in_specs=[pl.BlockSpec(memory_space=pltpu.SMEM)]
        + [pl.BlockSpec(memory_space=pl.ANY)] * len(pieces),
        out_specs=[pl.BlockSpec(memory_space=pl.ANY)] * len(shapes),
        out_shape=[jax.ShapeDtypeStruct(shape, bf16) for shape in shapes],
        scratch_shapes=[pltpu.VMEM(p.shape, bf16) for p in pieces]
        + [pltpu.SemaphoreType.DMA((total,)), pltpu.SemaphoreType.DMA((count,))],
        compiler_params=pltpu.CompilerParams(vmem_limit_bytes=40 << 20),
        cost_estimate=SMALL_COST,
    )(coords, *pieces)


def pick(value, index, axis):
    return lax.dynamic_index_in_dim(value, index, axis, keepdims=False)


def by_place(own, other, at, axis):
    return jnp.where(at == 0, jnp.stack([own, other], axis), jnp.stack([other, own], axis))


def phase(values, *units, settle=()):
    values, flights, ended = lax.optimization_barrier(
        (values, [u.flight for u in units], [u.flight for u in settle])
    )
    for unit, flight in zip(settle, ended):
        unit.flight = flight
    nexts = [u.local(flight) for u, flight in zip(units, flights)]
    values, sends = lax.optimization_barrier((values, [[v for v, _ in n] for n in nexts]))
    for unit, arrays, targets in zip(units, sends, nexts):
        unit.flight = [send(array, to) for array, (_, to) in zip(arrays, targets)]
    return values


class GatherUnit:
    def __init__(self, coords, pack, shapes, parts):
        self.coords, self.pack, self.shapes, self.parts = coords, pack, shapes, parts
        self.flight, self.step = [pack], 0

    def local(self, got):
        self.step += 1
        if self.step == 1:
            self.kept = got[0][None]
            return [(self.kept, TO_PAIR)]
        if self.step < 5:
            self.kept = jnp.concatenate([got[0], self.kept])
            sends = [(self.kept, (TO_ODD, TO_NEAR, TO_FAR)[self.step - 2])]
            return sends + [(self.kept, TO_CORE)] * (self.step == 4)
        self.kept = [self.kept, *got]
        return [(got[0], TO_CORE)]

    def result(self):
        width = self.pack.shape[1]

        def by_block(z, y, x, c, src, dst):
            out = []
            for n in range(4):
                core, far = (c if n < 2 else 1 - c), n % 2
                for near in (1, 0):
                    y2 = y ^ jnp.where(core == 0, near, far)
                    x2 = x ^ jnp.where(core == 0, far, near)
                    for odd in (1, 0):
                        for pair in (1, 0):
                            block = 4 * (1 - near) + 2 * (1 - odd) + 1 - pair
                            for lo, hi, target, column in self.parts:
                                view = None
                                if dst:
                                    spans = (slice(0, hi - lo), slice(column * width, (column + 1) * width))
                                    view = dst[target].at[(z ^ odd ^ (2 * pair), y2, x2, core) + spans]
                                out.append((n, src and src[n].at[block, lo:hi], view))
            return out

        return place(
            self.coords, self.kept + self.flight, [(4, 2, 2, 2) + shape for shape in self.shapes], by_block
        )


FAR_FIRST = (TO_FAR, TO_NEAR, TO_ODD, TO_PAIR)
Z_FIRST = (TO_ODD, TO_PAIR, TO_FAR, TO_NEAR)


class SumUnit:
    def __init__(self, parts, route=FAR_FIRST):
        self.flight, self.step, self.route = list(parts), 0, route

    def local(self, got):
        self.step += 1
        if self.step == 1:
            leaving, self.kept = got
        elif self.step < 5:
            half = self.kept.shape[0] // 2
            add = lambda a, b: a.astype(f32) + b.astype(f32)
            leaving = add(self.kept[:half], got[0][:half]).astype(bf16)
            self.kept = add(self.kept[half:], got[0][half:])
            if self.step < 4:
                self.kept = self.kept.astype(bf16)
        else:
            self.kept = self.kept + got[0].astype(f32)
            return []
        return [(leaving, self.route[self.step - 1])]


Sums = collections.namedtuple("Sums", "o i a")


class SmallUnit(SumUnit):
    def local(self, got):
        if self.step < 2:
            return super().local(got)
        self.step += 1
        if self.step > 3:
            self.kept = self.kept + sum(value.astype(f32) for value in got)
            return []
        rows = self.kept.shape[0] // 4
        total = self.kept.astype(f32) + got[0].astype(f32)
        blocks = [total[n * rows : (n + 1) * rows] for n in range(4)]
        self.kept = blocks[3]
        return [(b.astype(bf16), to) for b, to in zip(blocks, (TO_BOTH, TO_ODD, TO_PAIR))]


def block_order(coords, z_first=False):
    z, y, x, c = coords[0], coords[1], coords[2], coords[3]
    order = []
    for core in (c, 1 - c):
        for first in range(4):
            for second in range(4):
                across, along = (second, first) if z_first else (first, second)
                far, near = 1 - across // 2, 1 - across % 2
                odd, pair = 1 - along // 2, 1 - along % 2
                y2 = y ^ jnp.where(core == 0, near, far)
                x2 = x ^ jnp.where(core == 0, far, near)
                order.append((z ^ odd ^ (2 * pair)) * 8 + y2 * 4 + x2 * 2 + core)
    return jnp.stack(order).astype(jnp.int32)


def order_matrices(order):
    block = D // 32
    wanted = (order[:, None] * block + lax.iota(jnp.int32, block)[None, :]).reshape(2, D // 2, 1)
    columns = lax.broadcasted_iota(jnp.int32, (2, D // 2, D), 2)
    chosen = (columns == wanted).astype(bf16)
    return chosen[0], chosen[1]


def selected(matrices, *arrays):
    count = len(arrays)

    def kernel(mine, theirs, *refs):
        for n in range(count):
            rows = refs[n][...]
            refs[count + 2 * n][...] = nt_dot(mine[...], rows).astype(bf16)
            refs[count + 2 * n + 1][...] = nt_dot(theirs[...], rows).astype(bf16)

    out = jax.ShapeDtypeStruct((D // 2, arrays[0].shape[0]), bf16)
    outs = pl.pallas_call(
        kernel,
        out_shape=[out] * (2 * count),
        compiler_params=pltpu.CompilerParams(vmem_limit_bytes=48 << 20),
        cost_estimate=SMALL_COST,
    )(*matrices, *arrays)
    return [tuple(outs[2 * n : 2 * n + 2]) for n in range(count)]


def weight_terms(*pairs_of, first=0, tile=1024):
    rows, tokens = pairs_of[0][0][0].shape
    counts = [pair[2] // tile for pair in pairs_of]
    starts = [sum(counts[:n]) for n in range(len(counts))]
    columns, half = sum(counts) * tile, rows // 2

    def kernel(*refs):
        leaving, kept = refs[-2:]
        j = pl.program_id(0)
        for n, (start, count) in enumerate(zip(starts, counts)):

            @pl.when((j >= start) & (j < start + count))
            def _(a1=refs[4 * n], a2=refs[4 * n + 1], b1=refs[4 * n + 2], b2=refs[4 * n + 3]):
                total = jnp.dot(a1[...], b1[...], preferred_element_type=f32)
                total = total + jnp.dot(a2[...], b2[...], preferred_element_type=f32)
                leaving[...] = total[:half].astype(bf16)
                kept[...] = total[half:].astype(bf16)

    in_specs, args = [], []
    for (left, right, _), start, count in zip(pairs_of, starts, counts):
        whole = pl.BlockSpec((rows, tokens), lambda j: (0, 0))
        cut = pl.BlockSpec((tokens, tile), lambda j, s=start, n=count: (0, jnp.clip(j - s, 0, n - 1) + first // tile))
        in_specs += [whole, whole, cut, cut]
        args += [*left, *right]
    out = jax.ShapeDtypeStruct((half, columns), bf16)
    return pl.pallas_call(
        kernel,
        grid=(columns // tile,),
        in_specs=in_specs,
        out_specs=[pl.BlockSpec((half, tile), lambda j: (0, j))] * 2,
        out_shape=[out, out],
        compiler_params=pltpu.CompilerParams(vmem_limit_bytes=48 << 20),
        cost_estimate=SMALL_COST,
    )(*args)


def wide_terms_of(order, left, right, part=0, parts=1):
    tokens, width = left[0].shape
    block = width // 32
    columns = right[0].shape[1] // parts

    def kernel(order_ref, *refs):
        a1, a2, (b1, b2, leaving, kept) = refs[:2], refs[2:4], refs[4:]
        one = (
            lax.broadcasted_iota(jnp.int32, (block, block), 0) == lax.broadcasted_iota(jnp.int32, (block, block), 1)
        ).astype(bf16)
        turned = lambda refs: jnp.concatenate([nt_dot(one, r[...]).astype(bf16) for r in refs], axis=0)
        total = jnp.dot(turned(a1), b1[...], preferred_element_type=f32)
        total = (total + jnp.dot(turned(a2), b2[...], preferred_element_type=f32)).astype(bf16)

        @pl.when(pl.program_id(0) < 4)
        def _():
            leaving[...] = total

        @pl.when(pl.program_id(0) >= 4)
        def _():
            kept[...] = total

    cut = lambda n: pl.BlockSpec((tokens, block), lambda j, order: (0, order[2 * j + n]))
    whole = pl.BlockSpec((tokens, columns), lambda j, order: (0, part))
    out = jax.ShapeDtypeStruct((width // 4, columns), bf16)
    return pl.pallas_call(
        kernel,
        grid_spec=pltpu.PrefetchScalarGridSpec(
            num_scalar_prefetch=1,
            grid=(8,),
            in_specs=[cut(0), cut(1), cut(0), cut(1), whole, whole],
            out_specs=[
                pl.BlockSpec((2 * block, columns), lambda j, order: (jnp.minimum(j, 3), 0)),
                pl.BlockSpec((2 * block, columns), lambda j, order: (jnp.maximum(j - 4, 0), 0)),
            ],
        ),
        out_shape=[out, out],
        compiler_params=pltpu.CompilerParams(vmem_limit_bytes=48 << 20),
        cost_estimate=SMALL_COST,
    )(order, left[0], left[0], left[1], left[1], *right)


BLOCK = 256
WINDOWS = (2 * BLOCK, 3 * BLOCK)
PAIR = 2 * HEAD_DIM


def query_starts(s):
    edge = (s // 2) ^ (s % 2)
    return edge * BLOCK, (1 - edge) * BLOCK


def window_starts(s):
    return (s % 2) * (2 * BLOCK), (1 - s % 2) * BLOCK


def nt_dot(left, right):
    return lax.dot_general(left, right, (((1,), (1,)), ((), ())), preferred_element_type=f32)


def only_head(value, head, axis):
    lane = lax.broadcasted_iota(jnp.int32, value.shape, axis)
    return jnp.where((lane < HEAD_DIM) if head == 0 else (lane >= HEAD_DIM), value, jnp.zeros_like(value))


def in_order(s, mine, other, scratch):
    for n, ref in ((0, mine), (1, other)):
        for slot in range(2):
            scratch[pl.ds((s ^ (n + 2 * slot)) * BLOCK, BLOCK), :] = ref[slot * BLOCK : (slot + 1) * BLOCK, :]


def attention_views(s):
    rows = [pl.ds(pl.multiple_of(start, BLOCK), BLOCK) for start in query_starts(s)]
    windows = [pl.ds(pl.multiple_of(start, BLOCK), width) for start, width in zip(window_starts(s), WINDOWS)]
    spans = [slice(h * HEAD_DIM, (h + 1) * HEAD_DIM) for h in range(2)]
    return rows, windows, spans, [slice(n * BLOCK, (n + 1) * BLOCK) for n in range(2)]


def attend_forward_kernel(
    s_ref, q_ref, km_ref, ko_ref, vm_ref, vo_ref, edge_ref, inner_ref, mixed_ref, total_ref, keys, values
):
    s = s_ref[0]
    in_order(s, km_ref, ko_ref, keys)
    in_order(s, vm_ref, vo_ref, values)
    rows, windows, spans, kinds = attention_views(s)
    biases = (edge_ref, inner_ref)
    scores = []
    for n in range(2):
        q = q_ref[rows[n], :] * jnp.asarray(HEAD_DIM**-0.5, bf16)
        k = keys[windows[n], :]
        scores += [nt_dot(k, only_head(q, head, 1)) for head in range(2)]
    raised, totals = [], []
    for m in range(4):
        n, head = divmod(m, 2)
        biased = scores[m] + biases[n][...]
        top = jnp.max(biased, axis=0, keepdims=True)
        up = jnp.exp(biased - top)
        totals.append(jnp.sum(up, axis=0, keepdims=True))
        total_ref[0, head : head + 1, kinds[n]] = top + jnp.log(totals[m])
        raised.append(up.astype(bf16))
    for n in range(2):
        v_t = values[windows[n], :].T
        halves = [
            jnp.dot(v_t[spans[h]], raised[2 * n + h], preferred_element_type=f32) / totals[2 * n + h]
            for h in range(2)
        ]
        mixed_ref[rows[n], :] = jnp.concatenate(halves, axis=0).T.astype(bf16)


def attend_backward_kernel(
    s_ref, q_ref, km_ref, ko_ref, vm_ref, vo_ref, edge_ref, inner_ref, mixed_ref, total_ref, grad_ref,
    dq_ref, mine_ref, sent_ref, keys, values, key_sum, value_sum,
):
    s = s_ref[0]
    in_order(s, km_ref, ko_ref, keys)
    in_order(s, vm_ref, vo_ref, values)
    key_sum[...] = jnp.zeros_like(key_sum)
    value_sum[...] = jnp.zeros_like(value_sum)
    rows, windows, spans, kinds = attention_views(s)
    biases = (edge_ref, inner_ref)
    scores, share_grads, queries, grads, inner = [], [], [], [], []
    for n in range(2):
        q = q_ref[rows[n], :] * jnp.asarray(HEAD_DIM**-0.5, bf16)
        g = grad_ref[rows[n], :]
        along = (g.astype(f32) * mixed_ref[rows[n], :].astype(f32)).T
        k, v = keys[windows[n], :], values[windows[n], :]
        for head in range(2):
            queries.append(only_head(q, head, 1))
            grads.append(only_head(g, head, 1))
            inner.append(jnp.sum(along[spans[head]], axis=0, keepdims=True))
            scores.append(nt_dot(k, queries[-1]))
            share_grads.append(nt_dot(v, grads[-1]))
    shares_low, grads_low = [], []
    for m in range(4):
        n, head = divmod(m, 2)
        shares = jnp.exp(scores[m] + biases[n][...] - total_ref[0, head : head + 1, kinds[n]])
        shares_low.append(shares.astype(bf16))
        grads_low.append((shares * (share_grads[m] - inner[m])).astype(bf16))
    both = lambda values, n, axis: jnp.concatenate(values[2 * n : 2 * n + 2], axis=axis)
    for n in range(2):
        k_t = keys[windows[n], :].T
        query_grads = [jnp.dot(k_t[spans[h]], grads_low[2 * n + h], preferred_element_type=f32) for h in range(2)]
        dq_ref[rows[n], :] = (jnp.concatenate(query_grads, axis=0).T * HEAD_DIM**-0.5).astype(bf16)
        key_sum[windows[n], :] += jnp.dot(both(grads_low, n, 1), both(queries, n, 0), preferred_element_type=f32)
        value_sum[windows[n], :] += jnp.dot(both(shares_low, n, 1), both(grads, n, 0), preferred_element_type=f32)
    for slot in range(2):
        here = slice(slot * BLOCK, (slot + 1) * BLOCK)
        mine, other = pl.ds((s ^ (2 * slot)) * BLOCK, BLOCK), pl.ds((s ^ (1 + 2 * slot)) * BLOCK, BLOCK)
        for n, sums in ((0, key_sum), (1, value_sum)):
            mine_ref[n, here, :] = sums[mine, :]
            sent_ref[n, here, :] = sums[other, :].astype(bf16)


def call_attention(kernel, s, own, other, bias, kept, outs, scratch):
    pairs_count = D // PAIR
    third = lambda n: pl.BlockSpec((2 * BLOCK, PAIR), lambda h: (0, h + n * pairs_count))
    cut = third(0)
    double = pl.BlockSpec((2, 2 * BLOCK, PAIR), lambda h: (0, 0, h))
    per_pair = pl.BlockSpec((1, 2, 2 * BLOCK), lambda h: (h, 0, 0))
    whole = [pl.BlockSpec(b.shape, lambda h: (0, 0)) for b in bias]
    in_specs = [pl.BlockSpec(memory_space=pltpu.SMEM), third(0), third(1), third(1), third(2), third(2), *whole]
    args = [s, own, own, other, own, other, *bias]
    if kept:
        in_specs += [cut, per_pair, cut]
        args += kept
    shapes, specs = [], []
    for kind, spec in outs:
        shapes.append(
            {
                0: jax.ShapeDtypeStruct((2 * BLOCK, D), kind),
                1: jax.ShapeDtypeStruct((pairs_count, 2, 2 * BLOCK), kind),
                2: jax.ShapeDtypeStruct((2, 2 * BLOCK, D), kind),
            }[spec]
        )
        specs.append((cut, per_pair, double)[spec])
    return pl.pallas_call(
        kernel,
        grid=(pairs_count,),
        in_specs=in_specs,
        out_specs=specs,
        out_shape=shapes,
        scratch_shapes=scratch,
        compiler_params=pltpu.CompilerParams(vmem_limit_bytes=48 << 20),
        cost_estimate=SMALL_COST,
    )(*args)


def attend_forward_blocks(s, own, other, bias):
    scratch = [pltpu.VMEM((SEQ_LEN, PAIR), bf16)] * 2
    return call_attention(attend_forward_kernel, s, own, other, bias, (), ((bf16, 0), (f32, 1)), scratch)


def attend_backward_blocks(s, own, other, bias, mixed, totals, grads):
    scratch = [pltpu.VMEM((SEQ_LEN, PAIR), bf16)] * 2 + [pltpu.VMEM((SEQ_LEN, PAIR), f32)] * 2
    outs = ((bf16, 0), (f32, 2), (bf16, 2))
    kept = (mixed, totals, grads)
    return call_attention(attend_backward_kernel, s, own, other, bias, kept, outs, scratch)


def window_bias(s, ids):
    out = []
    for start, width, first in zip(window_starts(s), WINDOWS, query_starts(s)):
        keys = lax.dynamic_slice_in_dim(ids, start, width)
        block = s ^ (2 * (first // BLOCK))
        queries = lax.dynamic_slice_in_dim(ids, block * BLOCK, BLOCK)
        out.append(jnp.where(keys[:, None] == queries[None, :], 0.0, -1e30).astype(f32))
    return tuple(out)


def norm_forward(total):
    center = jnp.mean(total, axis=-1, keepdims=True)
    centered = total - center
    spread = jnp.mean(centered * centered, axis=-1, keepdims=True)
    scale = lax.rsqrt(spread + epsilon)
    return centered * scale, scale


def norm_backward(total, gain, upstream):
    unit, scale = norm_forward(total)
    lifted = upstream * gain
    grad = scale * (
        lifted
        - jnp.mean(lifted, axis=-1, keepdims=True)
        - unit * jnp.mean(lifted * unit, axis=-1, keepdims=True)
    )
    return grad, jnp.sum(upstream * unit, axis=0), jnp.sum(upstream, axis=0)


def column_sum(values):
    return jnp.sum(values.astype(f32), axis=0)


def heads_of(rows):
    return rows.reshape(rows.shape[0], HEADS, HEAD_DIM)


def masked_scores(queries, keys, allowed):
    scores = jnp.einsum("qhd,khd->hqk", queries, keys, preferred_element_type=f32)
    return jnp.where(allowed[None], scores * HEAD_DIM ** (-0.5), -1e30)


def attend_forward(queries, keys, values, allowed):
    scores = masked_scores(heads_of(queries), heads_of(keys), allowed)
    top_score = jnp.max(scores, axis=2, keepdims=True)
    raised = jnp.exp(scores - top_score)
    totals = jnp.sum(raised, axis=2, keepdims=True)
    shares = (raised / totals).astype(bf16)
    mixed = jnp.einsum("hqk,khd->qhd", shares, heads_of(values), preferred_element_type=f32)
    return mixed.astype(bf16).reshape(queries.shape), top_score + jnp.log(totals)


def attend_backward(queries, keys, values, allowed, log_total, grads):
    queries, keys, values, grads = map(heads_of, (queries, keys, values, grads))
    scale = HEAD_DIM ** (-0.5)
    shares = jnp.exp(masked_scores(queries, keys, allowed) - log_total)
    share_grads = jnp.einsum("qhd,khd->hqk", grads, values, preferred_element_type=f32)
    inner_sums = jnp.sum(shares * share_grads, axis=2, keepdims=True)
    score_grads = (shares * (share_grads - inner_sums)).astype(bf16)
    query_grad = jnp.einsum("hqk,khd->qhd", score_grads, keys, preferred_element_type=f32) * scale
    key_grad = jnp.einsum("hqk,qhd->khd", score_grads, queries, preferred_element_type=f32) * scale
    value_grad = jnp.einsum(
        "hqk,qhd->khd", shares.astype(bf16), grads, preferred_element_type=f32
    )
    flat = lambda a: a.reshape(a.shape[0], D)
    return flat(query_grad).astype(bf16), flat(key_grad), flat(value_grad)


def product(rows, weight, tile, finish, outs, by_column=(), tiles=(), transposed=False, sums=0):
    tokens, depth = rows.shape
    width = weight.shape[0 if transposed else 1]

    def kernel(rows_ref, weight_ref, *refs):
        total = (nt_dot if transposed else lambda a, b: jnp.dot(a, b, preferred_element_type=f32))(
            rows_ref[...], weight_ref[...]
        )
        inputs = [r[...] for r in refs[: len(by_column) + len(tiles)]]
        for ref, value in zip(refs[len(inputs) :], finish(total, *inputs)):
            ref[...] = value.astype(ref.dtype)

    cut = pl.BlockSpec((tokens, tile), lambda j: (0, j))
    if transposed:
        weight_spec = pl.BlockSpec((tile, depth), lambda j: (j, 0))
    else:
        weight_spec = pl.BlockSpec((depth, tile), lambda j: (0, j))
    return pl.pallas_call(
        kernel,
        grid=(width // tile,),
        in_specs=[pl.BlockSpec((tokens, depth), lambda j: (0, 0)), weight_spec]
        + [pl.BlockSpec((1, tile), lambda j: (0, j))] * len(by_column)
        + [cut] * len(tiles),
        out_specs=[cut] * len(outs) + [pl.BlockSpec((1, tile), lambda j: (0, j))] * sums,
        out_shape=[jax.ShapeDtypeStruct((tokens, width), kind) for kind in outs]
        + [jax.ShapeDtypeStruct((1, width), f32)] * sums,
        compiler_params=pltpu.CompilerParams(vmem_limit_bytes=48 << 20),
        cost_estimate=SMALL_COST,
    )(rows, weight, *[v.reshape(1, width) for v in by_column], *tiles)


def gelu_parts(total, bias):
    inner = total + bias
    below = 0.5 * (1.0 + lax.erf(inner * (0.5**0.5)))
    slope = below + inner * jnp.exp(-0.5 * inner * inner) * (2 * math.pi) ** -0.5
    return inner * below, slope


def norm_backward_rows(total, gain, upstream):
    tokens, width = total.shape
    tile = 128

    def kernel(total_ref, gain_ref, up_ref, grad_ref, low_ref, sums_ref):
        unit, scale = norm_forward(total_ref[...])
        up = up_ref[...]
        lifted = up * gain_ref[...]
        grad = scale * (
            lifted
            - jnp.mean(lifted, axis=-1, keepdims=True)
            - unit * jnp.mean(lifted * unit, axis=-1, keepdims=True)
        )
        low = grad.astype(bf16)
        grad_ref[...] = grad
        low_ref[...] = low

        @pl.when(pl.program_id(0) == 0)
        def _():
            sums_ref[...] = jnp.zeros_like(sums_ref)

        for n, value in enumerate((up * unit, up, low.astype(f32))):
            sums_ref[n : n + 1, :] += jnp.sum(value, axis=0, keepdims=True)

    cut = pl.BlockSpec((tile, width), lambda j: (j, 0))
    out = jax.ShapeDtypeStruct((tokens, width), f32)
    return pl.pallas_call(
        kernel,
        grid=(tokens // tile,),
        in_specs=[cut, pl.BlockSpec((1, width), lambda j: (0, 0)), cut],
        out_specs=[cut, cut, pl.BlockSpec((8, width), lambda j: (0, 0))],
        out_shape=[out, jax.ShapeDtypeStruct((tokens, width), bf16), jax.ShapeDtypeStruct((8, width), f32)],
        compiler_params=pltpu.CompilerParams(vmem_limit_bytes=32 << 20),
        cost_estimate=SMALL_COST,
    )(total, gain.reshape(1, width), upstream)


def merged(query_low, own, back):
    tokens = query_low.shape[0]
    tile = D // 2

    def kernel(query_ref, own_ref, back_ref, low_ref, sum_ref):
        def put(low):
            low_ref[...] = low
            sum_ref[...] = jnp.sum(low.astype(f32), axis=0, keepdims=True)

        @pl.when(pl.program_id(0) < 2)
        def _():
            put(query_ref[...])

        @pl.when(pl.program_id(0) >= 2)
        def _():
            put((own_ref[0] + back_ref[0].astype(f32)).astype(bf16))

    part = pl.BlockSpec((1, tokens, tile), lambda j: (jnp.maximum(j - 2, 0) // 2, 0, jnp.maximum(j - 2, 0) % 2))
    return pl.pallas_call(
        kernel,
        grid=(6,),
        in_specs=[pl.BlockSpec((tokens, tile), lambda j: (0, jnp.minimum(j, 1))), part, part],
        out_specs=[pl.BlockSpec((tokens, tile), lambda j: (0, j)), pl.BlockSpec((1, tile), lambda j: (0, j))],
        out_shape=[jax.ShapeDtypeStruct((tokens, 3 * D), bf16), jax.ShapeDtypeStruct((1, 3 * D), f32)],
        compiler_params=pltpu.CompilerParams(vmem_limit_bytes=32 << 20),
        cost_estimate=SMALL_COST,
    )(query_low, own, back)


SMALL = 8


def staged_body(tokens, doc_lengths, cotangent, *shards):
    (
        query_weight,
        key_weight,
        value_weight,
        mix_weight,
        query_bias,
        value_bias,
        mix_bias,
        first_gain,
        first_shift,
        inner_weight,
        inner_bias,
        outer_weight,
        outer_bias,
        second_gain,
        second_shift,
    ) = shards
    layer_count = query_weight.shape[0]
    devices = 32
    length = SEQ_LEN // 4
    rows_held, inner_held = D // devices, FF // devices
    seq = lax.axis_index("seq")
    row = seq // 2
    coords = coordinates()
    z, y, x, c = coords[0], coords[1], coords[2], coords[3]
    place_of = seq.reshape(1).astype(jnp.int32)

    def split_rows(both):
        both = both.reshape(2, length, D)
        return pick(both, row, 0), pick(both, 1 - row, 0)

    token_kept, token_left = split_rows(tokens)
    upstream_kept, upstream_left = split_rows(cotangent)

    def unit_a(layer):
        r = rows_held
        parts = [w[layer] for w in (query_weight, key_weight, value_weight)]
        rows, outs = [(r * n, r * (n + 1), 0, n) for n in range(3)], [(r, 3 * D)]
        if layer:
            parts, rows, outs = parts + [mix_weight[layer]], rows + [(3 * r, 4 * r, 1, 0)], outs + [(r, D)]
        return GatherUnit(coords, jnp.concatenate(parts), outs, rows)

    def unit_i(layer):
        r, inner = rows_held, inner_weight[layer]
        parts = [inner[:, D * n : D * (n + 1)] for n in range(4)]
        rows, outs = [(r * n, r * (n + 1), 0, n) for n in range(4)], [(r, FF)]
        if not layer:
            parts, rows, outs = parts + [mix_weight[layer]], rows + [(4 * r, 5 * r, 1, 0)], outs + [(r, D)]
        return GatherUnit(coords, jnp.concatenate(parts), outs, rows)

    def unit_o(layer):
        return GatherUnit(coords, outer_weight[layer], [(inner_held, D)], [(0, inner_held, 0, 0)])

    units = [[make(layer) for make in (unit_a, unit_i, unit_o)] for layer in range(layer_count)]

    small_vectors = (
        query_bias,
        value_bias,
        mix_bias,
        first_gain,
        first_shift,
        outer_bias,
        second_gain,
        second_shift,
    )
    vector_count = SMALL * layer_count
    small_held = vector_count * rows_held
    mine = jnp.concatenate(
        [jnp.concatenate([v[layer] for v in small_vectors]) for layer in range(layer_count)]
        + [inner_bias.reshape(-1)]
    )
    held = mine.shape[0]
    padded = jnp.pad(mine, (0, 1024 - held)).reshape(8, 128)

    u = [unit for layer_units in units for unit in layer_units]
    padded = phase(padded, u[0])
    token_got = send(token_left, TO_X)
    every = jnp.roll(jnp.stack([padded] + [send(padded, TO_Z[4 - k]) for k in (1, 2, 3)]), z, axis=0)

    lengths = pick(doc_lengths.reshape(2, NDOC), row, 0)
    places = lax.iota(jnp.int32, SEQ_LEN)
    segment = jnp.sum((places[:, None] >= jnp.cumsum(lengths)[None, :]).astype(jnp.int32), axis=1)
    bias = window_bias(seq, jnp.where(segment == NDOC - 1, NDOC + places, segment))
    order, order_z = block_order(coords), block_order(coords, True)
    matrices = order_matrices(order)

    token_got, every = phase((token_got, every), u[0])
    every = by_place(every, send(every, TO_Y), y, 1)
    every, bias = phase((every, bias), u[0], u[1])
    every = by_place(every, send(every, TO_X), x, 2)
    every, matrices = phase((every, matrices), u[0], u[1], u[2])
    every = by_place(every, send(every, TO_CORE), c, 3)
    every = every.reshape(devices, 1024)[:, :held].astype(f32)
    small_all = (
        every[:, :small_held]
        .reshape(devices, vector_count, rows_held)
        .transpose(1, 0, 2)
        .reshape(layer_count, SMALL, D)
    )
    wide_all = (
        every[:, small_held:]
        .reshape(devices, layer_count, inner_held)
        .transpose(1, 0, 2)
        .reshape(layer_count, FF)
    )
    stream = jnp.concatenate([token_kept, token_got]).astype(f32)
    stream, small_all, wide_all = phase((stream, small_all, wide_all), u[0], u[1], u[2], u[3])
    saved = []
    for layer in range(layer_count):
        a_unit, i_unit, o_unit = units[layer]
        next_a, next_i, next_o = units[layer + 1] if layer + 1 < layer_count else (None,) * 3
        q_bias, v_bias, m_bias, gain1, shift1, o_bias, gain2, shift2 = [small_all[layer, n] for n in range(SMALL)]
        w_three, *w_rest = a_unit.result()
        w_three = w_three.reshape(D, 3 * D)
        stream_low = stream.astype(bf16)
        three_bias = jnp.concatenate([q_bias, jnp.zeros_like(q_bias), v_bias])
        (three,) = product(stream_low, w_three, 1024, lambda total, b: (total + b,), (bf16,), (three_bias,))
        if next_a:
            three = phase(three, i_unit, next_a, next_i, settle=[o_unit])
        else:
            three = phase(three, i_unit)
        three_got = send(three, TO_CORE)
        (left_stream,) = selected(matrices, tie(stream_low, three))
        three, left_stream = lax.optimization_barrier((three, left_stream))
        left_stream = (left_stream[0], send(left_stream[1], TO_CORE))
        mixed, totals = attend_forward_blocks(place_of, three, three_got, bias)
        if next_a:
            mixed, totals, left_stream = phase(
                (mixed, totals, left_stream), i_unit, o_unit, next_a, next_i, next_o
            )
        else:
            mixed, totals, left_stream = phase((mixed, totals, left_stream), i_unit, o_unit)
        w_inner, *w_more = i_unit.result()
        (w_mix,) = w_rest + w_more
        w_inner, w_mix = w_inner.reshape(D, FF), w_mix.reshape(D, D)
        first_sum = stream + (dot(mixed, w_mix) + m_bias)
        first = norm_forward(first_sum)[0] * gain1 + shift1
        first_low = first.astype(bf16)
        if next_a:
            first_low = phase(first_low, o_unit, next_o, settle=[next_a, next_i])
        else:
            first_low = phase(first_low, o_unit)
        left_mix, left_first = selected(matrices, mixed, first_low)
        first_low, left_mix, left_first = lax.optimization_barrier((first_low, left_mix, left_first))
        left_mix, left_first = [(m, send(t, TO_CORE)) for m, t in (left_mix, left_first)]
        active, slope = product(first_low, w_inner, 1024, gelu_parts, (bf16, bf16), (wide_all[layer],))
        if next_a:
            active, slope, left_mix, left_first = phase(
                (active, slope, left_mix, left_first), o_unit, next_a, settle=[next_o]
            )
        else:
            active, slope, left_mix, left_first = phase((active, slope, left_mix, left_first), o_unit)
        if not next_a:
            upstream_left, active = lax.optimization_barrier((upstream_left, active))
            upstream_got = send(upstream_left, TO_X)
        (w_outer,) = o_unit.result()
        active_got = send(tie(active, w_outer), TO_CORE)
        w_outer = w_outer.reshape(FF, D)
        (second_sum,) = product(
            active, w_outer, 256, lambda total, b, f: (f + (total + b),), (f32,), (o_bias,), (first,)
        )
        if next_a:
            second_sum, active_got = lax.optimization_barrier((second_sum, active_got))
        else:
            second_sum, active_got, upstream_got = lax.optimization_barrier((second_sum, active_got, upstream_got))
        left_active = (active, active_got)
        stream = norm_forward(second_sum)[0] * gain2 + shift2
        if next_a:
            stream = phase(stream, next_a, next_i)
        saved.append(
            (
                (w_three, w_mix, w_inner, w_outer, gain1, gain2),
                (three, three_got, totals, mixed),
                (first_sum, slope, second_sum),
                (left_stream, left_mix, left_first, left_active),
            )
        )

    def both_rows(kept, got):
        got = got.astype(f32)
        return jnp.where(row == 0, jnp.stack([kept, got]), jnp.stack([got, kept])).reshape(tokens.shape)

    output = stream
    output_got = send(output[length:].astype(bf16), TO_X)

    upstream = jnp.concatenate([upstream_kept, upstream_got]).astype(f32)
    small_grads, wide_grads = [None] * layer_count, [None] * layer_count
    sums = [None] * layer_count
    before = None
    for layer in reversed(range(layer_count)):
        weights, kept, rest, lefts = saved[layer]
        w_three, w_mix, w_inner, w_outer, gain1, gain2 = weights
        three, three_got, totals, mixed = kept
        first_sum, slope, second_sum = rest
        left_stream, left_mix, left_first, left_active = lefts

        def with_sum(total, slopes):
            low = (total * slopes).astype(bf16)
            return low, jnp.sum(low.astype(f32), axis=0, keepdims=True)

        second_grad, second_low, second_sums = norm_backward_rows(second_sum, gain2, upstream)
        second_got = send(second_low, TO_CORE)
        inner_low, inner_sum = product(
            second_low, w_outer, 1024, with_sum, (bf16,), (), (slope,), transposed=True, sums=1
        )
        if before:
            inner_low, second_got = phase((inner_low, second_got), before.o[0], before.i, before.a)
        else:
            inner_low, second_got, output_got = lax.optimization_barrier((inner_low, second_got, output_got))
        inner_got = send(inner_low, TO_CORE)
        second_pair = (second_low, second_got)
        if before:
            o_sums = (
                SumUnit(wide_terms_of(order_z, left_active, second_pair, 0, 2), Z_FIRST),
                SumUnit(wide_terms_of(order, left_active, second_pair, 1, 2)),
            )
            second_grad, inner_low = phase(
                (second_grad, inner_low), *o_sums, before.a, before.i, settle=before.o
            )
        else:
            o_sums = (SumUnit(wide_terms_of(order, left_active, second_pair)),)
            second_grad, inner_low = phase((second_grad, inner_low), *o_sums)
        (first_grad,) = product(
            inner_low, w_inner, 256, lambda total, g: (g + total,), (f32,), (), (second_grad,), transposed=True
        )
        first_sum_grad, branch_low, first_sums = norm_backward_rows(first_sum, gain1, first_grad)
        branch_got = send(branch_low, TO_CORE)
        (mixed_grad,) = product(branch_low, w_mix, 512, lambda total: (total,), (bf16,), transposed=True)
        mixed_grad, inner_got, branch_got = lax.optimization_barrier((mixed_grad, inner_got, branch_got))
        i_sum = SumUnit(
            weight_terms((left_first, (inner_low, inner_got), FF), (left_mix, (branch_low, branch_got), D))
        )
        if before:
            mixed_grad = phase(mixed_grad, i_sum, *o_sums, before.a, settle=[before.i])
        else:
            mixed_grad = phase(mixed_grad, i_sum, settle=o_sums)
        query_low, own_grads, sent_grads = attend_backward_blocks(
            place_of, three, three_got, bias, mixed, totals, mixed_grad
        )
        grads_back = send(sent_grads, TO_CORE)
        if before:
            query_low, own_grads = phase((query_low, own_grads), i_sum, *o_sums, before.a)
        else:
            query_low, own_grads = phase((query_low, own_grads), *o_sums, settle=[i_sum])
        low, low_sums = merged(query_low, own_grads, grads_back)
        low_got = send(low, TO_CORE)
        if layer:
            (upstream,) = product(
                low, w_three, 256, lambda total, g: (g + total,), (f32,), (), (first_sum_grad,), transposed=True
            )
            a_sum = SumUnit(weight_terms((left_stream, tie((low, low_got), upstream), 3 * D)))
        else:
            a_sum = SumUnit(weight_terms((left_stream, (low, low_got), 3 * D)))
            low, low_sums = phase((low, low_sums), a_sum, settle=[before.a] if before else [])
            (upstream,) = product(
                low, w_three, 256, lambda total, g: (g + total,), (f32,), (), (first_sum_grad,), transposed=True
            )
        small_grads[layer] = jnp.stack(
            [
                low_sums[0, :D],
                low_sums[0, 2 * D :],
                first_sums[2],
                first_sums[0],
                first_sums[1],
                second_sums[2],
                second_sums[0],
                second_sums[1],
            ]
        )
        wide_grads[layer] = inner_sum[0]
        if layer:
            upstream, small_grads[layer] = phase((upstream, small_grads[layer]), *o_sums, i_sum, settle=[a_sum])
        sums[layer] = before = Sums(o_sums, i_sum, a_sum)

    small_terms = (
        jnp.stack(small_grads)
        .reshape(vector_count, devices, rows_held)
        .transpose(1, 0, 2)
        .reshape(devices, small_held)
    )
    wide_terms = (
        jnp.stack(wide_grads)
        .reshape(layer_count, devices, inner_held)
        .transpose(1, 0, 2)
        .reshape(devices, layer_count * inner_held)
    )
    terms = jnp.pad(jnp.concatenate([small_terms, wide_terms], axis=1), ((0, 0), (0, 1024 - held)))
    chosen = (order[:, None] == lax.iota(jnp.int32, devices)[None, :]).astype(f32)
    terms = jnp.dot(chosen, terms, precision=lax.Precision.HIGHEST).reshape(2, 128, 128)
    terms = (terms[0] + send(terms[1].astype(bf16), TO_CORE).astype(f32)).astype(bf16)
    small_sum = SmallUnit((terms[:64], terms[64:]))

    last = sums[0]
    done = [unit for layer in range(1, layer_count) for unit in (*sums[layer].o, sums[layer].i, sums[layer].a)]
    upstream, output_got = phase((upstream, output_got), last.a, last.i, *last.o, small_sum, *done)
    token_left = upstream[length:].astype(bf16)
    upstream, token_left = phase((upstream, token_left), last.a, last.i, *last.o, small_sum)
    token_back = send(token_left, TO_X)
    upstream, token_back = phase((upstream, token_back), last.a, last.i, small_sum)
    phase((), last.a, small_sum)
    own_terms = small_sum.kept.reshape(-1)[:held]
    small_own = own_terms[:small_held].reshape(layer_count, SMALL, rows_held)
    wide_own = own_terms[small_held:].reshape(layer_count, inner_held)
    for layer in range(layer_count):
        for unit in (*sums[layer].o, sums[layer].i, sums[layer].a):
            while unit.step < 5:
                phase((), unit)
    o_all = jnp.stack([jnp.concatenate([unit.kept for unit in group.o], axis=1) for group in sums])
    i_all, a_all = [jnp.stack([group[n].kept for group in sums]) for n in (1, 2)]
    return (
        both_rows(output[:length], output_got),
        both_rows(upstream[:length], token_back),
        a_all[:, :, :D],
        a_all[:, :, D : 2 * D],
        a_all[:, :, 2 * D : 3 * D],
        i_all[:, :, FF:],
        small_own[:, 0],
        small_own[:, 1],
        small_own[:, 2],
        small_own[:, 3],
        small_own[:, 4],
        i_all[:, :, :FF],
        wide_own,
        o_all,
        small_own[:, 5],
        small_own[:, 6],
        small_own[:, 7],
    )


def plain_body(fsdp_size, seq_size):
    half = seq_size // 2
    device_count = fsdp_size * seq_size
    across = [(i, (i + half) % seq_size) for i in range(seq_size)]
    groups = [[m * half + j for j in range(half)] for m in range(2)]
    length = SEQ_LEN // seq_size

    def gather_siblings(rows):
        return lax.all_gather(rows, "seq", axis_index_groups=groups)

    def scatter_siblings(own_order):
        return lax.psum_scatter(own_order, "seq", axis_index_groups=groups)

    def body(tokens, doc_lengths, cotangent, *shards):
        (
            query_weight,
            key_weight,
            value_weight,
            mix_weight,
            query_bias,
            value_bias,
            mix_bias,
            first_gain,
            first_shift,
            inner_weight,
            inner_bias,
            outer_weight,
            outer_bias,
            second_gain,
            second_shift,
        ) = shards
        layer_count = query_weight.shape[0]
        seq = lax.axis_index("seq")
        row = seq // half
        rows_held = D // device_count
        inner_held = FF // device_count

        def vector_rows(small, wide):
            return jnp.concatenate(
                [jnp.concatenate([v[layer] for v in small]) for layer in range(layer_count)]
                + [wide.reshape(-1)]
            )

        small_vectors = (
            query_bias,
            value_bias,
            mix_bias,
            first_gain,
            first_shift,
            outer_bias,
            second_gain,
            second_shift,
        )
        vector_count = len(small_vectors) * layer_count
        mine = vector_rows(small_vectors, inner_bias)
        held = mine.shape[0]
        every = lax.all_gather(mine, AXES)
        every = every.astype(f32)
        small_held = vector_count * rows_held
        small_all = (
            every[:, :small_held]
            .reshape(device_count, vector_count, rows_held)
            .transpose(1, 0, 2)
            .reshape(layer_count, len(small_vectors), D)
        )
        wide_all = (
            every[:, small_held:]
            .reshape(device_count, layer_count, inner_held)
            .transpose(1, 0, 2)
            .reshape(layer_count, FF)
        )

        def whole_weights(layer):
            weights = (query_weight, key_weight, value_weight, mix_weight, inner_weight, outer_weight)
            return [lax.all_gather(w[layer], AXES, axis=0, tiled=True) for w in weights]

        def own_row(both_rows):
            kept = pick(both_rows, row, 0)
            return jnp.concatenate(
                [kept, lax.ppermute(pick(both_rows, 1 - row, 0), "seq", across)]
            )

        def both_rows(values):
            kept = values[:length]
            other = lax.ppermute(values[length:].astype(bf16), "seq", across).astype(f32)
            return jnp.where(row == 0, jnp.stack([kept, other]), jnp.stack([other, kept]))

        stream_start = own_row(tokens.reshape(2, length, D))
        upstream_start = own_row(cotangent.reshape(2, length, D))

        lengths = pick(doc_lengths.reshape(2, NDOC), row, 0)
        bounds = jnp.cumsum(lengths)
        within = lax.iota(jnp.int32, length)

        def positions(s):
            return jnp.concatenate([s * length + within, (s + half) % seq_size * length + within])

        def segments(places):
            return jnp.sum((places[:, None] >= bounds[None, :]).astype(jnp.int32), axis=1)

        query_places = positions(seq)
        key_places = jnp.concatenate([positions(row * half + j) for j in range(half)])
        query_segment, key_segment = segments(query_places), segments(key_places)
        allowed = (
            (query_segment[:, None] == key_segment[None, :]) & (key_segment[None, :] != NDOC - 1)
        ) | (query_places[:, None] == key_places[None, :])

        stream = stream_start.astype(f32)
        saved = []
        for layer in range(layer_count):
            q_bias, v_bias, m_bias, gain1, shift1, o_bias, gain2, shift2 = [
                small_all[layer, n] for n in range(len(small_vectors))
            ]
            w_query, w_key, w_value, w_mix, w_inner, w_outer = whole_weights(layer)
            stream_low = stream.astype(bf16)
            queries = (dot(stream_low, w_query) + q_bias).astype(bf16)
            key_rows = dot(stream_low, w_key).astype(bf16)
            values = (dot(stream_low, w_value) + v_bias).astype(bf16)
            all_keys = gather_siblings(key_rows).reshape(SEQ_LEN, D)
            all_values = gather_siblings(values).reshape(SEQ_LEN, D)
            mixed, log_total = attend_forward(queries, all_keys, all_values, allowed)
            first_sum = stream + (dot(mixed, w_mix) + m_bias)
            first = norm_forward(first_sum)[0] * gain1 + shift1
            first_low = first.astype(bf16)
            inner = dot(first_low, w_inner) + wide_all[layer]
            below = 0.5 * (1.0 + lax.erf(inner * (0.5**0.5)))
            active = (inner * below).astype(bf16)
            slope = (below + inner * jnp.exp(-0.5 * inner * inner) * (2 * math.pi) ** -0.5).astype(
                bf16
            )
            second_sum = first + (dot(active, w_outer) + o_bias)
            stream = norm_forward(second_sum)[0] * gain2 + shift2
            saved.append(
                (
                    (w_query, w_key, w_value, w_mix, w_inner, w_outer, gain1, gain2),
                    (stream_low, queries, all_keys, all_values, log_total, mixed),
                    (first_sum, first_low, slope, active, second_sum),
                )
            )
        activations = both_rows(stream)

        upstream = upstream_start.astype(f32)
        small_grads = [None] * layer_count
        wide_grads = [None] * layer_count
        results = [None] * layer_count

        def reduced(grads):
            return [lax.psum_scatter(g, AXES, scatter_dimension=0, tiled=True) for g in grads]

        for layer in reversed(range(layer_count)):
            (w_query, w_key, w_value, w_mix, w_inner, w_outer, gain1, gain2), kept, rest = saved[layer]
            stream_low, queries, all_keys, all_values, log_total, mixed = kept
            first_sum, first_low, slope, active, second_sum = rest
            second_grad, gain2_grad, shift2_grad = norm_backward(second_sum, gain2, upstream)
            second_low = second_grad.astype(bf16)
            (outer_grad,) = reduced([contract_rows(active, second_low)])
            inner_low = (contract_cols(second_low, w_outer) * slope).astype(bf16)
            (inner_grad,) = reduced([contract_rows(first_low, inner_low)])
            first_grad = second_grad + contract_cols(inner_low, w_inner)
            first_sum_grad, gain1_grad, shift1_grad = norm_backward(first_sum, gain1, first_grad)
            branch_low = first_sum_grad.astype(bf16)
            mix_terms = contract_rows(mixed, branch_low)
            mixed_grad = contract_cols(branch_low, w_mix).astype(bf16)
            query_low, key_terms, value_terms = attend_backward(
                queries, all_keys, all_values, allowed, log_total, mixed_grad
            )
            n = 2 * length
            key_low = scatter_siblings(key_terms.reshape(half, n, D)).astype(bf16)
            value_low = scatter_siblings(value_terms.reshape(half, n, D)).astype(bf16)
            value_grad, mix_grad = reduced([contract_rows(stream_low, value_low), mix_terms])
            query_grad, key_grad = reduced(
                [contract_rows(stream_low, query_low), contract_rows(stream_low, key_low)]
            )
            upstream = (
                first_sum_grad
                + contract_cols(query_low, w_query)
                + contract_cols(key_low, w_key)
                + contract_cols(value_low, w_value)
            )
            small_grads[layer] = jnp.stack(
                [
                    column_sum(query_low),
                    column_sum(value_low),
                    column_sum(branch_low),
                    gain1_grad,
                    shift1_grad,
                    column_sum(second_low),
                    gain2_grad,
                    shift2_grad,
                ]
            )
            wide_grads[layer] = column_sum(inner_low)
            results[layer] = (query_grad, key_grad, value_grad, mix_grad, inner_grad, outer_grad)
        token_grad = both_rows(upstream)

        small_terms = (
            jnp.stack(small_grads)
            .reshape(vector_count, device_count, rows_held)
            .transpose(1, 0, 2)
            .reshape(device_count, small_held)
        )
        wide_terms = (
            jnp.stack(wide_grads)
            .reshape(layer_count, device_count, inner_held)
            .transpose(1, 0, 2)
            .reshape(device_count, layer_count * inner_held)
        )
        terms = jnp.concatenate([small_terms, wide_terms], axis=1)
        own_terms = lax.psum_scatter(terms, AXES, scatter_dimension=0, tiled=False)
        small_own = own_terms[:small_held].reshape(layer_count, len(small_vectors), rows_held)
        wide_own = own_terms[small_held:].reshape(layer_count, inner_held)
        query_g, key_g, value_g, mix_g, inner_g, outer_g = [
            jnp.stack([results[layer][n] for layer in range(layer_count)]) for n in range(6)
        ]
        return (
            activations.reshape(tokens.shape),
            token_grad.reshape(tokens.shape),
            query_g,
            key_g,
            value_g,
            mix_g,
            small_own[:, 0],
            small_own[:, 1],
            small_own[:, 2],
            small_own[:, 3],
            small_own[:, 4],
            inner_g,
            wide_own,
            outer_g,
            small_own[:, 5],
            small_own[:, 6],
            small_own[:, 7],
        )

    return body


def solution(mesh):
    tokens = P(None, "fsdp", "seq", None)
    matrix, vector = P(None, AXES, None), P(None, AXES)
    in_specs = (tokens, P(None, "fsdp", None), tokens) + (matrix,) * 4 + (vector,) * 5
    in_specs += (matrix, vector, matrix, vector, vector, vector)
    out_specs = (tokens, tokens) + (matrix,) * 4 + (vector,) * 5
    out_specs += (matrix, vector, matrix, vector, vector, vector)
    sizes = (mesh.shape["fsdp"], mesh.shape["seq"])
    body = staged_body if sizes == (8, 4) else plain_body(*sizes)
    return jax.shard_map(body, mesh=mesh, in_specs=in_specs, out_specs=out_specs, check_vma=False)
```

```python
import collections
import math

import jax
import jax.numpy as jnp
from jax import lax
from jax.experimental import pallas as pl
from jax.experimental.pallas import tpu as pltpu
from jax.sharding import PartitionSpec as P

D = 1024
FF = 4096
HEAD_DIM = 64
HEADS = D // HEAD_DIM
SEQ_LEN = 1024
NDOC = 16
epsilon = 1e-05
AXES = ("fsdp", "seq")
f32 = jnp.float32
bf16 = jnp.bfloat16


def dot(left, right):
    return jnp.dot(left, right, preferred_element_type=f32)


def contract_rows(left, right):
    return lax.dot_general(left, right, (((0,), (0,)), ((), ())), preferred_element_type=f32)


def contract_cols(left, right):
    return lax.dot_general(left, right, (((1,), (1,)), ((), ())), preferred_element_type=f32)


SMALL_COST = pl.CostEstimate(flops=1024, bytes_accessed=1024, transcendentals=0)


def tie(value, *others):
    return lax.optimization_barrier((value, others))[0]


def pairs(move):
    out = []
    for i in range(32):
        z, y, x, c = i // 8, i // 4 % 2, i // 2 % 2, i % 2
        z, y, x, c = move(z, y, x, c)
        out.append((i, z * 8 + y * 4 + x * 2 + c))
    return out


TO_CORE = pairs(lambda z, y, x, c: (z, y, x, 1 - c))
TO_X = pairs(lambda z, y, x, c: (z, y, 1 - x, c))
TO_Y = pairs(lambda z, y, x, c: (z, 1 - y, x, c))
TO_FAR = pairs(lambda z, y, x, c: (z, y if c == 0 else 1 - y, 1 - x if c == 0 else x, c))
TO_NEAR = pairs(lambda z, y, x, c: (z, 1 - y if c == 0 else y, x if c == 0 else 1 - x, c))
TO_ODD = pairs(lambda z, y, x, c: (z ^ 1, y, x, c))
TO_PAIR = pairs(lambda z, y, x, c: (z ^ 2, y, x, c))
TO_Z = [pairs(lambda z, y, x, c, k=k: ((z + k) % 4, y, x, c)) for k in range(4)]


def send(value, to):
    return lax.ppermute(value, AXES, to)


def coordinates():
    fsdp, seq = lax.axis_index("fsdp"), lax.axis_index("seq")
    return jnp.stack([fsdp // 2, fsdp % 2, seq // 2, seq % 2]).astype(jnp.int32)


def place(coords, pieces, shapes, moves):
    count = len(moves(0, 0, 0, 0, None, None))

    total = len(pieces)

    def kernel(coords_ref, *refs):
        sources, targets = refs[:total], refs[total : total + len(shapes)]
        buffers, in_sems, out_sems = refs[total + len(shapes) : -2], refs[-2], refs[-1]
        loads = [
            pltpu.make_async_copy(source, buffer, in_sems.at[n])
            for n, (source, buffer) in enumerate(zip(sources, buffers))
        ]
        for load in loads:
            load.start()
        todo = moves(coords_ref[0], coords_ref[1], coords_ref[2], coords_ref[3], buffers, targets)
        stores = [
            (n, pltpu.make_async_copy(view, target, out_sems.at[k]))
            for k, (n, view, target) in enumerate(todo)
        ]
        for piece, load in enumerate(loads):
            load.wait()
            for n, store in stores:
                if n == piece:
                    store.start()
        for _, store in stores:
            store.wait()

    return pl.pallas_call(
        kernel,
        in_specs=[pl.BlockSpec(memory_space=pltpu.SMEM)]
        + [pl.BlockSpec(memory_space=pl.ANY)] * len(pieces),
        out_specs=[pl.BlockSpec(memory_space=pltpu.HBM)] * len(shapes),
        out_shape=[jax.ShapeDtypeStruct(shape, bf16) for shape in shapes],
        scratch_shapes=[pltpu.VMEM(p.shape, bf16) for p in pieces]
        + [pltpu.SemaphoreType.DMA((total,)), pltpu.SemaphoreType.DMA((count,))],
        compiler_params=pltpu.CompilerParams(vmem_limit_bytes=40 << 20),
        cost_estimate=SMALL_COST,
    )(coords, *pieces)


def in_hbm(value):
    return pltpu.with_memory_space_constraint(value, pltpu.HBM)


def pick(value, index, axis):
    return lax.dynamic_index_in_dim(value, index, axis, keepdims=False)


def by_place(own, other, at, axis):
    return jnp.where(at == 0, jnp.stack([own, other], axis), jnp.stack([other, own], axis))


def phase(values, *units, settle=()):
    values, flights, ended = lax.optimization_barrier(
        (values, [u.flight for u in units], [u.flight for u in settle])
    )
    for unit, flight in zip(settle, ended):
        unit.flight = flight
    nexts = [u.local(flight) for u, flight in zip(units, flights)]
    values, sends = lax.optimization_barrier((values, [[v for v, _ in n] for n in nexts]))
    for unit, arrays, targets in zip(units, sends, nexts):
        unit.flight = [send(array, to) for array, (_, to) in zip(arrays, targets)]
    return values


class GatherUnit:
    def __init__(self, coords, pack, shapes, parts):
        self.coords, self.pack, self.shapes, self.parts = coords, pack, shapes, parts
        self.flight, self.step = [pack], 0

    def local(self, got):
        self.step += 1
        if self.step == 1:
            self.kept = got[0][None]
            return [(self.kept, TO_PAIR)]
        if self.step < 5:
            self.kept = jnp.concatenate([got[0], self.kept])
            sends = [(self.kept, (TO_ODD, TO_NEAR, TO_FAR)[self.step - 2])]
            return sends + [(self.kept, TO_CORE)] * (self.step == 4)
        self.kept = [self.kept, *got]
        return [(got[0], TO_CORE)]

    def result(self):
        width = self.pack.shape[1]

        def by_block(z, y, x, c, src, dst):
            out = []
            for n in range(4):
                core, far = (c if n < 2 else 1 - c), n % 2
                for near in (1, 0):
                    y2 = y ^ jnp.where(core == 0, near, far)
                    x2 = x ^ jnp.where(core == 0, far, near)
                    for odd in (1, 0):
                        for pair in (1, 0):
                            block = 4 * (1 - near) + 2 * (1 - odd) + 1 - pair
                            for lo, hi, target, column in self.parts:
                                view = None
                                if dst:
                                    spans = (slice(0, hi - lo), slice(column * width, (column + 1) * width))
                                    view = dst[target].at[(z ^ odd ^ (2 * pair), y2, x2, core) + spans]
                                out.append((n, src and src[n].at[block, lo:hi], view))
            return out

        return place(
            self.coords, self.kept + self.flight, [(4, 2, 2, 2) + shape for shape in self.shapes], by_block
        )


FAR_FIRST = (TO_FAR, TO_NEAR, TO_ODD, TO_PAIR)
Z_FIRST = (TO_ODD, TO_PAIR, TO_FAR, TO_NEAR)


class SumUnit:
    def __init__(self, parts, route=FAR_FIRST):
        self.flight, self.step, self.route = list(parts), 0, route

    def local(self, got):
        self.step += 1
        if self.step == 1:
            leaving, self.kept = got
        elif self.step < 5:
            half = self.kept.shape[0] // 2
            add = lambda a, b: a.astype(f32) + b.astype(f32)
            leaving = add(self.kept[:half], got[0][:half]).astype(bf16)
            self.kept = add(self.kept[half:], got[0][half:])
            if self.step < 4:
                self.kept = self.kept.astype(bf16)
        else:
            self.kept = self.kept + got[0].astype(f32)
            return []
        return [(leaving, self.route[self.step - 1])]


Sums = collections.namedtuple("Sums", "o i a")


def block_order(coords, z_first=False):
    z, y, x, c = coords[0], coords[1], coords[2], coords[3]
    order = []
    for core in (c, 1 - c):
        for first in range(4):
            for second in range(4):
                across, along = (second, first) if z_first else (first, second)
                far, near = 1 - across // 2, 1 - across % 2
                odd, pair = 1 - along // 2, 1 - along % 2
                y2 = y ^ jnp.where(core == 0, near, far)
                x2 = x ^ jnp.where(core == 0, far, near)
                order.append((z ^ odd ^ (2 * pair)) * 8 + y2 * 4 + x2 * 2 + core)
    return jnp.stack(order).astype(jnp.int32)


def order_matrices(order):
    block = D // 32
    wanted = (order[:, None] * block + lax.iota(jnp.int32, block)[None, :]).reshape(2, D // 2, 1)
    columns = lax.broadcasted_iota(jnp.int32, (2, D // 2, D), 2)
    chosen = (columns == wanted).astype(bf16)
    return chosen[0], chosen[1]


def selected(matrices, *arrays):
    count = len(arrays)

    def kernel(mine, theirs, *refs):
        for n in range(count):
            rows = refs[n][...]
            refs[count + 2 * n][...] = nt_dot(mine[...], rows).astype(bf16)
            refs[count + 2 * n + 1][...] = nt_dot(theirs[...], rows).astype(bf16)

    out = jax.ShapeDtypeStruct((D // 2, arrays[0].shape[0]), bf16)
    outs = pl.pallas_call(
        kernel,
        out_shape=[out] * (2 * count),
        compiler_params=pltpu.CompilerParams(vmem_limit_bytes=48 << 20),
        cost_estimate=SMALL_COST,
    )(*matrices, *arrays)
    return [tuple(outs[2 * n : 2 * n + 2]) for n in range(count)]


def weight_terms(*pairs_of, first=0, tile=1024):
    rows, tokens = pairs_of[0][0][0].shape
    counts = [pair[2] // tile for pair in pairs_of]
    starts = [sum(counts[:n]) for n in range(len(counts))]
    columns, half = sum(counts) * tile, rows // 2

    def kernel(*refs):
        leaving, kept = refs[-2:]
        j = pl.program_id(0)
        for n, (start, count) in enumerate(zip(starts, counts)):

            @pl.when((j >= start) & (j < start + count))
            def _(a1=refs[4 * n], a2=refs[4 * n + 1], b1=refs[4 * n + 2], b2=refs[4 * n + 3]):
                total = jnp.dot(a1[...], b1[...], preferred_element_type=f32)
                total = total + jnp.dot(a2[...], b2[...], preferred_element_type=f32)
                leaving[...] = total[:half].astype(bf16)
                kept[...] = total[half:].astype(bf16)

    in_specs, args = [], []
    for (left, right, _), start, count in zip(pairs_of, starts, counts):
        whole = pl.BlockSpec((rows, tokens), lambda j: (0, 0))
        cut = pl.BlockSpec((tokens, tile), lambda j, s=start, n=count: (0, jnp.clip(j - s, 0, n - 1) + first // tile))
        in_specs += [whole, whole, cut, cut]
        args += [*map(in_hbm, left), *right]
    out = jax.ShapeDtypeStruct((half, columns), bf16)
    return pl.pallas_call(
        kernel,
        grid=(columns // tile,),
        in_specs=in_specs,
        out_specs=[pl.BlockSpec((half, tile), lambda j: (0, j))] * 2,
        out_shape=[out, out],
        compiler_params=pltpu.CompilerParams(vmem_limit_bytes=48 << 20),
        cost_estimate=SMALL_COST,
    )(*args)


def wide_terms_of(order, left, right, part=0, parts=1):
    tokens, width = left[0].shape
    block = width // 32
    columns = right[0].shape[1] // parts

    def kernel(order_ref, *refs):
        a1, a2, (b1, b2, leaving, kept) = refs[:2], refs[2:4], refs[4:]
        one = (
            lax.broadcasted_iota(jnp.int32, (block, block), 0) == lax.broadcasted_iota(jnp.int32, (block, block), 1)
        ).astype(bf16)
        turned = lambda refs: jnp.concatenate([nt_dot(one, r[...]).astype(bf16) for r in refs], axis=0)
        total = jnp.dot(turned(a1), b1[...], preferred_element_type=f32)
        total = (total + jnp.dot(turned(a2), b2[...], preferred_element_type=f32)).astype(bf16)

        @pl.when(pl.program_id(0) < 4)
        def _():
            leaving[...] = total

        @pl.when(pl.program_id(0) >= 4)
        def _():
            kept[...] = total

    cut = lambda n: pl.BlockSpec((tokens, block), lambda j, order: (0, order[2 * j + n]))
    whole = pl.BlockSpec((tokens, columns), lambda j, order: (0, part))
    out = jax.ShapeDtypeStruct((width // 4, columns), bf16)
    return pl.pallas_call(
        kernel,
        grid_spec=pltpu.PrefetchScalarGridSpec(
            num_scalar_prefetch=1,
            grid=(8,),
            in_specs=[cut(0), cut(1), cut(0), cut(1), whole, whole],
            out_specs=[
                pl.BlockSpec((2 * block, columns), lambda j, order: (jnp.minimum(j, 3), 0)),
                pl.BlockSpec((2 * block, columns), lambda j, order: (jnp.maximum(j - 4, 0), 0)),
            ],
        ),
        out_shape=[out, out],
        compiler_params=pltpu.CompilerParams(vmem_limit_bytes=48 << 20),
        cost_estimate=SMALL_COST,
    )(order, *map(in_hbm, (left[0], left[0], left[1], left[1])), *right)


BLOCK = 256
WINDOWS = (2 * BLOCK, 3 * BLOCK)
PAIR = 2 * HEAD_DIM


def query_starts(s):
    edge = (s // 2) ^ (s % 2)
    return edge * BLOCK, (1 - edge) * BLOCK


def window_starts(s):
    return (s % 2) * (2 * BLOCK), (1 - s % 2) * BLOCK


def nt_dot(left, right):
    return lax.dot_general(left, right, (((1,), (1,)), ((), ())), preferred_element_type=f32)


def only_head(value, head, axis):
    lane = lax.broadcasted_iota(jnp.int32, value.shape, axis)
    return jnp.where((lane < HEAD_DIM) if head == 0 else (lane >= HEAD_DIM), value, jnp.zeros_like(value))


def in_order(s, mine, other, scratch):
    for n, ref in ((0, mine), (1, other)):
        for slot in range(2):
            scratch[pl.ds((s ^ (n + 2 * slot)) * BLOCK, BLOCK), :] = ref[slot * BLOCK : (slot + 1) * BLOCK, :]


def attention_views(s):
    rows = [pl.ds(pl.multiple_of(start, BLOCK), BLOCK) for start in query_starts(s)]
    windows = [pl.ds(pl.multiple_of(start, BLOCK), width) for start, width in zip(window_starts(s), WINDOWS)]
    spans = [slice(h * HEAD_DIM, (h + 1) * HEAD_DIM) for h in range(2)]
    return rows, windows, spans, [slice(n * BLOCK, (n + 1) * BLOCK) for n in range(2)]


def attend_forward_kernel(
    s_ref, q_ref, km_ref, ko_ref, vm_ref, vo_ref, edge_ref, inner_ref, mixed_ref, total_ref, keys, values
):
    s = s_ref[0]
    in_order(s, km_ref, ko_ref, keys)
    in_order(s, vm_ref, vo_ref, values)
    rows, windows, spans, kinds = attention_views(s)
    biases = (edge_ref, inner_ref)
    scores = []
    for n in range(2):
        q = q_ref[rows[n], :] * jnp.asarray(HEAD_DIM**-0.5, bf16)
        k = keys[windows[n], :]
        scores += [nt_dot(k, only_head(q, head, 1)) for head in range(2)]
    raised, totals = [], []
    for m in range(4):
        n, head = divmod(m, 2)
        biased = scores[m] + biases[n][...]
        top = jnp.max(biased, axis=0, keepdims=True)
        up = jnp.exp(biased - top)
        totals.append(jnp.sum(up, axis=0, keepdims=True))
        total_ref[0, head : head + 1, kinds[n]] = top + jnp.log(totals[m])
        raised.append(up.astype(bf16))
    for n in range(2):
        v_t = values[windows[n], :].T
        halves = [
            jnp.dot(v_t[spans[h]], raised[2 * n + h], preferred_element_type=f32) / totals[2 * n + h]
            for h in range(2)
        ]
        mixed_ref[rows[n], :] = jnp.concatenate(halves, axis=0).T.astype(bf16)


def attend_backward_kernel(
    s_ref, q_ref, km_ref, ko_ref, vm_ref, vo_ref, edge_ref, inner_ref, mixed_ref, total_ref, grad_ref,
    dq_ref, mine_ref, sent_ref, keys, values, key_sum, value_sum,
):
    s = s_ref[0]
    in_order(s, km_ref, ko_ref, keys)
    in_order(s, vm_ref, vo_ref, values)
    key_sum[...] = jnp.zeros_like(key_sum)
    value_sum[...] = jnp.zeros_like(value_sum)
    rows, windows, spans, kinds = attention_views(s)
    biases = (edge_ref, inner_ref)
    scores, share_grads, queries, grads, inner = [], [], [], [], []
    for n in range(2):
        q = q_ref[rows[n], :] * jnp.asarray(HEAD_DIM**-0.5, bf16)
        g = grad_ref[rows[n], :]
        along = (g.astype(f32) * mixed_ref[rows[n], :].astype(f32)).T
        k, v = keys[windows[n], :], values[windows[n], :]
        for head in range(2):
            queries.append(only_head(q, head, 1))
            grads.append(only_head(g, head, 1))
            inner.append(jnp.sum(along[spans[head]], axis=0, keepdims=True))
            scores.append(nt_dot(k, queries[-1]))
            share_grads.append(nt_dot(v, grads[-1]))
    shares_low, grads_low = [], []
    for m in range(4):
        n, head = divmod(m, 2)
        shares = jnp.exp(scores[m] + biases[n][...] - total_ref[0, head : head + 1, kinds[n]])
        shares_low.append(shares.astype(bf16))
        grads_low.append((shares * (share_grads[m] - inner[m])).astype(bf16))
    both = lambda values, n, axis: jnp.concatenate(values[2 * n : 2 * n + 2], axis=axis)
    for n in range(2):
        k_t = keys[windows[n], :].T
        query_grads = [jnp.dot(k_t[spans[h]], grads_low[2 * n + h], preferred_element_type=f32) for h in range(2)]
        dq_ref[rows[n], :] = (jnp.concatenate(query_grads, axis=0).T * HEAD_DIM**-0.5).astype(bf16)
        key_sum[windows[n], :] += jnp.dot(both(grads_low, n, 1), both(queries, n, 0), preferred_element_type=f32)
        value_sum[windows[n], :] += jnp.dot(both(shares_low, n, 1), both(grads, n, 0), preferred_element_type=f32)
    for slot in range(2):
        here = slice(slot * BLOCK, (slot + 1) * BLOCK)
        mine, other = pl.ds((s ^ (2 * slot)) * BLOCK, BLOCK), pl.ds((s ^ (1 + 2 * slot)) * BLOCK, BLOCK)
        for n, sums in ((0, key_sum), (1, value_sum)):
            mine_ref[n, here, :] = sums[mine, :]
            sent_ref[n, here, :] = sums[other, :].astype(bf16)


def call_attention(kernel, s, own, other, bias, kept, outs, scratch):
    pairs_count = D // PAIR
    third = lambda n: pl.BlockSpec((2 * BLOCK, PAIR), lambda h: (0, h + n * pairs_count))
    cut = third(0)
    double = pl.BlockSpec((2, 2 * BLOCK, PAIR), lambda h: (0, 0, h))
    per_pair = pl.BlockSpec((1, 2, 2 * BLOCK), lambda h: (h, 0, 0))
    whole = [pl.BlockSpec(b.shape, lambda h: (0, 0)) for b in bias]
    in_specs = [pl.BlockSpec(memory_space=pltpu.SMEM), third(0), third(1), third(1), third(2), third(2), *whole]
    args = [s, own, own, other, own, other, *bias]
    if kept:
        in_specs += [cut, per_pair, cut]
        args += kept
    shapes, specs = [], []
    for kind, spec in outs:
        shapes.append(
            {
                0: jax.ShapeDtypeStruct((2 * BLOCK, D), kind),
                1: jax.ShapeDtypeStruct((pairs_count, 2, 2 * BLOCK), kind),
                2: jax.ShapeDtypeStruct((2, 2 * BLOCK, D), kind),
            }[spec]
        )
        specs.append((cut, per_pair, double)[spec])
    return pl.pallas_call(
        kernel,
        grid=(pairs_count,),
        in_specs=in_specs,
        out_specs=specs,
        out_shape=shapes,
        scratch_shapes=scratch,
        compiler_params=pltpu.CompilerParams(vmem_limit_bytes=48 << 20),
        cost_estimate=SMALL_COST,
    )(*args)


def attend_forward_blocks(s, own, other, bias):
    scratch = [pltpu.VMEM((SEQ_LEN, PAIR), bf16)] * 2
    return call_attention(attend_forward_kernel, s, own, other, bias, (), ((bf16, 0), (f32, 1)), scratch)


def attend_backward_blocks(s, own, other, bias, mixed, totals, grads):
    scratch = [pltpu.VMEM((SEQ_LEN, PAIR), bf16)] * 2 + [pltpu.VMEM((SEQ_LEN, PAIR), f32)] * 2
    outs = ((bf16, 0), (f32, 2), (bf16, 2))
    kept = (mixed, totals, grads)
    return call_attention(attend_backward_kernel, s, own, other, bias, kept, outs, scratch)


def window_bias(s, ids):
    out = []
    for start, width, first in zip(window_starts(s), WINDOWS, query_starts(s)):
        keys = lax.dynamic_slice_in_dim(ids, start, width)
        block = s ^ (2 * (first // BLOCK))
        queries = lax.dynamic_slice_in_dim(ids, block * BLOCK, BLOCK)
        out.append(jnp.where(keys[:, None] == queries[None, :], 0.0, -1e30).astype(f32))
    return tuple(out)


def norm_forward(total):
    center = jnp.mean(total, axis=-1, keepdims=True)
    centered = total - center
    spread = jnp.mean(centered * centered, axis=-1, keepdims=True)
    scale = lax.rsqrt(spread + epsilon)
    return centered * scale, scale


def norm_backward(total, gain, upstream):
    unit, scale = norm_forward(total)
    lifted = upstream * gain
    grad = scale * (
        lifted
        - jnp.mean(lifted, axis=-1, keepdims=True)
        - unit * jnp.mean(lifted * unit, axis=-1, keepdims=True)
    )
    return grad, jnp.sum(upstream * unit, axis=0), jnp.sum(upstream, axis=0)


def column_sum(values):
    return jnp.sum(values.astype(f32), axis=0)


def heads_of(rows):
    return rows.reshape(rows.shape[0], HEADS, HEAD_DIM)


def masked_scores(queries, keys, allowed):
    scores = jnp.einsum("qhd,khd->hqk", queries, keys, preferred_element_type=f32)
    return jnp.where(allowed[None], scores * HEAD_DIM ** (-0.5), -1e30)


def attend_forward(queries, keys, values, allowed):
    scores = masked_scores(heads_of(queries), heads_of(keys), allowed)
    top_score = jnp.max(scores, axis=2, keepdims=True)
    raised = jnp.exp(scores - top_score)
    totals = jnp.sum(raised, axis=2, keepdims=True)
    shares = (raised / totals).astype(bf16)
    mixed = jnp.einsum("hqk,khd->qhd", shares, heads_of(values), preferred_element_type=f32)
    return mixed.astype(bf16).reshape(queries.shape), top_score + jnp.log(totals)


def attend_backward(queries, keys, values, allowed, log_total, grads):
    queries, keys, values, grads = map(heads_of, (queries, keys, values, grads))
    scale = HEAD_DIM ** (-0.5)
    shares = jnp.exp(masked_scores(queries, keys, allowed) - log_total)
    share_grads = jnp.einsum("qhd,khd->hqk", grads, values, preferred_element_type=f32)
    inner_sums = jnp.sum(shares * share_grads, axis=2, keepdims=True)
    score_grads = (shares * (share_grads - inner_sums)).astype(bf16)
    query_grad = jnp.einsum("hqk,khd->qhd", score_grads, keys, preferred_element_type=f32) * scale
    key_grad = jnp.einsum("hqk,qhd->khd", score_grads, queries, preferred_element_type=f32) * scale
    value_grad = jnp.einsum(
        "hqk,qhd->khd", shares.astype(bf16), grads, preferred_element_type=f32
    )
    flat = lambda a: a.reshape(a.shape[0], D)
    return flat(query_grad).astype(bf16), flat(key_grad), flat(value_grad)


def product(rows, weight, tile, finish, outs, by_column=(), tiles=(), transposed=False, sums=0):
    tokens, depth = rows.shape
    width = weight.shape[0 if transposed else 1]

    def kernel(rows_ref, weight_ref, *refs):
        total = (nt_dot if transposed else lambda a, b: jnp.dot(a, b, preferred_element_type=f32))(
            rows_ref[...], weight_ref[...]
        )
        inputs = [r[...] for r in refs[: len(by_column) + len(tiles)]]
        for ref, value in zip(refs[len(inputs) :], finish(total, *inputs)):
            ref[...] = value.astype(ref.dtype)

    cut = pl.BlockSpec((tokens, tile), lambda j: (0, j))
    if transposed:
        weight_spec = pl.BlockSpec((tile, depth), lambda j: (j, 0))
    else:
        weight_spec = pl.BlockSpec((depth, tile), lambda j: (0, j))
    return pl.pallas_call(
        kernel,
        grid=(width // tile,),
        in_specs=[pl.BlockSpec((tokens, depth), lambda j: (0, 0)), weight_spec]
        + [pl.BlockSpec((1, tile), lambda j: (0, j))] * len(by_column)
        + [cut] * len(tiles),
        out_specs=[cut] * len(outs) + [pl.BlockSpec((1, tile), lambda j: (0, j))] * sums,
        out_shape=[jax.ShapeDtypeStruct((tokens, width), kind) for kind in outs]
        + [jax.ShapeDtypeStruct((1, width), f32)] * sums,
        compiler_params=pltpu.CompilerParams(vmem_limit_bytes=48 << 20),
        cost_estimate=SMALL_COST,
    )(rows, in_hbm(weight), *[v.reshape(1, width) for v in by_column], *tiles)


def gelu_parts(total, bias):
    inner = total + bias
    below = 0.5 * (1.0 + lax.erf(inner * (0.5**0.5)))
    slope = below + inner * jnp.exp(-0.5 * inner * inner) * (2 * math.pi) ** -0.5
    return inner * below, slope


def norm_backward_rows(total, gain, upstream):
    tokens, width = total.shape
    tile = 128

    def kernel(total_ref, gain_ref, up_ref, grad_ref, low_ref, sums_ref):
        unit, scale = norm_forward(total_ref[...])
        up = up_ref[...]
        lifted = up * gain_ref[...]
        grad = scale * (
            lifted
            - jnp.mean(lifted, axis=-1, keepdims=True)
            - unit * jnp.mean(lifted * unit, axis=-1, keepdims=True)
        )
        low = grad.astype(bf16)
        grad_ref[...] = grad
        low_ref[...] = low

        @pl.when(pl.program_id(0) == 0)
        def _():
            sums_ref[...] = jnp.zeros_like(sums_ref)

        for n, value in enumerate((up * unit, up, low.astype(f32))):
            sums_ref[n : n + 1, :] += jnp.sum(value, axis=0, keepdims=True)

    cut = pl.BlockSpec((tile, width), lambda j: (j, 0))
    out = jax.ShapeDtypeStruct((tokens, width), f32)
    return pl.pallas_call(
        kernel,
        grid=(tokens // tile,),
        in_specs=[cut, pl.BlockSpec((1, width), lambda j: (0, 0)), cut],
        out_specs=[cut, cut, pl.BlockSpec((8, width), lambda j: (0, 0))],
        out_shape=[out, jax.ShapeDtypeStruct((tokens, width), bf16), jax.ShapeDtypeStruct((8, width), f32)],
        compiler_params=pltpu.CompilerParams(vmem_limit_bytes=32 << 20),
        cost_estimate=SMALL_COST,
    )(total, gain.reshape(1, width), upstream)


def merged(query_low, own, back):
    tokens = query_low.shape[0]
    tile = D // 2

    def kernel(query_ref, own_ref, back_ref, low_ref, sum_ref):
        def put(low):
            low_ref[...] = low
            sum_ref[...] = jnp.sum(low.astype(f32), axis=0, keepdims=True)

        @pl.when(pl.program_id(0) < 2)
        def _():
            put(query_ref[...])

        @pl.when(pl.program_id(0) >= 2)
        def _():
            put((own_ref[0] + back_ref[0].astype(f32)).astype(bf16))

    part = pl.BlockSpec((1, tokens, tile), lambda j: (jnp.maximum(j - 2, 0) // 2, 0, jnp.maximum(j - 2, 0) % 2))
    return pl.pallas_call(
        kernel,
        grid=(6,),
        in_specs=[pl.BlockSpec((tokens, tile), lambda j: (0, jnp.minimum(j, 1))), part, part],
        out_specs=[pl.BlockSpec((tokens, tile), lambda j: (0, j)), pl.BlockSpec((1, tile), lambda j: (0, j))],
        out_shape=[jax.ShapeDtypeStruct((tokens, 3 * D), bf16), jax.ShapeDtypeStruct((1, 3 * D), f32)],
        compiler_params=pltpu.CompilerParams(vmem_limit_bytes=32 << 20),
        cost_estimate=SMALL_COST,
    )(query_low, own, back)


SMALL = 8


def staged_body(tokens, doc_lengths, cotangent, *shards):
    (
        query_weight,
        key_weight,
        value_weight,
        mix_weight,
        query_bias,
        value_bias,
        mix_bias,
        first_gain,
        first_shift,
        inner_weight,
        inner_bias,
        outer_weight,
        outer_bias,
        second_gain,
        second_shift,
    ) = shards
    layer_count = query_weight.shape[0]
    devices = 32
    length = SEQ_LEN // 4
    rows_held, inner_held = D // devices, FF // devices
    seq = lax.axis_index("seq")
    row = seq // 2
    coords = coordinates()
    z, y, x, c = coords[0], coords[1], coords[2], coords[3]
    place_of = seq.reshape(1).astype(jnp.int32)

    def split_rows(both):
        both = both.reshape(2, length, D)
        return pick(both, row, 0), pick(both, 1 - row, 0)

    token_kept, token_left = split_rows(tokens)
    upstream_kept, upstream_left = split_rows(cotangent)

    def unit_a(layer):
        r = rows_held
        parts = [w[layer] for w in (query_weight, key_weight, value_weight)]
        rows, outs = [(r * n, r * (n + 1), 0, n) for n in range(3)], [(r, 3 * D)]
        if layer:
            parts, rows, outs = parts + [mix_weight[layer]], rows + [(3 * r, 4 * r, 1, 0)], outs + [(r, D)]
        return GatherUnit(coords, jnp.concatenate(parts), outs, rows)

    def unit_i(layer):
        r, inner = rows_held, inner_weight[layer]
        parts = [inner[:, D * n : D * (n + 1)] for n in range(4)]
        rows, outs = [(r * n, r * (n + 1), 0, n) for n in range(4)], [(r, FF)]
        if not layer:
            parts, rows, outs = parts + [mix_weight[layer]], rows + [(4 * r, 5 * r, 1, 0)], outs + [(r, D)]
        return GatherUnit(coords, jnp.concatenate(parts), outs, rows)

    def unit_o(layer):
        return GatherUnit(coords, outer_weight[layer], [(inner_held, D)], [(0, inner_held, 0, 0)])

    units = [[make(layer) for make in (unit_a, unit_i, unit_o)] for layer in range(layer_count)]

    small_vectors = (
        query_bias,
        value_bias,
        mix_bias,
        first_gain,
        first_shift,
        outer_bias,
        second_gain,
        second_shift,
    )
    vector_count = SMALL * layer_count
    small_held = vector_count * rows_held
    mine = jnp.concatenate(
        [jnp.concatenate([v[layer] for v in small_vectors]) for layer in range(layer_count)]
        + [inner_bias.reshape(-1)]
    )
    held = mine.shape[0]
    padded = jnp.pad(mine, (0, 1024 - held)).reshape(8, 128)

    u = [unit for layer_units in units for unit in layer_units]
    padded = phase(padded, u[0])
    token_got = send(token_left, TO_X)
    every = jnp.roll(jnp.stack([padded] + [send(padded, TO_Z[4 - k]) for k in (1, 2, 3)]), z, axis=0)

    lengths = pick(doc_lengths.reshape(2, NDOC), row, 0)
    places = lax.iota(jnp.int32, SEQ_LEN)
    segment = jnp.sum((places[:, None] >= jnp.cumsum(lengths)[None, :]).astype(jnp.int32), axis=1)
    bias = window_bias(seq, jnp.where(segment == NDOC - 1, NDOC + places, segment))
    order, order_z = block_order(coords), block_order(coords, True)
    matrices = order_matrices(order)

    token_got, every = phase((token_got, every), u[0], u[1])
    every, upstream_left = lax.optimization_barrier((every, upstream_left))
    upstream_got = send(upstream_left, TO_X)
    every = by_place(every, send(every, TO_Y), y, 1)
    every, bias, upstream_got = phase((every, bias, upstream_got), u[0], settle=[u[1]])
    every = by_place(every, send(every, TO_X), x, 2)
    every, matrices = phase((every, matrices), u[0], u[1])
    every = by_place(every, send(every, TO_CORE), c, 3)
    every = every.reshape(devices, 1024)[:, :held].astype(f32)
    small_all = (
        every[:, :small_held]
        .reshape(devices, vector_count, rows_held)
        .transpose(1, 0, 2)
        .reshape(layer_count, SMALL, D)
    )
    wide_all = (
        every[:, small_held:]
        .reshape(devices, layer_count, inner_held)
        .transpose(1, 0, 2)
        .reshape(layer_count, FF)
    )
    stream = jnp.concatenate([token_kept, token_got]).astype(f32)
    stream, small_all, wide_all = phase((stream, small_all, wide_all), u[0], u[1], u[2], u[3])
    saved, active_gots = [], []
    for layer in range(layer_count):
        a_unit, i_unit, o_unit = units[layer]
        next_a, next_i, next_o = units[layer + 1] if layer + 1 < layer_count else (None,) * 3
        q_bias, v_bias, m_bias, gain1, shift1, o_bias, gain2, shift2 = [small_all[layer, n] for n in range(SMALL)]
        w_three, *w_rest = a_unit.result()
        w_three = w_three.reshape(D, 3 * D)
        stream_low = stream.astype(bf16)
        three_bias = jnp.concatenate([q_bias, jnp.zeros_like(q_bias), v_bias])
        (three,) = product(stream_low, w_three, 1024, lambda total, b: (total + b,), (bf16,), (three_bias,))
        if next_a:
            three = phase(three, i_unit, o_unit, next_a)
        else:
            three = phase(three, i_unit, settle=[o_unit])
        three_got = send(three, TO_CORE)
        (left_stream,) = selected(matrices, tie(stream_low, three))
        three, left_stream = lax.optimization_barrier((three, left_stream))
        left_stream = (left_stream[0], send(left_stream[1], TO_CORE))
        mixed, totals = attend_forward_blocks(place_of, three, three_got, bias)
        if next_a:
            mixed, totals, left_stream = phase(
                (mixed, totals, left_stream), i_unit, o_unit, next_a, next_i
            )
        else:
            mixed, totals, left_stream, active_gots = phase(
                (mixed, totals, left_stream, active_gots), i_unit, o_unit
            )
        w_inner, *w_more = i_unit.result()
        (w_mix,) = w_rest + w_more
        w_inner, w_mix = w_inner.reshape(D, FF), w_mix.reshape(D, D)
        first_sum = stream + (dot(mixed, w_mix) + m_bias)
        first = norm_forward(first_sum)[0] * gain1 + shift1
        first_low = first.astype(bf16)
        if next_a:
            first_low = phase(first_low, o_unit, next_i, settle=[next_a])
        else:
            first_low = phase(first_low, o_unit)
        left_mix, left_first = selected(matrices, mixed, first_low)
        first_low, left_mix, left_first = lax.optimization_barrier((first_low, left_mix, left_first))
        left_mix, left_first = [(m, send(t, TO_CORE)) for m, t in (left_mix, left_first)]
        active, slope = product(first_low, w_inner, 1024, gelu_parts, (bf16, bf16), (wide_all[layer],))
        if next_a:
            active, slope, left_mix, left_first = phase(
                (active, slope, left_mix, left_first), o_unit, next_a, next_o, settle=[next_i]
            )
        else:
            active, slope, left_mix, left_first = phase((active, slope, left_mix, left_first), o_unit)
        (w_outer,) = o_unit.result()
        active_got = send(tie(active, w_outer), TO_CORE)
        w_outer = w_outer.reshape(FF, D)
        (second_sum,) = product(
            active, w_outer, 256, lambda total, b, f: (f + (total + b),), (f32,), (o_bias,), (first,)
        )
        if not next_a:
            second_sum, active_got = lax.optimization_barrier((second_sum, active_got))
        active_gots.append(active_got)
        stream = norm_forward(second_sum)[0] * gain2 + shift2
        if next_a:
            stream = phase(stream, next_a, next_i, next_o)
        saved.append(
            (
                (w_three, w_mix, w_inner, w_outer, gain1, gain2),
                (three, three_got, totals, mixed),
                (first_sum, slope, second_sum),
                (left_stream, left_mix, left_first, active),
            )
        )

    def both_rows(kept, got):
        got = got.astype(f32)
        return jnp.where(row == 0, jnp.stack([kept, got]), jnp.stack([got, kept])).reshape(tokens.shape)

    output = stream
    output_got = send(output[length:].astype(bf16), TO_X)

    upstream = jnp.concatenate([upstream_kept, upstream_got]).astype(f32)
    small_grads, wide_grads = [None] * layer_count, [None] * layer_count
    sums = [None] * layer_count
    before = None
    for layer in reversed(range(layer_count)):
        weights, kept, rest, lefts = saved[layer]
        w_three, w_mix, w_inner, w_outer, gain1, gain2 = weights
        three, three_got, totals, mixed = kept
        first_sum, slope, second_sum = rest
        left_stream, left_mix, left_first, active = lefts
        left_active = (active, active_gots[layer])

        def with_sum(total, slopes):
            low = (total * slopes).astype(bf16)
            return low, jnp.sum(low.astype(f32), axis=0, keepdims=True)

        second_grad, second_low, second_sums = norm_backward_rows(second_sum, gain2, upstream)
        second_got = send(second_low, TO_CORE)
        inner_low, inner_sum = product(
            second_low, w_outer, 1024, with_sum, (bf16,), (), (slope,), transposed=True, sums=1
        )
        if before:
            inner_low, second_got = phase((inner_low, second_got), before.o[0], before.i, before.a)
        else:
            inner_low, second_got = lax.optimization_barrier((inner_low, second_got))
        inner_got = send(inner_low, TO_CORE)
        second_pair = (second_low, second_got)
        if before:
            o_sums = (
                SumUnit(wide_terms_of(order_z, left_active, second_pair, 0, 2), Z_FIRST),
                SumUnit(wide_terms_of(order, left_active, second_pair, 1, 2)),
            )
            second_grad, inner_low, inner_got = phase(
                (second_grad, inner_low, inner_got), *o_sums, before.a, before.i, settle=before.o
            )
        else:
            o_sums = (SumUnit(wide_terms_of(order, left_active, second_pair)),)
            second_grad, inner_low, inner_got, output_got = phase(
                (second_grad, inner_low, inner_got, output_got), *o_sums
            )
        (first_grad,) = product(
            inner_low, w_inner, 256, lambda total, g: (g + total,), (f32,), (), (second_grad,), transposed=True
        )
        first_sum_grad, branch_low, first_sums = norm_backward_rows(first_sum, gain1, first_grad)
        branch_got = send(branch_low, TO_CORE)
        (mixed_grad,) = product(branch_low, w_mix, 512, lambda total: (total,), (bf16,), transposed=True)
        i_sum = SumUnit(weight_terms((left_first, tie((inner_low, inner_got), mixed_grad), FF)))
        if before:
            mixed_grad = phase(mixed_grad, i_sum, *o_sums, before.a, settle=[before.i])
        else:
            mixed_grad = phase(mixed_grad, i_sum, settle=o_sums)
        query_low, own_grads, sent_grads = attend_backward_blocks(
            place_of, in_hbm(three), in_hbm(three_got), bias, in_hbm(mixed), in_hbm(totals), mixed_grad
        )
        grads_back = send(sent_grads, TO_CORE)
        if before:
            query_low, own_grads, branch_got = phase((query_low, own_grads, branch_got), i_sum, *o_sums, before.a)
        else:
            query_low, own_grads, branch_got = phase((query_low, own_grads, branch_got), *o_sums, settle=[i_sum])
        low, low_sums = merged(query_low, own_grads, grads_back)
        low_got = send(low, TO_CORE)
        if layer:
            (upstream,) = product(
                low, w_three, 256, lambda total, g: (g + total,), (f32,), (), (first_sum_grad,), transposed=True
            )
            mix_pair = (left_mix, (branch_low, branch_got), D)
            a_sum = SumUnit(weight_terms((left_stream, tie((low, low_got), upstream), 3 * D), mix_pair))
        else:
            mix_pair = (left_mix, (branch_low, branch_got), D)
            a_sum = SumUnit(weight_terms((left_stream, (low, low_got), 3 * D), mix_pair))
            low, low_sums = phase((low, low_sums), a_sum, settle=[i_sum, before.a] if before else [i_sum])
            (upstream,) = product(
                low, w_three, 256, lambda total, g: (g + total,), (f32,), (), (first_sum_grad,), transposed=True
            )
        small_grads[layer] = jnp.stack(
            [
                low_sums[0, :D],
                low_sums[0, 2 * D :],
                first_sums[2],
                first_sums[0],
                first_sums[1],
                second_sums[2],
                second_sums[0],
                second_sums[1],
            ]
        )
        wide_grads[layer] = inner_sum[0]
        if layer:
            upstream, small_grads[layer] = phase((upstream, small_grads[layer]), *o_sums, i_sum, settle=[a_sum])
        sums[layer] = before = Sums(o_sums, i_sum, a_sum)

    small_terms = (
        jnp.stack(small_grads)
        .reshape(vector_count, devices, rows_held)
        .transpose(1, 0, 2)
        .reshape(devices, small_held)
    )
    wide_terms = (
        jnp.stack(wide_grads)
        .reshape(layer_count, devices, inner_held)
        .transpose(1, 0, 2)
        .reshape(devices, layer_count * inner_held)
    )
    terms = jnp.pad(jnp.concatenate([small_terms, wide_terms], axis=1), ((0, 0), (0, 1024 - held)))
    chosen = (order[:, None] == lax.iota(jnp.int32, devices)[None, :]).astype(f32)
    terms = jnp.dot(chosen, terms, precision=lax.Precision.HIGHEST).reshape(2, 128, 128)
    terms = (terms[0] + send(terms[1].astype(bf16), TO_CORE).astype(f32)).astype(bf16)
    small_sum = SumUnit((terms[:64], terms[64:]))

    phase((), small_sum)
    last = sums[0]
    done = [unit for layer in range(1, layer_count) for unit in (*sums[layer].o, sums[layer].i, sums[layer].a)]
    upstream, output_got = phase((upstream, output_got), last.a, last.i, *last.o, small_sum, *done)
    token_left = upstream[length:].astype(bf16)
    upstream, token_left = phase((upstream, token_left), last.a, last.i, *last.o, small_sum)
    token_back = send(token_left, TO_X)
    upstream, token_back = phase((upstream, token_back), last.a, last.i, small_sum)
    phase((), last.a, small_sum)
    own_terms = small_sum.kept.reshape(-1)[:held]
    small_own = own_terms[:small_held].reshape(layer_count, SMALL, rows_held)
    wide_own = own_terms[small_held:].reshape(layer_count, inner_held)
    for layer in range(layer_count):
        for unit in (*sums[layer].o, sums[layer].i, sums[layer].a):
            while unit.step < 5:
                phase((), unit)
    o_all = jnp.stack([jnp.concatenate([unit.kept for unit in group.o], axis=1) for group in sums])
    i_all, a_all = [jnp.stack([group[n].kept for group in sums]) for n in (1, 2)]
    return (
        both_rows(output[:length], output_got),
        both_rows(upstream[:length], token_back),
        a_all[:, :, :D],
        a_all[:, :, D : 2 * D],
        a_all[:, :, 2 * D : 3 * D],
        a_all[:, :, 3 * D :],
        small_own[:, 0],
        small_own[:, 1],
        small_own[:, 2],
        small_own[:, 3],
        small_own[:, 4],
        i_all,
        wide_own,
        o_all,
        small_own[:, 5],
        small_own[:, 6],
        small_own[:, 7],
    )


def plain_body(fsdp_size, seq_size):
    half = seq_size // 2
    device_count = fsdp_size * seq_size
    across = [(i, (i + half) % seq_size) for i in range(seq_size)]
    groups = [[m * half + j for j in range(half)] for m in range(2)]
    length = SEQ_LEN // seq_size

    def gather_siblings(rows):
        return lax.all_gather(rows, "seq", axis_index_groups=groups)

    def scatter_siblings(own_order):
        return lax.psum_scatter(own_order, "seq", axis_index_groups=groups)

    def body(tokens, doc_lengths, cotangent, *shards):
        (
            query_weight,
            key_weight,
            value_weight,
            mix_weight,
            query_bias,
            value_bias,
            mix_bias,
            first_gain,
            first_shift,
            inner_weight,
            inner_bias,
            outer_weight,
            outer_bias,
            second_gain,
            second_shift,
        ) = shards
        layer_count = query_weight.shape[0]
        seq = lax.axis_index("seq")
        row = seq // half
        rows_held = D // device_count
        inner_held = FF // device_count

        def vector_rows(small, wide):
            return jnp.concatenate(
                [jnp.concatenate([v[layer] for v in small]) for layer in range(layer_count)]
                + [wide.reshape(-1)]
            )

        small_vectors = (
            query_bias,
            value_bias,
            mix_bias,
            first_gain,
            first_shift,
            outer_bias,
            second_gain,
            second_shift,
        )
        vector_count = len(small_vectors) * layer_count
        mine = vector_rows(small_vectors, inner_bias)
        held = mine.shape[0]
        every = lax.all_gather(mine, AXES)
        every = every.astype(f32)
        small_held = vector_count * rows_held
        small_all = (
            every[:, :small_held]
            .reshape(device_count, vector_count, rows_held)
            .transpose(1, 0, 2)
            .reshape(layer_count, len(small_vectors), D)
        )
        wide_all = (
            every[:, small_held:]
            .reshape(device_count, layer_count, inner_held)
            .transpose(1, 0, 2)
            .reshape(layer_count, FF)
        )

        def whole_weights(layer):
            weights = (query_weight, key_weight, value_weight, mix_weight, inner_weight, outer_weight)
            return [lax.all_gather(w[layer], AXES, axis=0, tiled=True) for w in weights]

        def own_row(both_rows):
            kept = pick(both_rows, row, 0)
            return jnp.concatenate(
                [kept, lax.ppermute(pick(both_rows, 1 - row, 0), "seq", across)]
            )

        def both_rows(values):
            kept = values[:length]
            other = lax.ppermute(values[length:].astype(bf16), "seq", across).astype(f32)
            return jnp.where(row == 0, jnp.stack([kept, other]), jnp.stack([other, kept]))

        stream_start = own_row(tokens.reshape(2, length, D))
        upstream_start = own_row(cotangent.reshape(2, length, D))

        lengths = pick(doc_lengths.reshape(2, NDOC), row, 0)
        bounds = jnp.cumsum(lengths)
        within = lax.iota(jnp.int32, length)

        def positions(s):
            return jnp.concatenate([s * length + within, (s + half) % seq_size * length + within])

        def segments(places):
            return jnp.sum((places[:, None] >= bounds[None, :]).astype(jnp.int32), axis=1)

        query_places = positions(seq)
        key_places = jnp.concatenate([positions(row * half + j) for j in range(half)])
        query_segment, key_segment = segments(query_places), segments(key_places)
        allowed = (
            (query_segment[:, None] == key_segment[None, :]) & (key_segment[None, :] != NDOC - 1)
        ) | (query_places[:, None] == key_places[None, :])

        stream = stream_start.astype(f32)
        saved = []
        for layer in range(layer_count):
            q_bias, v_bias, m_bias, gain1, shift1, o_bias, gain2, shift2 = [
                small_all[layer, n] for n in range(len(small_vectors))
            ]
            w_query, w_key, w_value, w_mix, w_inner, w_outer = whole_weights(layer)
            stream_low = stream.astype(bf16)
            queries = (dot(stream_low, w_query) + q_bias).astype(bf16)
            key_rows = dot(stream_low, w_key).astype(bf16)
            values = (dot(stream_low, w_value) + v_bias).astype(bf16)
            all_keys = gather_siblings(key_rows).reshape(SEQ_LEN, D)
            all_values = gather_siblings(values).reshape(SEQ_LEN, D)
            mixed, log_total = attend_forward(queries, all_keys, all_values, allowed)
            first_sum = stream + (dot(mixed, w_mix) + m_bias)
            first = norm_forward(first_sum)[0] * gain1 + shift1
            first_low = first.astype(bf16)
            inner = dot(first_low, w_inner) + wide_all[layer]
            below = 0.5 * (1.0 + lax.erf(inner * (0.5**0.5)))
            active = (inner * below).astype(bf16)
            slope = (below + inner * jnp.exp(-0.5 * inner * inner) * (2 * math.pi) ** -0.5).astype(
                bf16
            )
            second_sum = first + (dot(active, w_outer) + o_bias)
            stream = norm_forward(second_sum)[0] * gain2 + shift2
            saved.append(
                (
                    (w_query, w_key, w_value, w_mix, w_inner, w_outer, gain1, gain2),
                    (stream_low, queries, all_keys, all_values, log_total, mixed),
                    (first_sum, first_low, slope, active, second_sum),
                )
            )
        activations = both_rows(stream)

        upstream = upstream_start.astype(f32)
        small_grads = [None] * layer_count
        wide_grads = [None] * layer_count
        results = [None] * layer_count

        def reduced(grads):
            return [lax.psum_scatter(g, AXES, scatter_dimension=0, tiled=True) for g in grads]

        for layer in reversed(range(layer_count)):
            (w_query, w_key, w_value, w_mix, w_inner, w_outer, gain1, gain2), kept, rest = saved[layer]
            stream_low, queries, all_keys, all_values, log_total, mixed = kept
            first_sum, first_low, slope, active, second_sum = rest
            second_grad, gain2_grad, shift2_grad = norm_backward(second_sum, gain2, upstream)
            second_low = second_grad.astype(bf16)
            (outer_grad,) = reduced([contract_rows(active, second_low)])
            inner_low = (contract_cols(second_low, w_outer) * slope).astype(bf16)
            (inner_grad,) = reduced([contract_rows(first_low, inner_low)])
            first_grad = second_grad + contract_cols(inner_low, w_inner)
            first_sum_grad, gain1_grad, shift1_grad = norm_backward(first_sum, gain1, first_grad)
            branch_low = first_sum_grad.astype(bf16)
            mix_terms = contract_rows(mixed, branch_low)
            mixed_grad = contract_cols(branch_low, w_mix).astype(bf16)
            query_low, key_terms, value_terms = attend_backward(
                queries, all_keys, all_values, allowed, log_total, mixed_grad
            )
            n = 2 * length
            key_low = scatter_siblings(key_terms.reshape(half, n, D)).astype(bf16)
            value_low = scatter_siblings(value_terms.reshape(half, n, D)).astype(bf16)
            value_grad, mix_grad = reduced([contract_rows(stream_low, value_low), mix_terms])
            query_grad, key_grad = reduced(
                [contract_rows(stream_low, query_low), contract_rows(stream_low, key_low)]
            )
            upstream = (
                first_sum_grad
                + contract_cols(query_low, w_query)
                + contract_cols(key_low, w_key)
                + contract_cols(value_low, w_value)
            )
            small_grads[layer] = jnp.stack(
                [
                    column_sum(query_low),
                    column_sum(value_low),
                    column_sum(branch_low),
                    gain1_grad,
                    shift1_grad,
                    column_sum(second_low),
                    gain2_grad,
                    shift2_grad,
                ]
            )
            wide_grads[layer] = column_sum(inner_low)
            results[layer] = (query_grad, key_grad, value_grad, mix_grad, inner_grad, outer_grad)
        token_grad = both_rows(upstream)

        small_terms = (
            jnp.stack(small_grads)
            .reshape(vector_count, device_count, rows_held)
            .transpose(1, 0, 2)
            .reshape(device_count, small_held)
        )
        wide_terms = (
            jnp.stack(wide_grads)
            .reshape(layer_count, device_count, inner_held)
            .transpose(1, 0, 2)
            .reshape(device_count, layer_count * inner_held)
        )
        terms = jnp.concatenate([small_terms, wide_terms], axis=1)
        own_terms = lax.psum_scatter(terms, AXES, scatter_dimension=0, tiled=False)
        small_own = own_terms[:small_held].reshape(layer_count, len(small_vectors), rows_held)
        wide_own = own_terms[small_held:].reshape(layer_count, inner_held)
        query_g, key_g, value_g, mix_g, inner_g, outer_g = [
            jnp.stack([results[layer][n] for layer in range(layer_count)]) for n in range(6)
        ]
        return (
            activations.reshape(tokens.shape),
            token_grad.reshape(tokens.shape),
            query_g,
            key_g,
            value_g,
            mix_g,
            small_own[:, 0],
            small_own[:, 1],
            small_own[:, 2],
            small_own[:, 3],
            small_own[:, 4],
            inner_g,
            wide_own,
            outer_g,
            small_own[:, 5],
            small_own[:, 6],
            small_own[:, 7],
        )

    return body


def solution(mesh):
    tokens = P(None, "fsdp", "seq", None)
    matrix, vector = P(None, AXES, None), P(None, AXES)
    in_specs = (tokens, P(None, "fsdp", None), tokens) + (matrix,) * 4 + (vector,) * 5
    in_specs += (matrix, vector, matrix, vector, vector, vector)
    out_specs = (tokens, tokens) + (matrix,) * 4 + (vector,) * 5
    out_specs += (matrix, vector, matrix, vector, vector, vector)
    sizes = (mesh.shape["fsdp"], mesh.shape["seq"])
    body = staged_body if sizes == (8, 4) else plain_body(*sizes)
    return jax.shard_map(body, mesh=mesh, in_specs=in_specs, out_specs=out_specs, check_vma=False)
```

```python
import collections
import math

import jax
import jax.numpy as jnp
from jax import lax
from jax.experimental import pallas as pl
from jax.experimental.pallas import tpu as pltpu
from jax.sharding import PartitionSpec as P

D = 1024
FF = 4096
HEAD_DIM = 64
HEADS = D // HEAD_DIM
SEQ_LEN = 1024
NDOC = 16
epsilon = 1e-05
AXES = ("fsdp", "seq")
f32 = jnp.float32
bf16 = jnp.bfloat16


def dot(left, right):
    return jnp.dot(left, right, preferred_element_type=f32)


def contract_rows(left, right):
    return lax.dot_general(left, right, (((0,), (0,)), ((), ())), preferred_element_type=f32)


def contract_cols(left, right):
    return lax.dot_general(left, right, (((1,), (1,)), ((), ())), preferred_element_type=f32)


SMALL_COST = pl.CostEstimate(flops=1024, bytes_accessed=1024, transcendentals=0)


def tie(value, *others):
    return lax.optimization_barrier((value, others))[0]


def pairs(move):
    out = []
    for i in range(32):
        z, y, x, c = i // 8, i // 4 % 2, i // 2 % 2, i % 2
        z, y, x, c = move(z, y, x, c)
        out.append((i, z * 8 + y * 4 + x * 2 + c))
    return out


TO_CORE = pairs(lambda z, y, x, c: (z, y, x, 1 - c))
TO_X = pairs(lambda z, y, x, c: (z, y, 1 - x, c))
TO_Y = pairs(lambda z, y, x, c: (z, 1 - y, x, c))
TO_FAR = pairs(lambda z, y, x, c: (z, y if c == 0 else 1 - y, 1 - x if c == 0 else x, c))
TO_NEAR = pairs(lambda z, y, x, c: (z, 1 - y if c == 0 else y, x if c == 0 else 1 - x, c))
TO_ODD = pairs(lambda z, y, x, c: (z ^ 1, y, x, c))
TO_PAIR = pairs(lambda z, y, x, c: (z ^ 2, y, x, c))
TO_Z = [pairs(lambda z, y, x, c, k=k: ((z + k) % 4, y, x, c)) for k in range(4)]


def send(value, to):
    return lax.ppermute(value, AXES, to)


def coordinates():
    fsdp, seq = lax.axis_index("fsdp"), lax.axis_index("seq")
    return jnp.stack([fsdp // 2, fsdp % 2, seq // 2, seq % 2]).astype(jnp.int32)


def place(coords, pieces, shapes, moves):
    count = len(moves(0, 0, 0, 0, None, None))

    total = len(pieces)

    def kernel(coords_ref, *refs):
        sources, targets = refs[:total], refs[total : total + len(shapes)]
        buffers, in_sems, out_sems = refs[total + len(shapes) : -2], refs[-2], refs[-1]
        loads = [
            pltpu.make_async_copy(source, buffer, in_sems.at[n])
            for n, (source, buffer) in enumerate(zip(sources, buffers))
        ]
        for load in loads:
            load.start()
        todo = moves(coords_ref[0], coords_ref[1], coords_ref[2], coords_ref[3], buffers, targets)
        stores = [
            (n, pltpu.make_async_copy(view, target, out_sems.at[k]))
            for k, (n, view, target) in enumerate(todo)
        ]
        for piece, load in enumerate(loads):
            load.wait()
            for n, store in stores:
                if n == piece:
                    store.start()
        for _, store in stores:
            store.wait()

    return pl.pallas_call(
        kernel,
        in_specs=[pl.BlockSpec(memory_space=pltpu.SMEM)]
        + [pl.BlockSpec(memory_space=pl.ANY)] * len(pieces),
        out_specs=[pl.BlockSpec(memory_space=pltpu.HBM)] * len(shapes),
        out_shape=[pltpu.HBM(shape, bf16) for shape in shapes],
        scratch_shapes=[pltpu.VMEM(p.shape, bf16) for p in pieces]
        + [pltpu.SemaphoreType.DMA((total,)), pltpu.SemaphoreType.DMA((count,))],
        compiler_params=pltpu.CompilerParams(vmem_limit_bytes=40 << 20),
        cost_estimate=SMALL_COST,
    )(coords, *pieces)


def in_hbm(value):
    return pltpu.with_memory_space_constraint(value, pltpu.HBM)


def pick(value, index, axis):
    return lax.dynamic_index_in_dim(value, index, axis, keepdims=False)


def by_place(own, other, at, axis):
    return jnp.where(at == 0, jnp.stack([own, other], axis), jnp.stack([other, own], axis))


def phase(values, *units, settle=()):
    values, flights, ended = lax.optimization_barrier(
        (values, [u.flight for u in units], [u.flight for u in settle])
    )
    for unit, flight in zip(settle, ended):
        unit.flight = flight
    nexts = [u.local(flight) for u, flight in zip(units, flights)]
    values, sends = lax.optimization_barrier((values, [[v for v, _ in n] for n in nexts]))
    for unit, arrays, targets in zip(units, sends, nexts):
        unit.flight = [send(array, to) for array, (_, to) in zip(arrays, targets)]
    return values


class GatherUnit:
    def __init__(self, coords, pack, shapes, parts):
        self.coords, self.pack, self.shapes, self.parts = coords, pack, shapes, parts
        self.flight, self.step = [pack], 0

    def local(self, got):
        self.step += 1
        if self.step == 1:
            self.kept = got[0][None]
            return [(self.kept, TO_PAIR)]
        if self.step < 5:
            self.kept = jnp.concatenate([got[0], self.kept])
            sends = [(self.kept, (TO_ODD, TO_NEAR, TO_FAR)[self.step - 2])]
            return sends + [(self.kept, TO_CORE)] * (self.step == 4)
        self.kept = [self.kept, *got]
        return [(got[0], TO_CORE)]

    def result(self):
        width = self.pack.shape[1]

        def by_block(z, y, x, c, src, dst):
            out = []
            for n in range(4):
                core, far = (c if n < 2 else 1 - c), n % 2
                for near in (1, 0):
                    y2 = y ^ jnp.where(core == 0, near, far)
                    x2 = x ^ jnp.where(core == 0, far, near)
                    for odd in (1, 0):
                        for pair in (1, 0):
                            block = 4 * (1 - near) + 2 * (1 - odd) + 1 - pair
                            for lo, hi, target, column in self.parts:
                                view = None
                                if dst:
                                    spans = (slice(0, hi - lo), slice(column * width, (column + 1) * width))
                                    view = dst[target].at[(z ^ odd ^ (2 * pair), y2, x2, core) + spans]
                                out.append((n, src and src[n].at[block, lo:hi], view))
            return out

        return place(
            self.coords, self.kept + self.flight, [(4, 2, 2, 2) + shape for shape in self.shapes], by_block
        )


FAR_FIRST = (TO_FAR, TO_NEAR, TO_ODD, TO_PAIR)
Z_FIRST = (TO_ODD, TO_PAIR, TO_FAR, TO_NEAR)


class SumUnit:
    def __init__(self, parts, route=FAR_FIRST):
        self.flight, self.step, self.route = list(parts), 0, route

    def local(self, got):
        self.step += 1
        if self.step == 1:
            leaving, self.kept = got
        elif self.step < 5:
            half = self.kept.shape[0] // 2
            add = lambda a, b: a.astype(f32) + b.astype(f32)
            leaving = add(self.kept[:half], got[0][:half]).astype(bf16)
            self.kept = add(self.kept[half:], got[0][half:])
            if self.step < 4:
                self.kept = self.kept.astype(bf16)
        else:
            self.kept = self.kept + got[0].astype(f32)
            return []
        return [(leaving, self.route[self.step - 1])]


Sums = collections.namedtuple("Sums", "o i a")


def block_order(coords, z_first=False):
    z, y, x, c = coords[0], coords[1], coords[2], coords[3]
    order = []
    for core in (c, 1 - c):
        for first in range(4):
            for second in range(4):
                across, along = (second, first) if z_first else (first, second)
                far, near = 1 - across // 2, 1 - across % 2
                odd, pair = 1 - along // 2, 1 - along % 2
                y2 = y ^ jnp.where(core == 0, near, far)
                x2 = x ^ jnp.where(core == 0, far, near)
                order.append((z ^ odd ^ (2 * pair)) * 8 + y2 * 4 + x2 * 2 + core)
    return jnp.stack(order).astype(jnp.int32)


def order_matrices(order):
    block = D // 32
    wanted = (order[:, None] * block + lax.iota(jnp.int32, block)[None, :]).reshape(2, D // 2, 1)
    columns = lax.broadcasted_iota(jnp.int32, (2, D // 2, D), 2)
    chosen = (columns == wanted).astype(bf16)
    return chosen[0], chosen[1]


def selected(matrices, *arrays):
    count = len(arrays)

    def kernel(mine, theirs, *refs):
        for n in range(count):
            rows = refs[n][...]
            refs[count + 2 * n][...] = nt_dot(mine[...], rows).astype(bf16)
            refs[count + 2 * n + 1][...] = nt_dot(theirs[...], rows).astype(bf16)

    out = jax.ShapeDtypeStruct((D // 2, arrays[0].shape[0]), bf16)
    outs = pl.pallas_call(
        kernel,
        out_shape=[out] * (2 * count),
        compiler_params=pltpu.CompilerParams(vmem_limit_bytes=48 << 20),
        cost_estimate=SMALL_COST,
    )(*matrices, *arrays)
    return [tuple(outs[2 * n : 2 * n + 2]) for n in range(count)]


def weight_terms(*pairs_of, first=0, tile=1024):
    rows, tokens = pairs_of[0][0][0].shape
    counts = [pair[2] // tile for pair in pairs_of]
    starts = [sum(counts[:n]) for n in range(len(counts))]
    columns, half = sum(counts) * tile, rows // 2

    def kernel(*refs):
        leaving, kept = refs[-2:]
        j = pl.program_id(0)
        for n, (start, count) in enumerate(zip(starts, counts)):

            @pl.when((j >= start) & (j < start + count))
            def _(a1=refs[4 * n], a2=refs[4 * n + 1], b1=refs[4 * n + 2], b2=refs[4 * n + 3]):
                total = jnp.dot(a1[...], b1[...], preferred_element_type=f32)
                total = total + jnp.dot(a2[...], b2[...], preferred_element_type=f32)
                leaving[...] = total[:half].astype(bf16)
                kept[...] = total[half:].astype(bf16)

    in_specs, args = [], []
    for (left, right, _), start, count in zip(pairs_of, starts, counts):
        whole = pl.BlockSpec((rows, tokens), lambda j: (0, 0))
        cut = pl.BlockSpec((tokens, tile), lambda j, s=start, n=count: (0, jnp.clip(j - s, 0, n - 1) + first // tile))
        in_specs += [whole, whole, cut, cut]
        args += [*map(in_hbm, left), *right]
    out = jax.ShapeDtypeStruct((half, columns), bf16)
    return pl.pallas_call(
        kernel,
        grid=(columns // tile,),
        in_specs=in_specs,
        out_specs=[pl.BlockSpec((half, tile), lambda j: (0, j))] * 2,
        out_shape=[out, out],
        compiler_params=pltpu.CompilerParams(vmem_limit_bytes=48 << 20),
        cost_estimate=SMALL_COST,
    )(*args)


def wide_terms_of(order, left, right):
    tokens, width = left[0].shape
    block = width // 32
    columns = right[0].shape[1]

    def kernel(order_ref, *refs):
        a1, a2, (b1, b2, leaving, kept) = refs[:2], refs[2:4], refs[4:]
        one = (
            lax.broadcasted_iota(jnp.int32, (block, block), 0) == lax.broadcasted_iota(jnp.int32, (block, block), 1)
        ).astype(bf16)
        turned = lambda refs: jnp.concatenate([nt_dot(one, r[...]).astype(bf16) for r in refs], axis=0)
        total = jnp.dot(turned(a1), b1[...], preferred_element_type=f32)
        total = (total + jnp.dot(turned(a2), b2[...], preferred_element_type=f32)).astype(bf16)

        @pl.when(pl.program_id(0) < 4)
        def _():
            leaving[...] = total

        @pl.when(pl.program_id(0) >= 4)
        def _():
            kept[...] = total

    cut = lambda n: pl.BlockSpec((tokens, block), lambda j, order: (0, order[2 * j + n]))
    whole = pl.BlockSpec((tokens, columns), lambda j, order: (0, 0))
    out = jax.ShapeDtypeStruct((width // 4, columns), bf16)
    return pl.pallas_call(
        kernel,
        grid_spec=pltpu.PrefetchScalarGridSpec(
            num_scalar_prefetch=1,
            grid=(8,),
            in_specs=[cut(0), cut(1), cut(0), cut(1), whole, whole],
            out_specs=[
                pl.BlockSpec((2 * block, columns), lambda j, order: (jnp.minimum(j, 3), 0)),
                pl.BlockSpec((2 * block, columns), lambda j, order: (jnp.maximum(j - 4, 0), 0)),
            ],
        ),
        out_shape=[out, out],
        compiler_params=pltpu.CompilerParams(vmem_limit_bytes=48 << 20),
        cost_estimate=SMALL_COST,
    )(order, *map(in_hbm, (left[0], left[0], left[1], left[1])), *right)


def wide_terms_split(order, order_z, left, right):
    tokens, width = left[0].shape
    block, columns = width // 32, right[0].shape[1] // 2
    same = order_z[:16, None] == order[None, :16]
    places = jnp.sum(jnp.where(same, lax.broadcasted_iota(jnp.int32, (16, 16), 1), 0), axis=1)

    def kernel(order_ref, place_ref, a1, a2, b1, b2, first, second):
        one = (
            lax.broadcasted_iota(jnp.int32, (block, block), 0) == lax.broadcasted_iota(jnp.int32, (block, block), 1)
        ).astype(bf16)
        total = sum(
            jnp.dot(nt_dot(one, a[...]).astype(bf16), b[...], preferred_element_type=f32)
            for a, b in ((a1, b1), (a2, b2))
        ).astype(bf16)
        first[0, 0] = total[:, :columns]
        second[0, 0] = total[:, columns:]

    cut = pl.BlockSpec((tokens, block), lambda j, order, place: (0, order[j]))
    whole = pl.BlockSpec((tokens, 2 * columns), lambda j, order, place: (0, 0))
    out = jax.ShapeDtypeStruct((2, 8, block, columns), bf16)
    outs = pl.pallas_call(
        kernel,
        grid_spec=pltpu.PrefetchScalarGridSpec(
            num_scalar_prefetch=2,
            grid=(16,),
            in_specs=[cut, cut, whole, whole],
            out_specs=[
                pl.BlockSpec((1, 1, block, columns), lambda j, order, place: (j // 8, j % 8, 0, 0)),
                pl.BlockSpec((1, 1, block, columns), lambda j, order, place: (place[j] // 8, place[j] % 8, 0, 0)),
            ],
        ),
        out_shape=[out, out],
        compiler_params=pltpu.CompilerParams(vmem_limit_bytes=48 << 20),
        cost_estimate=SMALL_COST,
    )(order_z, places, *map(in_hbm, left), *right)
    return [[part.reshape(8 * block, columns) for part in (o[0], o[1])] for o in outs]


BLOCK = 256
WINDOWS = (2 * BLOCK, 3 * BLOCK)
PAIR = 2 * HEAD_DIM


def query_starts(s):
    edge = (s // 2) ^ (s % 2)
    return edge * BLOCK, (1 - edge) * BLOCK


def window_starts(s):
    return (s % 2) * (2 * BLOCK), (1 - s % 2) * BLOCK


def nt_dot(left, right):
    return lax.dot_general(left, right, (((1,), (1,)), ((), ())), preferred_element_type=f32)


def only_head(value, head, axis):
    lane = lax.broadcasted_iota(jnp.int32, value.shape, axis)
    return jnp.where((lane < HEAD_DIM) if head == 0 else (lane >= HEAD_DIM), value, jnp.zeros_like(value))


def in_order(s, mine, other, scratch):
    for n, ref in ((0, mine), (1, other)):
        for slot in range(2):
            scratch[pl.ds((s ^ (n + 2 * slot)) * BLOCK, BLOCK), :] = ref[slot * BLOCK : (slot + 1) * BLOCK, :]


def attention_views(s):
    rows = [pl.ds(pl.multiple_of(start, BLOCK), BLOCK) for start in query_starts(s)]
    windows = [pl.ds(pl.multiple_of(start, BLOCK), width) for start, width in zip(window_starts(s), WINDOWS)]
    spans = [slice(h * HEAD_DIM, (h + 1) * HEAD_DIM) for h in range(2)]
    return rows, windows, spans, [slice(n * BLOCK, (n + 1) * BLOCK) for n in range(2)]


def attend_forward_kernel(
    s_ref, q_ref, km_ref, ko_ref, vm_ref, vo_ref, edge_ref, inner_ref, mixed_ref, total_ref, keys, values
):
    s = s_ref[0]
    in_order(s, km_ref, ko_ref, keys)
    in_order(s, vm_ref, vo_ref, values)
    rows, windows, spans, kinds = attention_views(s)
    biases = (edge_ref, inner_ref)
    scores = []
    for n in range(2):
        q = q_ref[rows[n], :] * jnp.asarray(HEAD_DIM**-0.5, bf16)
        k = keys[windows[n], :]
        scores += [nt_dot(k, only_head(q, head, 1)) for head in range(2)]
    raised, totals = [], []
    for m in range(4):
        n, head = divmod(m, 2)
        biased = scores[m] + biases[n][...]
        top = jnp.max(biased, axis=0, keepdims=True)
        up = jnp.exp(biased - top)
        totals.append(jnp.sum(up, axis=0, keepdims=True))
        total_ref[0, head : head + 1, kinds[n]] = top + jnp.log(totals[m])
        raised.append(up.astype(bf16))
    for n in range(2):
        v_t = values[windows[n], :].T
        halves = [
            jnp.dot(v_t[spans[h]], raised[2 * n + h], preferred_element_type=f32) / totals[2 * n + h]
            for h in range(2)
        ]
        mixed_ref[rows[n], :] = jnp.concatenate(halves, axis=0).T.astype(bf16)


def attend_backward_kernel(
    s_ref, q_ref, km_ref, ko_ref, vm_ref, vo_ref, edge_ref, inner_ref, mixed_ref, total_ref, grad_ref,
    dq_ref, mine_ref, sent_ref, keys, values, key_sum, value_sum,
):
    s = s_ref[0]
    in_order(s, km_ref, ko_ref, keys)
    in_order(s, vm_ref, vo_ref, values)
    key_sum[...] = jnp.zeros_like(key_sum)
    value_sum[...] = jnp.zeros_like(value_sum)
    rows, windows, spans, kinds = attention_views(s)
    biases = (edge_ref, inner_ref)
    scores, share_grads, queries, grads, inner = [], [], [], [], []
    for n in range(2):
        q = q_ref[rows[n], :] * jnp.asarray(HEAD_DIM**-0.5, bf16)
        g = grad_ref[rows[n], :]
        along = (g.astype(f32) * mixed_ref[rows[n], :].astype(f32)).T
        k, v = keys[windows[n], :], values[windows[n], :]
        for head in range(2):
            queries.append(only_head(q, head, 1))
            grads.append(only_head(g, head, 1))
            inner.append(jnp.sum(along[spans[head]], axis=0, keepdims=True))
            scores.append(nt_dot(k, queries[-1]))
            share_grads.append(nt_dot(v, grads[-1]))
    shares_low, grads_low = [], []
    for m in range(4):
        n, head = divmod(m, 2)
        shares = jnp.exp(scores[m] + biases[n][...] - total_ref[0, head : head + 1, kinds[n]])
        shares_low.append(shares.astype(bf16))
        grads_low.append((shares * (share_grads[m] - inner[m])).astype(bf16))
    both = lambda values, n, axis: jnp.concatenate(values[2 * n : 2 * n + 2], axis=axis)
    for n in range(2):
        k_t = keys[windows[n], :].T
        query_grads = [jnp.dot(k_t[spans[h]], grads_low[2 * n + h], preferred_element_type=f32) for h in range(2)]
        dq_ref[rows[n], :] = (jnp.concatenate(query_grads, axis=0).T * HEAD_DIM**-0.5).astype(bf16)
        key_sum[windows[n], :] += jnp.dot(both(grads_low, n, 1), both(queries, n, 0), preferred_element_type=f32)
        value_sum[windows[n], :] += jnp.dot(both(shares_low, n, 1), both(grads, n, 0), preferred_element_type=f32)
    for slot in range(2):
        here = slice(slot * BLOCK, (slot + 1) * BLOCK)
        mine, other = pl.ds((s ^ (2 * slot)) * BLOCK, BLOCK), pl.ds((s ^ (1 + 2 * slot)) * BLOCK, BLOCK)
        for n, sums in ((0, key_sum), (1, value_sum)):
            mine_ref[n, here, :] = sums[mine, :]
            sent_ref[n, here, :] = sums[other, :].astype(bf16)


def call_attention(kernel, s, own, other, bias, kept, outs, scratch):
    pairs_count = D // PAIR
    third = lambda n: pl.BlockSpec((2 * BLOCK, PAIR), lambda h: (0, h + n * pairs_count))
    cut = third(0)
    double = pl.BlockSpec((2, 2 * BLOCK, PAIR), lambda h: (0, 0, h))
    per_pair = pl.BlockSpec((1, 2, 2 * BLOCK), lambda h: (h, 0, 0))
    whole = [pl.BlockSpec(b.shape, lambda h: (0, 0)) for b in bias]
    in_specs = [pl.BlockSpec(memory_space=pltpu.SMEM), third(0), third(1), third(1), third(2), third(2), *whole]
    args = [s, own, own, other, own, other, *bias]
    if kept:
        in_specs += [cut, per_pair, cut]
        args += kept
    shapes, specs = [], []
    for kind, spec in outs:
        shapes.append(
            {
                0: jax.ShapeDtypeStruct((2 * BLOCK, D), kind),
                1: jax.ShapeDtypeStruct((pairs_count, 2, 2 * BLOCK), kind),
                2: jax.ShapeDtypeStruct((2, 2 * BLOCK, D), kind),
            }[spec]
        )
        specs.append((cut, per_pair, double)[spec])
    return pl.pallas_call(
        kernel,
        grid=(pairs_count,),
        in_specs=in_specs,
        out_specs=specs,
        out_shape=shapes,
        scratch_shapes=scratch,
        compiler_params=pltpu.CompilerParams(vmem_limit_bytes=48 << 20),
        cost_estimate=SMALL_COST,
    )(*args)


def attend_forward_blocks(s, own, other, bias):
    scratch = [pltpu.VMEM((SEQ_LEN, PAIR), bf16)] * 2
    return call_attention(attend_forward_kernel, s, own, other, bias, (), ((bf16, 0), (f32, 1)), scratch)


def attend_backward_blocks(s, own, other, bias, mixed, totals, grads):
    scratch = [pltpu.VMEM((SEQ_LEN, PAIR), bf16)] * 2 + [pltpu.VMEM((SEQ_LEN, PAIR), f32)] * 2
    outs = ((bf16, 0), (f32, 2), (bf16, 2))
    kept = (mixed, totals, grads)
    return call_attention(attend_backward_kernel, s, own, other, bias, kept, outs, scratch)


def window_bias(s, ids):
    out = []
    for start, width, first in zip(window_starts(s), WINDOWS, query_starts(s)):
        keys = lax.dynamic_slice_in_dim(ids, start, width)
        block = s ^ (2 * (first // BLOCK))
        queries = lax.dynamic_slice_in_dim(ids, block * BLOCK, BLOCK)
        out.append(jnp.where(keys[:, None] == queries[None, :], 0.0, -1e30).astype(f32))
    return tuple(out)


def norm_forward(total):
    center = jnp.mean(total, axis=-1, keepdims=True)
    centered = total - center
    spread = jnp.mean(centered * centered, axis=-1, keepdims=True)
    scale = lax.rsqrt(spread + epsilon)
    return centered * scale, scale


def norm_backward(total, gain, upstream):
    unit, scale = norm_forward(total)
    lifted = upstream * gain
    grad = scale * (
        lifted
        - jnp.mean(lifted, axis=-1, keepdims=True)
        - unit * jnp.mean(lifted * unit, axis=-1, keepdims=True)
    )
    return grad, jnp.sum(upstream * unit, axis=0), jnp.sum(upstream, axis=0)


def column_sum(values):
    return jnp.sum(values.astype(f32), axis=0)


def heads_of(rows):
    return rows.reshape(rows.shape[0], HEADS, HEAD_DIM)


def masked_scores(queries, keys, allowed):
    scores = jnp.einsum("qhd,khd->hqk", queries, keys, preferred_element_type=f32)
    return jnp.where(allowed[None], scores * HEAD_DIM ** (-0.5), -1e30)


def attend_forward(queries, keys, values, allowed):
    scores = masked_scores(heads_of(queries), heads_of(keys), allowed)
    top_score = jnp.max(scores, axis=2, keepdims=True)
    raised = jnp.exp(scores - top_score)
    totals = jnp.sum(raised, axis=2, keepdims=True)
    shares = (raised / totals).astype(bf16)
    mixed = jnp.einsum("hqk,khd->qhd", shares, heads_of(values), preferred_element_type=f32)
    return mixed.astype(bf16).reshape(queries.shape), top_score + jnp.log(totals)


def attend_backward(queries, keys, values, allowed, log_total, grads):
    queries, keys, values, grads = map(heads_of, (queries, keys, values, grads))
    scale = HEAD_DIM ** (-0.5)
    shares = jnp.exp(masked_scores(queries, keys, allowed) - log_total)
    share_grads = jnp.einsum("qhd,khd->hqk", grads, values, preferred_element_type=f32)
    inner_sums = jnp.sum(shares * share_grads, axis=2, keepdims=True)
    score_grads = (shares * (share_grads - inner_sums)).astype(bf16)
    query_grad = jnp.einsum("hqk,khd->qhd", score_grads, keys, preferred_element_type=f32) * scale
    key_grad = jnp.einsum("hqk,qhd->khd", score_grads, queries, preferred_element_type=f32) * scale
    value_grad = jnp.einsum(
        "hqk,qhd->khd", shares.astype(bf16), grads, preferred_element_type=f32
    )
    flat = lambda a: a.reshape(a.shape[0], D)
    return flat(query_grad).astype(bf16), flat(key_grad), flat(value_grad)


def product(rows, weight, tile, finish, outs, by_column=(), tiles=(), transposed=False, sums=0):
    tokens, depth = rows.shape
    width = weight.shape[0 if transposed else 1]

    def kernel(rows_ref, weight_ref, *refs):
        total = (nt_dot if transposed else lambda a, b: jnp.dot(a, b, preferred_element_type=f32))(
            rows_ref[...], weight_ref[...]
        )
        inputs = [r[...] for r in refs[: len(by_column) + len(tiles)]]
        for ref, value in zip(refs[len(inputs) :], finish(total, *inputs)):
            ref[...] = value.astype(ref.dtype)

    cut = pl.BlockSpec((tokens, tile), lambda j: (0, j))
    if transposed:
        weight_spec = pl.BlockSpec((tile, depth), lambda j: (j, 0))
    else:
        weight_spec = pl.BlockSpec((depth, tile), lambda j: (0, j))
    return pl.pallas_call(
        kernel,
        grid=(width // tile,),
        in_specs=[pl.BlockSpec((tokens, depth), lambda j: (0, 0)), weight_spec]
        + [pl.BlockSpec((1, tile), lambda j: (0, j))] * len(by_column)
        + [cut] * len(tiles),
        out_specs=[cut] * len(outs) + [pl.BlockSpec((1, tile), lambda j: (0, j))] * sums,
        out_shape=[jax.ShapeDtypeStruct((tokens, width), kind) for kind in outs]
        + [jax.ShapeDtypeStruct((1, width), f32)] * sums,
        compiler_params=pltpu.CompilerParams(vmem_limit_bytes=48 << 20),
        cost_estimate=SMALL_COST,
    )(rows, in_hbm(weight), *[v.reshape(1, width) for v in by_column], *tiles)


def gelu_parts(total, bias):
    inner = total + bias
    below = 0.5 * (1.0 + lax.erf(inner * (0.5**0.5)))
    slope = below + inner * jnp.exp(-0.5 * inner * inner) * (2 * math.pi) ** -0.5
    return inner * below, slope


def mixed_norm(mixed, weight, stream, bias, gain, shift):
    tokens, width = stream.shape
    tile = 256

    def kernel(mixed_ref, weight_ref, stream_ref, bias_ref, gain_ref, shift_ref, sum_ref, first_ref, low_ref):
        total = jnp.dot(mixed_ref[...], weight_ref[...], preferred_element_type=f32)
        total = stream_ref[...] + (total + bias_ref[...])
        first = norm_forward(total)[0] * gain_ref[...] + shift_ref[...]
        sum_ref[...] = total
        first_ref[...] = first
        low_ref[...] = first.astype(bf16)

    cut = pl.BlockSpec((tile, width), lambda j: (j, 0))
    vector = pl.BlockSpec((1, width), lambda j: (0, 0))
    out = jax.ShapeDtypeStruct((tokens, width), f32)
    return pl.pallas_call(
        kernel,
        grid=(tokens // tile,),
        in_specs=[cut, pl.BlockSpec(weight.shape, lambda j: (0, 0)), cut, vector, vector, vector],
        out_specs=[cut] * 3,
        out_shape=[out, out, jax.ShapeDtypeStruct((tokens, width), bf16)],
        compiler_params=pltpu.CompilerParams(vmem_limit_bytes=48 << 20),
        cost_estimate=SMALL_COST,
    )(mixed, in_hbm(weight), stream, *[v.reshape(1, width) for v in (bias, gain, shift)])


def norm_backward_rows(total, gain, upstream):
    tokens, width = total.shape
    tile = 128

    def kernel(total_ref, gain_ref, up_ref, grad_ref, low_ref, sums_ref):
        unit, scale = norm_forward(total_ref[...])
        up = up_ref[...]
        lifted = up * gain_ref[...]
        grad = scale * (
            lifted
            - jnp.mean(lifted, axis=-1, keepdims=True)
            - unit * jnp.mean(lifted * unit, axis=-1, keepdims=True)
        )
        low = grad.astype(bf16)
        grad_ref[...] = grad
        low_ref[...] = low

        @pl.when(pl.program_id(0) == 0)
        def _():
            sums_ref[...] = jnp.zeros_like(sums_ref)

        for n, value in enumerate((up * unit, up, low.astype(f32))):
            sums_ref[n : n + 1, :] += jnp.sum(value, axis=0, keepdims=True)

    cut = pl.BlockSpec((tile, width), lambda j: (j, 0))
    out = jax.ShapeDtypeStruct((tokens, width), f32)
    return pl.pallas_call(
        kernel,
        grid=(tokens // tile,),
        in_specs=[cut, pl.BlockSpec((1, width), lambda j: (0, 0)), cut],
        out_specs=[cut, cut, pl.BlockSpec((8, width), lambda j: (0, 0))],
        out_shape=[out, jax.ShapeDtypeStruct((tokens, width), bf16), jax.ShapeDtypeStruct((8, width), f32)],
        compiler_params=pltpu.CompilerParams(vmem_limit_bytes=32 << 20),
        cost_estimate=SMALL_COST,
    )(total, gain.reshape(1, width), upstream)


def merged(query_low, own, back):
    tokens = query_low.shape[0]
    tile = D // 2

    def kernel(query_ref, own_ref, back_ref, low_ref, sum_ref):
        def put(low):
            low_ref[...] = low
            sum_ref[...] = jnp.sum(low.astype(f32), axis=0, keepdims=True)

        @pl.when(pl.program_id(0) < 2)
        def _():
            put(query_ref[...])

        @pl.when(pl.program_id(0) >= 2)
        def _():
            put((own_ref[0] + back_ref[0].astype(f32)).astype(bf16))

    part = pl.BlockSpec((1, tokens, tile), lambda j: (jnp.maximum(j - 2, 0) // 2, 0, jnp.maximum(j - 2, 0) % 2))
    return pl.pallas_call(
        kernel,
        grid=(6,),
        in_specs=[pl.BlockSpec((tokens, tile), lambda j: (0, jnp.minimum(j, 1))), part, part],
        out_specs=[pl.BlockSpec((tokens, tile), lambda j: (0, j)), pl.BlockSpec((1, tile), lambda j: (0, j))],
        out_shape=[jax.ShapeDtypeStruct((tokens, 3 * D), bf16), jax.ShapeDtypeStruct((1, 3 * D), f32)],
        compiler_params=pltpu.CompilerParams(vmem_limit_bytes=32 << 20),
        cost_estimate=SMALL_COST,
    )(query_low, own, back)


SMALL = 8


def staged_body(tokens, doc_lengths, cotangent, *shards):
    (
        query_weight,
        key_weight,
        value_weight,
        mix_weight,
        query_bias,
        value_bias,
        mix_bias,
        first_gain,
        first_shift,
        inner_weight,
        inner_bias,
        outer_weight,
        outer_bias,
        second_gain,
        second_shift,
    ) = shards
    layer_count = query_weight.shape[0]
    devices = 32
    length = SEQ_LEN // 4
    rows_held, inner_held = D // devices, FF // devices
    seq = lax.axis_index("seq")
    row = seq // 2
    coords = coordinates()
    z, y, x, c = coords[0], coords[1], coords[2], coords[3]
    place_of = seq.reshape(1).astype(jnp.int32)

    def split_rows(both):
        both = both.reshape(2, length, D)
        return pick(both, row, 0), pick(both, 1 - row, 0)

    token_kept, token_left = split_rows(tokens)
    upstream_kept, upstream_left = split_rows(cotangent)

    def unit_a(layer):
        r = rows_held
        parts = [w[layer] for w in (query_weight, key_weight, value_weight)]
        rows, outs = [(r * n, r * (n + 1), 0, n) for n in range(3)], [(r, 3 * D)]
        if layer:
            parts, rows, outs = parts + [mix_weight[layer]], rows + [(3 * r, 4 * r, 1, 0)], outs + [(r, D)]
        return GatherUnit(coords, jnp.concatenate(parts), outs, rows)

    def unit_i(layer):
        r, inner = rows_held, inner_weight[layer]
        parts = [inner[:, D * n : D * (n + 1)] for n in range(4)]
        rows, outs = [(r * n, r * (n + 1), 0, n) for n in range(4)], [(r, FF)]
        if not layer:
            parts, rows, outs = parts + [mix_weight[layer]], rows + [(4 * r, 5 * r, 1, 0)], outs + [(r, D)]
        return GatherUnit(coords, jnp.concatenate(parts), outs, rows)

    def unit_o(layer):
        return GatherUnit(coords, outer_weight[layer], [(inner_held, D)], [(0, inner_held, 0, 0)])

    units = [[make(layer) for make in (unit_a, unit_i, unit_o)] for layer in range(layer_count)]

    small_vectors = (
        query_bias,
        value_bias,
        mix_bias,
        first_gain,
        first_shift,
        outer_bias,
        second_gain,
        second_shift,
    )
    vector_count = SMALL * layer_count
    small_held = vector_count * rows_held
    mine = jnp.concatenate(
        [jnp.concatenate([v[layer] for v in small_vectors]) for layer in range(layer_count)]
        + [inner_bias.reshape(-1)]
    )
    held = mine.shape[0]
    padded = jnp.pad(mine, (0, 1024 - held)).reshape(8, 128)

    u = [unit for layer_units in units for unit in layer_units]
    padded = phase(padded, u[0])
    token_got = send(token_left, TO_X)
    every = jnp.roll(jnp.stack([padded] + [send(padded, TO_Z[4 - k]) for k in (1, 2, 3)]), z, axis=0)

    lengths = pick(doc_lengths.reshape(2, NDOC), row, 0)
    places = lax.iota(jnp.int32, SEQ_LEN)
    segment = jnp.sum((places[:, None] >= jnp.cumsum(lengths)[None, :]).astype(jnp.int32), axis=1)
    bias = window_bias(seq, jnp.where(segment == NDOC - 1, NDOC + places, segment))
    order, order_z = block_order(coords), block_order(coords, True)
    matrices = order_matrices(order)

    token_got, every = phase((token_got, every), u[0], u[1])
    every, upstream_left = lax.optimization_barrier((every, upstream_left))
    upstream_got = send(upstream_left, TO_X)
    every = by_place(every, send(every, TO_Y), y, 1)
    every, bias, upstream_got = phase((every, bias, upstream_got), u[0], settle=[u[1]])
    every = by_place(every, send(every, TO_X), x, 2)
    every, matrices = phase((every, matrices), u[0], u[1])
    every = by_place(every, send(every, TO_CORE), c, 3)
    every = every.reshape(devices, 1024)[:, :held].astype(f32)
    small_all = (
        every[:, :small_held]
        .reshape(devices, vector_count, rows_held)
        .transpose(1, 0, 2)
        .reshape(layer_count, SMALL, D)
    )
    wide_all = (
        every[:, small_held:]
        .reshape(devices, layer_count, inner_held)
        .transpose(1, 0, 2)
        .reshape(layer_count, FF)
    )
    stream = jnp.concatenate([token_kept, token_got]).astype(f32)
    stream, small_all, wide_all = phase((stream, small_all, wide_all), u[0], u[1], u[2])
    saved, active_gots = [], []
    for layer in range(layer_count):
        a_unit, i_unit, o_unit = units[layer]
        next_a, next_i, next_o = units[layer + 1] if layer + 1 < layer_count else (None,) * 3
        q_bias, v_bias, m_bias, gain1, shift1, o_bias, gain2, shift2 = [small_all[layer, n] for n in range(SMALL)]
        w_three, *w_rest = a_unit.result()
        w_three = w_three.reshape(D, 3 * D)
        stream_low = stream.astype(bf16)
        three_bias = jnp.concatenate([q_bias, jnp.zeros_like(q_bias), v_bias])
        (three,) = product(stream_low, w_three, 1024, lambda total, b: (total + b,), (bf16,), (three_bias,))
        if next_a:
            three = phase(three, i_unit, o_unit, next_a)
        else:
            three = phase(three, i_unit, settle=[o_unit])
        three_got = send(three, TO_CORE)
        (left_stream,) = selected(matrices, tie(stream_low, three))
        three, left_stream = lax.optimization_barrier((three, left_stream))
        left_stream = (left_stream[0], send(left_stream[1], TO_CORE))
        mixed, totals = attend_forward_blocks(place_of, three, three_got, bias)
        if next_a:
            mixed, totals, left_stream = phase(
                (mixed, totals, left_stream), i_unit, o_unit, next_a, next_i
            )
        else:
            mixed, totals, left_stream, active_gots = phase(
                (mixed, totals, left_stream, active_gots), i_unit, o_unit
            )
        w_inner, *w_more = i_unit.result()
        (w_mix,) = w_rest + w_more
        w_inner, w_mix = w_inner.reshape(D, FF), w_mix.reshape(D, D)
        first_sum, first, first_low = mixed_norm(mixed, w_mix, stream, m_bias, gain1, shift1)
        if next_a:
            first_low = phase(first_low, o_unit, next_a, next_i)
        else:
            first_low = phase(first_low, o_unit)
        left_mix, left_first = selected(matrices, mixed, first_low)
        first_low, left_mix, left_first = lax.optimization_barrier((first_low, left_mix, left_first))
        left_mix, left_first = [(m, send(t, TO_CORE)) for m, t in (left_mix, left_first)]
        active, slope = product(first_low, w_inner, 1024, gelu_parts, (bf16, bf16), (wide_all[layer],))
        if next_a:
            active, slope, left_mix, left_first = phase(
                (active, slope, left_mix, left_first), o_unit, next_a, next_o, settle=[next_i]
            )
        else:
            active, slope, left_mix, left_first = phase((active, slope, left_mix, left_first), o_unit)
        (w_outer,) = o_unit.result()
        active_got = send(tie(active, w_outer), TO_CORE)
        w_outer = w_outer.reshape(FF, D)
        (second_sum,) = product(
            active, w_outer, 256, lambda total, b, f: (f + (total + b),), (f32,), (o_bias,), (first,)
        )
        if not next_a:
            second_sum, active_got = lax.optimization_barrier((second_sum, active_got))
        active_gots.append(active_got)
        stream = norm_forward(second_sum)[0] * gain2 + shift2
        if next_a:
            stream = phase(stream, next_a, next_i, next_o)
        saved.append(
            (
                (w_three, w_mix, w_inner, w_outer, gain1, gain2),
                (three, three_got, totals, mixed),
                (first_sum, slope, second_sum),
                (left_stream, left_mix, left_first, active),
            )
        )

    def both_rows(kept, got):
        got = got.astype(f32)
        return jnp.where(row == 0, jnp.stack([kept, got]), jnp.stack([got, kept])).reshape(tokens.shape)

    output = stream
    output_got = send(output[length:].astype(bf16), TO_X)

    upstream = jnp.concatenate([upstream_kept, upstream_got]).astype(f32)
    small_grads, wide_grads = [None] * layer_count, [None] * layer_count
    sums = [None] * layer_count
    before = None
    for layer in reversed(range(layer_count)):
        weights, kept, rest, lefts = saved[layer]
        w_three, w_mix, w_inner, w_outer, gain1, gain2 = weights
        three, three_got, totals, mixed = kept
        first_sum, slope, second_sum = rest
        left_stream, left_mix, left_first, active = lefts
        left_active = (active, active_gots[layer])

        def with_sum(total, slopes):
            low = (total * slopes).astype(bf16)
            return low, jnp.sum(low.astype(f32), axis=0, keepdims=True)

        second_grad, second_low, second_sums = norm_backward_rows(second_sum, gain2, upstream)
        second_got = send(second_low, TO_CORE)
        inner_low, inner_sum = product(
            second_low, w_outer, 1024, with_sum, (bf16,), (), (slope,), transposed=True, sums=1
        )
        if before:
            inner_low, second_got = phase((inner_low, second_got), before.o[0], before.i, before.a)
        else:
            inner_low, second_got = lax.optimization_barrier((inner_low, second_got))
        inner_got = send(inner_low, TO_CORE)
        second_pair = (second_low, second_got)
        if before:
            by_z, by_far = wide_terms_split(order, order_z, left_active, second_pair)
            o_sums = (SumUnit(by_z, Z_FIRST), SumUnit(by_far))
            second_grad, inner_low, inner_got = phase(
                (second_grad, inner_low, inner_got), *o_sums, before.a, before.i, settle=before.o
            )
        else:
            o_sums = (SumUnit(wide_terms_of(order, left_active, second_pair)),)
            second_grad, inner_low, inner_got, output_got = phase(
                (second_grad, inner_low, inner_got, output_got), *o_sums
            )
        (first_grad,) = product(
            inner_low, w_inner, 256, lambda total, g: (g + total,), (f32,), (), (second_grad,), transposed=True
        )
        first_sum_grad, branch_low, first_sums = norm_backward_rows(first_sum, gain1, first_grad)
        branch_got = send(branch_low, TO_CORE)
        (mixed_grad,) = product(branch_low, w_mix, 512, lambda total: (total,), (bf16,), transposed=True)
        i_sum = SumUnit(weight_terms((left_first, tie((inner_low, inner_got), mixed_grad), FF)))
        if before:
            mixed_grad = phase(mixed_grad, i_sum, *o_sums, before.a, settle=[before.i])
        else:
            mixed_grad = phase(mixed_grad, i_sum, settle=o_sums)
        query_low, own_grads, sent_grads = attend_backward_blocks(
            place_of, in_hbm(three), in_hbm(three_got), bias, in_hbm(mixed), in_hbm(totals), mixed_grad
        )
        grads_back = send(sent_grads, TO_CORE)
        if before:
            query_low, own_grads = phase((query_low, own_grads), i_sum, *o_sums, before.a)
        else:
            query_low, own_grads = phase((query_low, own_grads), *o_sums, settle=[i_sum])
        low, low_sums = merged(query_low, own_grads, grads_back)
        low, branch_got = lax.optimization_barrier((low, branch_got))
        low_got = send(low, TO_CORE)
        if layer:
            (upstream,) = product(
                low, w_three, 256, lambda total, g: (g + total,), (f32,), (), (first_sum_grad,), transposed=True
            )
            mix_pair = (left_mix, (branch_low, branch_got), D)
            a_sum = SumUnit(weight_terms((left_stream, tie((low, low_got), upstream), 3 * D), mix_pair))
        else:
            mix_pair = (left_mix, (branch_low, branch_got), D)
            a_sum = SumUnit(weight_terms((left_stream, (low, low_got), 3 * D), mix_pair))
            low, low_sums = phase((low, low_sums), a_sum, settle=[i_sum, before.a] if before else [i_sum])
            (upstream,) = product(
                low, w_three, 256, lambda total, g: (g + total,), (f32,), (), (first_sum_grad,), transposed=True
            )
        small_grads[layer] = jnp.stack(
            [
                low_sums[0, :D],
                low_sums[0, 2 * D :],
                first_sums[2],
                first_sums[0],
                first_sums[1],
                second_sums[2],
                second_sums[0],
                second_sums[1],
            ]
        )
        wide_grads[layer] = inner_sum[0]
        if layer:
            upstream, small_grads[layer] = phase((upstream, small_grads[layer]), *o_sums, i_sum, settle=[a_sum])
        sums[layer] = before = Sums(o_sums, i_sum, a_sum)

    small_terms = (
        jnp.stack(small_grads)
        .reshape(vector_count, devices, rows_held)
        .transpose(1, 0, 2)
        .reshape(devices, small_held)
    )
    wide_terms = (
        jnp.stack(wide_grads)
        .reshape(layer_count, devices, inner_held)
        .transpose(1, 0, 2)
        .reshape(devices, layer_count * inner_held)
    )
    terms = jnp.pad(jnp.concatenate([small_terms, wide_terms], axis=1), ((0, 0), (0, 1024 - held)))
    chosen = (order[:, None] == lax.iota(jnp.int32, devices)[None, :]).astype(f32)
    terms = jnp.dot(chosen, terms, precision=lax.Precision.HIGHEST).reshape(2, 128, 128)
    terms = (terms[0] + send(terms[1].astype(bf16), TO_CORE).astype(f32)).astype(bf16)
    small_sum = SumUnit((terms[:64], terms[64:]))

    phase((), small_sum)
    last = sums[0]
    done = [unit for layer in range(1, layer_count) for unit in (*sums[layer].o, sums[layer].i, sums[layer].a)]
    upstream, output_got = phase((upstream, output_got), last.a, last.i, *last.o, small_sum, *done)
    token_left = upstream[length:].astype(bf16)
    upstream, token_left = phase((upstream, token_left), last.a, last.i, *last.o, small_sum)
    token_back = send(token_left, TO_X)
    upstream, token_back = phase((upstream, token_back), last.a, last.i, small_sum)
    phase((), last.a, small_sum)
    own_terms = small_sum.kept.reshape(-1)[:held]
    small_own = own_terms[:small_held].reshape(layer_count, SMALL, rows_held)
    wide_own = own_terms[small_held:].reshape(layer_count, inner_held)
    for layer in range(layer_count):
        for unit in (*sums[layer].o, sums[layer].i, sums[layer].a):
            while unit.step < 5:
                phase((), unit)
    o_all = jnp.stack([jnp.concatenate([unit.kept for unit in group.o], axis=1) for group in sums])
    i_all, a_all = [jnp.stack([group[n].kept for group in sums]) for n in (1, 2)]
    return (
        both_rows(output[:length], output_got),
        both_rows(upstream[:length], token_back),
        a_all[:, :, :D],
        a_all[:, :, D : 2 * D],
        a_all[:, :, 2 * D : 3 * D],
        a_all[:, :, 3 * D :],
        small_own[:, 0],
        small_own[:, 1],
        small_own[:, 2],
        small_own[:, 3],
        small_own[:, 4],
        i_all,
        wide_own,
        o_all,
        small_own[:, 5],
        small_own[:, 6],
        small_own[:, 7],
    )


def plain_body(fsdp_size, seq_size):
    half = seq_size // 2
    device_count = fsdp_size * seq_size
    across = [(i, (i + half) % seq_size) for i in range(seq_size)]
    groups = [[m * half + j for j in range(half)] for m in range(2)]
    length = SEQ_LEN // seq_size

    def gather_siblings(rows):
        return lax.all_gather(rows, "seq", axis_index_groups=groups)

    def scatter_siblings(own_order):
        return lax.psum_scatter(own_order, "seq", axis_index_groups=groups)

    def body(tokens, doc_lengths, cotangent, *shards):
        (
            query_weight,
            key_weight,
            value_weight,
            mix_weight,
            query_bias,
            value_bias,
            mix_bias,
            first_gain,
            first_shift,
            inner_weight,
            inner_bias,
            outer_weight,
            outer_bias,
            second_gain,
            second_shift,
        ) = shards
        layer_count = query_weight.shape[0]
        seq = lax.axis_index("seq")
        row = seq // half
        rows_held = D // device_count
        inner_held = FF // device_count

        def vector_rows(small, wide):
            return jnp.concatenate(
                [jnp.concatenate([v[layer] for v in small]) for layer in range(layer_count)]
                + [wide.reshape(-1)]
            )

        small_vectors = (
            query_bias,
            value_bias,
            mix_bias,
            first_gain,
            first_shift,
            outer_bias,
            second_gain,
            second_shift,
        )
        vector_count = len(small_vectors) * layer_count
        mine = vector_rows(small_vectors, inner_bias)
        held = mine.shape[0]
        every = lax.all_gather(mine, AXES)
        every = every.astype(f32)
        small_held = vector_count * rows_held
        small_all = (
            every[:, :small_held]
            .reshape(device_count, vector_count, rows_held)
            .transpose(1, 0, 2)
            .reshape(layer_count, len(small_vectors), D)
        )
        wide_all = (
            every[:, small_held:]
            .reshape(device_count, layer_count, inner_held)
            .transpose(1, 0, 2)
            .reshape(layer_count, FF)
        )

        def whole_weights(layer):
            weights = (query_weight, key_weight, value_weight, mix_weight, inner_weight, outer_weight)
            return [lax.all_gather(w[layer], AXES, axis=0, tiled=True) for w in weights]

        def own_row(both_rows):
            kept = pick(both_rows, row, 0)
            return jnp.concatenate(
                [kept, lax.ppermute(pick(both_rows, 1 - row, 0), "seq", across)]
            )

        def both_rows(values):
            kept = values[:length]
            other = lax.ppermute(values[length:].astype(bf16), "seq", across).astype(f32)
            return jnp.where(row == 0, jnp.stack([kept, other]), jnp.stack([other, kept]))

        stream_start = own_row(tokens.reshape(2, length, D))
        upstream_start = own_row(cotangent.reshape(2, length, D))

        lengths = pick(doc_lengths.reshape(2, NDOC), row, 0)
        bounds = jnp.cumsum(lengths)
        within = lax.iota(jnp.int32, length)

        def positions(s):
            return jnp.concatenate([s * length + within, (s + half) % seq_size * length + within])

        def segments(places):
            return jnp.sum((places[:, None] >= bounds[None, :]).astype(jnp.int32), axis=1)

        query_places = positions(seq)
        key_places = jnp.concatenate([positions(row * half + j) for j in range(half)])
        query_segment, key_segment = segments(query_places), segments(key_places)
        allowed = (
            (query_segment[:, None] == key_segment[None, :]) & (key_segment[None, :] != NDOC - 1)
        ) | (query_places[:, None] == key_places[None, :])

        stream = stream_start.astype(f32)
        saved = []
        for layer in range(layer_count):
            q_bias, v_bias, m_bias, gain1, shift1, o_bias, gain2, shift2 = [
                small_all[layer, n] for n in range(len(small_vectors))
            ]
            w_query, w_key, w_value, w_mix, w_inner, w_outer = whole_weights(layer)
            stream_low = stream.astype(bf16)
            queries = (dot(stream_low, w_query) + q_bias).astype(bf16)
            key_rows = dot(stream_low, w_key).astype(bf16)
            values = (dot(stream_low, w_value) + v_bias).astype(bf16)
            all_keys = gather_siblings(key_rows).reshape(SEQ_LEN, D)
            all_values = gather_siblings(values).reshape(SEQ_LEN, D)
            mixed, log_total = attend_forward(queries, all_keys, all_values, allowed)
            first_sum = stream + (dot(mixed, w_mix) + m_bias)
            first = norm_forward(first_sum)[0] * gain1 + shift1
            first_low = first.astype(bf16)
            inner = dot(first_low, w_inner) + wide_all[layer]
            below = 0.5 * (1.0 + lax.erf(inner * (0.5**0.5)))
            active = (inner * below).astype(bf16)
            slope = (below + inner * jnp.exp(-0.5 * inner * inner) * (2 * math.pi) ** -0.5).astype(
                bf16
            )
            second_sum = first + (dot(active, w_outer) + o_bias)
            stream = norm_forward(second_sum)[0] * gain2 + shift2
            saved.append(
                (
                    (w_query, w_key, w_value, w_mix, w_inner, w_outer, gain1, gain2),
                    (stream_low, queries, all_keys, all_values, log_total, mixed),
                    (first_sum, first_low, slope, active, second_sum),
                )
            )
        activations = both_rows(stream)

        upstream = upstream_start.astype(f32)
        small_grads = [None] * layer_count
        wide_grads = [None] * layer_count
        results = [None] * layer_count

        def reduced(grads):
            return [lax.psum_scatter(g, AXES, scatter_dimension=0, tiled=True) for g in grads]

        for layer in reversed(range(layer_count)):
            (w_query, w_key, w_value, w_mix, w_inner, w_outer, gain1, gain2), kept, rest = saved[layer]
            stream_low, queries, all_keys, all_values, log_total, mixed = kept
            first_sum, first_low, slope, active, second_sum = rest
            second_grad, gain2_grad, shift2_grad = norm_backward(second_sum, gain2, upstream)
            second_low = second_grad.astype(bf16)
            (outer_grad,) = reduced([contract_rows(active, second_low)])
            inner_low = (contract_cols(second_low, w_outer) * slope).astype(bf16)
            (inner_grad,) = reduced([contract_rows(first_low, inner_low)])
            first_grad = second_grad + contract_cols(inner_low, w_inner)
            first_sum_grad, gain1_grad, shift1_grad = norm_backward(first_sum, gain1, first_grad)
            branch_low = first_sum_grad.astype(bf16)
            mix_terms = contract_rows(mixed, branch_low)
            mixed_grad = contract_cols(branch_low, w_mix).astype(bf16)
            query_low, key_terms, value_terms = attend_backward(
                queries, all_keys, all_values, allowed, log_total, mixed_grad
            )
            n = 2 * length
            key_low = scatter_siblings(key_terms.reshape(half, n, D)).astype(bf16)
            value_low = scatter_siblings(value_terms.reshape(half, n, D)).astype(bf16)
            value_grad, mix_grad = reduced([contract_rows(stream_low, value_low), mix_terms])
            query_grad, key_grad = reduced(
                [contract_rows(stream_low, query_low), contract_rows(stream_low, key_low)]
            )
            upstream = (
                first_sum_grad
                + contract_cols(query_low, w_query)
                + contract_cols(key_low, w_key)
                + contract_cols(value_low, w_value)
            )
            small_grads[layer] = jnp.stack(
                [
                    column_sum(query_low),
                    column_sum(value_low),
                    column_sum(branch_low),
                    gain1_grad,
                    shift1_grad,
                    column_sum(second_low),
                    gain2_grad,
                    shift2_grad,
                ]
            )
            wide_grads[layer] = column_sum(inner_low)
            results[layer] = (query_grad, key_grad, value_grad, mix_grad, inner_grad, outer_grad)
        token_grad = both_rows(upstream)

        small_terms = (
            jnp.stack(small_grads)
            .reshape(vector_count, device_count, rows_held)
            .transpose(1, 0, 2)
            .reshape(device_count, small_held)
        )
        wide_terms = (
            jnp.stack(wide_grads)
            .reshape(layer_count, device_count, inner_held)
            .transpose(1, 0, 2)
            .reshape(device_count, layer_count * inner_held)
        )
        terms = jnp.concatenate([small_terms, wide_terms], axis=1)
        own_terms = lax.psum_scatter(terms, AXES, scatter_dimension=0, tiled=False)
        small_own = own_terms[:small_held].reshape(layer_count, len(small_vectors), rows_held)
        wide_own = own_terms[small_held:].reshape(layer_count, inner_held)
        query_g, key_g, value_g, mix_g, inner_g, outer_g = [
            jnp.stack([results[layer][n] for layer in range(layer_count)]) for n in range(6)
        ]
        return (
            activations.reshape(tokens.shape),
            token_grad.reshape(tokens.shape),
            query_g,
            key_g,
            value_g,
            mix_g,
            small_own[:, 0],
            small_own[:, 1],
            small_own[:, 2],
            small_own[:, 3],
            small_own[:, 4],
            inner_g,
            wide_own,
            outer_g,
            small_own[:, 5],
            small_own[:, 6],
            small_own[:, 7],
        )

    return body


def solution(mesh):
    tokens = P(None, "fsdp", "seq", None)
    matrix, vector = P(None, AXES, None), P(None, AXES)
    in_specs = (tokens, P(None, "fsdp", None), tokens) + (matrix,) * 4 + (vector,) * 5
    in_specs += (matrix, vector, matrix, vector, vector, vector)
    out_specs = (tokens, tokens) + (matrix,) * 4 + (vector,) * 5
    out_specs += (matrix, vector, matrix, vector, vector, vector)
    sizes = (mesh.shape["fsdp"], mesh.shape["seq"])
    body = staged_body if sizes == (8, 4) else plain_body(*sizes)
    return jax.shard_map(body, mesh=mesh, in_specs=in_specs, out_specs=out_specs, check_vma=False)
```

```python
import collections
import math

import jax
import jax.numpy as jnp
from jax import lax
from jax.experimental import pallas as pl
from jax.experimental.pallas import tpu as pltpu
from jax.sharding import PartitionSpec as P

D = 1024
FF = 4096
HEAD_DIM = 64
HEADS = D // HEAD_DIM
SEQ_LEN = 1024
NDOC = 16
epsilon = 1e-05
AXES = ("fsdp", "seq")
f32 = jnp.float32
bf16 = jnp.bfloat16


def dot(left, right):
    return jnp.dot(left, right, preferred_element_type=f32)


def contract_rows(left, right):
    return lax.dot_general(left, right, (((0,), (0,)), ((), ())), preferred_element_type=f32)


def contract_cols(left, right):
    return lax.dot_general(left, right, (((1,), (1,)), ((), ())), preferred_element_type=f32)


SMALL_COST = pl.CostEstimate(flops=1024, bytes_accessed=1024, transcendentals=0)


def tie(value, *others):
    return lax.optimization_barrier((value, others))[0]


def pairs(move):
    out = []
    for i in range(32):
        z, y, x, c = i // 8, i // 4 % 2, i // 2 % 2, i % 2
        z, y, x, c = move(z, y, x, c)
        out.append((i, z * 8 + y * 4 + x * 2 + c))
    return out


TO_CORE = pairs(lambda z, y, x, c: (z, y, x, 1 - c))
TO_X = pairs(lambda z, y, x, c: (z, y, 1 - x, c))
TO_Y = pairs(lambda z, y, x, c: (z, 1 - y, x, c))
TO_FAR = pairs(lambda z, y, x, c: (z, y if c == 0 else 1 - y, 1 - x if c == 0 else x, c))
TO_NEAR = pairs(lambda z, y, x, c: (z, 1 - y if c == 0 else y, x if c == 0 else 1 - x, c))
TO_ODD = pairs(lambda z, y, x, c: (z ^ 1, y, x, c))
TO_PAIR = pairs(lambda z, y, x, c: (z ^ 2, y, x, c))
TO_Z = [pairs(lambda z, y, x, c, k=k: ((z + k) % 4, y, x, c)) for k in range(4)]


def send(value, to):
    return lax.ppermute(value, AXES, to)


def coordinates():
    fsdp, seq = lax.axis_index("fsdp"), lax.axis_index("seq")
    return jnp.stack([fsdp // 2, fsdp % 2, seq // 2, seq % 2]).astype(jnp.int32)


def place(coords, pieces, shapes, moves):
    count = len(moves(0, 0, 0, 0, None, None))

    total = len(pieces)

    def kernel(coords_ref, *refs):
        sources, targets = refs[:total], refs[total : total + len(shapes)]
        buffers, in_sems, out_sems = refs[total + len(shapes) : -2], refs[-2], refs[-1]
        loads = [
            pltpu.make_async_copy(source, buffer, in_sems.at[n])
            for n, (source, buffer) in enumerate(zip(sources, buffers))
        ]
        for load in loads:
            load.start()
        todo = moves(coords_ref[0], coords_ref[1], coords_ref[2], coords_ref[3], buffers, targets)
        stores = [
            (n, pltpu.make_async_copy(view, target, out_sems.at[k]))
            for k, (n, view, target) in enumerate(todo)
        ]
        for piece, load in enumerate(loads):
            load.wait()
            for n, store in stores:
                if n == piece:
                    store.start()
        for _, store in stores:
            store.wait()

    return pl.pallas_call(
        kernel,
        in_specs=[pl.BlockSpec(memory_space=pltpu.SMEM)]
        + [pl.BlockSpec(memory_space=pl.ANY)] * len(pieces),
        out_specs=[pl.BlockSpec(memory_space=pltpu.HBM)] * len(shapes),
        out_shape=[pltpu.HBM(shape, bf16) for shape in shapes],
        scratch_shapes=[pltpu.VMEM(p.shape, bf16) for p in pieces]
        + [pltpu.SemaphoreType.DMA((total,)), pltpu.SemaphoreType.DMA((count,))],
        compiler_params=pltpu.CompilerParams(vmem_limit_bytes=40 << 20),
        cost_estimate=SMALL_COST,
    )(coords, *pieces)


def in_hbm(value):
    return pltpu.with_memory_space_constraint(value, pltpu.HBM)


def pick(value, index, axis):
    return lax.dynamic_index_in_dim(value, index, axis, keepdims=False)


def by_place(own, other, at, axis):
    return jnp.where(at == 0, jnp.stack([own, other], axis), jnp.stack([other, own], axis))


def phase(values, *units, settle=()):
    values, flights, ended = lax.optimization_barrier(
        (values, [u.flight for u in units], [u.flight for u in settle])
    )
    for unit, flight in zip(settle, ended):
        unit.flight = flight
    nexts = [u.local(flight) for u, flight in zip(units, flights)]
    values, sends = lax.optimization_barrier((values, [[v for v, _ in n] for n in nexts]))
    for unit, arrays, targets in zip(units, sends, nexts):
        unit.flight = [send(array, to) for array, (_, to) in zip(arrays, targets)]
    return values


class GatherUnit:
    def __init__(self, coords, pack, shapes, parts):
        self.coords, self.pack, self.shapes, self.parts = coords, pack, shapes, parts
        self.flight, self.step = [pack], 0

    def local(self, got):
        self.step += 1
        if self.step == 1:
            self.kept = got[0][None]
            return [(self.kept, TO_PAIR)]
        if self.step < 5:
            self.kept = jnp.concatenate([got[0], self.kept])
            sends = [(self.kept, (TO_ODD, TO_NEAR, TO_FAR)[self.step - 2])]
            return sends + [(self.kept, TO_CORE)] * (self.step == 4)
        self.kept = [self.kept, *got]
        return [(got[0], TO_CORE)]

    def result(self):
        width = self.pack.shape[1]

        def by_block(z, y, x, c, src, dst):
            out = []
            for n in range(4):
                core, far = (c if n < 2 else 1 - c), n % 2
                for near in (1, 0):
                    y2 = y ^ jnp.where(core == 0, near, far)
                    x2 = x ^ jnp.where(core == 0, far, near)
                    for odd in (1, 0):
                        for pair in (1, 0):
                            block = 4 * (1 - near) + 2 * (1 - odd) + 1 - pair
                            for lo, hi, target, column in self.parts:
                                view = None
                                if dst:
                                    spans = (slice(0, hi - lo), slice(column * width, (column + 1) * width))
                                    view = dst[target].at[(z ^ odd ^ (2 * pair), y2, x2, core) + spans]
                                out.append((n, src and src[n].at[block, lo:hi], view))
            return out

        return place(
            self.coords, self.kept + self.flight, [(4, 2, 2, 2) + shape for shape in self.shapes], by_block
        )


FAR_FIRST = (TO_FAR, TO_NEAR, TO_ODD, TO_PAIR)
Z_FIRST = (TO_ODD, TO_PAIR, TO_FAR, TO_NEAR)


class SumUnit:
    def __init__(self, parts, route=FAR_FIRST):
        self.flight, self.step, self.route = list(parts), 0, route

    def local(self, got):
        self.step += 1
        if self.step == 1:
            leaving, self.kept = got
        elif self.step < 5:
            half = self.kept.shape[0] // 2
            add = lambda a, b: a.astype(f32) + b.astype(f32)
            leaving = add(self.kept[:half], got[0][:half]).astype(bf16)
            self.kept = add(self.kept[half:], got[0][half:])
            if self.step < 4:
                self.kept = self.kept.astype(bf16)
        else:
            self.kept = self.kept + got[0].astype(f32)
            return []
        return [(leaving, self.route[self.step - 1])]


Sums = collections.namedtuple("Sums", "o i a")


def block_order(coords, z_first=False):
    z, y, x, c = coords[0], coords[1], coords[2], coords[3]
    order = []
    for core in (c, 1 - c):
        for first in range(4):
            for second in range(4):
                across, along = (second, first) if z_first else (first, second)
                far, near = 1 - across // 2, 1 - across % 2
                odd, pair = 1 - along // 2, 1 - along % 2
                y2 = y ^ jnp.where(core == 0, near, far)
                x2 = x ^ jnp.where(core == 0, far, near)
                order.append((z ^ odd ^ (2 * pair)) * 8 + y2 * 4 + x2 * 2 + core)
    return jnp.stack(order).astype(jnp.int32)


def order_matrices(order):
    block = D // 32
    wanted = (order[:, None] * block + lax.iota(jnp.int32, block)[None, :]).reshape(2, D // 2, 1)
    columns = lax.broadcasted_iota(jnp.int32, (2, D // 2, D), 2)
    chosen = (columns == wanted).astype(bf16)
    return chosen[0], chosen[1]


def selected(matrices, *arrays):
    count = len(arrays)

    def kernel(mine, theirs, *refs):
        for n in range(count):
            rows = refs[n][...]
            refs[count + 2 * n][...] = nt_dot(mine[...], rows).astype(bf16)
            refs[count + 2 * n + 1][...] = nt_dot(theirs[...], rows).astype(bf16)

    out = jax.ShapeDtypeStruct((D // 2, arrays[0].shape[0]), bf16)
    outs = pl.pallas_call(
        kernel,
        out_shape=[out] * (2 * count),
        compiler_params=pltpu.CompilerParams(vmem_limit_bytes=48 << 20),
        cost_estimate=SMALL_COST,
    )(*matrices, *arrays)
    return [tuple(outs[2 * n : 2 * n + 2]) for n in range(count)]


def weight_terms(*pairs_of, first=0, tile=1024):
    rows, tokens = pairs_of[0][0][0].shape
    counts = [pair[2] // tile for pair in pairs_of]
    starts = [sum(counts[:n]) for n in range(len(counts))]
    columns, half = sum(counts) * tile, rows // 2

    def kernel(*refs):
        leaving, kept = refs[-2:]
        j = pl.program_id(0)
        for n, (start, count) in enumerate(zip(starts, counts)):

            @pl.when((j >= start) & (j < start + count))
            def _(a1=refs[4 * n], a2=refs[4 * n + 1], b1=refs[4 * n + 2], b2=refs[4 * n + 3]):
                total = jnp.dot(a1[...], b1[...], preferred_element_type=f32)
                total = total + jnp.dot(a2[...], b2[...], preferred_element_type=f32)
                leaving[...] = total[:half].astype(bf16)
                kept[...] = total[half:].astype(bf16)

    in_specs, args = [], []
    for (left, right, _), start, count in zip(pairs_of, starts, counts):
        whole = pl.BlockSpec((rows, tokens), lambda j: (0, 0))
        cut = pl.BlockSpec((tokens, tile), lambda j, s=start, n=count: (0, jnp.clip(j - s, 0, n - 1) + first // tile))
        in_specs += [whole, whole, cut, cut]
        args += [*map(in_hbm, left), *right]
    out = jax.ShapeDtypeStruct((half, columns), bf16)
    return pl.pallas_call(
        kernel,
        grid=(columns // tile,),
        in_specs=in_specs,
        out_specs=[pl.BlockSpec((half, tile), lambda j: (0, j))] * 2,
        out_shape=[out, out],
        compiler_params=pltpu.CompilerParams(vmem_limit_bytes=48 << 20),
        cost_estimate=SMALL_COST,
    )(*args)


def wide_terms_of(order, left, right):
    tokens, width = left[0].shape
    block = width // 32
    columns = right[0].shape[1]

    def kernel(order_ref, *refs):
        a1, a2, (b1, b2, leaving, kept) = refs[:2], refs[2:4], refs[4:]
        one = (
            lax.broadcasted_iota(jnp.int32, (block, block), 0) == lax.broadcasted_iota(jnp.int32, (block, block), 1)
        ).astype(bf16)
        turned = lambda refs: jnp.concatenate([nt_dot(one, r[...]).astype(bf16) for r in refs], axis=0)
        total = jnp.dot(turned(a1), b1[...], preferred_element_type=f32)
        total = (total + jnp.dot(turned(a2), b2[...], preferred_element_type=f32)).astype(bf16)

        @pl.when(pl.program_id(0) < 4)
        def _():
            leaving[...] = total

        @pl.when(pl.program_id(0) >= 4)
        def _():
            kept[...] = total

    cut = lambda n: pl.BlockSpec((tokens, block), lambda j, order: (0, order[2 * j + n]))
    whole = pl.BlockSpec((tokens, columns), lambda j, order: (0, 0))
    out = jax.ShapeDtypeStruct((width // 4, columns), bf16)
    return pl.pallas_call(
        kernel,
        grid_spec=pltpu.PrefetchScalarGridSpec(
            num_scalar_prefetch=1,
            grid=(8,),
            in_specs=[cut(0), cut(1), cut(0), cut(1), whole, whole],
            out_specs=[
                pl.BlockSpec((2 * block, columns), lambda j, order: (jnp.minimum(j, 3), 0)),
                pl.BlockSpec((2 * block, columns), lambda j, order: (jnp.maximum(j - 4, 0), 0)),
            ],
        ),
        out_shape=[out, out],
        compiler_params=pltpu.CompilerParams(vmem_limit_bytes=48 << 20),
        cost_estimate=SMALL_COST,
    )(order, *map(in_hbm, (left[0], left[0], left[1], left[1])), *right)


def wide_terms_split(order, order_z, left, right):
    tokens, width = left[0].shape
    block, columns = width // 32, right[0].shape[1] // 2
    same = order_z[:16, None] == order[None, :16]
    places = jnp.sum(jnp.where(same, lax.broadcasted_iota(jnp.int32, (16, 16), 1), 0), axis=1)

    def kernel(order_ref, place_ref, a1, a2, b1, b2, first, second):
        one = (
            lax.broadcasted_iota(jnp.int32, (block, block), 0) == lax.broadcasted_iota(jnp.int32, (block, block), 1)
        ).astype(bf16)
        total = sum(
            jnp.dot(nt_dot(one, a[...]).astype(bf16), b[...], preferred_element_type=f32)
            for a, b in ((a1, b1), (a2, b2))
        ).astype(bf16)
        first[0, 0] = total[:, :columns]
        second[0, 0] = total[:, columns:]

    cut = pl.BlockSpec((tokens, block), lambda j, order, place: (0, order[j]))
    whole = pl.BlockSpec((tokens, 2 * columns), lambda j, order, place: (0, 0))
    out = jax.ShapeDtypeStruct((2, 8, block, columns), bf16)
    outs = pl.pallas_call(
        kernel,
        grid_spec=pltpu.PrefetchScalarGridSpec(
            num_scalar_prefetch=2,
            grid=(16,),
            in_specs=[cut, cut, whole, whole],
            out_specs=[
                pl.BlockSpec((1, 1, block, columns), lambda j, order, place: (j // 8, j % 8, 0, 0)),
                pl.BlockSpec((1, 1, block, columns), lambda j, order, place: (place[j] // 8, place[j] % 8, 0, 0)),
            ],
        ),
        out_shape=[out, out],
        compiler_params=pltpu.CompilerParams(vmem_limit_bytes=48 << 20),
        cost_estimate=SMALL_COST,
    )(order_z, places, *map(in_hbm, left), *right)
    return [[part.reshape(8 * block, columns) for part in (o[0], o[1])] for o in outs]


BLOCK = 256
WINDOWS = (2 * BLOCK, 3 * BLOCK)
PAIR = 2 * HEAD_DIM


def query_starts(s):
    edge = (s // 2) ^ (s % 2)
    return edge * BLOCK, (1 - edge) * BLOCK


def window_starts(s):
    return (s % 2) * (2 * BLOCK), (1 - s % 2) * BLOCK


def nt_dot(left, right):
    return lax.dot_general(left, right, (((1,), (1,)), ((), ())), preferred_element_type=f32)


def only_head(value, head, axis):
    lane = lax.broadcasted_iota(jnp.int32, value.shape, axis)
    return jnp.where((lane < HEAD_DIM) if head == 0 else (lane >= HEAD_DIM), value, jnp.zeros_like(value))


def in_order(s, mine, other, scratch):
    for n, ref in ((0, mine), (1, other)):
        for slot in range(2):
            scratch[pl.ds((s ^ (n + 2 * slot)) * BLOCK, BLOCK), :] = ref[slot * BLOCK : (slot + 1) * BLOCK, :]


def attention_views(s):
    rows = [pl.ds(pl.multiple_of(start, BLOCK), BLOCK) for start in query_starts(s)]
    windows = [pl.ds(pl.multiple_of(start, BLOCK), width) for start, width in zip(window_starts(s), WINDOWS)]
    spans = [slice(h * HEAD_DIM, (h + 1) * HEAD_DIM) for h in range(2)]
    return rows, windows, spans, [slice(n * BLOCK, (n + 1) * BLOCK) for n in range(2)]


def attend_forward_kernel(
    s_ref, q_ref, km_ref, ko_ref, vm_ref, vo_ref, edge_ref, inner_ref, mixed_ref, total_ref, keys, values
):
    s = s_ref[0]
    in_order(s, km_ref, ko_ref, keys)
    in_order(s, vm_ref, vo_ref, values)
    rows, windows, spans, kinds = attention_views(s)
    biases = (edge_ref, inner_ref)
    scores = []
    for n in range(2):
        q = q_ref[rows[n], :] * jnp.asarray(HEAD_DIM**-0.5, bf16)
        k = keys[windows[n], :]
        scores += [nt_dot(k, only_head(q, head, 1)) for head in range(2)]
    raised, totals = [], []
    for m in range(4):
        n, head = divmod(m, 2)
        biased = scores[m] + biases[n][...]
        top = jnp.max(biased, axis=0, keepdims=True)
        up = jnp.exp(biased - top)
        totals.append(jnp.sum(up, axis=0, keepdims=True))
        total_ref[0, head : head + 1, kinds[n]] = top + jnp.log(totals[m])
        raised.append(up.astype(bf16))
    for n in range(2):
        v_t = values[windows[n], :].T
        halves = [
            jnp.dot(v_t[spans[h]], raised[2 * n + h], preferred_element_type=f32) / totals[2 * n + h]
            for h in range(2)
        ]
        mixed_ref[rows[n], :] = jnp.concatenate(halves, axis=0).T.astype(bf16)


def attend_backward_kernel(
    s_ref, q_ref, km_ref, ko_ref, vm_ref, vo_ref, edge_ref, inner_ref, mixed_ref, total_ref, grad_ref,
    dq_ref, mine_ref, sent_ref, keys, values, key_sum, value_sum,
):
    s = s_ref[0]
    in_order(s, km_ref, ko_ref, keys)
    in_order(s, vm_ref, vo_ref, values)
    key_sum[...] = jnp.zeros_like(key_sum)
    value_sum[...] = jnp.zeros_like(value_sum)
    rows, windows, spans, kinds = attention_views(s)
    biases = (edge_ref, inner_ref)
    scores, share_grads, queries, grads, inner = [], [], [], [], []
    for n in range(2):
        q = q_ref[rows[n], :] * jnp.asarray(HEAD_DIM**-0.5, bf16)
        g = grad_ref[rows[n], :]
        along = (g.astype(f32) * mixed_ref[rows[n], :].astype(f32)).T
        k, v = keys[windows[n], :], values[windows[n], :]
        for head in range(2):
            queries.append(only_head(q, head, 1))
            grads.append(only_head(g, head, 1))
            inner.append(jnp.sum(along[spans[head]], axis=0, keepdims=True))
            scores.append(nt_dot(k, queries[-1]))
            share_grads.append(nt_dot(v, grads[-1]))
    shares_low, grads_low = [], []
    for m in range(4):
        n, head = divmod(m, 2)
        shares = jnp.exp(scores[m] + biases[n][...] - total_ref[0, head : head + 1, kinds[n]])
        shares_low.append(shares.astype(bf16))
        grads_low.append((shares * (share_grads[m] - inner[m])).astype(bf16))
    both = lambda values, n, axis: jnp.concatenate(values[2 * n : 2 * n + 2], axis=axis)
    for n in range(2):
        k_t = keys[windows[n], :].T
        query_grads = [jnp.dot(k_t[spans[h]], grads_low[2 * n + h], preferred_element_type=f32) for h in range(2)]
        dq_ref[rows[n], :] = (jnp.concatenate(query_grads, axis=0).T * HEAD_DIM**-0.5).astype(bf16)
        key_sum[windows[n], :] += jnp.dot(both(grads_low, n, 1), both(queries, n, 0), preferred_element_type=f32)
        value_sum[windows[n], :] += jnp.dot(both(shares_low, n, 1), both(grads, n, 0), preferred_element_type=f32)
    for slot in range(2):
        here = slice(slot * BLOCK, (slot + 1) * BLOCK)
        mine, other = pl.ds((s ^ (2 * slot)) * BLOCK, BLOCK), pl.ds((s ^ (1 + 2 * slot)) * BLOCK, BLOCK)
        for n, sums in ((0, key_sum), (1, value_sum)):
            mine_ref[n, here, :] = sums[mine, :]
            sent_ref[n, here, :] = sums[other, :].astype(bf16)


def call_attention(kernel, s, own, other, bias, kept, outs, scratch):
    pairs_count = D // PAIR
    third = lambda n: pl.BlockSpec((2 * BLOCK, PAIR), lambda h: (0, h + n * pairs_count))
    cut = third(0)
    double = pl.BlockSpec((2, 2 * BLOCK, PAIR), lambda h: (0, 0, h))
    per_pair = pl.BlockSpec((1, 2, 2 * BLOCK), lambda h: (h, 0, 0))
    whole = [pl.BlockSpec(b.shape, lambda h: (0, 0)) for b in bias]
    in_specs = [pl.BlockSpec(memory_space=pltpu.SMEM), third(0), third(1), third(1), third(2), third(2), *whole]
    args = [s, own, own, other, own, other, *bias]
    if kept:
        in_specs += [cut, per_pair, cut]
        args += kept
    shapes, specs = [], []
    for kind, spec in outs:
        shapes.append(
            {
                0: jax.ShapeDtypeStruct((2 * BLOCK, D), kind),
                1: jax.ShapeDtypeStruct((pairs_count, 2, 2 * BLOCK), kind),
                2: jax.ShapeDtypeStruct((2, 2 * BLOCK, D), kind),
            }[spec]
        )
        specs.append((cut, per_pair, double)[spec])
    return pl.pallas_call(
        kernel,
        grid=(pairs_count,),
        in_specs=in_specs,
        out_specs=specs,
        out_shape=shapes,
        scratch_shapes=scratch,
        compiler_params=pltpu.CompilerParams(vmem_limit_bytes=48 << 20),
        cost_estimate=SMALL_COST,
    )(*args)


def attend_forward_blocks(s, own, other, bias):
    scratch = [pltpu.VMEM((SEQ_LEN, PAIR), bf16)] * 2
    return call_attention(attend_forward_kernel, s, own, other, bias, (), ((bf16, 0), (f32, 1)), scratch)


def attend_backward_blocks(s, own, other, bias, mixed, totals, grads):
    scratch = [pltpu.VMEM((SEQ_LEN, PAIR), bf16)] * 2 + [pltpu.VMEM((SEQ_LEN, PAIR), f32)] * 2
    outs = ((bf16, 0), (f32, 2), (bf16, 2))
    kept = (mixed, totals, grads)
    return call_attention(attend_backward_kernel, s, own, other, bias, kept, outs, scratch)


def window_bias(s, ids):
    out = []
    for start, width, first in zip(window_starts(s), WINDOWS, query_starts(s)):
        keys = lax.dynamic_slice_in_dim(ids, start, width)
        block = s ^ (2 * (first // BLOCK))
        queries = lax.dynamic_slice_in_dim(ids, block * BLOCK, BLOCK)
        out.append(jnp.where(keys[:, None] == queries[None, :], 0.0, -1e30).astype(f32))
    return tuple(out)


def norm_forward(total):
    center = jnp.mean(total, axis=-1, keepdims=True)
    centered = total - center
    spread = jnp.mean(centered * centered, axis=-1, keepdims=True)
    scale = lax.rsqrt(spread + epsilon)
    return centered * scale, scale


def norm_backward(total, gain, upstream):
    unit, scale = norm_forward(total)
    lifted = upstream * gain
    grad = scale * (
        lifted
        - jnp.mean(lifted, axis=-1, keepdims=True)
        - unit * jnp.mean(lifted * unit, axis=-1, keepdims=True)
    )
    return grad, jnp.sum(upstream * unit, axis=0), jnp.sum(upstream, axis=0)


def column_sum(values):
    return jnp.sum(values.astype(f32), axis=0)


def heads_of(rows):
    return rows.reshape(rows.shape[0], HEADS, HEAD_DIM)


def masked_scores(queries, keys, allowed):
    scores = jnp.einsum("qhd,khd->hqk", queries, keys, preferred_element_type=f32)
    return jnp.where(allowed[None], scores * HEAD_DIM ** (-0.5), -1e30)


def attend_forward(queries, keys, values, allowed):
    scores = masked_scores(heads_of(queries), heads_of(keys), allowed)
    top_score = jnp.max(scores, axis=2, keepdims=True)
    raised = jnp.exp(scores - top_score)
    totals = jnp.sum(raised, axis=2, keepdims=True)
    shares = (raised / totals).astype(bf16)
    mixed = jnp.einsum("hqk,khd->qhd", shares, heads_of(values), preferred_element_type=f32)
    return mixed.astype(bf16).reshape(queries.shape), top_score + jnp.log(totals)


def attend_backward(queries, keys, values, allowed, log_total, grads):
    queries, keys, values, grads = map(heads_of, (queries, keys, values, grads))
    scale = HEAD_DIM ** (-0.5)
    shares = jnp.exp(masked_scores(queries, keys, allowed) - log_total)
    share_grads = jnp.einsum("qhd,khd->hqk", grads, values, preferred_element_type=f32)
    inner_sums = jnp.sum(shares * share_grads, axis=2, keepdims=True)
    score_grads = (shares * (share_grads - inner_sums)).astype(bf16)
    query_grad = jnp.einsum("hqk,khd->qhd", score_grads, keys, preferred_element_type=f32) * scale
    key_grad = jnp.einsum("hqk,qhd->khd", score_grads, queries, preferred_element_type=f32) * scale
    value_grad = jnp.einsum(
        "hqk,qhd->khd", shares.astype(bf16), grads, preferred_element_type=f32
    )
    flat = lambda a: a.reshape(a.shape[0], D)
    return flat(query_grad).astype(bf16), flat(key_grad), flat(value_grad)


def product(rows, weight, tile, finish, outs, by_column=(), tiles=(), transposed=False, sums=0):
    tokens, depth = rows.shape
    width = weight.shape[0 if transposed else 1]

    def kernel(rows_ref, weight_ref, *refs):
        total = (nt_dot if transposed else lambda a, b: jnp.dot(a, b, preferred_element_type=f32))(
            rows_ref[...], weight_ref[...]
        )
        inputs = [r[...] for r in refs[: len(by_column) + len(tiles)]]
        for ref, value in zip(refs[len(inputs) :], finish(total, *inputs)):
            ref[...] = value.astype(ref.dtype)

    cut = pl.BlockSpec((tokens, tile), lambda j: (0, j))
    if transposed:
        weight_spec = pl.BlockSpec((tile, depth), lambda j: (j, 0))
    else:
        weight_spec = pl.BlockSpec((depth, tile), lambda j: (0, j))
    return pl.pallas_call(
        kernel,
        grid=(width // tile,),
        in_specs=[pl.BlockSpec((tokens, depth), lambda j: (0, 0)), weight_spec]
        + [pl.BlockSpec((1, tile), lambda j: (0, j))] * len(by_column)
        + [cut] * len(tiles),
        out_specs=[cut] * len(outs) + [pl.BlockSpec((1, tile), lambda j: (0, j))] * sums,
        out_shape=[jax.ShapeDtypeStruct((tokens, width), kind) for kind in outs]
        + [jax.ShapeDtypeStruct((1, width), f32)] * sums,
        compiler_params=pltpu.CompilerParams(vmem_limit_bytes=48 << 20),
        cost_estimate=SMALL_COST,
    )(rows, in_hbm(weight), *[v.reshape(1, width) for v in by_column], *tiles)


def gelu_parts(total, bias):
    inner = total + bias
    below = 0.5 * (1.0 + lax.erf(inner * (0.5**0.5)))
    slope = below + inner * jnp.exp(-0.5 * inner * inner) * (2 * math.pi) ** -0.5
    return inner * below, slope


def mixed_norm(mixed, weight, stream, bias, gain, shift):
    tokens, width = stream.shape
    tile = 256

    def kernel(mixed_ref, weight_ref, stream_ref, bias_ref, gain_ref, shift_ref, sum_ref, first_ref, low_ref):
        total = jnp.dot(mixed_ref[...], weight_ref[...], preferred_element_type=f32)
        total = stream_ref[...] + (total + bias_ref[...])
        first = norm_forward(total)[0] * gain_ref[...] + shift_ref[...]
        sum_ref[...] = total
        first_ref[...] = first
        low_ref[...] = first.astype(bf16)

    cut = pl.BlockSpec((tile, width), lambda j: (j, 0))
    vector = pl.BlockSpec((1, width), lambda j: (0, 0))
    out = jax.ShapeDtypeStruct((tokens, width), f32)
    return pl.pallas_call(
        kernel,
        grid=(tokens // tile,),
        in_specs=[cut, pl.BlockSpec(weight.shape, lambda j: (0, 0)), cut, vector, vector, vector],
        out_specs=[cut] * 3,
        out_shape=[out, out, jax.ShapeDtypeStruct((tokens, width), bf16)],
        compiler_params=pltpu.CompilerParams(vmem_limit_bytes=48 << 20),
        cost_estimate=SMALL_COST,
    )(mixed, in_hbm(weight), stream, *[v.reshape(1, width) for v in (bias, gain, shift)])


def norm_backward_rows(total, gain, upstream):
    tokens, width = total.shape
    tile = 128

    def kernel(total_ref, gain_ref, up_ref, grad_ref, low_ref, sums_ref):
        unit, scale = norm_forward(total_ref[...])
        up = up_ref[...]
        lifted = up * gain_ref[...]
        grad = scale * (
            lifted
            - jnp.mean(lifted, axis=-1, keepdims=True)
            - unit * jnp.mean(lifted * unit, axis=-1, keepdims=True)
        )
        low = grad.astype(bf16)
        grad_ref[...] = grad
        low_ref[...] = low

        @pl.when(pl.program_id(0) == 0)
        def _():
            sums_ref[...] = jnp.zeros_like(sums_ref)

        for n, value in enumerate((up * unit, up, low.astype(f32))):
            sums_ref[n : n + 1, :] += jnp.sum(value, axis=0, keepdims=True)

    cut = pl.BlockSpec((tile, width), lambda j: (j, 0))
    out = jax.ShapeDtypeStruct((tokens, width), f32)
    return pl.pallas_call(
        kernel,
        grid=(tokens // tile,),
        in_specs=[cut, pl.BlockSpec((1, width), lambda j: (0, 0)), cut],
        out_specs=[cut, cut, pl.BlockSpec((8, width), lambda j: (0, 0))],
        out_shape=[out, jax.ShapeDtypeStruct((tokens, width), bf16), jax.ShapeDtypeStruct((8, width), f32)],
        compiler_params=pltpu.CompilerParams(vmem_limit_bytes=32 << 20),
        cost_estimate=SMALL_COST,
    )(total, gain.reshape(1, width), upstream)


def merged(query_low, own, back):
    tokens = query_low.shape[0]
    tile = D // 2

    def kernel(query_ref, own_ref, back_ref, low_ref, sum_ref):
        def put(low):
            low_ref[...] = low
            sum_ref[...] = jnp.sum(low.astype(f32), axis=0, keepdims=True)

        @pl.when(pl.program_id(0) < 2)
        def _():
            put(query_ref[...])

        @pl.when(pl.program_id(0) >= 2)
        def _():
            put((own_ref[0] + back_ref[0].astype(f32)).astype(bf16))

    part = pl.BlockSpec((1, tokens, tile), lambda j: (jnp.maximum(j - 2, 0) // 2, 0, jnp.maximum(j - 2, 0) % 2))
    return pl.pallas_call(
        kernel,
        grid=(6,),
        in_specs=[pl.BlockSpec((tokens, tile), lambda j: (0, jnp.minimum(j, 1))), part, part],
        out_specs=[pl.BlockSpec((tokens, tile), lambda j: (0, j)), pl.BlockSpec((1, tile), lambda j: (0, j))],
        out_shape=[jax.ShapeDtypeStruct((tokens, 3 * D), bf16), jax.ShapeDtypeStruct((1, 3 * D), f32)],
        compiler_params=pltpu.CompilerParams(vmem_limit_bytes=32 << 20),
        cost_estimate=SMALL_COST,
    )(query_low, own, back)


SMALL = 8


def staged_body(tokens, doc_lengths, cotangent, *shards):
    (
        query_weight,
        key_weight,
        value_weight,
        mix_weight,
        query_bias,
        value_bias,
        mix_bias,
        first_gain,
        first_shift,
        inner_weight,
        inner_bias,
        outer_weight,
        outer_bias,
        second_gain,
        second_shift,
    ) = shards
    layer_count = query_weight.shape[0]
    devices = 32
    length = SEQ_LEN // 4
    rows_held, inner_held = D // devices, FF // devices
    seq = lax.axis_index("seq")
    row = seq // 2
    coords = coordinates()
    z, y, x, c = coords[0], coords[1], coords[2], coords[3]
    place_of = seq.reshape(1).astype(jnp.int32)

    def split_rows(both):
        both = both.reshape(2, length, D)
        return pick(both, row, 0), pick(both, 1 - row, 0)

    token_kept, token_left = split_rows(tokens)
    upstream_kept, upstream_left = split_rows(cotangent)

    def unit_a(layer):
        r = rows_held
        parts = [w[layer] for w in (query_weight, key_weight, value_weight)]
        rows, outs = [(r * n, r * (n + 1), 0, n) for n in range(3)], [(r, 3 * D)]
        if layer:
            parts, rows, outs = parts + [mix_weight[layer]], rows + [(3 * r, 4 * r, 1, 0)], outs + [(r, D)]
        return GatherUnit(coords, jnp.concatenate(parts), outs, rows)

    def unit_i(layer):
        r, inner = rows_held, inner_weight[layer]
        parts = [inner[:, D * n : D * (n + 1)] for n in range(4)]
        rows, outs = [(r * n, r * (n + 1), 0, n) for n in range(4)], [(r, FF)]
        if not layer:
            parts, rows, outs = parts + [mix_weight[layer]], rows + [(4 * r, 5 * r, 1, 0)], outs + [(r, D)]
        return GatherUnit(coords, jnp.concatenate(parts), outs, rows)

    def unit_o(layer):
        return GatherUnit(coords, outer_weight[layer], [(inner_held, D)], [(0, inner_held, 0, 0)])

    units = [[make(layer) for make in (unit_a, unit_i, unit_o)] for layer in range(layer_count)]

    small_vectors = (
        query_bias,
        value_bias,
        mix_bias,
        first_gain,
        first_shift,
        outer_bias,
        second_gain,
        second_shift,
    )
    vector_count = SMALL * layer_count
    small_held = vector_count * rows_held
    mine = jnp.concatenate(
        [jnp.concatenate([v[layer] for v in small_vectors]) for layer in range(layer_count)]
        + [inner_bias.reshape(-1)]
    )
    held = mine.shape[0]
    padded = jnp.pad(mine, (0, 1024 - held)).reshape(8, 128)

    u = [unit for layer_units in units for unit in layer_units]
    padded = phase(padded, u[0])
    token_got = send(token_left, TO_X)
    every = jnp.roll(jnp.stack([padded] + [send(padded, TO_Z[4 - k]) for k in (1, 2, 3)]), z, axis=0)

    lengths = pick(doc_lengths.reshape(2, NDOC), row, 0)
    places = lax.iota(jnp.int32, SEQ_LEN)
    segment = jnp.sum((places[:, None] >= jnp.cumsum(lengths)[None, :]).astype(jnp.int32), axis=1)
    bias = window_bias(seq, jnp.where(segment == NDOC - 1, NDOC + places, segment))
    order, order_z = block_order(coords), block_order(coords, True)
    matrices = order_matrices(order)

    token_got, every = phase((token_got, every), u[0], u[1])
    every, upstream_left = lax.optimization_barrier((every, upstream_left))
    upstream_got = send(upstream_left, TO_X)
    every = by_place(every, send(every, TO_Y), y, 1)
    every, bias, upstream_got = phase((every, bias, upstream_got), u[0], settle=[u[1]])
    every = by_place(every, send(every, TO_X), x, 2)
    every, matrices = phase((every, matrices), u[0], u[1])
    every = by_place(every, send(every, TO_CORE), c, 3)
    every = every.reshape(devices, 1024)[:, :held].astype(f32)
    small_all = (
        every[:, :small_held]
        .reshape(devices, vector_count, rows_held)
        .transpose(1, 0, 2)
        .reshape(layer_count, SMALL, D)
    )
    wide_all = (
        every[:, small_held:]
        .reshape(devices, layer_count, inner_held)
        .transpose(1, 0, 2)
        .reshape(layer_count, FF)
    )
    stream = jnp.concatenate([token_kept, token_got]).astype(f32)
    stream, small_all, wide_all = phase((stream, small_all, wide_all), u[0], u[1], u[2])
    saved, active_gots = [], []
    for layer in range(layer_count):
        a_unit, i_unit, o_unit = units[layer]
        next_a, next_i, next_o = units[layer + 1] if layer + 1 < layer_count else (None,) * 3
        q_bias, v_bias, m_bias, gain1, shift1, o_bias, gain2, shift2 = [small_all[layer, n] for n in range(SMALL)]
        w_three, *w_rest = a_unit.result()
        w_three = w_three.reshape(D, 3 * D)
        stream_low = stream.astype(bf16)
        three_bias = jnp.concatenate([q_bias, jnp.zeros_like(q_bias), v_bias])
        (three,) = product(stream_low, w_three, 1024, lambda total, b: (total + b,), (bf16,), (three_bias,))
        if next_a:
            three = phase(three, i_unit, o_unit, next_a)
        else:
            three = phase(three, i_unit, settle=[o_unit])
        three_got = send(three, TO_CORE)
        (left_stream,) = selected(matrices, tie(stream_low, three))
        three, left_stream = lax.optimization_barrier((three, left_stream))
        left_stream = (left_stream[0], send(left_stream[1], TO_CORE))
        mixed, totals = attend_forward_blocks(place_of, three, three_got, bias)
        if next_a:
            mixed, totals, left_stream = phase(
                (mixed, totals, left_stream), i_unit, o_unit, next_a, next_i
            )
        else:
            mixed, totals, left_stream, active_gots = phase(
                (mixed, totals, left_stream, active_gots), i_unit, o_unit
            )
        w_inner, *w_more = i_unit.result()
        (w_mix,) = w_rest + w_more
        w_inner, w_mix = w_inner.reshape(D, FF), w_mix.reshape(D, D)
        first_sum, first, first_low = mixed_norm(mixed, w_mix, stream, m_bias, gain1, shift1)
        if next_a:
            first_low = phase(first_low, o_unit, next_a, next_i)
        else:
            first_low = phase(first_low, o_unit)
        left_mix, left_first = selected(matrices, mixed, first_low)
        first_low, left_mix, left_first = lax.optimization_barrier((first_low, left_mix, left_first))
        left_mix, left_first = [(m, send(t, TO_CORE)) for m, t in (left_mix, left_first)]
        active, slope = product(first_low, w_inner, 1024, gelu_parts, (bf16, bf16), (wide_all[layer],))
        if next_a:
            active, slope, left_mix, left_first = phase(
                (active, slope, left_mix, left_first), o_unit, next_a, next_o, settle=[next_i]
            )
        else:
            active, slope, left_mix, left_first = phase((active, slope, left_mix, left_first), o_unit)
        (w_outer,) = o_unit.result()
        active_got = send(tie(active, w_outer), TO_CORE)
        w_outer = w_outer.reshape(FF, D)
        (second_sum,) = product(
            active, w_outer, 256, lambda total, b, f: (f + (total + b),), (f32,), (o_bias,), (first,)
        )
        if not next_a:
            second_sum, active_got = lax.optimization_barrier((second_sum, active_got))
        active_gots.append(active_got)
        stream = norm_forward(second_sum)[0] * gain2 + shift2
        if next_a:
            stream = phase(stream, next_a, next_i, next_o)
        saved.append(
            (
                (w_three, w_mix, w_inner, w_outer, gain1, gain2),
                (three, three_got, totals, mixed),
                (first_sum, slope, second_sum),
                (left_stream, left_mix, left_first, active),
            )
        )

    def both_rows(kept, got):
        got = got.astype(f32)
        return jnp.where(row == 0, jnp.stack([kept, got]), jnp.stack([got, kept])).reshape(tokens.shape)

    output = stream
    output_got = send(output[length:].astype(bf16), TO_X)

    upstream = jnp.concatenate([upstream_kept, upstream_got]).astype(f32)
    small_grads, wide_grads = [None] * layer_count, [None] * layer_count
    sums = [None] * layer_count
    before = None
    for layer in reversed(range(layer_count)):
        weights, kept, rest, lefts = saved[layer]
        w_three, w_mix, w_inner, w_outer, gain1, gain2 = weights
        three, three_got, totals, mixed = kept
        first_sum, slope, second_sum = rest
        left_stream, left_mix, left_first, active = lefts
        left_active = (active, active_gots[layer])

        def with_sum(total, slopes):
            low = (total * slopes).astype(bf16)
            return low, jnp.sum(low.astype(f32), axis=0, keepdims=True)

        second_grad, second_low, second_sums = norm_backward_rows(second_sum, gain2, upstream)
        second_got = send(second_low, TO_CORE)
        inner_low, inner_sum = product(
            second_low, w_outer, 1024, with_sum, (bf16,), (), (slope,), transposed=True, sums=1
        )
        if before:
            inner_low, second_got = phase((inner_low, second_got), before.o[0], before.i, before.a)
        else:
            inner_low, second_got = lax.optimization_barrier((inner_low, second_got))
        inner_got = send(inner_low, TO_CORE)
        second_pair = (second_low, second_got)
        if before:
            by_z, by_far = wide_terms_split(order, order_z, left_active, second_pair)
            o_sums = (SumUnit(by_z, Z_FIRST), SumUnit(by_far))
            second_grad, inner_low, inner_got = phase(
                (second_grad, inner_low, inner_got), *o_sums, before.a, before.i, settle=before.o
            )
        else:
            o_sums = (SumUnit(wide_terms_of(order, left_active, second_pair)),)
            second_grad, inner_low, inner_got, output_got = phase(
                (second_grad, inner_low, inner_got, output_got), *o_sums
            )
        (first_grad,) = product(
            inner_low, w_inner, 256, lambda total, g: (g + total,), (f32,), (), (second_grad,), transposed=True
        )
        first_sum_grad, branch_low, first_sums = norm_backward_rows(first_sum, gain1, first_grad)
        branch_got = send(branch_low, TO_CORE)
        (mixed_grad,) = product(branch_low, w_mix, 512, lambda total: (total,), (bf16,), transposed=True)
        i_sum = SumUnit(weight_terms((left_first, tie((inner_low, inner_got), mixed_grad), FF)))
        if before:
            mixed_grad = phase(mixed_grad, i_sum, *o_sums, before.a, settle=[before.i])
        else:
            mixed_grad = phase(mixed_grad, i_sum, settle=o_sums)
        query_low, own_grads, sent_grads = attend_backward_blocks(
            place_of, in_hbm(three), in_hbm(three_got), bias, in_hbm(mixed), in_hbm(totals), mixed_grad
        )
        grads_back = send(sent_grads, TO_CORE)
        if before:
            query_low, own_grads = phase((query_low, own_grads), i_sum, *o_sums, before.a)
        else:
            query_low, own_grads = phase((query_low, own_grads), *o_sums, settle=[i_sum])
        low, low_sums = merged(query_low, own_grads, grads_back)
        low, branch_got = lax.optimization_barrier((low, branch_got))
        low_got = send(low, TO_CORE)
        if layer:
            (upstream,) = product(
                low, w_three, 256, lambda total, g: (g + total,), (f32,), (), (first_sum_grad,), transposed=True
            )
            mix_pair = (left_mix, (branch_low, branch_got), D)
            a_sum = SumUnit(weight_terms((left_stream, tie((low, low_got), upstream), 3 * D), mix_pair))
        else:
            mix_pair = (left_mix, (branch_low, branch_got), D)
            a_sum = SumUnit(weight_terms((left_stream, (low, low_got), 3 * D), mix_pair))
            low, low_sums = phase((low, low_sums), a_sum, settle=[i_sum, *o_sums, before.a] if before else [i_sum])
            (upstream,) = product(
                low, w_three, 256, lambda total, g: (g + total,), (f32,), (), (first_sum_grad,), transposed=True
            )
        small_grads[layer] = jnp.stack(
            [
                low_sums[0, :D],
                low_sums[0, 2 * D :],
                first_sums[2],
                first_sums[0],
                first_sums[1],
                second_sums[2],
                second_sums[0],
                second_sums[1],
            ]
        )
        wide_grads[layer] = inner_sum[0]
        if layer:
            upstream, small_grads[layer] = phase((upstream, small_grads[layer]), *o_sums, i_sum, settle=[a_sum])
        sums[layer] = before = Sums(o_sums, i_sum, a_sum)

    small_terms = (
        jnp.stack(small_grads)
        .reshape(vector_count, devices, rows_held)
        .transpose(1, 0, 2)
        .reshape(devices, small_held)
    )
    wide_terms = (
        jnp.stack(wide_grads)
        .reshape(layer_count, devices, inner_held)
        .transpose(1, 0, 2)
        .reshape(devices, layer_count * inner_held)
    )
    terms = jnp.pad(jnp.concatenate([small_terms, wide_terms], axis=1), ((0, 0), (0, 1024 - held)))
    chosen = (order[:, None] == lax.iota(jnp.int32, devices)[None, :]).astype(f32)
    terms = jnp.dot(chosen, terms, precision=lax.Precision.HIGHEST).reshape(2, 128, 128)
    terms = (terms[0] + send(terms[1].astype(bf16), TO_CORE).astype(f32)).astype(bf16)
    small_sum = SumUnit((terms[:64], terms[64:]))

    phase((), small_sum)
    last = sums[0]
    done = [unit for layer in range(1, layer_count) for unit in (*sums[layer].o, sums[layer].i, sums[layer].a)]
    upstream, output_got = phase((upstream, output_got), last.a, last.i, *last.o, small_sum, *done)
    token_left = upstream[length:].astype(bf16)
    upstream, token_left = phase((upstream, token_left), last.a, last.i, *last.o, small_sum)
    token_back = send(token_left, TO_X)
    upstream, token_back = phase((upstream, token_back), last.a, last.i, small_sum)
    phase((), last.a, small_sum)
    own_terms = small_sum.kept.reshape(-1)[:held]
    small_own = own_terms[:small_held].reshape(layer_count, SMALL, rows_held)
    wide_own = own_terms[small_held:].reshape(layer_count, inner_held)
    for layer in range(layer_count):
        for unit in (*sums[layer].o, sums[layer].i, sums[layer].a):
            while unit.step < 5:
                phase((), unit)
    o_all = jnp.stack([jnp.concatenate([unit.kept for unit in group.o], axis=1) for group in sums])
    i_all, a_all = [jnp.stack([group[n].kept for group in sums]) for n in (1, 2)]
    return (
        both_rows(output[:length], output_got),
        both_rows(upstream[:length], token_back),
        a_all[:, :, :D],
        a_all[:, :, D : 2 * D],
        a_all[:, :, 2 * D : 3 * D],
        a_all[:, :, 3 * D :],
        small_own[:, 0],
        small_own[:, 1],
        small_own[:, 2],
        small_own[:, 3],
        small_own[:, 4],
        i_all,
        wide_own,
        o_all,
        small_own[:, 5],
        small_own[:, 6],
        small_own[:, 7],
    )


def plain_body(fsdp_size, seq_size):
    half = seq_size // 2
    device_count = fsdp_size * seq_size
    across = [(i, (i + half) % seq_size) for i in range(seq_size)]
    groups = [[m * half + j for j in range(half)] for m in range(2)]
    length = SEQ_LEN // seq_size

    def gather_siblings(rows):
        return lax.all_gather(rows, "seq", axis_index_groups=groups)

    def scatter_siblings(own_order):
        return lax.psum_scatter(own_order, "seq", axis_index_groups=groups)

    def body(tokens, doc_lengths, cotangent, *shards):
        (
            query_weight,
            key_weight,
            value_weight,
            mix_weight,
            query_bias,
            value_bias,
            mix_bias,
            first_gain,
            first_shift,
            inner_weight,
            inner_bias,
            outer_weight,
            outer_bias,
            second_gain,
            second_shift,
        ) = shards
        layer_count = query_weight.shape[0]
        seq = lax.axis_index("seq")
        row = seq // half
        rows_held = D // device_count
        inner_held = FF // device_count

        def vector_rows(small, wide):
            return jnp.concatenate(
                [jnp.concatenate([v[layer] for v in small]) for layer in range(layer_count)]
                + [wide.reshape(-1)]
            )

        small_vectors = (
            query_bias,
            value_bias,
            mix_bias,
            first_gain,
            first_shift,
            outer_bias,
            second_gain,
            second_shift,
        )
        vector_count = len(small_vectors) * layer_count
        mine = vector_rows(small_vectors, inner_bias)
        held = mine.shape[0]
        every = lax.all_gather(mine, AXES)
        every = every.astype(f32)
        small_held = vector_count * rows_held
        small_all = (
            every[:, :small_held]
            .reshape(device_count, vector_count, rows_held)
            .transpose(1, 0, 2)
            .reshape(layer_count, len(small_vectors), D)
        )
        wide_all = (
            every[:, small_held:]
            .reshape(device_count, layer_count, inner_held)
            .transpose(1, 0, 2)
            .reshape(layer_count, FF)
        )

        def whole_weights(layer):
            weights = (query_weight, key_weight, value_weight, mix_weight, inner_weight, outer_weight)
            return [lax.all_gather(w[layer], AXES, axis=0, tiled=True) for w in weights]

        def own_row(both_rows):
            kept = pick(both_rows, row, 0)
            return jnp.concatenate(
                [kept, lax.ppermute(pick(both_rows, 1 - row, 0), "seq", across)]
            )

        def both_rows(values):
            kept = values[:length]
            other = lax.ppermute(values[length:].astype(bf16), "seq", across).astype(f32)
            return jnp.where(row == 0, jnp.stack([kept, other]), jnp.stack([other, kept]))

        stream_start = own_row(tokens.reshape(2, length, D))
        upstream_start = own_row(cotangent.reshape(2, length, D))

        lengths = pick(doc_lengths.reshape(2, NDOC), row, 0)
        bounds = jnp.cumsum(lengths)
        within = lax.iota(jnp.int32, length)

        def positions(s):
            return jnp.concatenate([s * length + within, (s + half) % seq_size * length + within])

        def segments(places):
            return jnp.sum((places[:, None] >= bounds[None, :]).astype(jnp.int32), axis=1)

        query_places = positions(seq)
        key_places = jnp.concatenate([positions(row * half + j) for j in range(half)])
        query_segment, key_segment = segments(query_places), segments(key_places)
        allowed = (
            (query_segment[:, None] == key_segment[None, :]) & (key_segment[None, :] != NDOC - 1)
        ) | (query_places[:, None] == key_places[None, :])

        stream = stream_start.astype(f32)
        saved = []
        for layer in range(layer_count):
            q_bias, v_bias, m_bias, gain1, shift1, o_bias, gain2, shift2 = [
                small_all[layer, n] for n in range(len(small_vectors))
            ]
            w_query, w_key, w_value, w_mix, w_inner, w_outer = whole_weights(layer)
            stream_low = stream.astype(bf16)
            queries = (dot(stream_low, w_query) + q_bias).astype(bf16)
            key_rows = dot(stream_low, w_key).astype(bf16)
            values = (dot(stream_low, w_value) + v_bias).astype(bf16)
            all_keys = gather_siblings(key_rows).reshape(SEQ_LEN, D)
            all_values = gather_siblings(values).reshape(SEQ_LEN, D)
            mixed, log_total = attend_forward(queries, all_keys, all_values, allowed)
            first_sum = stream + (dot(mixed, w_mix) + m_bias)
            first = norm_forward(first_sum)[0] * gain1 + shift1
            first_low = first.astype(bf16)
            inner = dot(first_low, w_inner) + wide_all[layer]
            below = 0.5 * (1.0 + lax.erf(inner * (0.5**0.5)))
            active = (inner * below).astype(bf16)
            slope = (below + inner * jnp.exp(-0.5 * inner * inner) * (2 * math.pi) ** -0.5).astype(
                bf16
            )
            second_sum = first + (dot(active, w_outer) + o_bias)
            stream = norm_forward(second_sum)[0] * gain2 + shift2
            saved.append(
                (
                    (w_query, w_key, w_value, w_mix, w_inner, w_outer, gain1, gain2),
                    (stream_low, queries, all_keys, all_values, log_total, mixed),
                    (first_sum, first_low, slope, active, second_sum),
                )
            )
        activations = both_rows(stream)

        upstream = upstream_start.astype(f32)
        small_grads = [None] * layer_count
        wide_grads = [None] * layer_count
        results = [None] * layer_count

        def reduced(grads):
            return [lax.psum_scatter(g, AXES, scatter_dimension=0, tiled=True) for g in grads]

        for layer in reversed(range(layer_count)):
            (w_query, w_key, w_value, w_mix, w_inner, w_outer, gain1, gain2), kept, rest = saved[layer]
            stream_low, queries, all_keys, all_values, log_total, mixed = kept
            first_sum, first_low, slope, active, second_sum = rest
            second_grad, gain2_grad, shift2_grad = norm_backward(second_sum, gain2, upstream)
            second_low = second_grad.astype(bf16)
            (outer_grad,) = reduced([contract_rows(active, second_low)])
            inner_low = (contract_cols(second_low, w_outer) * slope).astype(bf16)
            (inner_grad,) = reduced([contract_rows(first_low, inner_low)])
            first_grad = second_grad + contract_cols(inner_low, w_inner)
            first_sum_grad, gain1_grad, shift1_grad = norm_backward(first_sum, gain1, first_grad)
            branch_low = first_sum_grad.astype(bf16)
            mix_terms = contract_rows(mixed, branch_low)
            mixed_grad = contract_cols(branch_low, w_mix).astype(bf16)
            query_low, key_terms, value_terms = attend_backward(
                queries, all_keys, all_values, allowed, log_total, mixed_grad
            )
            n = 2 * length
            key_low = scatter_siblings(key_terms.reshape(half, n, D)).astype(bf16)
            value_low = scatter_siblings(value_terms.reshape(half, n, D)).astype(bf16)
            value_grad, mix_grad = reduced([contract_rows(stream_low, value_low), mix_terms])
            query_grad, key_grad = reduced(
                [contract_rows(stream_low, query_low), contract_rows(stream_low, key_low)]
            )
            upstream = (
                first_sum_grad
                + contract_cols(query_low, w_query)
                + contract_cols(key_low, w_key)
                + contract_cols(value_low, w_value)
            )
            small_grads[layer] = jnp.stack(
                [
                    column_sum(query_low),
                    column_sum(value_low),
                    column_sum(branch_low),
                    gain1_grad,
                    shift1_grad,
                    column_sum(second_low),
                    gain2_grad,
                    shift2_grad,
                ]
            )
            wide_grads[layer] = column_sum(inner_low)
            results[layer] = (query_grad, key_grad, value_grad, mix_grad, inner_grad, outer_grad)
        token_grad = both_rows(upstream)

        small_terms = (
            jnp.stack(small_grads)
            .reshape(vector_count, device_count, rows_held)
            .transpose(1, 0, 2)
            .reshape(device_count, small_held)
        )
        wide_terms = (
            jnp.stack(wide_grads)
            .reshape(layer_count, device_count, inner_held)
            .transpose(1, 0, 2)
            .reshape(device_count, layer_count * inner_held)
        )
        terms = jnp.concatenate([small_terms, wide_terms], axis=1)
        own_terms = lax.psum_scatter(terms, AXES, scatter_dimension=0, tiled=False)
        small_own = own_terms[:small_held].reshape(layer_count, len(small_vectors), rows_held)
        wide_own = own_terms[small_held:].reshape(layer_count, inner_held)
        query_g, key_g, value_g, mix_g, inner_g, outer_g = [
            jnp.stack([results[layer][n] for layer in range(layer_count)]) for n in range(6)
        ]
        return (
            activations.reshape(tokens.shape),
            token_grad.reshape(tokens.shape),
            query_g,
            key_g,
            value_g,
            mix_g,
            small_own[:, 0],
            small_own[:, 1],
            small_own[:, 2],
            small_own[:, 3],
            small_own[:, 4],
            inner_g,
            wide_own,
            outer_g,
            small_own[:, 5],
            small_own[:, 6],
            small_own[:, 7],
        )

    return body


def solution(mesh):
    tokens = P(None, "fsdp", "seq", None)
    matrix, vector = P(None, AXES, None), P(None, AXES)
    in_specs = (tokens, P(None, "fsdp", None), tokens) + (matrix,) * 4 + (vector,) * 5
    in_specs += (matrix, vector, matrix, vector, vector, vector)
    out_specs = (tokens, tokens) + (matrix,) * 4 + (vector,) * 5
    out_specs += (matrix, vector, matrix, vector, vector, vector)
    sizes = (mesh.shape["fsdp"], mesh.shape["seq"])
    body = staged_body if sizes == (8, 4) else plain_body(*sizes)
    return jax.shard_map(body, mesh=mesh, in_specs=in_specs, out_specs=out_specs, check_vma=False)
```

```python
import collections
import math

import jax
import jax.numpy as jnp
from jax import lax
from jax.experimental import pallas as pl
from jax.experimental.pallas import tpu as pltpu
from jax.sharding import PartitionSpec as P

D = 1024
FF = 4096
HEAD_DIM = 64
HEADS = D // HEAD_DIM
SEQ_LEN = 1024
NDOC = 16
epsilon = 1e-05
AXES = ("fsdp", "seq")
f32 = jnp.float32
bf16 = jnp.bfloat16


def dot(left, right):
    return jnp.dot(left, right, preferred_element_type=f32)


def contract_rows(left, right):
    return lax.dot_general(left, right, (((0,), (0,)), ((), ())), preferred_element_type=f32)


def contract_cols(left, right):
    return lax.dot_general(left, right, (((1,), (1,)), ((), ())), preferred_element_type=f32)


SMALL_COST = pl.CostEstimate(flops=1024, bytes_accessed=1024, transcendentals=0)


def tie(value, *others):
    return lax.optimization_barrier((value, others))[0]


def pairs(move):
    out = []
    for i in range(32):
        z, y, x, c = i // 8, i // 4 % 2, i // 2 % 2, i % 2
        z, y, x, c = move(z, y, x, c)
        out.append((i, z * 8 + y * 4 + x * 2 + c))
    return out


TO_CORE = pairs(lambda z, y, x, c: (z, y, x, 1 - c))
TO_X = pairs(lambda z, y, x, c: (z, y, 1 - x, c))
TO_Y = pairs(lambda z, y, x, c: (z, 1 - y, x, c))
TO_FAR = pairs(lambda z, y, x, c: (z, y if c == 0 else 1 - y, 1 - x if c == 0 else x, c))
TO_NEAR = pairs(lambda z, y, x, c: (z, 1 - y if c == 0 else y, x if c == 0 else 1 - x, c))
TO_ODD = pairs(lambda z, y, x, c: (z ^ 1, y, x, c))
TO_PAIR = pairs(lambda z, y, x, c: (z ^ 2, y, x, c))
TO_Z = [pairs(lambda z, y, x, c, k=k: ((z + k) % 4, y, x, c)) for k in range(4)]


def send(value, to):
    return lax.ppermute(value, AXES, to)


def coordinates():
    fsdp, seq = lax.axis_index("fsdp"), lax.axis_index("seq")
    return jnp.stack([fsdp // 2, fsdp % 2, seq // 2, seq % 2]).astype(jnp.int32)


def place(coords, pieces, shapes, moves):
    count = len(moves(0, 0, 0, 0, None, None))

    total = len(pieces)

    def kernel(coords_ref, *refs):
        sources, targets = refs[:total], refs[total : total + len(shapes)]
        buffers, in_sems, out_sems = refs[total + len(shapes) : -2], refs[-2], refs[-1]
        loads = [
            pltpu.make_async_copy(source, buffer, in_sems.at[n])
            for n, (source, buffer) in enumerate(zip(sources, buffers))
        ]
        for load in loads:
            load.start()
        todo = moves(coords_ref[0], coords_ref[1], coords_ref[2], coords_ref[3], buffers, targets)
        stores = [
            (n, pltpu.make_async_copy(view, target, out_sems.at[k]))
            for k, (n, view, target) in enumerate(todo)
        ]
        for piece, load in enumerate(loads):
            load.wait()
            for n, store in stores:
                if n == piece:
                    store.start()
        for _, store in stores:
            store.wait()

    return pl.pallas_call(
        kernel,
        in_specs=[pl.BlockSpec(memory_space=pltpu.SMEM)]
        + [pl.BlockSpec(memory_space=pl.ANY)] * len(pieces),
        out_specs=[pl.BlockSpec(memory_space=pltpu.HBM)] * len(shapes),
        out_shape=[pltpu.HBM(shape, bf16) for shape in shapes],
        scratch_shapes=[pltpu.VMEM(p.shape, bf16) for p in pieces]
        + [pltpu.SemaphoreType.DMA((total,)), pltpu.SemaphoreType.DMA((count,))],
        compiler_params=pltpu.CompilerParams(vmem_limit_bytes=40 << 20),
        cost_estimate=SMALL_COST,
    )(coords, *pieces)


def in_hbm(value):
    return pltpu.with_memory_space_constraint(value, pltpu.HBM)


def pick(value, index, axis):
    return lax.dynamic_index_in_dim(value, index, axis, keepdims=False)


def by_place(own, other, at, axis):
    return jnp.where(at == 0, jnp.stack([own, other], axis), jnp.stack([other, own], axis))


def phase(values, *units, settle=()):
    values, flights, ended = lax.optimization_barrier(
        (values, [u.flight for u in units], [u.flight for u in settle])
    )
    for unit, flight in zip(settle, ended):
        unit.flight = flight
    nexts = [u.local(flight) for u, flight in zip(units, flights)]
    values, sends = lax.optimization_barrier((values, [[v for v, _ in n] for n in nexts]))
    for unit, arrays, targets in zip(units, sends, nexts):
        unit.flight = [send(array, to) for array, (_, to) in zip(arrays, targets)]
    return values


class GatherUnit:
    def __init__(self, coords, pack, shapes, parts):
        self.coords, self.pack, self.shapes, self.parts = coords, pack, shapes, parts
        self.flight, self.step = [pack], 0

    def local(self, got):
        self.step += 1
        if self.step == 1:
            self.kept = got[0][None]
            return [(self.kept, TO_PAIR)]
        if self.step < 5:
            self.kept = jnp.concatenate([got[0], self.kept])
            sends = [(self.kept, (TO_ODD, TO_NEAR, TO_FAR)[self.step - 2])]
            return sends + [(self.kept, TO_CORE)] * (self.step == 4)
        self.kept = [self.kept, *got]
        return [(got[0], TO_CORE)]

    def result(self):
        width = self.pack.shape[1]

        def by_block(z, y, x, c, src, dst):
            out = []
            for n in range(4):
                core, far = (c if n < 2 else 1 - c), n % 2
                for near in (1, 0):
                    y2 = y ^ jnp.where(core == 0, near, far)
                    x2 = x ^ jnp.where(core == 0, far, near)
                    for odd in (1, 0):
                        for pair in (1, 0):
                            block = 4 * (1 - near) + 2 * (1 - odd) + 1 - pair
                            for lo, hi, target, column in self.parts:
                                view = None
                                if dst:
                                    spans = (slice(0, hi - lo), slice(column * width, (column + 1) * width))
                                    view = dst[target].at[(z ^ odd ^ (2 * pair), y2, x2, core) + spans]
                                out.append((n, src and src[n].at[block, lo:hi], view))
            return out

        return place(
            self.coords, self.kept + self.flight, [(4, 2, 2, 2) + shape for shape in self.shapes], by_block
        )


FAR_FIRST = (TO_FAR, TO_NEAR, TO_ODD, TO_PAIR)
Z_FIRST = (TO_ODD, TO_PAIR, TO_FAR, TO_NEAR)


class SumUnit:
    def __init__(self, parts, route=FAR_FIRST):
        self.flight, self.step, self.route = list(parts), 0, route

    def local(self, got):
        self.step += 1
        if self.step == 1:
            leaving, self.kept = got
        elif self.step < 5:
            half = self.kept.shape[0] // 2
            add = lambda a, b: a.astype(f32) + b.astype(f32)
            leaving = add(self.kept[:half], got[0][:half]).astype(bf16)
            self.kept = add(self.kept[half:], got[0][half:])
            if self.step < 4:
                self.kept = self.kept.astype(bf16)
        else:
            self.kept = self.kept + got[0].astype(f32)
            return []
        return [(leaving, self.route[self.step - 1])]


Sums = collections.namedtuple("Sums", "o i a")


def block_order(coords, z_first=False):
    z, y, x, c = coords[0], coords[1], coords[2], coords[3]
    order = []
    for core in (c, 1 - c):
        for first in range(4):
            for second in range(4):
                across, along = (second, first) if z_first else (first, second)
                far, near = 1 - across // 2, 1 - across % 2
                odd, pair = 1 - along // 2, 1 - along % 2
                y2 = y ^ jnp.where(core == 0, near, far)
                x2 = x ^ jnp.where(core == 0, far, near)
                order.append((z ^ odd ^ (2 * pair)) * 8 + y2 * 4 + x2 * 2 + core)
    return jnp.stack(order).astype(jnp.int32)


def order_matrices(order):
    block = D // 32
    wanted = (order[:, None] * block + lax.iota(jnp.int32, block)[None, :]).reshape(2, D // 2, 1)
    columns = lax.broadcasted_iota(jnp.int32, (2, D // 2, D), 2)
    chosen = (columns == wanted).astype(bf16)
    return chosen[0], chosen[1]


def selected(matrices, *arrays):
    count = len(arrays)

    def kernel(mine, theirs, *refs):
        for n in range(count):
            rows = refs[n][...]
            refs[count + 2 * n][...] = nt_dot(mine[...], rows).astype(bf16)
            refs[count + 2 * n + 1][...] = nt_dot(theirs[...], rows).astype(bf16)

    out = jax.ShapeDtypeStruct((D // 2, arrays[0].shape[0]), bf16)
    outs = pl.pallas_call(
        kernel,
        out_shape=[out] * (2 * count),
        compiler_params=pltpu.CompilerParams(vmem_limit_bytes=48 << 20),
        cost_estimate=SMALL_COST,
    )(*matrices, *arrays)
    return [tuple(outs[2 * n : 2 * n + 2]) for n in range(count)]


def weight_terms(*pairs_of, first=0, tile=1024):
    rows, tokens = pairs_of[0][0][0].shape
    counts = [pair[2] // tile for pair in pairs_of]
    starts = [sum(counts[:n]) for n in range(len(counts))]
    columns, half = sum(counts) * tile, rows // 2

    def kernel(*refs):
        leaving, kept = refs[-2:]
        j = pl.program_id(0)
        for n, (start, count) in enumerate(zip(starts, counts)):

            @pl.when((j >= start) & (j < start + count))
            def _(a1=refs[4 * n], a2=refs[4 * n + 1], b1=refs[4 * n + 2], b2=refs[4 * n + 3]):
                total = jnp.dot(a1[...], b1[...], preferred_element_type=f32)
                total = total + jnp.dot(a2[...], b2[...], preferred_element_type=f32)
                leaving[...] = total[:half].astype(bf16)
                kept[...] = total[half:].astype(bf16)

    in_specs, args = [], []
    for (left, right, _), start, count in zip(pairs_of, starts, counts):
        whole = pl.BlockSpec((rows, tokens), lambda j: (0, 0))
        cut = pl.BlockSpec((tokens, tile), lambda j, s=start, n=count: (0, jnp.clip(j - s, 0, n - 1) + first // tile))
        in_specs += [whole, whole, cut, cut]
        args += [*map(in_hbm, left), *right]
    out = jax.ShapeDtypeStruct((half, columns), bf16)
    return pl.pallas_call(
        kernel,
        grid=(columns // tile,),
        in_specs=in_specs,
        out_specs=[pl.BlockSpec((half, tile), lambda j: (0, j))] * 2,
        out_shape=[out, out],
        compiler_params=pltpu.CompilerParams(vmem_limit_bytes=48 << 20),
        cost_estimate=SMALL_COST,
    )(*args)


def wide_terms_of(order, left, right):
    tokens, width = left[0].shape
    block = width // 32
    columns = right[0].shape[1]

    def kernel(order_ref, *refs):
        a1, a2, (b1, b2, leaving, kept) = refs[:2], refs[2:4], refs[4:]
        one = (
            lax.broadcasted_iota(jnp.int32, (block, block), 0) == lax.broadcasted_iota(jnp.int32, (block, block), 1)
        ).astype(bf16)
        turned = lambda refs: jnp.concatenate([nt_dot(one, r[...]).astype(bf16) for r in refs], axis=0)
        total = jnp.dot(turned(a1), b1[...], preferred_element_type=f32)
        total = (total + jnp.dot(turned(a2), b2[...], preferred_element_type=f32)).astype(bf16)

        @pl.when(pl.program_id(0) < 4)
        def _():
            leaving[...] = total

        @pl.when(pl.program_id(0) >= 4)
        def _():
            kept[...] = total

    cut = lambda n: pl.BlockSpec((tokens, block), lambda j, order: (0, order[2 * j + n]))
    whole = pl.BlockSpec((tokens, columns), lambda j, order: (0, 0))
    out = jax.ShapeDtypeStruct((width // 4, columns), bf16)
    return pl.pallas_call(
        kernel,
        grid_spec=pltpu.PrefetchScalarGridSpec(
            num_scalar_prefetch=1,
            grid=(8,),
            in_specs=[cut(0), cut(1), cut(0), cut(1), whole, whole],
            out_specs=[
                pl.BlockSpec((2 * block, columns), lambda j, order: (jnp.minimum(j, 3), 0)),
                pl.BlockSpec((2 * block, columns), lambda j, order: (jnp.maximum(j - 4, 0), 0)),
            ],
        ),
        out_shape=[out, out],
        compiler_params=pltpu.CompilerParams(vmem_limit_bytes=48 << 20),
        cost_estimate=SMALL_COST,
    )(order, *map(in_hbm, (left[0], left[0], left[1], left[1])), *right)


def wide_terms_split(order, order_z, left, right):
    tokens, width = left[0].shape
    block, columns = width // 32, right[0].shape[1] // 2
    same = order_z[:16, None] == order[None, :16]
    places = jnp.sum(jnp.where(same, lax.broadcasted_iota(jnp.int32, (16, 16), 1), 0), axis=1)

    def kernel(order_ref, place_ref, a1, a2, b1, b2, first, second):
        one = (
            lax.broadcasted_iota(jnp.int32, (block, block), 0) == lax.broadcasted_iota(jnp.int32, (block, block), 1)
        ).astype(bf16)
        total = sum(
            jnp.dot(nt_dot(one, a[...]).astype(bf16), b[...], preferred_element_type=f32)
            for a, b in ((a1, b1), (a2, b2))
        ).astype(bf16)
        first[0, 0] = total[:, :columns]
        second[0, 0] = total[:, columns:]

    cut = pl.BlockSpec((tokens, block), lambda j, order, place: (0, order[j]))
    whole = pl.BlockSpec((tokens, 2 * columns), lambda j, order, place: (0, 0))
    out = jax.ShapeDtypeStruct((2, 8, block, columns), bf16)
    outs = pl.pallas_call(
        kernel,
        grid_spec=pltpu.PrefetchScalarGridSpec(
            num_scalar_prefetch=2,
            grid=(16,),
            in_specs=[cut, cut, whole, whole],
            out_specs=[
                pl.BlockSpec((1, 1, block, columns), lambda j, order, place: (j // 8, j % 8, 0, 0)),
                pl.BlockSpec((1, 1, block, columns), lambda j, order, place: (place[j] // 8, place[j] % 8, 0, 0)),
            ],
        ),
        out_shape=[out, out],
        compiler_params=pltpu.CompilerParams(vmem_limit_bytes=48 << 20),
        cost_estimate=SMALL_COST,
    )(order_z, places, *map(in_hbm, left), *right)
    return [[part.reshape(8 * block, columns) for part in (o[0], o[1])] for o in outs]


BLOCK = 256
WINDOWS = (2 * BLOCK, 3 * BLOCK)
PAIR = 2 * HEAD_DIM


def query_starts(s):
    edge = (s // 2) ^ (s % 2)
    return edge * BLOCK, (1 - edge) * BLOCK


def window_starts(s):
    return (s % 2) * (2 * BLOCK), (1 - s % 2) * BLOCK


def nt_dot(left, right):
    return lax.dot_general(left, right, (((1,), (1,)), ((), ())), preferred_element_type=f32)


def only_head(value, head, axis):
    lane = lax.broadcasted_iota(jnp.int32, value.shape, axis)
    return jnp.where((lane < HEAD_DIM) if head == 0 else (lane >= HEAD_DIM), value, jnp.zeros_like(value))


def in_order(s, mine, other, scratch):
    for n, ref in ((0, mine), (1, other)):
        for slot in range(2):
            scratch[pl.ds((s ^ (n + 2 * slot)) * BLOCK, BLOCK), :] = ref[slot * BLOCK : (slot + 1) * BLOCK, :]


def attention_views(s):
    rows = [pl.ds(pl.multiple_of(start, BLOCK), BLOCK) for start in query_starts(s)]
    windows = [pl.ds(pl.multiple_of(start, BLOCK), width) for start, width in zip(window_starts(s), WINDOWS)]
    spans = [slice(h * HEAD_DIM, (h + 1) * HEAD_DIM) for h in range(2)]
    return rows, windows, spans, [slice(n * BLOCK, (n + 1) * BLOCK) for n in range(2)]


def attend_forward_kernel(
    s_ref, q_ref, km_ref, ko_ref, vm_ref, vo_ref, edge_ref, inner_ref, mixed_ref, total_ref, keys, values
):
    s = s_ref[0]
    in_order(s, km_ref, ko_ref, keys)
    in_order(s, vm_ref, vo_ref, values)
    rows, windows, spans, kinds = attention_views(s)
    biases = (edge_ref, inner_ref)
    scores = []
    for n in range(2):
        q = q_ref[rows[n], :] * jnp.asarray(HEAD_DIM**-0.5, bf16)
        k = keys[windows[n], :]
        scores += [nt_dot(k, only_head(q, head, 1)) for head in range(2)]
    raised, totals = [], []
    for m in range(4):
        n, head = divmod(m, 2)
        biased = scores[m] + biases[n][...]
        top = jnp.max(biased, axis=0, keepdims=True)
        up = jnp.exp(biased - top)
        totals.append(jnp.sum(up, axis=0, keepdims=True))
        total_ref[0, head : head + 1, kinds[n]] = top + jnp.log(totals[m])
        raised.append(up.astype(bf16))
    for n in range(2):
        v_t = values[windows[n], :].T
        halves = [
            jnp.dot(v_t[spans[h]], raised[2 * n + h], preferred_element_type=f32) / totals[2 * n + h]
            for h in range(2)
        ]
        mixed_ref[rows[n], :] = jnp.concatenate(halves, axis=0).T.astype(bf16)


def attend_backward_kernel(
    s_ref, q_ref, km_ref, ko_ref, vm_ref, vo_ref, edge_ref, inner_ref, mixed_ref, total_ref, grad_ref,
    dq_ref, mine_ref, sent_ref, keys, values, key_sum, value_sum,
):
    s = s_ref[0]
    in_order(s, km_ref, ko_ref, keys)
    in_order(s, vm_ref, vo_ref, values)
    key_sum[...] = jnp.zeros_like(key_sum)
    value_sum[...] = jnp.zeros_like(value_sum)
    rows, windows, spans, kinds = attention_views(s)
    biases = (edge_ref, inner_ref)
    scores, share_grads, queries, grads, inner = [], [], [], [], []
    for n in range(2):
        q = q_ref[rows[n], :] * jnp.asarray(HEAD_DIM**-0.5, bf16)
        g = grad_ref[rows[n], :]
        along = (g.astype(f32) * mixed_ref[rows[n], :].astype(f32)).T
        k, v = keys[windows[n], :], values[windows[n], :]
        for head in range(2):
            queries.append(only_head(q, head, 1))
            grads.append(only_head(g, head, 1))
            inner.append(jnp.sum(along[spans[head]], axis=0, keepdims=True))
            scores.append(nt_dot(k, queries[-1]))
            share_grads.append(nt_dot(v, grads[-1]))
    shares_low, grads_low = [], []
    for m in range(4):
        n, head = divmod(m, 2)
        shares = jnp.exp(scores[m] + biases[n][...] - total_ref[0, head : head + 1, kinds[n]])
        shares_low.append(shares.astype(bf16))
        grads_low.append((shares * (share_grads[m] - inner[m])).astype(bf16))
    both = lambda values, n, axis: jnp.concatenate(values[2 * n : 2 * n + 2], axis=axis)
    for n in range(2):
        k_t = keys[windows[n], :].T
        query_grads = [jnp.dot(k_t[spans[h]], grads_low[2 * n + h], preferred_element_type=f32) for h in range(2)]
        dq_ref[rows[n], :] = (jnp.concatenate(query_grads, axis=0).T * HEAD_DIM**-0.5).astype(bf16)
        key_sum[windows[n], :] += jnp.dot(both(grads_low, n, 1), both(queries, n, 0), preferred_element_type=f32)
        value_sum[windows[n], :] += jnp.dot(both(shares_low, n, 1), both(grads, n, 0), preferred_element_type=f32)
    for slot in range(2):
        here = slice(slot * BLOCK, (slot + 1) * BLOCK)
        mine, other = pl.ds((s ^ (2 * slot)) * BLOCK, BLOCK), pl.ds((s ^ (1 + 2 * slot)) * BLOCK, BLOCK)
        for n, sums in ((0, key_sum), (1, value_sum)):
            mine_ref[n, here, :] = sums[mine, :]
            sent_ref[n, here, :] = sums[other, :].astype(bf16)


def call_attention(kernel, s, own, other, bias, kept, outs, scratch):
    pairs_count = D // PAIR
    third = lambda n: pl.BlockSpec((2 * BLOCK, PAIR), lambda h: (0, h + n * pairs_count))
    cut = third(0)
    double = pl.BlockSpec((2, 2 * BLOCK, PAIR), lambda h: (0, 0, h))
    per_pair = pl.BlockSpec((1, 2, 2 * BLOCK), lambda h: (h, 0, 0))
    whole = [pl.BlockSpec(b.shape, lambda h: (0, 0)) for b in bias]
    in_specs = [pl.BlockSpec(memory_space=pltpu.SMEM), third(0), third(1), third(1), third(2), third(2), *whole]
    args = [s, own, own, other, own, other, *bias]
    if kept:
        in_specs += [cut, per_pair, cut]
        args += kept
    shapes, specs = [], []
    for kind, spec in outs:
        shapes.append(
            {
                0: jax.ShapeDtypeStruct((2 * BLOCK, D), kind),
                1: jax.ShapeDtypeStruct((pairs_count, 2, 2 * BLOCK), kind),
                2: jax.ShapeDtypeStruct((2, 2 * BLOCK, D), kind),
            }[spec]
        )
        specs.append((cut, per_pair, double)[spec])
    return pl.pallas_call(
        kernel,
        grid=(pairs_count,),
        in_specs=in_specs,
        out_specs=specs,
        out_shape=shapes,
        scratch_shapes=scratch,
        compiler_params=pltpu.CompilerParams(vmem_limit_bytes=48 << 20),
        cost_estimate=SMALL_COST,
    )(*args)


def attend_forward_blocks(s, own, other, bias):
    scratch = [pltpu.VMEM((SEQ_LEN, PAIR), bf16)] * 2
    return call_attention(attend_forward_kernel, s, own, other, bias, (), ((bf16, 0), (f32, 1)), scratch)


def attend_backward_blocks(s, own, other, bias, mixed, totals, grads):
    scratch = [pltpu.VMEM((SEQ_LEN, PAIR), bf16)] * 2 + [pltpu.VMEM((SEQ_LEN, PAIR), f32)] * 2
    outs = ((bf16, 0), (f32, 2), (bf16, 2))
    kept = (mixed, totals, grads)
    return call_attention(attend_backward_kernel, s, own, other, bias, kept, outs, scratch)


def window_bias(s, ids):
    out = []
    for start, width, first in zip(window_starts(s), WINDOWS, query_starts(s)):
        keys = lax.dynamic_slice_in_dim(ids, start, width)
        block = s ^ (2 * (first // BLOCK))
        queries = lax.dynamic_slice_in_dim(ids, block * BLOCK, BLOCK)
        out.append(jnp.where(keys[:, None] == queries[None, :], 0.0, -1e30).astype(f32))
    return tuple(out)


def norm_forward(total):
    center = jnp.mean(total, axis=-1, keepdims=True)
    centered = total - center
    spread = jnp.mean(centered * centered, axis=-1, keepdims=True)
    scale = lax.rsqrt(spread + epsilon)
    return centered * scale, scale


def norm_backward(total, gain, upstream):
    unit, scale = norm_forward(total)
    lifted = upstream * gain
    grad = scale * (
        lifted
        - jnp.mean(lifted, axis=-1, keepdims=True)
        - unit * jnp.mean(lifted * unit, axis=-1, keepdims=True)
    )
    return grad, jnp.sum(upstream * unit, axis=0), jnp.sum(upstream, axis=0)


def column_sum(values):
    return jnp.sum(values.astype(f32), axis=0)


def heads_of(rows):
    return rows.reshape(rows.shape[0], HEADS, HEAD_DIM)


def masked_scores(queries, keys, allowed):
    scores = jnp.einsum("qhd,khd->hqk", queries, keys, preferred_element_type=f32)
    return jnp.where(allowed[None], scores * HEAD_DIM ** (-0.5), -1e30)


def attend_forward(queries, keys, values, allowed):
    scores = masked_scores(heads_of(queries), heads_of(keys), allowed)
    top_score = jnp.max(scores, axis=2, keepdims=True)
    raised = jnp.exp(scores - top_score)
    totals = jnp.sum(raised, axis=2, keepdims=True)
    shares = (raised / totals).astype(bf16)
    mixed = jnp.einsum("hqk,khd->qhd", shares, heads_of(values), preferred_element_type=f32)
    return mixed.astype(bf16).reshape(queries.shape), top_score + jnp.log(totals)


def attend_backward(queries, keys, values, allowed, log_total, grads):
    queries, keys, values, grads = map(heads_of, (queries, keys, values, grads))
    scale = HEAD_DIM ** (-0.5)
    shares = jnp.exp(masked_scores(queries, keys, allowed) - log_total)
    share_grads = jnp.einsum("qhd,khd->hqk", grads, values, preferred_element_type=f32)
    inner_sums = jnp.sum(shares * share_grads, axis=2, keepdims=True)
    score_grads = (shares * (share_grads - inner_sums)).astype(bf16)
    query_grad = jnp.einsum("hqk,khd->qhd", score_grads, keys, preferred_element_type=f32) * scale
    key_grad = jnp.einsum("hqk,qhd->khd", score_grads, queries, preferred_element_type=f32) * scale
    value_grad = jnp.einsum(
        "hqk,qhd->khd", shares.astype(bf16), grads, preferred_element_type=f32
    )
    flat = lambda a: a.reshape(a.shape[0], D)
    return flat(query_grad).astype(bf16), flat(key_grad), flat(value_grad)


def product(rows, weight, tile, finish, outs, by_column=(), tiles=(), transposed=False, sums=0):
    tokens, depth = rows.shape
    width = weight.shape[0 if transposed else 1]

    def kernel(rows_ref, weight_ref, *refs):
        total = (nt_dot if transposed else lambda a, b: jnp.dot(a, b, preferred_element_type=f32))(
            rows_ref[...], weight_ref[...]
        )
        inputs = [r[...] for r in refs[: len(by_column) + len(tiles)]]
        for ref, value in zip(refs[len(inputs) :], finish(total, *inputs)):
            ref[...] = value.astype(ref.dtype)

    cut = pl.BlockSpec((tokens, tile), lambda j: (0, j))
    if transposed:
        weight_spec = pl.BlockSpec((tile, depth), lambda j: (j, 0))
    else:
        weight_spec = pl.BlockSpec((depth, tile), lambda j: (0, j))
    return pl.pallas_call(
        kernel,
        grid=(width // tile,),
        in_specs=[pl.BlockSpec((tokens, depth), lambda j: (0, 0)), weight_spec]
        + [pl.BlockSpec((1, tile), lambda j: (0, j))] * len(by_column)
        + [cut] * len(tiles),
        out_specs=[cut] * len(outs) + [pl.BlockSpec((1, tile), lambda j: (0, j))] * sums,
        out_shape=[jax.ShapeDtypeStruct((tokens, width), kind) for kind in outs]
        + [jax.ShapeDtypeStruct((1, width), f32)] * sums,
        compiler_params=pltpu.CompilerParams(vmem_limit_bytes=48 << 20),
        cost_estimate=SMALL_COST,
    )(rows, in_hbm(weight), *[v.reshape(1, width) for v in by_column], *tiles)


def gelu_parts(total, bias):
    inner = total + bias
    below = 0.5 * (1.0 + lax.erf(inner * (0.5**0.5)))
    slope = below + inner * jnp.exp(-0.5 * inner * inner) * (2 * math.pi) ** -0.5
    return inner * below, slope


def mixed_norm(mixed, weight, stream, bias, gain, shift):
    tokens, width = stream.shape
    tile = 256

    def kernel(mixed_ref, weight_ref, stream_ref, bias_ref, gain_ref, shift_ref, sum_ref, first_ref, low_ref):
        total = jnp.dot(mixed_ref[...], weight_ref[...], preferred_element_type=f32)
        total = stream_ref[...] + (total + bias_ref[...])
        first = norm_forward(total)[0] * gain_ref[...] + shift_ref[...]
        sum_ref[...] = total
        first_ref[...] = first
        low_ref[...] = first.astype(bf16)

    cut = pl.BlockSpec((tile, width), lambda j: (j, 0))
    vector = pl.BlockSpec((1, width), lambda j: (0, 0))
    out = jax.ShapeDtypeStruct((tokens, width), f32)
    return pl.pallas_call(
        kernel,
        grid=(tokens // tile,),
        in_specs=[cut, pl.BlockSpec(weight.shape, lambda j: (0, 0)), cut, vector, vector, vector],
        out_specs=[cut] * 3,
        out_shape=[out, out, jax.ShapeDtypeStruct((tokens, width), bf16)],
        compiler_params=pltpu.CompilerParams(vmem_limit_bytes=48 << 20),
        cost_estimate=SMALL_COST,
    )(mixed, in_hbm(weight), stream, *[v.reshape(1, width) for v in (bias, gain, shift)])


def norm_backward_rows(total, gain, upstream):
    tokens, width = total.shape
    tile = 128

    def kernel(total_ref, gain_ref, up_ref, grad_ref, low_ref, sums_ref):
        unit, scale = norm_forward(total_ref[...])
        up = up_ref[...]
        lifted = up * gain_ref[...]
        grad = scale * (
            lifted
            - jnp.mean(lifted, axis=-1, keepdims=True)
            - unit * jnp.mean(lifted * unit, axis=-1, keepdims=True)
        )
        low = grad.astype(bf16)
        grad_ref[...] = grad
        low_ref[...] = low

        @pl.when(pl.program_id(0) == 0)
        def _():
            sums_ref[...] = jnp.zeros_like(sums_ref)

        for n, value in enumerate((up * unit, up, low.astype(f32))):
            sums_ref[n : n + 1, :] += jnp.sum(value, axis=0, keepdims=True)

    cut = pl.BlockSpec((tile, width), lambda j: (j, 0))
    out = jax.ShapeDtypeStruct((tokens, width), f32)
    return pl.pallas_call(
        kernel,
        grid=(tokens // tile,),
        in_specs=[cut, pl.BlockSpec((1, width), lambda j: (0, 0)), cut],
        out_specs=[cut, cut, pl.BlockSpec((8, width), lambda j: (0, 0))],
        out_shape=[out, jax.ShapeDtypeStruct((tokens, width), bf16), jax.ShapeDtypeStruct((8, width), f32)],
        compiler_params=pltpu.CompilerParams(vmem_limit_bytes=32 << 20),
        cost_estimate=SMALL_COST,
    )(total, gain.reshape(1, width), upstream)


def merged(query_low, own, back):
    tokens = query_low.shape[0]
    tile = D // 2

    def kernel(query_ref, own_ref, back_ref, low_ref, sum_ref):
        def put(low):
            low_ref[...] = low
            sum_ref[...] = jnp.sum(low.astype(f32), axis=0, keepdims=True)

        @pl.when(pl.program_id(0) < 2)
        def _():
            put(query_ref[...])

        @pl.when(pl.program_id(0) >= 2)
        def _():
            put((own_ref[0] + back_ref[0].astype(f32)).astype(bf16))

    part = pl.BlockSpec((1, tokens, tile), lambda j: (jnp.maximum(j - 2, 0) // 2, 0, jnp.maximum(j - 2, 0) % 2))
    return pl.pallas_call(
        kernel,
        grid=(6,),
        in_specs=[pl.BlockSpec((tokens, tile), lambda j: (0, jnp.minimum(j, 1))), part, part],
        out_specs=[pl.BlockSpec((tokens, tile), lambda j: (0, j)), pl.BlockSpec((1, tile), lambda j: (0, j))],
        out_shape=[jax.ShapeDtypeStruct((tokens, 3 * D), bf16), jax.ShapeDtypeStruct((1, 3 * D), f32)],
        compiler_params=pltpu.CompilerParams(vmem_limit_bytes=32 << 20),
        cost_estimate=SMALL_COST,
    )(query_low, own, back)


SMALL = 8


def staged_body(tokens, doc_lengths, cotangent, *shards):
    (
        query_weight,
        key_weight,
        value_weight,
        mix_weight,
        query_bias,
        value_bias,
        mix_bias,
        first_gain,
        first_shift,
        inner_weight,
        inner_bias,
        outer_weight,
        outer_bias,
        second_gain,
        second_shift,
    ) = shards
    layer_count = query_weight.shape[0]
    devices = 32
    length = SEQ_LEN // 4
    rows_held, inner_held = D // devices, FF // devices
    seq = lax.axis_index("seq")
    row = seq // 2
    coords = coordinates()
    z, y, x, c = coords[0], coords[1], coords[2], coords[3]
    place_of = seq.reshape(1).astype(jnp.int32)

    def split_rows(both):
        both = both.reshape(2, length, D)
        return pick(both, row, 0), pick(both, 1 - row, 0)

    token_kept, token_left = split_rows(tokens)
    upstream_kept, upstream_left = split_rows(cotangent)

    def unit_a(layer):
        r = rows_held
        parts = [w[layer] for w in (query_weight, key_weight, value_weight)]
        rows, outs = [(r * n, r * (n + 1), 0, n) for n in range(3)], [(r, 3 * D)]
        if layer:
            parts, rows, outs = parts + [mix_weight[layer]], rows + [(3 * r, 4 * r, 1, 0)], outs + [(r, D)]
        return GatherUnit(coords, jnp.concatenate(parts), outs, rows)

    def unit_i(layer):
        r, inner = rows_held, inner_weight[layer]
        parts = [inner[:, D * n : D * (n + 1)] for n in range(4)]
        rows, outs = [(r * n, r * (n + 1), 0, n) for n in range(4)], [(r, FF)]
        if not layer:
            parts, rows, outs = parts + [mix_weight[layer]], rows + [(4 * r, 5 * r, 1, 0)], outs + [(r, D)]
        return GatherUnit(coords, jnp.concatenate(parts), outs, rows)

    def unit_o(layer):
        return GatherUnit(coords, outer_weight[layer], [(inner_held, D)], [(0, inner_held, 0, 0)])

    units = [[make(layer) for make in (unit_a, unit_i, unit_o)] for layer in range(layer_count)]

    small_vectors = (
        query_bias,
        value_bias,
        mix_bias,
        first_gain,
        first_shift,
        outer_bias,
        second_gain,
        second_shift,
    )
    vector_count = SMALL * layer_count
    small_held = vector_count * rows_held
    mine = jnp.concatenate(
        [jnp.concatenate([v[layer] for v in small_vectors]) for layer in range(layer_count)]
        + [inner_bias.reshape(-1)]
    )
    held = mine.shape[0]
    padded = jnp.pad(mine, (0, 1024 - held)).reshape(8, 128)

    u = [unit for layer_units in units for unit in layer_units]
    padded = phase(padded, u[0])
    token_got = send(token_left, TO_X)
    every = jnp.roll(jnp.stack([padded] + [send(padded, TO_Z[4 - k]) for k in (1, 2, 3)]), z, axis=0)

    lengths = pick(doc_lengths.reshape(2, NDOC), row, 0)
    places = lax.iota(jnp.int32, SEQ_LEN)
    segment = jnp.sum((places[:, None] >= jnp.cumsum(lengths)[None, :]).astype(jnp.int32), axis=1)
    bias = window_bias(seq, jnp.where(segment == NDOC - 1, NDOC + places, segment))
    order, order_z = block_order(coords), block_order(coords, True)
    matrices = order_matrices(order)

    token_got, every = phase((token_got, every), u[0], u[1])
    every, upstream_left = lax.optimization_barrier((every, upstream_left))
    upstream_got = send(upstream_left, TO_X)
    every = by_place(every, send(every, TO_Y), y, 1)
    every, bias, upstream_got = phase((every, bias, upstream_got), u[0], settle=[u[1]])
    every = by_place(every, send(every, TO_X), x, 2)
    every, matrices = phase((every, matrices), u[0], u[1])
    every = by_place(every, send(every, TO_CORE), c, 3)
    every = every.reshape(devices, 1024)[:, :held].astype(f32)
    small_all = (
        every[:, :small_held]
        .reshape(devices, vector_count, rows_held)
        .transpose(1, 0, 2)
        .reshape(layer_count, SMALL, D)
    )
    wide_all = (
        every[:, small_held:]
        .reshape(devices, layer_count, inner_held)
        .transpose(1, 0, 2)
        .reshape(layer_count, FF)
    )
    stream = jnp.concatenate([token_kept, token_got]).astype(f32)
    stream, small_all, wide_all = phase((stream, small_all, wide_all), u[0], u[1], u[2])
    saved, active_gots = [], []
    for layer in range(layer_count):
        a_unit, i_unit, o_unit = units[layer]
        next_a, next_i, next_o = units[layer + 1] if layer + 1 < layer_count else (None,) * 3
        q_bias, v_bias, m_bias, gain1, shift1, o_bias, gain2, shift2 = [small_all[layer, n] for n in range(SMALL)]
        w_three, *w_rest = a_unit.result()
        w_three = w_three.reshape(D, 3 * D)
        stream_low = stream.astype(bf16)
        three_bias = jnp.concatenate([q_bias, jnp.zeros_like(q_bias), v_bias])
        (three,) = product(stream_low, w_three, 1024, lambda total, b: (total + b,), (bf16,), (three_bias,))
        if next_a:
            three = phase(three, i_unit, o_unit, next_a)
        else:
            three = phase(three, i_unit, settle=[o_unit])
        three_got = send(three, TO_CORE)
        (left_stream,) = selected(matrices, tie(stream_low, three))
        three, left_stream = lax.optimization_barrier((three, left_stream))
        left_stream = (left_stream[0], send(left_stream[1], TO_CORE))
        mixed, totals = attend_forward_blocks(place_of, three, three_got, bias)
        if next_a:
            mixed, totals, left_stream = phase(
                (mixed, totals, left_stream), i_unit, o_unit, next_a, next_i
            )
        else:
            mixed, totals, left_stream, active_gots = phase(
                (mixed, totals, left_stream, active_gots), i_unit, o_unit
            )
        w_inner, *w_more = i_unit.result()
        (w_mix,) = w_rest + w_more
        w_inner, w_mix = w_inner.reshape(D, FF), w_mix.reshape(D, D)
        first_sum, first, first_low = mixed_norm(mixed, w_mix, stream, m_bias, gain1, shift1)
        if next_a:
            first_low = phase(first_low, o_unit, next_a, next_i)
        else:
            first_low = phase(first_low, o_unit)
        left_mix, left_first = selected(matrices, mixed, first_low)
        first_low, left_mix, left_first = lax.optimization_barrier((first_low, left_mix, left_first))
        left_mix, left_first = [(m, send(t, TO_CORE)) for m, t in (left_mix, left_first)]
        active, slope = product(first_low, w_inner, 1024, gelu_parts, (bf16, bf16), (wide_all[layer],))
        if next_a:
            active, slope, left_mix, left_first = phase(
                (active, slope, left_mix, left_first), o_unit, next_a, next_o, settle=[next_i]
            )
        else:
            active, slope, left_mix, left_first = phase((active, slope, left_mix, left_first), o_unit)
        (w_outer,) = o_unit.result()
        active_got = send(tie(active, w_outer), TO_CORE)
        w_outer = w_outer.reshape(FF, D)
        (second_sum,) = product(
            active, w_outer, 256, lambda total, b, f: (f + (total + b),), (f32,), (o_bias,), (first,)
        )
        if not next_a:
            second_sum, active_got = lax.optimization_barrier((second_sum, active_got))
        active_gots.append(active_got)
        stream = norm_forward(second_sum)[0] * gain2 + shift2
        if next_a:
            stream = phase(stream, next_a, next_i, next_o)
        saved.append(
            (
                (w_three, w_mix, w_inner, w_outer, gain1, gain2),
                (three, three_got, totals, mixed),
                (first_sum, slope, second_sum),
                (left_stream, left_mix, left_first, active),
            )
        )

    def both_rows(kept, got):
        got = got.astype(f32)
        return jnp.where(row == 0, jnp.stack([kept, got]), jnp.stack([got, kept])).reshape(tokens.shape)

    output = stream
    output_got = send(output[length:].astype(bf16), TO_X)

    upstream = jnp.concatenate([upstream_kept, upstream_got]).astype(f32)
    small_grads, wide_grads = [None] * layer_count, [None] * layer_count
    sums = [None] * layer_count
    before = None
    for layer in reversed(range(layer_count)):
        weights, kept, rest, lefts = saved[layer]
        w_three, w_mix, w_inner, w_outer, gain1, gain2 = weights
        three, three_got, totals, mixed = kept
        first_sum, slope, second_sum = rest
        left_stream, left_mix, left_first, active = lefts
        left_active = (active, active_gots[layer])

        def with_sum(total, slopes):
            low = (total * slopes).astype(bf16)
            return low, jnp.sum(low.astype(f32), axis=0, keepdims=True)

        second_grad, second_low, second_sums = norm_backward_rows(second_sum, gain2, upstream)
        second_got = send(second_low, TO_CORE)
        inner_low, inner_sum = product(
            second_low, w_outer, 1024, with_sum, (bf16,), (), (slope,), transposed=True, sums=1
        )
        if before:
            inner_low, second_got = phase((inner_low, second_got), before.o[0], before.i, before.a)
        else:
            inner_low, second_got = lax.optimization_barrier((inner_low, second_got))
        inner_got = send(inner_low, TO_CORE)
        second_pair = (second_low, second_got)
        if before:
            by_z, by_far = wide_terms_split(order, order_z, left_active, second_pair)
            o_sums = (SumUnit(by_z, Z_FIRST), SumUnit(by_far))
            second_grad, inner_low, inner_got = phase(
                (second_grad, inner_low, inner_got), *o_sums, before.a, before.i, settle=before.o
            )
        else:
            o_sums = (SumUnit(wide_terms_of(order, left_active, second_pair)),)
            second_grad, inner_low, inner_got, output_got = phase(
                (second_grad, inner_low, inner_got, output_got), *o_sums
            )
        (first_grad,) = product(
            inner_low, w_inner, 512, lambda total, g: (g + total,), (f32,), (), (second_grad,), transposed=True
        )
        first_sum_grad, branch_low, first_sums = norm_backward_rows(first_sum, gain1, first_grad)
        branch_got = send(branch_low, TO_CORE)
        (mixed_grad,) = product(branch_low, w_mix, 512, lambda total: (total,), (bf16,), transposed=True)
        i_sum = SumUnit(weight_terms((left_first, tie((inner_low, inner_got), mixed_grad), FF)))
        if before:
            mixed_grad = phase(mixed_grad, i_sum, *o_sums, before.a, settle=[before.i])
        else:
            mixed_grad = phase(mixed_grad, i_sum, settle=o_sums)
        query_low, own_grads, sent_grads = attend_backward_blocks(
            place_of, in_hbm(three), in_hbm(three_got), bias, in_hbm(mixed), in_hbm(totals), mixed_grad
        )
        grads_back = send(sent_grads, TO_CORE)
        if before:
            query_low, own_grads = phase((query_low, own_grads), i_sum, *o_sums, before.a)
        else:
            query_low, own_grads = phase((query_low, own_grads), *o_sums, settle=[i_sum])
        low, low_sums = merged(query_low, own_grads, grads_back)
        low, branch_got = lax.optimization_barrier((low, branch_got))
        low_got = send(low, TO_CORE)
        if layer:
            (upstream,) = product(
                low, w_three, 512, lambda total, g: (g + total,), (f32,), (), (first_sum_grad,), transposed=True
            )
            mix_pair = (left_mix, (branch_low, branch_got), D)
            a_sum = SumUnit(weight_terms((left_stream, tie((low, low_got), upstream), 3 * D), mix_pair))
        else:
            mix_pair = (left_mix, (branch_low, branch_got), D)
            a_sum = SumUnit(weight_terms((left_stream, (low, low_got), 3 * D), mix_pair))
            low, low_sums = phase((low, low_sums), a_sum, settle=[i_sum, *o_sums, before.a] if before else [i_sum])
            (upstream,) = product(
                low, w_three, 512, lambda total, g: (g + total,), (f32,), (), (first_sum_grad,), transposed=True
            )
        small_grads[layer] = jnp.stack(
            [
                low_sums[0, :D],
                low_sums[0, 2 * D :],
                first_sums[2],
                first_sums[0],
                first_sums[1],
                second_sums[2],
                second_sums[0],
                second_sums[1],
            ]
        )
        wide_grads[layer] = inner_sum[0]
        if layer:
            upstream, small_grads[layer] = phase((upstream, small_grads[layer]), *o_sums, i_sum, settle=[a_sum])
        sums[layer] = before = Sums(o_sums, i_sum, a_sum)

    small_terms = (
        jnp.stack(small_grads)
        .reshape(vector_count, devices, rows_held)
        .transpose(1, 0, 2)
        .reshape(devices, small_held)
    )
    wide_terms = (
        jnp.stack(wide_grads)
        .reshape(layer_count, devices, inner_held)
        .transpose(1, 0, 2)
        .reshape(devices, layer_count * inner_held)
    )
    terms = jnp.pad(jnp.concatenate([small_terms, wide_terms], axis=1), ((0, 0), (0, 1024 - held)))
    chosen = (order[:, None] == lax.iota(jnp.int32, devices)[None, :]).astype(f32)
    terms = jnp.dot(chosen, terms, precision=lax.Precision.HIGHEST).reshape(2, 128, 128)
    terms = (terms[0] + send(terms[1].astype(bf16), TO_CORE).astype(f32)).astype(bf16)
    small_sum = SumUnit((terms[:64], terms[64:]))

    phase((), small_sum)
    last = sums[0]
    done = [unit for layer in range(1, layer_count) for unit in (*sums[layer].o, sums[layer].i, sums[layer].a)]
    upstream, output_got = phase((upstream, output_got), last.a, last.i, *last.o, small_sum, *done)
    token_left = upstream[length:].astype(bf16)
    upstream, token_left = phase((upstream, token_left), last.a, last.i, *last.o, small_sum)
    token_back = send(token_left, TO_X)
    upstream, token_back = phase((upstream, token_back), last.a, last.i, small_sum)
    phase((), last.a, small_sum)
    own_terms = small_sum.kept.reshape(-1)[:held]
    small_own = own_terms[:small_held].reshape(layer_count, SMALL, rows_held)
    wide_own = own_terms[small_held:].reshape(layer_count, inner_held)
    for layer in range(layer_count):
        for unit in (*sums[layer].o, sums[layer].i, sums[layer].a):
            while unit.step < 5:
                phase((), unit)
    o_all = jnp.stack([jnp.concatenate([unit.kept for unit in group.o], axis=1) for group in sums])
    i_all, a_all = [jnp.stack([group[n].kept for group in sums]) for n in (1, 2)]
    return (
        both_rows(output[:length], output_got),
        both_rows(upstream[:length], token_back),
        a_all[:, :, :D],
        a_all[:, :, D : 2 * D],
        a_all[:, :, 2 * D : 3 * D],
        a_all[:, :, 3 * D :],
        small_own[:, 0],
        small_own[:, 1],
        small_own[:, 2],
        small_own[:, 3],
        small_own[:, 4],
        i_all,
        wide_own,
        o_all,
        small_own[:, 5],
        small_own[:, 6],
        small_own[:, 7],
    )


def plain_body(fsdp_size, seq_size):
    half = seq_size // 2
    device_count = fsdp_size * seq_size
    across = [(i, (i + half) % seq_size) for i in range(seq_size)]
    groups = [[m * half + j for j in range(half)] for m in range(2)]
    length = SEQ_LEN // seq_size

    def gather_siblings(rows):
        return lax.all_gather(rows, "seq", axis_index_groups=groups)

    def scatter_siblings(own_order):
        return lax.psum_scatter(own_order, "seq", axis_index_groups=groups)

    def body(tokens, doc_lengths, cotangent, *shards):
        (
            query_weight,
            key_weight,
            value_weight,
            mix_weight,
            query_bias,
            value_bias,
            mix_bias,
            first_gain,
            first_shift,
            inner_weight,
            inner_bias,
            outer_weight,
            outer_bias,
            second_gain,
            second_shift,
        ) = shards
        layer_count = query_weight.shape[0]
        seq = lax.axis_index("seq")
        row = seq // half
        rows_held = D // device_count
        inner_held = FF // device_count

        def vector_rows(small, wide):
            return jnp.concatenate(
                [jnp.concatenate([v[layer] for v in small]) for layer in range(layer_count)]
                + [wide.reshape(-1)]
            )

        small_vectors = (
            query_bias,
            value_bias,
            mix_bias,
            first_gain,
            first_shift,
            outer_bias,
            second_gain,
            second_shift,
        )
        vector_count = len(small_vectors) * layer_count
        mine = vector_rows(small_vectors, inner_bias)
        held = mine.shape[0]
        every = lax.all_gather(mine, AXES)
        every = every.astype(f32)
        small_held = vector_count * rows_held
        small_all = (
            every[:, :small_held]
            .reshape(device_count, vector_count, rows_held)
            .transpose(1, 0, 2)
            .reshape(layer_count, len(small_vectors), D)
        )
        wide_all = (
            every[:, small_held:]
            .reshape(device_count, layer_count, inner_held)
            .transpose(1, 0, 2)
            .reshape(layer_count, FF)
        )

        def whole_weights(layer):
            weights = (query_weight, key_weight, value_weight, mix_weight, inner_weight, outer_weight)
            return [lax.all_gather(w[layer], AXES, axis=0, tiled=True) for w in weights]

        def own_row(both_rows):
            kept = pick(both_rows, row, 0)
            return jnp.concatenate(
                [kept, lax.ppermute(pick(both_rows, 1 - row, 0), "seq", across)]
            )

        def both_rows(values):
            kept = values[:length]
            other = lax.ppermute(values[length:].astype(bf16), "seq", across).astype(f32)
            return jnp.where(row == 0, jnp.stack([kept, other]), jnp.stack([other, kept]))

        stream_start = own_row(tokens.reshape(2, length, D))
        upstream_start = own_row(cotangent.reshape(2, length, D))

        lengths = pick(doc_lengths.reshape(2, NDOC), row, 0)
        bounds = jnp.cumsum(lengths)
        within = lax.iota(jnp.int32, length)

        def positions(s):
            return jnp.concatenate([s * length + within, (s + half) % seq_size * length + within])

        def segments(places):
            return jnp.sum((places[:, None] >= bounds[None, :]).astype(jnp.int32), axis=1)

        query_places = positions(seq)
        key_places = jnp.concatenate([positions(row * half + j) for j in range(half)])
        query_segment, key_segment = segments(query_places), segments(key_places)
        allowed = (
            (query_segment[:, None] == key_segment[None, :]) & (key_segment[None, :] != NDOC - 1)
        ) | (query_places[:, None] == key_places[None, :])

        stream = stream_start.astype(f32)
        saved = []
        for layer in range(layer_count):
            q_bias, v_bias, m_bias, gain1, shift1, o_bias, gain2, shift2 = [
                small_all[layer, n] for n in range(len(small_vectors))
            ]
            w_query, w_key, w_value, w_mix, w_inner, w_outer = whole_weights(layer)
            stream_low = stream.astype(bf16)
            queries = (dot(stream_low, w_query) + q_bias).astype(bf16)
            key_rows = dot(stream_low, w_key).astype(bf16)
            values = (dot(stream_low, w_value) + v_bias).astype(bf16)
            all_keys = gather_siblings(key_rows).reshape(SEQ_LEN, D)
            all_values = gather_siblings(values).reshape(SEQ_LEN, D)
            mixed, log_total = attend_forward(queries, all_keys, all_values, allowed)
            first_sum = stream + (dot(mixed, w_mix) + m_bias)
            first = norm_forward(first_sum)[0] * gain1 + shift1
            first_low = first.astype(bf16)
            inner = dot(first_low, w_inner) + wide_all[layer]
            below = 0.5 * (1.0 + lax.erf(inner * (0.5**0.5)))
            active = (inner * below).astype(bf16)
            slope = (below + inner * jnp.exp(-0.5 * inner * inner) * (2 * math.pi) ** -0.5).astype(
                bf16
            )
            second_sum = first + (dot(active, w_outer) + o_bias)
            stream = norm_forward(second_sum)[0] * gain2 + shift2
            saved.append(
                (
                    (w_query, w_key, w_value, w_mix, w_inner, w_outer, gain1, gain2),
                    (stream_low, queries, all_keys, all_values, log_total, mixed),
                    (first_sum, first_low, slope, active, second_sum),
                )
            )
        activations = both_rows(stream)

        upstream = upstream_start.astype(f32)
        small_grads = [None] * layer_count
        wide_grads = [None] * layer_count
        results = [None] * layer_count

        def reduced(grads):
            return [lax.psum_scatter(g, AXES, scatter_dimension=0, tiled=True) for g in grads]

        for layer in reversed(range(layer_count)):
            (w_query, w_key, w_value, w_mix, w_inner, w_outer, gain1, gain2), kept, rest = saved[layer]
            stream_low, queries, all_keys, all_values, log_total, mixed = kept
            first_sum, first_low, slope, active, second_sum = rest
            second_grad, gain2_grad, shift2_grad = norm_backward(second_sum, gain2, upstream)
            second_low = second_grad.astype(bf16)
            (outer_grad,) = reduced([contract_rows(active, second_low)])
            inner_low = (contract_cols(second_low, w_outer) * slope).astype(bf16)
            (inner_grad,) = reduced([contract_rows(first_low, inner_low)])
            first_grad = second_grad + contract_cols(inner_low, w_inner)
            first_sum_grad, gain1_grad, shift1_grad = norm_backward(first_sum, gain1, first_grad)
            branch_low = first_sum_grad.astype(bf16)
            mix_terms = contract_rows(mixed, branch_low)
            mixed_grad = contract_cols(branch_low, w_mix).astype(bf16)
            query_low, key_terms, value_terms = attend_backward(
                queries, all_keys, all_values, allowed, log_total, mixed_grad
            )
            n = 2 * length
            key_low = scatter_siblings(key_terms.reshape(half, n, D)).astype(bf16)
            value_low = scatter_siblings(value_terms.reshape(half, n, D)).astype(bf16)
            value_grad, mix_grad = reduced([contract_rows(stream_low, value_low), mix_terms])
            query_grad, key_grad = reduced(
                [contract_rows(stream_low, query_low), contract_rows(stream_low, key_low)]
            )
            upstream = (
                first_sum_grad
                + contract_cols(query_low, w_query)
                + contract_cols(key_low, w_key)
                + contract_cols(value_low, w_value)
            )
            small_grads[layer] = jnp.stack(
                [
                    column_sum(query_low),
                    column_sum(value_low),
                    column_sum(branch_low),
                    gain1_grad,
                    shift1_grad,
                    column_sum(second_low),
                    gain2_grad,
                    shift2_grad,
                ]
            )
            wide_grads[layer] = column_sum(inner_low)
            results[layer] = (query_grad, key_grad, value_grad, mix_grad, inner_grad, outer_grad)
        token_grad = both_rows(upstream)

        small_terms = (
            jnp.stack(small_grads)
            .reshape(vector_count, device_count, rows_held)
            .transpose(1, 0, 2)
            .reshape(device_count, small_held)
        )
        wide_terms = (
            jnp.stack(wide_grads)
            .reshape(layer_count, device_count, inner_held)
            .transpose(1, 0, 2)
            .reshape(device_count, layer_count * inner_held)
        )
        terms = jnp.concatenate([small_terms, wide_terms], axis=1)
        own_terms = lax.psum_scatter(terms, AXES, scatter_dimension=0, tiled=False)
        small_own = own_terms[:small_held].reshape(layer_count, len(small_vectors), rows_held)
        wide_own = own_terms[small_held:].reshape(layer_count, inner_held)
        query_g, key_g, value_g, mix_g, inner_g, outer_g = [
            jnp.stack([results[layer][n] for layer in range(layer_count)]) for n in range(6)
        ]
        return (
            activations.reshape(tokens.shape),
            token_grad.reshape(tokens.shape),
            query_g,
            key_g,
            value_g,
            mix_g,
            small_own[:, 0],
            small_own[:, 1],
            small_own[:, 2],
            small_own[:, 3],
            small_own[:, 4],
            inner_g,
            wide_own,
            outer_g,
            small_own[:, 5],
            small_own[:, 6],
            small_own[:, 7],
        )

    return body


def solution(mesh):
    tokens = P(None, "fsdp", "seq", None)
    matrix, vector = P(None, AXES, None), P(None, AXES)
    in_specs = (tokens, P(None, "fsdp", None), tokens) + (matrix,) * 4 + (vector,) * 5
    in_specs += (matrix, vector, matrix, vector, vector, vector)
    out_specs = (tokens, tokens) + (matrix,) * 4 + (vector,) * 5
    out_specs += (matrix, vector, matrix, vector, vector, vector)
    sizes = (mesh.shape["fsdp"], mesh.shape["seq"])
    body = staged_body if sizes == (8, 4) else plain_body(*sizes)
    return jax.shard_map(body, mesh=mesh, in_specs=in_specs, out_specs=out_specs, check_vma=False)
```
